32 devices in a mesh: seq: 4 (over y, x), shard: 8 (over z, core).
Axes of the slice: x: 2, y: 2, z: 4, core: 2. Of those that a mesh axis runs over, the one named last changes fastest.
Arguments:
- tokens: bfloat16 [8, 1024, 768], P('shard', 'seq'), may hold values from -6 to 6
- lengths: int32 [8], P('shard'), may hold values from 128 to 1024, as said below
- w_qkv: bfloat16 [768, 2304], P('shard'), may hold values from -0.21875 to 0.21875
- q_bias: bfloat16 [768], P('shard'), may hold values from -3 to 3
- v_bias: bfloat16 [768], P('shard'), may hold values from -3 to 3
- w_out: bfloat16 [768, 768], P('shard'), may hold values from -1.25 to 1.25
- out_bias: bfloat16 [768], P('shard'), may hold values from -3 to 3
- gain_one: bfloat16 [768], P('shard'), may hold values from 0.5 to 1.5
- shift_one: bfloat16 [768], P('shard'), may hold values from -3 to 3
- w_up: bfloat16 [768, 3072], P('shard'), may hold values from -0.21875 to 0.21875
- up_bias: bfloat16 [3072], P('shard'), may hold values from -3 to 3
- w_down: bfloat16 [3072, 768], P('shard'), may hold values from -0.109375 to 0.109375
- down_bias: bfloat16 [768], P('shard'), may hold values from -3 to 3
- gain_two: bfloat16 [768], P('shard'), may hold values from 0.5 to 1.5
- shift_two: bfloat16 [768], P('shard'), may hold values from -3 to 3
- cotangent: bfloat16 [8, 1024, 768], P('shard', 'seq'), may hold values from -6 to 6
Outputs:
- output: bfloat16 [8, 1024, 768], P('shard', 'seq')
- grad_tokens: bfloat16 [8, 1024, 768], P('shard', 'seq')
- grad_w_qkv: float32 [768, 2304], P('shard')
- grad_q_bias: float32 [768], P('shard')
- grad_v_bias: float32 [768], P('shard')
- grad_w_out: float32 [768, 768], P('shard')
- grad_out_bias: float32 [768], P('shard')
- grad_gain_one: float32 [768], P('shard')
- grad_shift_one: float32 [768], P('shard')
- grad_w_up: float32 [768, 3072], P('shard')
- grad_up_bias: float32 [3072], P('shard')
- grad_w_down: float32 [3072, 768], P('shard')
- grad_down_bias: float32 [768], P('shard')
- grad_gain_two: float32 [768], P('shard')
- grad_shift_two: float32 [768], P('shard')
The draws below stay inside these ranges and needn't reach their ends.
Inputs may be any that keep to these rules, and one draw needn't show every extreme that they name: `lengths`: each sequence has from 128 to 1024 valid positions; in every draw some sequence has exactly 1024 and another exactly 128.
All inputs are finite; a program needn't handle non-finite values.
Results may differ from the reference program's by a relative error of at most 0.015.
Values may be sent and summed in bfloat16 or wider, within the bound.
No kernel may reach another device: no remote copies, remote signals or barrier semaphores. Data moves between devices by JAX's collectives and lax.ppermute only.
A program may use at most 128 MiB of HBM per device.

```python
import jax
import jax.numpy as jnp
from jax import lax

D = 768
HEAD_DIM = 64
FF = 3072
LEN = 1024
SEQS = 8


def draw_lengths(key, part):
    key_values, key_full, key_short = jax.random.split(key, 3)
    values = jax.random.randint(key_values, (SEQS,), LEN // 8, LEN + 1)
    full_at = jax.random.randint(key_full, (), 0, SEQS)
    short_at = (full_at + jax.random.randint(key_short, (), 1, SEQS)) % SEQS
    values = values.at[full_at].set(LEN)
    values = values.at[short_at].set(LEN // 8)
    return values.astype(jnp.int32)


def levels(stream_key, dims, cuts, smallest, top_value):
    level = 1.0
    for position, blocks in cuts:
        draws = jax.random.uniform(jax.random.fold_in(jax.random.fold_in(stream_key, 6), position), (blocks,), jnp.float32, smallest / len(cuts), top_value / len(cuts))
        level = level * jnp.repeat(jnp.exp(draws), dims[position] // blocks).reshape((-1,) + (1,) * (len(dims) - 1 - position))
    return level


def scatter_about(rng, shape, deviation, most, cuts=(), held_as=jnp.bfloat16):
    drawn = deviation * jax.random.normal(rng, shape, jnp.float32)
    if cuts:
        drawn = drawn * levels(rng, shape, cuts, -0.22, 0.18)
    return jnp.clip(drawn, -most, most).astype(held_as)


def setup_inputs(seed: int = 0) -> dict:
    splits = jax.random.split(jax.random.key(seed), 17)
    tokens = scatter_about(splits[0], (SEQS, LEN, D), 1.0, 6.0, ((0, 8), (1, 4)))
    lengths = draw_lengths(jax.random.fold_in(splits[16], 71), 0)
    w_qkv = scatter_about(splits[2], (D, 3 * D), D ** -0.5, 0.21875, ((0, 8),))
    q_bias = scatter_about(splits[3], (D,), 0.5, 3.0, ((0, 8),))
    v_bias = scatter_about(splits[4], (D,), 0.5, 3.0, ((0, 8),))
    w_out = scatter_about(splits[5], (D, D), (D // 32) ** -0.5, 1.25, ((0, 8),))
    out_bias = scatter_about(splits[6], (D,), 0.5, 3.0, ((0, 8),))
    gain_one = jnp.clip(1.0 + 0.1 * jax.random.normal(splits[7], (D,), jnp.float32), 0.5, 1.5).astype(jnp.bfloat16)
    shift_one = scatter_about(splits[8], (D,), 0.5, 3.0, ((0, 8),))
    w_up = scatter_about(splits[9], (D, FF), D ** -0.5, 0.21875, ((0, 8),))
    up_bias = scatter_about(splits[10], (FF,), 0.5, 3.0, ((0, 8),))
    w_down = scatter_about(splits[11], (FF, D), FF ** -0.5, 0.109375, ((0, 8),))
    down_bias = scatter_about(splits[12], (D,), 0.5, 3.0, ((0, 8),))
    gain_two = jnp.clip(1.0 + 0.1 * jax.random.normal(splits[13], (D,), jnp.float32), 0.5, 1.5).astype(jnp.bfloat16)
    shift_two = scatter_about(splits[14], (D,), 0.5, 3.0, ((0, 8),))
    cotangent = scatter_about(splits[15], (SEQS, LEN, D), 1.0, 6.0, ((0, 8), (1, 4)))
    return dict(tokens=tokens, lengths=lengths, w_qkv=w_qkv, q_bias=q_bias, v_bias=v_bias, w_out=w_out, out_bias=out_bias, gain_one=gain_one, shift_one=shift_one, w_up=w_up, up_bias=up_bias, w_down=w_down, down_bias=down_bias, gain_two=gain_two, shift_two=shift_two, cotangent=cotangent)


epsilon = 1e-05
masked_score = -1000000000.0

@jax.custom_vjp
def low(v):
    return lax.optimization_barrier(v.astype(jnp.bfloat16)).astype(jnp.float32)

@jax.custom_vjp
def low_back(v):
    return v

def low_keep(v):
    return (low(v), None)

def low_pass(kept, grad):
    return (grad,)

def back_keep(v):
    return (v, None)

def back_low(kept, grad):
    return (low(grad),)
low.defvjp(low_keep, low_pass)
low_back.defvjp(back_keep, back_low)

def matmul_high(left, right):
    return jnp.dot(left, right, precision=lax.Precision.HIGHEST)

def layer_norm(values, gain, shift):
    center = values - lax.optimization_barrier(jnp.mean(values, axis=-1, keepdims=True))
    spread = lax.optimization_barrier(jnp.mean(center * center, axis=-1, keepdims=True))
    return center * lax.rsqrt(spread + epsilon) * gain + shift

def sequence_forward(params, sequence, length):
    w_qkv, q_bias, v_bias, w_out, out_bias, gain_one, shift_one, w_up, up_bias, w_down, down_bias, gain_two, shift_two = params
    head_count = D // HEAD_DIM
    score_scale = HEAD_DIM ** (-0.5)
    joined_bias = jnp.concatenate([q_bias, jnp.zeros((D,), jnp.float32), v_bias])
    projected = matmul_high(low(sequence), w_qkv) + joined_bias
    qkv = low(low_back(projected)).reshape(LEN, 3, head_count, HEAD_DIM)
    queries, keys_all, values_all = (qkv[:, 0], qkv[:, 1], qkv[:, 2])
    scores = jnp.einsum('qhd,khd->hqk', queries, keys_all, precision=lax.Precision.HIGHEST) * score_scale
    scores = low_back(scores)
    key_valid = jnp.arange(LEN) < length
    scores = jnp.where(key_valid[None, None, :], scores, masked_score)
    attn_probs = jax.nn.softmax(scores, axis=-1)
    context = jnp.einsum('hqk,khd->qhd', low(attn_probs), values_all, precision=lax.Precision.HIGHEST)
    context = low(low_back(context)).reshape(LEN, D)
    residual_one = sequence + low_back(matmul_high(context, w_out)) + out_bias
    normed_one = layer_norm(residual_one, gain_one, shift_one)
    up_rows = low_back(matmul_high(low(normed_one), w_up)) + up_bias
    active = jax.nn.gelu(up_rows, approximate=False)
    residual_two = normed_one + low_back(matmul_high(low(active), w_down)) + down_bias
    return layer_norm(residual_two, gain_two, shift_two)

def reference(tokens, lengths, w_qkv, q_bias, v_bias, w_out, out_bias, gain_one, shift_one, w_up, up_bias, w_down, down_bias, gain_two, shift_two, cotangent):
    params = tuple((weight.astype(jnp.float32) for weight in (w_qkv, q_bias, v_bias, w_out, out_bias, gain_one, shift_one, w_up, up_bias, w_down, down_bias, gain_two, shift_two)))

    def one_sequence(accum, seq_item):
        sequence, length, seq_grad = seq_item
        result, pull = jax.vjp(lambda weights, values: sequence_forward(weights, values, length), params, sequence)
        grad_params, grad_values = pull(seq_grad)
        accum = jax.tree.map(lambda left, right: left + right, accum, grad_params)
        return (accum, (result.astype(jnp.bfloat16), grad_values.astype(jnp.bfloat16)))
    zeros_tree = tuple((jnp.zeros(weight.shape, jnp.float32) for weight in params))
    grads, (output, grad_tokens) = lax.scan(one_sequence, zeros_tree, (tokens.astype(jnp.float32), lengths, cotangent.astype(jnp.float32)))
    return (output, grad_tokens, grads[0], grads[1], grads[2], grads[3], grads[4], grads[5], grads[6], grads[7], grads[8], grads[9], grads[10], grads[11], grads[12])
```

```python
import jax
import jax.numpy as jnp
from jax import lax
from jax.experimental import pallas as pl
from jax.experimental.pallas import tpu as pltpu
from jax.sharding import PartitionSpec as P

HEAD_DIM = 64
LEN = 1024
Q_BLOCK = 512


epsilon = 1e-05
masked_score = -1000000000.0


def layer_norm(values, gain, shift):
    center = values - jnp.mean(values, axis=-1, keepdims=True)
    spread = jnp.mean(center * center, axis=-1, keepdims=True)
    return center * lax.rsqrt(spread + epsilon) * gain + shift


def gelu_exact(values):
    return jax.nn.gelu(values, approximate=False)


def contract_rows(left, right):
    return lax.dot_general(
        left, right, (((0,), (0,)), ((), ())), preferred_element_type=jnp.float32
    )


def contract_cols(left, right):
    return lax.dot_general(
        left, right, (((1,), (1,)), ((), ())), preferred_element_type=jnp.float32
    )


def block_scores(q_block, k_seq, key_valid):
    scores = jnp.einsum(
        "qhd,khd->hqk", q_block, k_seq, preferred_element_type=jnp.float32
    ) * HEAD_DIM ** (-0.5)
    return jnp.where(key_valid[None, None, :], scores, masked_score)


def attend_forward(q_seq, k_seq, v_seq, length):
    local_heads = q_seq.shape[1]
    key_valid = jnp.arange(LEN, dtype=jnp.int32) < length
    q_blocks = q_seq.reshape(LEN // Q_BLOCK, Q_BLOCK, local_heads, HEAD_DIM)

    def one_block(q_block):
        scores = block_scores(q_block, k_seq, key_valid)
        row_peak = jnp.max(scores, axis=-1, keepdims=True)
        shifted = jnp.exp(scores - row_peak)
        row_total = jnp.sum(shifted, axis=-1, keepdims=True)
        attn_probs = (shifted / row_total).astype(jnp.bfloat16)
        context = jnp.einsum("hqk,khd->qhd", attn_probs, v_seq, preferred_element_type=jnp.float32)
        return (context.astype(jnp.bfloat16), (row_peak + jnp.log(row_total))[..., 0])

    context, log_total = lax.map(one_block, q_blocks)
    return (context.reshape(LEN, local_heads, HEAD_DIM), log_total)


def attend_backward(q_seq, k_seq, v_seq, grad_seq, log_total, length):
    local_heads = q_seq.shape[1]
    score_scale = HEAD_DIM ** (-0.5)
    key_valid = jnp.arange(LEN, dtype=jnp.int32) < length
    q_blocks = q_seq.reshape(LEN // Q_BLOCK, Q_BLOCK, local_heads, HEAD_DIM)
    g_blocks = grad_seq.reshape(LEN // Q_BLOCK, Q_BLOCK, local_heads, HEAD_DIM)

    def one_block(accum, block_item):
        q_block, g_block, lse_block = block_item
        scores = block_scores(q_block, k_seq, key_valid)
        attn_probs = jnp.exp(scores - lse_block[..., None])
        grad_probs = jnp.einsum("qhd,khd->hqk", g_block, v_seq, preferred_element_type=jnp.float32)
        row_dot = jnp.sum(attn_probs * grad_probs, axis=-1, keepdims=True)
        grad_scores = (attn_probs * (grad_probs - row_dot)).astype(jnp.bfloat16)
        grad_q = (
            jnp.einsum("hqk,khd->qhd", grad_scores, k_seq, preferred_element_type=jnp.float32)
            * score_scale
        )
        grad_k = (
            accum[0]
            + jnp.einsum("hqk,qhd->khd", grad_scores, q_block, preferred_element_type=jnp.float32)
            * score_scale
        )
        grad_v = accum[1] + jnp.einsum(
            "hqk,qhd->khd",
            attn_probs.astype(jnp.bfloat16),
            g_block,
            preferred_element_type=jnp.float32,
        )
        return ((grad_k, grad_v), grad_q.astype(jnp.bfloat16))

    zero_keys = jnp.zeros((LEN, local_heads, HEAD_DIM), jnp.float32)
    (grad_k, grad_v), grad_q = lax.scan(
        one_block, (zero_keys, zero_keys), (q_blocks, g_blocks, log_total)
    )
    return (
        grad_q.reshape(LEN, local_heads, HEAD_DIM),
        grad_k.astype(jnp.bfloat16),
        grad_v.astype(jnp.bfloat16),
    )


def body(
    tokens,
    lengths,
    w_qkv,
    q_bias,
    v_bias,
    w_out,
    out_bias,
    gain_one,
    shift_one,
    w_up,
    up_bias,
    w_down,
    down_bias,
    gain_two,
    shift_two,
    cotangent,
):
    seq_count, local_len, model_width = tokens.shape
    row_count = seq_count * local_len
    head_count = model_width // HEAD_DIM
    gathered = (
        lax.all_gather(w_qkv, "shard", axis=0, tiled=True),
        lax.all_gather(q_bias, "shard", axis=0, tiled=True),
        lax.all_gather(v_bias, "shard", axis=0, tiled=True),
        lax.all_gather(w_out, "shard", axis=0, tiled=True),
        lax.all_gather(out_bias, "shard", axis=0, tiled=True),
        lax.all_gather(gain_one, "shard", axis=0, tiled=True),
        lax.all_gather(shift_one, "shard", axis=0, tiled=True),
        lax.all_gather(w_up, "shard", axis=0, tiled=True),
        lax.all_gather(up_bias, "shard", axis=0, tiled=True),
        lax.all_gather(w_down, "shard", axis=0, tiled=True),
        lax.all_gather(down_bias, "shard", axis=0, tiled=True),
        lax.all_gather(gain_two, "shard", axis=0, tiled=True),
        lax.all_gather(shift_two, "shard", axis=0, tiled=True),
    )
    (
        full_qkv,
        full_q_bias,
        full_v_bias,
        full_out,
        full_out_bias,
        full_gain_one,
        full_shift_one,
        full_up,
        full_up_bias,
        full_down,
        full_down_bias,
        full_gain_two,
        full_shift_two,
    ) = gathered
    token_rows = tokens.reshape(row_count, model_width)
    joined_bias = jnp.concatenate([full_q_bias, jnp.zeros_like(full_q_bias), full_v_bias]).astype(
        jnp.float32
    )
    qkv_rows = (
        jnp.dot(token_rows, full_qkv, preferred_element_type=jnp.float32) + joined_bias
    ).astype(jnp.bfloat16)
    qkv_tokens = qkv_rows.reshape(seq_count, local_len, 3, head_count, HEAD_DIM)
    qkv_heads = lax.all_to_all(qkv_tokens, "seq", split_axis=3, concat_axis=1, tiled=True)

    def forward_seq(seq_item):
        qkv_seq, length = seq_item
        return attend_forward(qkv_seq[:, 0], qkv_seq[:, 1], qkv_seq[:, 2], length)

    context_heads, log_total = lax.map(forward_seq, (qkv_heads, lengths))
    context_tokens = lax.all_to_all(context_heads, "seq", split_axis=1, concat_axis=2, tiled=True)
    context_rows = context_tokens.reshape(row_count, model_width)
    residual_one = (
        token_rows.astype(jnp.float32)
        + jnp.dot(context_rows, full_out, preferred_element_type=jnp.float32)
        + full_out_bias.astype(jnp.float32)
    )
    normed_one, norm_one_pull = jax.vjp(
        layer_norm,
        residual_one,
        full_gain_one.astype(jnp.float32),
        full_shift_one.astype(jnp.float32),
    )
    normed_low = normed_one.astype(jnp.bfloat16)
    up_rows = jnp.dot(
        normed_low, full_up, preferred_element_type=jnp.float32
    ) + full_up_bias.astype(jnp.float32)
    active, gelu_pull = jax.vjp(gelu_exact, up_rows)
    active_low = active.astype(jnp.bfloat16)
    residual_two = (
        normed_one
        + jnp.dot(active_low, full_down, preferred_element_type=jnp.float32)
        + full_down_bias.astype(jnp.float32)
    )
    final_rows, norm_two_pull = jax.vjp(
        layer_norm,
        residual_two,
        full_gain_two.astype(jnp.float32),
        full_shift_two.astype(jnp.float32),
    )
    output = final_rows.astype(jnp.bfloat16).reshape(tokens.shape)
    back_qkv, back_out, back_up, back_down = (full_qkv, full_out, full_up, full_down)
    grad_rows = cotangent.reshape(row_count, model_width).astype(jnp.float32)
    grad_two, grad_gain_two, grad_shift_two = norm_two_pull(grad_rows)
    grad_down_bias = jnp.sum(grad_two, axis=0)
    grad_two_low = grad_two.astype(jnp.bfloat16)
    grad_w_down = contract_rows(active_low, grad_two_low)
    grad_active = contract_cols(grad_two_low, back_down)
    (grad_up,) = gelu_pull(grad_active)
    grad_up_bias = jnp.sum(grad_up, axis=0)
    grad_up_low = grad_up.astype(jnp.bfloat16)
    grad_w_up = contract_rows(normed_low, grad_up_low)
    grad_normed = grad_two + contract_cols(grad_up_low, back_up)
    grad_one, grad_gain_one, grad_shift_one = norm_one_pull(grad_normed)
    grad_out_bias = jnp.sum(grad_one, axis=0)
    grad_one_low = grad_one.astype(jnp.bfloat16)
    grad_w_out = contract_rows(context_rows, grad_one_low)
    grad_context = contract_cols(grad_one_low, back_out).astype(jnp.bfloat16)
    grad_context = grad_context.reshape(seq_count, local_len, head_count, HEAD_DIM)
    grad_context_heads = lax.all_to_all(
        grad_context, "seq", split_axis=2, concat_axis=1, tiled=True
    )

    def backward_seq(seq_item):
        qkv_seq, grad_seq, lse_seq, length = seq_item
        grad_q, grad_k, grad_v = attend_backward(
            qkv_seq[:, 0], qkv_seq[:, 1], qkv_seq[:, 2], grad_seq, lse_seq, length
        )
        return jnp.stack([grad_q, grad_k, grad_v], axis=1)

    grad_qkv_heads = lax.map(backward_seq, (qkv_heads, grad_context_heads, log_total, lengths))
    grad_qkv_tokens = lax.all_to_all(grad_qkv_heads, "seq", split_axis=1, concat_axis=3, tiled=True)
    grad_qkv_rows = grad_qkv_tokens.reshape(row_count, 3 * model_width)
    grad_q_bias = jnp.sum(grad_qkv_rows[:, :model_width], axis=0, dtype=jnp.float32)
    grad_v_bias = jnp.sum(grad_qkv_rows[:, 2 * model_width :], axis=0, dtype=jnp.float32)
    grad_w_qkv = contract_rows(token_rows, grad_qkv_rows)
    grad_tokens = grad_one + contract_cols(grad_qkv_rows, back_qkv)
    grad_tokens = grad_tokens.astype(jnp.bfloat16).reshape(tokens.shape)
    owned = (
        lax.psum_scatter(grad_w_qkv, "shard", scatter_dimension=0, tiled=True),
        lax.psum_scatter(grad_q_bias, "shard", scatter_dimension=0, tiled=True),
        lax.psum_scatter(grad_v_bias, "shard", scatter_dimension=0, tiled=True),
        lax.psum_scatter(grad_w_out, "shard", scatter_dimension=0, tiled=True),
        lax.psum_scatter(grad_out_bias, "shard", scatter_dimension=0, tiled=True),
        lax.psum_scatter(grad_gain_one, "shard", scatter_dimension=0, tiled=True),
        lax.psum_scatter(grad_shift_one, "shard", scatter_dimension=0, tiled=True),
        lax.psum_scatter(grad_w_up, "shard", scatter_dimension=0, tiled=True),
        lax.psum_scatter(grad_up_bias, "shard", scatter_dimension=0, tiled=True),
        lax.psum_scatter(grad_w_down, "shard", scatter_dimension=0, tiled=True),
        lax.psum_scatter(grad_down_bias, "shard", scatter_dimension=0, tiled=True),
        lax.psum_scatter(grad_gain_two, "shard", scatter_dimension=0, tiled=True),
        lax.psum_scatter(grad_shift_two, "shard", scatter_dimension=0, tiled=True),
    )
    owned_columns = (
        lax.psum_scatter(
            owned[0].astype(jnp.bfloat16), "seq", scatter_dimension=1, tiled=True
        ).astype(jnp.float32),
        lax.psum_scatter(
            owned[3].astype(jnp.bfloat16), "seq", scatter_dimension=1, tiled=True
        ).astype(jnp.float32),
        lax.psum_scatter(
            owned[7].astype(jnp.bfloat16), "seq", scatter_dimension=1, tiled=True
        ).astype(jnp.float32),
        lax.psum_scatter(
            owned[9].astype(jnp.bfloat16), "seq", scatter_dimension=1, tiled=True
        ).astype(jnp.float32),
    )
    matrices = (
        lax.all_gather(owned_columns[0].astype(jnp.bfloat16), "seq", axis=1, tiled=True).astype(
            jnp.float32
        ),
        lax.all_gather(owned_columns[1].astype(jnp.bfloat16), "seq", axis=1, tiled=True).astype(
            jnp.float32
        ),
        lax.all_gather(owned_columns[2].astype(jnp.bfloat16), "seq", axis=1, tiled=True).astype(
            jnp.float32
        ),
        lax.all_gather(owned_columns[3].astype(jnp.bfloat16), "seq", axis=1, tiled=True).astype(
            jnp.float32
        ),
    )
    vectors = lax.psum(
        (
            owned[1],
            owned[2],
            owned[4],
            owned[5],
            owned[6],
            owned[8],
            owned[10],
            owned[11],
            owned[12],
        ),
        "seq",
    )
    result_qkv, result_out, result_up, result_down = (
        matrices[0],
        matrices[1],
        matrices[2],
        matrices[3],
    )
    result_q_bias, result_v_bias, result_out_bias = (vectors[0], vectors[1], vectors[2])
    result_gain_one, result_shift_one, result_up_bias = (vectors[3], vectors[4], vectors[5])
    result_down_bias, result_gain_two, result_shift_two = (vectors[6], vectors[7], vectors[8])
    return (
        output,
        grad_tokens,
        result_qkv,
        result_q_bias,
        result_v_bias,
        result_out,
        result_out_bias,
        result_gain_one,
        result_shift_one,
        result_up,
        result_up_bias,
        result_down,
        result_down_bias,
        result_gain_two,
        result_shift_two,
    )


AXES = ("seq", "z", "core")
NORMAL_SCALE = 0.3989422804014327
HALF_ROOT = 0.7071067811865476


def dot_nn(left, right):
    return lax.dot_general(
        left, right, (((1,), (0,)), ((), ())), preferred_element_type=jnp.float32
    )


def dot_nt(left, right):
    return contract_cols(left, right)


def dot_tn(left, right):
    return contract_rows(left, right)


def vmem_specs(count):
    return [pl.BlockSpec(memory_space=pltpu.VMEM)] * count


def smem_spec():
    return pl.BlockSpec(memory_space=pltpu.SMEM)


def key_bias(sc, block_rows):
    length, place = sc[0], sc[1]
    columns = []
    for j in range(4):
        position = (place ^ j) * block_rows + lax.broadcasted_iota(
            jnp.int32, (block_rows, 1), 0
        )
        columns.append(jnp.where(position < length, 0.0, masked_score))
    return jnp.concatenate(columns, axis=0)


def attend_forward_kernel(
    sc, t0, t1, t2, t3, own, other, qkv, ctx_t, c0, c1, c2, c3, lse, weight
):
    place, core = sc[1], sc[2]
    rows = t0.shape[0]
    shard_rows = weight.shape[2]
    width = weight.shape[3]
    head_width = width // 3
    heads = head_width // HEAD_DIM
    weight[:, pl.ds(core, 1)] = own[:, :shard_rows, :][:, None]
    weight[:, pl.ds(1 - core, 1)] = other[:, :shard_rows, :][:, None]
    full = weight[...].reshape(-1, width)
    bias = (
        own[place, shard_rows : shard_rows + 1, :].astype(jnp.float32)
        + other[place, shard_rows : shard_rows + 1, :].astype(jnp.float32)
    )
    for j, block in enumerate((t0, t1, t2, t3)):
        qkv[j * rows : (j + 1) * rows, :] = (dot_nn(block[...], full) + bias).astype(jnp.bfloat16)
    mask = key_bias(sc, rows)
    for j, out in enumerate((c0, c1, c2, c3)):
        parts = []
        q_all = qkv[j * rows : (j + 1) * rows, 0:head_width] * jnp.bfloat16(HEAD_DIM**-0.5)
        for h in range(heads):
            low = h * HEAD_DIM
            q = q_all[:, low : low + HEAD_DIM]
            k = qkv[:, head_width + low : head_width + low + HEAD_DIM]
            v = qkv[:, 2 * head_width + low : 2 * head_width + low + HEAD_DIM]
            scores = dot_nt(k, q) + mask
            peak = jnp.max(scores, axis=0, keepdims=True)
            shifted = jnp.exp(scores - peak)
            total = jnp.sum(shifted, axis=0, keepdims=True)
            part = dot_tn(v, shifted.astype(jnp.bfloat16)) / total
            parts.append(part)
            lse[h : h + 1, j * rows : (j + 1) * rows] = peak + jnp.log(total)
        joined = jnp.concatenate(parts, axis=0)
        ctx_t[:, j * rows : (j + 1) * rows] = joined
        out[...] = joined.T.astype(jnp.bfloat16)


def attend_backward_kernel(sc, qkv, ctx_t, lse, g0, g1, g2, g3, dqkv, dk_acc, dv_acc):
    rows = g0.shape[0]
    head_width = g0.shape[1]
    heads = head_width // HEAD_DIM
    mask = key_bias(sc, rows)
    scale = jnp.bfloat16(HEAD_DIM**-0.5)
    for j, g_ref in enumerate((g0, g1, g2, g3)):
        span = slice(j * rows, (j + 1) * rows)
        g_all = g_ref[...]
        product = g_all.astype(jnp.float32).T * ctx_t[:, span]
        q_all = qkv[span, 0:head_width] * scale
        parts = []
        for h in range(heads):
            low = h * HEAD_DIM
            q = q_all[:, low : low + HEAD_DIM]
            g = g_all[:, low : low + HEAD_DIM]
            k = qkv[:, head_width + low : head_width + low + HEAD_DIM]
            v = qkv[:, 2 * head_width + low : 2 * head_width + low + HEAD_DIM]
            probs = jnp.exp(dot_nt(k, q) + mask - lse[h : h + 1, span])
            row_dot = jnp.sum(product[low : low + HEAD_DIM, :], axis=0, keepdims=True)
            grad_scores = (probs * (dot_nt(v, g) - row_dot)).astype(jnp.bfloat16)
            grad_v = dot_nn(probs.astype(jnp.bfloat16), g)
            grad_k = dot_nn(grad_scores, q)
            if j == 0:
                dv_acc[h] = grad_v
                dk_acc[h] = grad_k
            else:
                dv_acc[h] += grad_v
                dk_acc[h] += grad_k
            parts.append(dot_tn(k, grad_scores) * (HEAD_DIM**-0.5))
        dqkv[span, 0:head_width] = jnp.concatenate(parts, axis=0).T.astype(jnp.bfloat16)
    dk = jnp.concatenate([dk_acc[h] for h in range(heads)], axis=1)
    dv = jnp.concatenate([dv_acc[h] for h in range(heads)], axis=1)
    dqkv[:, head_width:] = jnp.concatenate([dk, dv], axis=1).astype(jnp.bfloat16)


def grad_qkv_weight_kernel(sc, t0, t1, t2, t3, dqkv, keep, send, sums):
    core = sc[2]
    rows = t0.shape[0]
    total = None
    for j, block in enumerate((t0, t1, t2, t3)):
        part = dot_tn(block[...], dqkv[j * rows : (j + 1) * rows, :])
        total = part if total is None else total + part
    sums[...] = jnp.sum(dqkv[...].astype(jnp.float32), axis=0, keepdims=True)
    shard_rows = keep.shape[1]
    low = total.astype(jnp.bfloat16)
    for z in range(keep.shape[0]):
        even = low[(2 * z) * shard_rows : (2 * z + 1) * shard_rows]
        odd = low[(2 * z + 1) * shard_rows : (2 * z + 2) * shard_rows]
        keep[z] = jnp.where(core == 0, even, odd)
        send[z] = jnp.where(core == 0, odd, even)


def grad_tokens_kernel(dqkv, weight, o0, o1, o2, o3):
    rows = o0.shape[0]
    full = weight[...].reshape(-1, weight.shape[3])
    for j, out in enumerate((o0, o1, o2, o3)):
        part = dot_nt(dqkv[j * rows : (j + 1) * rows, :], full)
        out[...] = part.astype(out.dtype)


def normalize(values):
    center = values - jnp.mean(values, axis=-1, keepdims=True)
    inverse = lax.rsqrt(jnp.mean(center * center, axis=-1, keepdims=True) + epsilon)
    return center * inverse, inverse


def normalize_back(grad, unit, inverse):
    return inverse * (
        grad
        - jnp.mean(grad, axis=-1, keepdims=True)
        - unit * jnp.mean(grad * unit, axis=-1, keepdims=True)
    )


def middle_kernel(
    sc,
    x0,
    x1,
    x2,
    x3,
    token,
    cotangent,
    own_out,
    other_out,
    small,
    up_bias,
    gathered,
    output,
    grad_one,
    y0,
    y1,
    y2,
    y3,
    keep,
    send,
    sums,
    up_sums,
    w_out,
    w_up,
    w_down,
    slope,
    active,
    grad_up,
    context,
    sems,
):
    place, core = sc[1], sc[2]
    blocks = w_up.shape[0]
    shard_rows = w_up.shape[2]
    width = w_up.shape[3]
    copies = []
    for b in range(blocks):
        copies.append(
            pltpu.make_async_copy(gathered.at[:, b, 0:shard_rows, :], w_up.at[b], sems.at[b])
        )
    copies.append(
        pltpu.make_async_copy(
            gathered.at[:, :, shard_rows : 2 * shard_rows, :], w_down, sems.at[blocks]
        )
    )
    for copy in copies:
        copy.start()
    w_out[:, pl.ds(core, 1)] = own_out[:, :shard_rows, :][:, None]
    w_out[:, pl.ds(1 - core, 1)] = other_out[:, :shard_rows, :][:, None]
    out_rows = 2 * shard_rows

    def out_block(j):
        return w_out[place ^ j].reshape(out_rows, width)

    residual = token[...].astype(jnp.float32) + small[0:1, :]
    for j, block in enumerate((x0, x1, x2, x3)):
        residual = residual + dot_nn(block[...], out_block(j))
    unit_one, inverse_one = normalize(residual)
    gain_one = small[1:2, :]
    normed = unit_one * gain_one + small[2:3, :]
    normed_low = normed.astype(jnp.bfloat16)
    for b in range(blocks):
        copies[b].wait()
        span = slice(b * width, (b + 1) * width)
        up = dot_nn(normed_low, w_up[b].reshape(width, width)) + up_bias[:, span]
        phi = 0.5 + 0.5 * lax.erf(up * HALF_ROOT)
        slope[:, span] = phi + up * (jnp.exp(-0.5 * up * up) * NORMAL_SCALE)
        active[:, span] = (up * phi).astype(jnp.bfloat16)
    copies[blocks].wait()
    residual = normed + small[3:4, :] + dot_nn(active[...], w_down[...].reshape(-1, width))
    unit_two, inverse_two = normalize(residual)
    gain_two = small[4:5, :]
    output[...] = (unit_two * gain_two + small[5:6, :]).astype(jnp.bfloat16)
    grad = cotangent[...].astype(jnp.float32)
    sums[3:4, :] = jnp.sum(grad * unit_two, axis=0, keepdims=True)
    sums[4:5, :] = jnp.sum(grad, axis=0, keepdims=True)
    grad_two = normalize_back(grad * gain_two, unit_two, inverse_two)
    sums[5:6, :] = jnp.sum(grad_two, axis=0, keepdims=True)
    two_low = grad_two.astype(jnp.bfloat16)
    grad_normed = grad_two
    per_block = w_down.shape[0] // blocks
    for b in range(blocks):
        span = slice(b * width, (b + 1) * width)
        rows_down = w_down[b * per_block : (b + 1) * per_block].reshape(width, width)
        part = dot_nt(two_low, rows_down) * slope[:, span]
        up_sums[:, span] = jnp.sum(part, axis=0, keepdims=True)
        part = part.astype(jnp.bfloat16)
        grad_up[:, span] = part
        grad_normed = grad_normed + dot_nt(part, w_up[b].reshape(width, width))
    sums[1:2, :] = jnp.sum(grad_normed * unit_one, axis=0, keepdims=True)
    sums[2:3, :] = jnp.sum(grad_normed, axis=0, keepdims=True)
    first = normalize_back(grad_normed * gain_one, unit_one, inverse_one)
    sums[0:1, :] = jnp.sum(first, axis=0, keepdims=True)
    sums[6:8, :] = jnp.zeros((2, width), jnp.float32)
    grad_one[...] = first
    one_low = first.astype(jnp.bfloat16)
    for j, out in enumerate((y0, y1, y2, y3)):
        out[...] = dot_nt(one_low, out_block(j)).astype(jnp.bfloat16)
    for j, block in enumerate((x0, x1, x2, x3)):
        context[place ^ j] = block[...]
    joined = jnp.concatenate([context[j] for j in range(4)], axis=1)
    half = width // 2
    down_rows = blocks * shard_rows
    for ref, mine in ((keep, core), (send, 1 - core)):
        for z in range(4):
            even = active[:, (2 * z) * down_rows : (2 * z + 1) * down_rows]
            odd = active[:, (2 * z + 1) * down_rows : (2 * z + 2) * down_rows]
            ref[:, z * down_rows : (z + 1) * down_rows] = jnp.where(mine == 0, even, odd)
        at = 4 * down_rows
        ref[:, at : at + width] = two_low
        at += width
        ref[:, at : at + width] = normed_low
        at += width
        ref[:, at : at + 2 * width] = jnp.where(
            mine == 0, grad_up[:, : 2 * width], grad_up[:, 2 * width :]
        )
        at += 2 * width
        ref[:, at : at + width] = joined
        at += width
        ref[:, at : at + half] = jnp.where(mine == 0, one_low[:, :half], one_low[:, half:])


def weight_grads_kernel(keep, got, g_down, g_up, g_out):
    width = g_down.shape[3]
    shard_rows = g_down.shape[2]
    zs = g_down.shape[1]
    ss = g_down.shape[0]
    half = width // 2
    down_rows = ss * shard_rows
    at_two = zs * down_rows
    at_norm = at_two + width
    at_up = at_norm + width
    at_ctx = at_up + 2 * width
    at_one = at_ctx + width

    def pair(left, right):
        return dot_tn(keep[:, left], keep[:, right]) + dot_tn(got[:, left], got[:, right])

    for z in range(zs):
        part = pair(
            slice(z * down_rows, (z + 1) * down_rows), slice(at_two, at_two + width)
        ).astype(jnp.bfloat16)
        for s in range(ss):
            g_down[s, z] = part[s * shard_rows : (s + 1) * shard_rows]
    up_cols = g_up.shape[3]
    for s in range(ss):
        part = pair(
            slice(at_norm, at_norm + width),
            slice(at_up + s * up_cols, at_up + (s + 1) * up_cols),
        ).astype(jnp.bfloat16)
        for z in range(zs):
            g_up[s, z] = part[2 * z * shard_rows : (2 * z + 2) * shard_rows]
    part = pair(slice(at_ctx, at_ctx + width), slice(at_one, at_one + half)).astype(jnp.bfloat16)
    for z in range(zs):
        g_out[z] = part[2 * z * shard_rows : (2 * z + 2) * shard_rows]


def fast_body(
    tokens,
    lengths,
    w_qkv,
    q_bias,
    v_bias,
    w_out,
    out_bias,
    gain_one,
    shift_one,
    w_up,
    up_bias,
    w_down,
    down_bias,
    gain_two,
    shift_two,
    cotangent,
):
    bf16, f32 = jnp.bfloat16, jnp.float32
    _, rows, width = tokens.shape
    shard_rows = w_qkv.shape[0]
    hidden = w_up.shape[1]
    head_width = width // 4
    place = lax.axis_index("seq")
    core = lax.axis_index("core")
    zs = 4
    swap = [(0, 1), (1, 0)]

    def struct(shape, dtype=bf16):
        return jax.ShapeDtypeStruct(shape, dtype)

    def across(value, step):
        return lax.ppermute(value, "seq", [(i, i ^ step) for i in range(4)])

    def partner(value):
        return lax.ppermute(value, "core", swap)

    def spread(value, axis):
        copies = jnp.broadcast_to(value[None], (4,) + value.shape)
        return lax.all_to_all(copies, axis, split_axis=0, concat_axis=0, tiled=True)

    token = tokens[0]
    quarter = jnp.concatenate(
        [
            lax.dynamic_slice_in_dim(w_up, place * width, width, axis=1),
            lax.dynamic_slice_in_dim(w_down, place * shard_rows, shard_rows, axis=0),
        ],
        axis=0,
    )
    gathered = lax.all_gather(quarter, ("z", "core", "seq"), axis=0, tiled=True)
    gathered = gathered.reshape(2 * zs, 4, 2 * shard_rows, width)
    columns = lax.dynamic_index_in_dim(
        w_qkv.reshape(shard_rows, 3, 4, head_width), place, axis=2, keepdims=False
    ).reshape(shard_rows, 3 * head_width)
    pair_rows = jnp.zeros((2, 2, shard_rows), bf16)
    placed_q = lax.dynamic_update_slice(pair_rows[0], q_bias[None], (core, 0)).reshape(1, -1)
    placed_v = lax.dynamic_update_slice(pair_rows[0], v_bias[None], (core, 0)).reshape(1, -1)
    bias_row = jnp.concatenate(
        [placed_q, jnp.zeros((1, head_width), bf16), placed_v], axis=1
    )
    own_block = jnp.concatenate(
        [columns, bias_row, jnp.zeros((15, 3 * head_width), bf16)], axis=0
    )
    t1, t2, t3 = across(token, 1), across(token, 2), across(token, 3)
    own_cols = spread(own_block, "z")
    other_cols = partner(own_cols)
    sc = jnp.stack([lengths[0], place, core]).astype(jnp.int32)
    all_rows = 4 * rows
    qkv, ctx_t, c0, c1, c2, c3, lse, full_qkv = pl.pallas_call(
        attend_forward_kernel,
        name="attend_forward",
        out_shape=(
            struct((all_rows, 3 * head_width)),
            struct((head_width, all_rows), f32),
            struct((rows, head_width)),
            struct((rows, head_width)),
            struct((rows, head_width)),
            struct((rows, head_width)),
            struct((head_width // HEAD_DIM, all_rows), f32),
            struct((zs, 2, shard_rows, 3 * head_width)),
        ),
        in_specs=[smem_spec()] + vmem_specs(6),
        out_specs=tuple(vmem_specs(8)),
    )(sc, token, t1, t2, t3, own_cols, other_cols)
    vectors = jnp.concatenate(
        [out_bias, gain_one, shift_one, down_bias, gain_two, shift_two, up_bias]
    )
    pad = 16 * width - vectors.shape[0]
    out_shard = jnp.concatenate(
        [w_out, jnp.pad(vectors, (0, pad)).reshape(16, width)], axis=0
    )
    own_out = spread(out_shard, "z")
    other_out = partner(own_out)
    x1, x2, x3 = across(c1, 1), across(c2, 2), across(c3, 3)
    own_vec = own_out[:, shard_rows : shard_rows + 2].reshape(zs, -1)[:, : vectors.shape[0]]
    other_vec = other_out[:, shard_rows : shard_rows + 2].reshape(zs, -1)[:, : vectors.shape[0]]
    first = core == 0
    all_vec = jnp.stack(
        [jnp.where(first, own_vec, other_vec), jnp.where(first, other_vec, own_vec)], axis=1
    ).astype(f32)
    all_vec = all_vec.reshape(2 * zs, -1)
    six = all_vec[:, : 6 * shard_rows].reshape(2 * zs, 6, shard_rows)
    six = six.transpose(1, 0, 2).reshape(6, width)
    small = jnp.concatenate([six, jnp.zeros((2, width), f32)], axis=0)
    full_up_bias = all_vec[:, 6 * shard_rows :].reshape(1, hidden)
    packed = hidden // 2 + 5 * width + width // 2
    output, grad_one, y0, y1, y2, y3, keep, send, sums, up_sums = pl.pallas_call(
        middle_kernel,
        name="middle",
        out_shape=(
            struct((rows, width)),
            struct((rows, width), f32),
            struct((rows, head_width)),
            struct((rows, head_width)),
            struct((rows, head_width)),
            struct((rows, head_width)),
            struct((rows, packed)),
            struct((rows, packed)),
            struct((8, width), f32),
            struct((1, hidden), f32),
        ),
        in_specs=[smem_spec()]
        + vmem_specs(10)
        + [pl.BlockSpec(memory_space=pl.ANY)],
        out_specs=tuple(vmem_specs(10)),
        scratch_shapes=[
            pltpu.VMEM((zs, 2, shard_rows, width), bf16),
            pltpu.VMEM((4, 2 * zs, shard_rows, width), bf16),
            pltpu.VMEM((2 * zs, 4, shard_rows, width), bf16),
            pltpu.VMEM((rows, hidden), f32),
            pltpu.VMEM((rows, hidden), bf16),
            pltpu.VMEM((rows, hidden), bf16),
            pltpu.VMEM((4, rows, head_width), bf16),
            pltpu.SemaphoreType.DMA((5,)),
        ],
    )(
        sc,
        c0,
        x1,
        x2,
        x3,
        token,
        cotangent[0],
        own_out,
        other_out,
        small,
        full_up_bias,
        gathered,
    )
    g1, g2, g3 = across(y1, 1), across(y2, 2), across(y3, 3)
    got = partner(send)
    g_down, g_up, g_out = pl.pallas_call(
        weight_grads_kernel,
        name="weight_grads",
        out_shape=(
            struct((4, zs, shard_rows, width)),
            struct((4, zs, 2 * shard_rows, hidden // 8)),
            struct((zs, 2 * shard_rows, width // 2)),
        ),
        in_specs=vmem_specs(2),
        out_specs=tuple(vmem_specs(3)),
    )(keep, got)

    def exchange(value, axis):
        return lax.all_to_all(value, axis, split_axis=0, concat_axis=0, tiled=True)

    def total(value):
        return jnp.sum(value.astype(f32), axis=0).astype(bf16)

    down_part = total(exchange(g_down, "seq"))
    up_part = total(exchange(g_up, "seq"))
    down_part = total(exchange(down_part, "z"))
    up_part = total(exchange(up_part, "z"))
    out_part = total(exchange(g_out, "z"))

    dqkv = pl.pallas_call(
        attend_backward_kernel,
        name="attend_backward",
        out_shape=struct((all_rows, 3 * head_width)),
        in_specs=[smem_spec()] + vmem_specs(7),
        out_specs=pl.BlockSpec(memory_space=pltpu.VMEM),
        scratch_shapes=[
            pltpu.VMEM((head_width // HEAD_DIM, all_rows, HEAD_DIM), f32),
            pltpu.VMEM((head_width // HEAD_DIM, all_rows, HEAD_DIM), f32),
        ],
    )(sc, qkv, ctx_t, lse, y0, g1, g2, g3)
    q_keep, q_send, q_sums = pl.pallas_call(
        grad_qkv_weight_kernel,
        name="grad_qkv_weight",
        out_shape=(
            struct((zs, shard_rows, 3 * head_width)),
            struct((zs, shard_rows, 3 * head_width)),
            struct((1, 3 * head_width), f32),
        ),
        in_specs=[smem_spec()] + vmem_specs(5),
        out_specs=tuple(vmem_specs(3)),
    )(sc, token, t1, t2, t3, dqkv)
    q_got = partner(q_send)
    o0, o1, o2, o3 = pl.pallas_call(
        grad_tokens_kernel,
        name="grad_tokens",
        out_shape=(
            struct((rows, width), f32),
            struct((rows, width)),
            struct((rows, width)),
            struct((rows, width)),
        ),
        in_specs=vmem_specs(2),
        out_specs=tuple(vmem_specs(4)),
    )(dqkv, full_qkv)
    q_part = (q_keep.astype(f32) + q_got.astype(f32)).astype(bf16)
    q_part = total(exchange(q_part, "z"))
    r1, r2, r3 = across(o1, 1), across(o2, 2), across(o3, 3)
    grad_tokens = (
        (grad_one + o0) + r1.astype(f32) + r2.astype(f32) + r3.astype(f32)
    ).astype(bf16)

    q_row = lax.dynamic_update_slice(
        jnp.zeros((1, width), f32), q_sums[:, :head_width], (0, place * head_width)
    )
    v_row = lax.dynamic_update_slice(
        jnp.zeros((1, width), f32), q_sums[:, 2 * head_width :], (0, place * head_width)
    )

    def everywhere(value):
        value = value + partner(value)
        value = value + across(value, 1)
        value = value + across(value, 2)
        for step in (1, 2):
            value = value + lax.ppermute(value, "z", [(i, i ^ step) for i in range(4)])
        return value

    early = everywhere(jnp.concatenate([sums[:6], up_sums.reshape(4, width)], axis=0))
    late = everywhere(jnp.concatenate([q_row, v_row], axis=0))
    shard = 2 * lax.axis_index("z") + core

    def owned(vector):
        size = vector.shape[0] // (2 * zs)
        return lax.dynamic_slice(vector, (shard * size,), (size,))

    up_two = up_part.reshape(2, shard_rows, hidden // 8)
    out_two = out_part.reshape(2, shard_rows, width // 2)
    out_two = total(spread(out_two, "seq"))

    def both_halves(value):
        mine = lax.dynamic_index_in_dim(value, core, axis=0, keepdims=False)
        theirs = lax.dynamic_index_in_dim(value, 1 - core, axis=0, keepdims=False)
        theirs = partner(theirs)
        return jnp.where(first, mine, theirs), jnp.where(first, theirs, mine)

    up_left, up_right = both_halves(up_two)
    out_left, out_right = both_halves(out_two)
    result_out = jnp.concatenate([out_left, out_right], axis=1).astype(f32)
    joined = jnp.concatenate(
        [down_part, jnp.concatenate([up_left, up_right], axis=1)], axis=0
    )
    blocks = spread(joined, "seq").astype(f32)
    result_down = blocks[:, :shard_rows].reshape(4 * shard_rows, width)
    up_blocks = blocks[:, shard_rows:].reshape(4, shard_rows, 2, hidden // 8)
    result_up = up_blocks.transpose(1, 2, 0, 3).reshape(shard_rows, hidden)
    q_blocks = spread(q_part, "seq").astype(f32).reshape(4, shard_rows, 3, head_width)
    result_qkv = q_blocks.transpose(1, 2, 0, 3).reshape(shard_rows, 3 * width)
    return (
        output[None],
        grad_tokens[None],
        result_qkv,
        owned(late[0]),
        owned(late[1]),
        result_out,
        owned(early[0]),
        owned(early[1]),
        owned(early[2]),
        result_up,
        owned(early[6:10].reshape(-1)),
        result_down,
        owned(early[5]),
        owned(early[3]),
        owned(early[4]),
    )


def solution(mesh):
    seq_count, shard_count = mesh.shape["seq"], mesh.shape["shard"]
    fast = seq_count == 4 and shard_count == 8
    if fast:
        grid = mesh.devices.reshape(seq_count, shard_count // 2, 2)
        mesh = jax.sharding.Mesh(grid, AXES)
    shard = ("z", "core") if fast else "shard"
    vector, matrix, rows = P(shard), P(shard, None), P(shard, "seq", None)
    return jax.shard_map(
        fast_body if fast else body,
        mesh=mesh,
        in_specs=(
            rows,
            vector,
            matrix,
            vector,
            vector,
            matrix,
            vector,
            vector,
            vector,
            matrix,
            vector,
            matrix,
            vector,
            vector,
            vector,
            rows,
        ),
        out_specs=(
            rows,
            rows,
            matrix,
            vector,
            vector,
            matrix,
            vector,
            vector,
            vector,
            matrix,
            vector,
            matrix,
            vector,
            vector,
            vector,
        ),
        check_vma=False,
    )
```

```python
import jax
import jax.numpy as jnp
from jax import lax
from jax.experimental import pallas as pl
from jax.experimental.pallas import tpu as pltpu
from jax.sharding import PartitionSpec as P

HEAD_DIM = 64
LEN = 1024
Q_BLOCK = 512


epsilon = 1e-05
masked_score = -1000000000.0


def layer_norm(values, gain, shift):
    center = values - jnp.mean(values, axis=-1, keepdims=True)
    spread = jnp.mean(center * center, axis=-1, keepdims=True)
    return center * lax.rsqrt(spread + epsilon) * gain + shift


def gelu_exact(values):
    return jax.nn.gelu(values, approximate=False)


def contract_rows(left, right):
    return lax.dot_general(
        left, right, (((0,), (0,)), ((), ())), preferred_element_type=jnp.float32
    )


def contract_cols(left, right):
    return lax.dot_general(
        left, right, (((1,), (1,)), ((), ())), preferred_element_type=jnp.float32
    )


def block_scores(q_block, k_seq, key_valid):
    scores = jnp.einsum(
        "qhd,khd->hqk", q_block, k_seq, preferred_element_type=jnp.float32
    ) * HEAD_DIM ** (-0.5)
    return jnp.where(key_valid[None, None, :], scores, masked_score)


def attend_forward(q_seq, k_seq, v_seq, length):
    local_heads = q_seq.shape[1]
    key_valid = jnp.arange(LEN, dtype=jnp.int32) < length
    q_blocks = q_seq.reshape(LEN // Q_BLOCK, Q_BLOCK, local_heads, HEAD_DIM)

    def one_block(q_block):
        scores = block_scores(q_block, k_seq, key_valid)
        row_peak = jnp.max(scores, axis=-1, keepdims=True)
        shifted = jnp.exp(scores - row_peak)
        row_total = jnp.sum(shifted, axis=-1, keepdims=True)
        attn_probs = (shifted / row_total).astype(jnp.bfloat16)
        context = jnp.einsum("hqk,khd->qhd", attn_probs, v_seq, preferred_element_type=jnp.float32)
        return (context.astype(jnp.bfloat16), (row_peak + jnp.log(row_total))[..., 0])

    context, log_total = lax.map(one_block, q_blocks)
    return (context.reshape(LEN, local_heads, HEAD_DIM), log_total)


def attend_backward(q_seq, k_seq, v_seq, grad_seq, log_total, length):
    local_heads = q_seq.shape[1]
    score_scale = HEAD_DIM ** (-0.5)
    key_valid = jnp.arange(LEN, dtype=jnp.int32) < length
    q_blocks = q_seq.reshape(LEN // Q_BLOCK, Q_BLOCK, local_heads, HEAD_DIM)
    g_blocks = grad_seq.reshape(LEN // Q_BLOCK, Q_BLOCK, local_heads, HEAD_DIM)

    def one_block(accum, block_item):
        q_block, g_block, lse_block = block_item
        scores = block_scores(q_block, k_seq, key_valid)
        attn_probs = jnp.exp(scores - lse_block[..., None])
        grad_probs = jnp.einsum("qhd,khd->hqk", g_block, v_seq, preferred_element_type=jnp.float32)
        row_dot = jnp.sum(attn_probs * grad_probs, axis=-1, keepdims=True)
        grad_scores = (attn_probs * (grad_probs - row_dot)).astype(jnp.bfloat16)
        grad_q = (
            jnp.einsum("hqk,khd->qhd", grad_scores, k_seq, preferred_element_type=jnp.float32)
            * score_scale
        )
        grad_k = (
            accum[0]
            + jnp.einsum("hqk,qhd->khd", grad_scores, q_block, preferred_element_type=jnp.float32)
            * score_scale
        )
        grad_v = accum[1] + jnp.einsum(
            "hqk,qhd->khd",
            attn_probs.astype(jnp.bfloat16),
            g_block,
            preferred_element_type=jnp.float32,
        )
        return ((grad_k, grad_v), grad_q.astype(jnp.bfloat16))

    zero_keys = jnp.zeros((LEN, local_heads, HEAD_DIM), jnp.float32)
    (grad_k, grad_v), grad_q = lax.scan(
        one_block, (zero_keys, zero_keys), (q_blocks, g_blocks, log_total)
    )
    return (
        grad_q.reshape(LEN, local_heads, HEAD_DIM),
        grad_k.astype(jnp.bfloat16),
        grad_v.astype(jnp.bfloat16),
    )


def body(
    tokens,
    lengths,
    w_qkv,
    q_bias,
    v_bias,
    w_out,
    out_bias,
    gain_one,
    shift_one,
    w_up,
    up_bias,
    w_down,
    down_bias,
    gain_two,
    shift_two,
    cotangent,
):
    seq_count, local_len, model_width = tokens.shape
    row_count = seq_count * local_len
    head_count = model_width // HEAD_DIM
    gathered = (
        lax.all_gather(w_qkv, "shard", axis=0, tiled=True),
        lax.all_gather(q_bias, "shard", axis=0, tiled=True),
        lax.all_gather(v_bias, "shard", axis=0, tiled=True),
        lax.all_gather(w_out, "shard", axis=0, tiled=True),
        lax.all_gather(out_bias, "shard", axis=0, tiled=True),
        lax.all_gather(gain_one, "shard", axis=0, tiled=True),
        lax.all_gather(shift_one, "shard", axis=0, tiled=True),
        lax.all_gather(w_up, "shard", axis=0, tiled=True),
        lax.all_gather(up_bias, "shard", axis=0, tiled=True),
        lax.all_gather(w_down, "shard", axis=0, tiled=True),
        lax.all_gather(down_bias, "shard", axis=0, tiled=True),
        lax.all_gather(gain_two, "shard", axis=0, tiled=True),
        lax.all_gather(shift_two, "shard", axis=0, tiled=True),
    )
    (
        full_qkv,
        full_q_bias,
        full_v_bias,
        full_out,
        full_out_bias,
        full_gain_one,
        full_shift_one,
        full_up,
        full_up_bias,
        full_down,
        full_down_bias,
        full_gain_two,
        full_shift_two,
    ) = gathered
    token_rows = tokens.reshape(row_count, model_width)
    joined_bias = jnp.concatenate([full_q_bias, jnp.zeros_like(full_q_bias), full_v_bias]).astype(
        jnp.float32
    )
    qkv_rows = (
        jnp.dot(token_rows, full_qkv, preferred_element_type=jnp.float32) + joined_bias
    ).astype(jnp.bfloat16)
    qkv_tokens = qkv_rows.reshape(seq_count, local_len, 3, head_count, HEAD_DIM)
    qkv_heads = lax.all_to_all(qkv_tokens, "seq", split_axis=3, concat_axis=1, tiled=True)

    def forward_seq(seq_item):
        qkv_seq, length = seq_item
        return attend_forward(qkv_seq[:, 0], qkv_seq[:, 1], qkv_seq[:, 2], length)

    context_heads, log_total = lax.map(forward_seq, (qkv_heads, lengths))
    context_tokens = lax.all_to_all(context_heads, "seq", split_axis=1, concat_axis=2, tiled=True)
    context_rows = context_tokens.reshape(row_count, model_width)
    residual_one = (
        token_rows.astype(jnp.float32)
        + jnp.dot(context_rows, full_out, preferred_element_type=jnp.float32)
        + full_out_bias.astype(jnp.float32)
    )
    normed_one, norm_one_pull = jax.vjp(
        layer_norm,
        residual_one,
        full_gain_one.astype(jnp.float32),
        full_shift_one.astype(jnp.float32),
    )
    normed_low = normed_one.astype(jnp.bfloat16)
    up_rows = jnp.dot(
        normed_low, full_up, preferred_element_type=jnp.float32
    ) + full_up_bias.astype(jnp.float32)
    active, gelu_pull = jax.vjp(gelu_exact, up_rows)
    active_low = active.astype(jnp.bfloat16)
    residual_two = (
        normed_one
        + jnp.dot(active_low, full_down, preferred_element_type=jnp.float32)
        + full_down_bias.astype(jnp.float32)
    )
    final_rows, norm_two_pull = jax.vjp(
        layer_norm,
        residual_two,
        full_gain_two.astype(jnp.float32),
        full_shift_two.astype(jnp.float32),
    )
    output = final_rows.astype(jnp.bfloat16).reshape(tokens.shape)
    back_qkv, back_out, back_up, back_down = (full_qkv, full_out, full_up, full_down)
    grad_rows = cotangent.reshape(row_count, model_width).astype(jnp.float32)
    grad_two, grad_gain_two, grad_shift_two = norm_two_pull(grad_rows)
    grad_down_bias = jnp.sum(grad_two, axis=0)
    grad_two_low = grad_two.astype(jnp.bfloat16)
    grad_w_down = contract_rows(active_low, grad_two_low)
    grad_active = contract_cols(grad_two_low, back_down)
    (grad_up,) = gelu_pull(grad_active)
    grad_up_bias = jnp.sum(grad_up, axis=0)
    grad_up_low = grad_up.astype(jnp.bfloat16)
    grad_w_up = contract_rows(normed_low, grad_up_low)
    grad_normed = grad_two + contract_cols(grad_up_low, back_up)
    grad_one, grad_gain_one, grad_shift_one = norm_one_pull(grad_normed)
    grad_out_bias = jnp.sum(grad_one, axis=0)
    grad_one_low = grad_one.astype(jnp.bfloat16)
    grad_w_out = contract_rows(context_rows, grad_one_low)
    grad_context = contract_cols(grad_one_low, back_out).astype(jnp.bfloat16)
    grad_context = grad_context.reshape(seq_count, local_len, head_count, HEAD_DIM)
    grad_context_heads = lax.all_to_all(
        grad_context, "seq", split_axis=2, concat_axis=1, tiled=True
    )

    def backward_seq(seq_item):
        qkv_seq, grad_seq, lse_seq, length = seq_item
        grad_q, grad_k, grad_v = attend_backward(
            qkv_seq[:, 0], qkv_seq[:, 1], qkv_seq[:, 2], grad_seq, lse_seq, length
        )
        return jnp.stack([grad_q, grad_k, grad_v], axis=1)

    grad_qkv_heads = lax.map(backward_seq, (qkv_heads, grad_context_heads, log_total, lengths))
    grad_qkv_tokens = lax.all_to_all(grad_qkv_heads, "seq", split_axis=1, concat_axis=3, tiled=True)
    grad_qkv_rows = grad_qkv_tokens.reshape(row_count, 3 * model_width)
    grad_q_bias = jnp.sum(grad_qkv_rows[:, :model_width], axis=0, dtype=jnp.float32)
    grad_v_bias = jnp.sum(grad_qkv_rows[:, 2 * model_width :], axis=0, dtype=jnp.float32)
    grad_w_qkv = contract_rows(token_rows, grad_qkv_rows)
    grad_tokens = grad_one + contract_cols(grad_qkv_rows, back_qkv)
    grad_tokens = grad_tokens.astype(jnp.bfloat16).reshape(tokens.shape)
    owned = (
        lax.psum_scatter(grad_w_qkv, "shard", scatter_dimension=0, tiled=True),
        lax.psum_scatter(grad_q_bias, "shard", scatter_dimension=0, tiled=True),
        lax.psum_scatter(grad_v_bias, "shard", scatter_dimension=0, tiled=True),
        lax.psum_scatter(grad_w_out, "shard", scatter_dimension=0, tiled=True),
        lax.psum_scatter(grad_out_bias, "shard", scatter_dimension=0, tiled=True),
        lax.psum_scatter(grad_gain_one, "shard", scatter_dimension=0, tiled=True),
        lax.psum_scatter(grad_shift_one, "shard", scatter_dimension=0, tiled=True),
        lax.psum_scatter(grad_w_up, "shard", scatter_dimension=0, tiled=True),
        lax.psum_scatter(grad_up_bias, "shard", scatter_dimension=0, tiled=True),
        lax.psum_scatter(grad_w_down, "shard", scatter_dimension=0, tiled=True),
        lax.psum_scatter(grad_down_bias, "shard", scatter_dimension=0, tiled=True),
        lax.psum_scatter(grad_gain_two, "shard", scatter_dimension=0, tiled=True),
        lax.psum_scatter(grad_shift_two, "shard", scatter_dimension=0, tiled=True),
    )
    owned_columns = (
        lax.psum_scatter(
            owned[0].astype(jnp.bfloat16), "seq", scatter_dimension=1, tiled=True
        ).astype(jnp.float32),
        lax.psum_scatter(
            owned[3].astype(jnp.bfloat16), "seq", scatter_dimension=1, tiled=True
        ).astype(jnp.float32),
        lax.psum_scatter(
            owned[7].astype(jnp.bfloat16), "seq", scatter_dimension=1, tiled=True
        ).astype(jnp.float32),
        lax.psum_scatter(
            owned[9].astype(jnp.bfloat16), "seq", scatter_dimension=1, tiled=True
        ).astype(jnp.float32),
    )
    matrices = (
        lax.all_gather(owned_columns[0].astype(jnp.bfloat16), "seq", axis=1, tiled=True).astype(
            jnp.float32
        ),
        lax.all_gather(owned_columns[1].astype(jnp.bfloat16), "seq", axis=1, tiled=True).astype(
            jnp.float32
        ),
        lax.all_gather(owned_columns[2].astype(jnp.bfloat16), "seq", axis=1, tiled=True).astype(
            jnp.float32
        ),
        lax.all_gather(owned_columns[3].astype(jnp.bfloat16), "seq", axis=1, tiled=True).astype(
            jnp.float32
        ),
    )
    vectors = lax.psum(
        (
            owned[1],
            owned[2],
            owned[4],
            owned[5],
            owned[6],
            owned[8],
            owned[10],
            owned[11],
            owned[12],
        ),
        "seq",
    )
    result_qkv, result_out, result_up, result_down = (
        matrices[0],
        matrices[1],
        matrices[2],
        matrices[3],
    )
    result_q_bias, result_v_bias, result_out_bias = (vectors[0], vectors[1], vectors[2])
    result_gain_one, result_shift_one, result_up_bias = (vectors[3], vectors[4], vectors[5])
    result_down_bias, result_gain_two, result_shift_two = (vectors[6], vectors[7], vectors[8])
    return (
        output,
        grad_tokens,
        result_qkv,
        result_q_bias,
        result_v_bias,
        result_out,
        result_out_bias,
        result_gain_one,
        result_shift_one,
        result_up,
        result_up_bias,
        result_down,
        result_down_bias,
        result_gain_two,
        result_shift_two,
    )


AXES = ("seq", "z", "core")
NORMAL_SCALE = 0.3989422804014327
HALF_ROOT = 0.7071067811865476


def dot_nn(left, right):
    return lax.dot_general(
        left, right, (((1,), (0,)), ((), ())), preferred_element_type=jnp.float32
    )


def dot_nt(left, right):
    return contract_cols(left, right)


def dot_tn(left, right):
    return contract_rows(left, right)


def vmem_specs(count):
    return [pl.BlockSpec(memory_space=pltpu.VMEM)] * count


def work(micros):
    return pl.CostEstimate(
        flops=int(micros * 9e8), transcendentals=0, bytes_accessed=int(micros * 3e6)
    )


def smem_spec():
    return pl.BlockSpec(memory_space=pltpu.SMEM)


def key_bias(sc, block_rows):
    length, place = sc[0], sc[1]
    columns = []
    for j in range(4):
        position = (place ^ j) * block_rows + lax.broadcasted_iota(
            jnp.int32, (block_rows, 1), 0
        )
        columns.append(jnp.where(position < length, 0.0, masked_score))
    return jnp.concatenate(columns, axis=0)


def attend_forward_kernel(
    sc, t0, t1, t2, t3, own, other, qkv, ctx_t, c0, c1, c2, c3, lse, weight, vectors
):
    place, core, level = sc[1], sc[2], sc[3]
    rows = t0.shape[0]
    shard_rows = weight.shape[2]
    width = weight.shape[3]
    head_width = width // 3
    heads = head_width // HEAD_DIM
    for k in range(4):
        for block, side in ((own, core), (other, 1 - core)):
            weight[level ^ k, side] = block[k, :shard_rows, :]
            vectors[level ^ k, side] = block[k, shard_rows + 1 : shard_rows + 3, :].astype(
                jnp.float32
            )
    full = weight[...].reshape(-1, width)
    bias = (
        own[level ^ place, shard_rows : shard_rows + 1, :].astype(jnp.float32)
        + other[level ^ place, shard_rows : shard_rows + 1, :].astype(jnp.float32)
    )
    for j, block in enumerate((t0, t1, t2, t3)):
        qkv[j * rows : (j + 1) * rows, :] = (dot_nn(block[...], full) + bias).astype(jnp.bfloat16)
    mask = key_bias(sc, rows)
    for j, out in enumerate((c0, c1, c2, c3)):
        parts = []
        q_all = qkv[j * rows : (j + 1) * rows, 0:head_width] * jnp.bfloat16(HEAD_DIM**-0.5)
        for h in range(heads):
            low = h * HEAD_DIM
            q = q_all[:, low : low + HEAD_DIM]
            k = qkv[:, head_width + low : head_width + low + HEAD_DIM]
            v = qkv[:, 2 * head_width + low : 2 * head_width + low + HEAD_DIM]
            scores = dot_nt(k, q) + mask
            peak = jnp.max(scores, axis=0, keepdims=True)
            shifted = jnp.exp(scores - peak)
            total = jnp.sum(shifted, axis=0, keepdims=True)
            part = dot_tn(v, shifted.astype(jnp.bfloat16)) / total
            parts.append(part)
            lse[h : h + 1, j * rows : (j + 1) * rows] = peak + jnp.log(total)
        joined = jnp.concatenate(parts, axis=0)
        ctx_t[:, j * rows : (j + 1) * rows] = joined
        out[...] = joined.T.astype(jnp.bfloat16)


def attend_backward_kernel(sc, qkv, ctx_t, lse, g0, g1, g2, g3, dqkv, dk_acc, dv_acc):
    rows = g0.shape[0]
    head_width = g0.shape[1]
    heads = head_width // HEAD_DIM
    mask = key_bias(sc, rows)
    scale = jnp.bfloat16(HEAD_DIM**-0.5)
    for j, g_ref in enumerate((g0, g1, g2, g3)):
        span = slice(j * rows, (j + 1) * rows)
        g_all = g_ref[...]
        product = g_all.astype(jnp.float32).T * ctx_t[:, span]
        q_all = qkv[span, 0:head_width] * scale
        parts = []
        for h in range(heads):
            low = h * HEAD_DIM
            q = q_all[:, low : low + HEAD_DIM]
            g = g_all[:, low : low + HEAD_DIM]
            k = qkv[:, head_width + low : head_width + low + HEAD_DIM]
            v = qkv[:, 2 * head_width + low : 2 * head_width + low + HEAD_DIM]
            probs = jnp.exp(dot_nt(k, q) + mask - lse[h : h + 1, span])
            row_dot = jnp.sum(product[low : low + HEAD_DIM, :], axis=0, keepdims=True)
            grad_scores = (probs * (dot_nt(v, g) - row_dot)).astype(jnp.bfloat16)
            grad_v = dot_nn(probs.astype(jnp.bfloat16), g)
            grad_k = dot_nn(grad_scores, q)
            if j == 0:
                dv_acc[h] = grad_v
                dk_acc[h] = grad_k
            else:
                dv_acc[h] += grad_v
                dk_acc[h] += grad_k
            parts.append(dot_tn(k, grad_scores) * (HEAD_DIM**-0.5))
        dqkv[span, 0:head_width] = jnp.concatenate(parts, axis=0).T.astype(jnp.bfloat16)
    dk = jnp.concatenate([dk_acc[h] for h in range(heads)], axis=1)
    dv = jnp.concatenate([dv_acc[h] for h in range(heads)], axis=1)
    dqkv[:, head_width:] = jnp.concatenate([dk, dv], axis=1).astype(jnp.bfloat16)


def grad_qkv_weight_kernel(sc, t0, t1, t2, t3, dqkv, keep, send, sums):
    core = sc[2]
    rows = t0.shape[0]
    total = None
    for j, block in enumerate((t0, t1, t2, t3)):
        part = dot_tn(block[...], dqkv[j * rows : (j + 1) * rows, :])
        total = part if total is None else total + part
    sums[...] = jnp.sum(dqkv[...].astype(jnp.float32), axis=0, keepdims=True)
    shard_rows = keep.shape[1]
    low = total.astype(jnp.bfloat16)
    for z in range(keep.shape[0]):
        even = low[(2 * z) * shard_rows : (2 * z + 1) * shard_rows]
        odd = low[(2 * z + 1) * shard_rows : (2 * z + 2) * shard_rows]
        keep[z] = jnp.where(core == 0, even, odd)
        send[z] = jnp.where(core == 0, odd, even)


def grad_tokens_kernel(dqkv, weight, o0, o1, o2, o3):
    rows = o0.shape[0]
    full = weight[...].reshape(-1, weight.shape[3])
    for j, out in enumerate((o0, o1, o2, o3)):
        part = dot_nt(dqkv[j * rows : (j + 1) * rows, :], full)
        out[...] = part.astype(out.dtype)


def normalize(values):
    center = values - jnp.mean(values, axis=-1, keepdims=True)
    inverse = lax.rsqrt(jnp.mean(center * center, axis=-1, keepdims=True) + epsilon)
    return center * inverse, inverse


def normalize_back(grad, unit, inverse):
    return inverse * (
        grad
        - jnp.mean(grad, axis=-1, keepdims=True)
        - unit * jnp.mean(grad * unit, axis=-1, keepdims=True)
    )


def middle_kernel(
    sc,
    x0,
    x1,
    x2,
    x3,
    token,
    cotangent,
    small,
    up_bias,
    gathered,
    output,
    grad_one,
    y0,
    y1,
    y2,
    y3,
    keep,
    send,
    sums,
    up_sums,
    w_out,
    w_up,
    w_down,
    slope,
    active,
    grad_up,
    context,
    sems,
):
    place, core = sc[1], sc[2]
    blocks = w_up.shape[0]
    shard_rows = w_up.shape[3]
    width = w_up.shape[4]
    third = shard_rows // 3
    copies = []
    for b in range(blocks):
        copies.append(
            pltpu.make_async_copy(gathered.at[:, :, b, 0:shard_rows, :], w_up.at[b], sems.at[b])
        )
    copies.append(
        pltpu.make_async_copy(
            gathered.at[:, :, :, shard_rows : 2 * shard_rows, :], w_down, sems.at[blocks]
        )
    )
    out_copies = [
        pltpu.make_async_copy(
            gathered.at[:, :, b, 2 * shard_rows : 2 * shard_rows + third, :],
            w_out.at[:, :, b * third : (b + 1) * third, :],
            sems.at[blocks + 1 + b],
        )
        for b in range(3)
    ]
    for copy in out_copies + copies:
        copy.start()
    for copy in out_copies:
        copy.wait()
    out_rows = 2 * shard_rows

    def out_block(j):
        return w_out[place ^ j].reshape(out_rows, width)

    residual = token[...].astype(jnp.float32) + small[0:1, :]
    for j, block in enumerate((x0, x1, x2, x3)):
        residual = residual + dot_nn(block[...], out_block(j))
    unit_one, inverse_one = normalize(residual)
    gain_one = small[1:2, :]
    normed = unit_one * gain_one + small[2:3, :]
    normed_low = normed.astype(jnp.bfloat16)
    for b in range(blocks):
        copies[b].wait()
        span = slice(b * width, (b + 1) * width)
        up = dot_nn(normed_low, w_up[b].reshape(width, width)) + up_bias[:, span]
        phi = 0.5 + 0.5 * lax.erf(up * HALF_ROOT)
        slope[:, span] = phi + up * (jnp.exp(-0.5 * up * up) * NORMAL_SCALE)
        active[:, span] = (up * phi).astype(jnp.bfloat16)
    copies[blocks].wait()
    residual = normed + small[3:4, :] + dot_nn(active[...], w_down[...].reshape(-1, width))
    unit_two, inverse_two = normalize(residual)
    gain_two = small[4:5, :]
    output[...] = (unit_two * gain_two + small[5:6, :]).astype(jnp.bfloat16)
    grad = cotangent[...].astype(jnp.float32)
    sums[3:4, :] = jnp.sum(grad * unit_two, axis=0, keepdims=True)
    sums[4:5, :] = jnp.sum(grad, axis=0, keepdims=True)
    grad_two = normalize_back(grad * gain_two, unit_two, inverse_two)
    sums[5:6, :] = jnp.sum(grad_two, axis=0, keepdims=True)
    two_low = grad_two.astype(jnp.bfloat16)
    grad_normed = grad_two
    for b in range(blocks):
        span = slice(b * width, (b + 1) * width)
        rows_down = w_down[b].reshape(width, width)
        part = dot_nt(two_low, rows_down) * slope[:, span]
        up_sums[:, span] = jnp.sum(part, axis=0, keepdims=True)
        part = part.astype(jnp.bfloat16)
        grad_up[:, span] = part
        grad_normed = grad_normed + dot_nt(part, w_up[b].reshape(width, width))
    sums[1:2, :] = jnp.sum(grad_normed * unit_one, axis=0, keepdims=True)
    sums[2:3, :] = jnp.sum(grad_normed, axis=0, keepdims=True)
    first = normalize_back(grad_normed * gain_one, unit_one, inverse_one)
    sums[0:1, :] = jnp.sum(first, axis=0, keepdims=True)
    sums[6:8, :] = jnp.zeros((2, width), jnp.float32)
    grad_one[...] = first
    one_low = first.astype(jnp.bfloat16)
    for j, out in enumerate((y0, y1, y2, y3)):
        out[...] = dot_nt(one_low, out_block(j)).astype(jnp.bfloat16)
    for j, block in enumerate((x0, x1, x2, x3)):
        context[place ^ j] = block[...]
    joined = jnp.concatenate([context[j] for j in range(4)], axis=1)
    half = width // 2
    down_rows = blocks * shard_rows
    for ref, mine in ((keep, core), (send, 1 - core)):
        for z in range(4):
            even = active[:, (2 * z) * down_rows : (2 * z + 1) * down_rows]
            odd = active[:, (2 * z + 1) * down_rows : (2 * z + 2) * down_rows]
            ref[:, z * down_rows : (z + 1) * down_rows] = jnp.where(mine == 0, even, odd)
        at = 4 * down_rows
        ref[:, at : at + width] = two_low
        at += width
        ref[:, at : at + width] = normed_low
        at += width
        ref[:, at : at + 2 * width] = jnp.where(
            mine == 0, grad_up[:, : 2 * width], grad_up[:, 2 * width :]
        )
        at += 2 * width
        ref[:, at : at + width] = joined
        at += width
        ref[:, at : at + half] = jnp.where(mine == 0, one_low[:, :half], one_low[:, half:])


def down_grad_kernel(sc, keep, got, d0, d1, d2, d3, part):
    place = sc[1]
    zs, shard_rows, width = d0.shape
    down_rows = 4 * shard_rows
    at_two = zs * down_rows
    right = slice(at_two, at_two + width)
    for z in range(zs):
        left = slice(z * down_rows, (z + 1) * down_rows)
        total = dot_tn(keep[:, left], keep[:, right]) + dot_tn(got[:, left], got[:, right])
        part[...] = total.astype(jnp.bfloat16).reshape(4, shard_rows, width)
        for j, out in enumerate((d0, d1, d2, d3)):
            out[z] = part[place ^ j]


def up_grad_kernel(sc, keep, got, u0, u1, u2, u3, part):
    place = sc[1]
    zs, block_rows, cols = u0.shape
    quarter = part.shape[2]
    pair_rows = block_rows - quarter
    width = zs * pair_rows
    at_norm = 2 * width + width
    at_up = at_norm + width
    at_ctx = at_up + 2 * width
    at_one = at_ctx + width
    left = slice(at_ctx, at_ctx + width)
    right = slice(at_one, at_one + cols)
    total = dot_tn(keep[:, left], keep[:, right]) + dot_tn(got[:, left], got[:, right])
    part[...] = total.astype(jnp.bfloat16).reshape(part.shape)
    left = slice(at_norm, at_norm + width)
    for j, out in enumerate((u0, u1, u2, u3)):
        right = pl.ds(pl.multiple_of(at_up + (place ^ j) * cols, 128), cols)
        total = dot_tn(keep[:, left], keep[:, right]) + dot_tn(got[:, left], got[:, right])
        total = total.astype(jnp.bfloat16)
        for z in range(zs):
            out[z, :pair_rows] = total[z * pair_rows : (z + 1) * pair_rows]
            out[z, pair_rows:] = part[z, place ^ j]


def level_blocks_kernel(sc, *refs):
    level = sc[3]
    ins, outs = refs[:-4], refs[-4:]
    for k, out in enumerate(outs):
        total = ins[0][level ^ k].astype(jnp.float32)
        for ref in ins[1:]:
            total = total + ref[level ^ k].astype(jnp.float32)
        out[...] = total.astype(jnp.bfloat16)


def block_sum(refs):
    total = refs[0][...].astype(jnp.float32)
    for ref in refs[1:]:
        total = total + ref[...].astype(jnp.float32)
    return total


def split_up_kernel(sc, e0, e1, e2, e3, keep, send, held):
    core = sc[2]
    shard_rows = (keep.shape[0] * 2) // 3
    held[...] = block_sum((e0, e1, e2, e3)).astype(jnp.bfloat16)
    for ref, side in ((keep, core), (send, 1 - core)):
        ref[:shard_rows] = held[pl.ds(pl.multiple_of(side * shard_rows, 16), shard_rows), :]
        ref[shard_rows:] = held[2 * shard_rows :, :]


def join_kernel(sc, e0, e1, e2, e3, keep, got, out):
    core = sc[2]
    shard_rows = e0.shape[0]
    cols = keep.shape[1]
    out[:shard_rows] = block_sum((e0, e1, e2, e3)).astype(jnp.bfloat16)
    for ref, side in ((keep, core), (got, 1 - core)):
        out[shard_rows:, pl.ds(pl.multiple_of(side * cols, 128), cols)] = ref[...]


def finish_kernel(sc, b0, b1, b2, b3, down, up, out):
    place, core = sc[1], sc[2]
    shard_rows = up.shape[0]
    quarter = shard_rows // 2
    cols = b0.shape[1] // 2
    for j, ref in enumerate((b0, b1, b2, b3)):
        where = place ^ j
        rows = pl.ds(pl.multiple_of(where * shard_rows, 8), shard_rows)
        down[rows, :] = ref[:shard_rows].astype(jnp.float32)
        for side in range(2):
            at = pl.multiple_of((side * 4 + where) * cols, 128)
            up[:, pl.ds(at, cols)] = ref[
                shard_rows : 2 * shard_rows, side * cols : (side + 1) * cols
            ].astype(jnp.float32)

        @pl.when(where // 2 == core)
        def _(ref=ref, where=where):
            at = pl.multiple_of((where % 2) * quarter, 8)
            out[pl.ds(at, quarter), :] = ref[2 * shard_rows :].astype(jnp.float32)


def sum_kernel(e0, e1, e2, e3, out):
    out[...] = block_sum((e0, e1, e2, e3)).astype(out.dtype)


def finish_qkv_kernel(sc, b0, b1, b2, b3, out, held):
    place = sc[1]
    head_width = b0.shape[1] // 3
    for j, ref in enumerate((b0, b1, b2, b3)):
        held[place ^ j] = ref[...].astype(jnp.float32)
    for part in range(3):
        for s in range(4):
            at = (part * 4 + s) * head_width
            out[:, at : at + head_width] = held[s, :, part * head_width : (part + 1) * head_width]


def finish_tokens_kernel(first, o0, o1, o2, o3, out):
    out[...] = (first[...] + block_sum((o0, o1, o2, o3))).astype(out.dtype)


def fast_body(
    tokens,
    lengths,
    w_qkv,
    q_bias,
    v_bias,
    w_out,
    out_bias,
    gain_one,
    shift_one,
    w_up,
    up_bias,
    w_down,
    down_bias,
    gain_two,
    shift_two,
    cotangent,
):
    bf16, f32 = jnp.bfloat16, jnp.float32
    _, rows, width = tokens.shape
    shard_rows = w_qkv.shape[0]
    hidden = w_up.shape[1]
    head_width = width // 4
    place = lax.axis_index("seq")
    core = lax.axis_index("core")
    zs = 4
    third = shard_rows // 3
    swap = [(0, 1), (1, 0)]

    def struct(shape, dtype=bf16):
        return jax.ShapeDtypeStruct(shape, dtype)

    def across(value, step):
        return lax.ppermute(value, "seq", [(i, i ^ step) for i in range(4)])

    def partner(value):
        return lax.ppermute(value, "core", swap)

    def level_across(value, step):
        return lax.ppermute(value, "z", [(i, i ^ step) for i in range(4)])

    token = tokens[0]
    quarter = jnp.concatenate(
        [
            lax.dynamic_slice_in_dim(w_up, place * width, width, axis=1),
            lax.dynamic_slice_in_dim(w_down, place * shard_rows, shard_rows, axis=0),
            lax.dynamic_slice_in_dim(w_out, jnp.minimum(place, 2) * third, third, axis=0),
        ],
        axis=0,
    )
    gathered = lax.all_gather(quarter, ("z", "core", "seq"), axis=0, tiled=True)
    gathered = gathered.reshape(zs, 2, 4, 2 * shard_rows + third, width)
    columns = lax.dynamic_index_in_dim(
        w_qkv.reshape(shard_rows, 3, 4, head_width), place, axis=2, keepdims=False
    ).reshape(shard_rows, 3 * head_width)
    pair_rows = jnp.zeros((2, 2, shard_rows), bf16)
    placed_q = lax.dynamic_update_slice(pair_rows[0], q_bias[None], (core, 0)).reshape(1, -1)
    placed_v = lax.dynamic_update_slice(pair_rows[0], v_bias[None], (core, 0)).reshape(1, -1)
    bias_row = jnp.concatenate(
        [placed_q, jnp.zeros((1, head_width), bf16), placed_v], axis=1
    )
    vectors = jnp.concatenate(
        [out_bias, gain_one, shift_one, down_bias, gain_two, shift_two, up_bias]
    )
    pad = 15 * 3 * head_width - vectors.shape[0]
    vector_rows = jnp.pad(vectors, (0, pad)).reshape(15, 3 * head_width)
    own_block = jnp.concatenate([columns, bias_row, vector_rows], axis=0)
    t1, t2, t3 = across(token, 1), across(token, 2), across(token, 3)
    own_cols = jnp.stack([own_block] + [level_across(own_block, k) for k in (1, 2, 3)])
    other_cols = partner(own_cols)
    sc = jnp.stack([lengths[0], place, core, lax.axis_index("z")]).astype(jnp.int32)
    all_rows = 4 * rows
    qkv, ctx_t, c0, c1, c2, c3, lse, full_qkv, vector_sets = pl.pallas_call(
        attend_forward_kernel,
        name="attend_forward",
        cost_estimate=work(13),
        out_shape=(
            struct((all_rows, 3 * head_width)),
            struct((head_width, all_rows), f32),
            struct((rows, head_width)),
            struct((rows, head_width)),
            struct((rows, head_width)),
            struct((rows, head_width)),
            struct((head_width // HEAD_DIM, all_rows), f32),
            struct((zs, 2, shard_rows, 3 * head_width)),
            struct((zs, 2, 2, 3 * head_width), f32),
        ),
        in_specs=[smem_spec()] + vmem_specs(6),
        out_specs=tuple(vmem_specs(9)),
    )(sc, token, t1, t2, t3, own_cols, other_cols)
    x1, x2, x3 = across(c1, 1), across(c2, 2), across(c3, 3)
    all_vec = vector_sets.reshape(2 * zs, -1)
    six = all_vec[:, : 6 * shard_rows].reshape(2 * zs, 6, shard_rows)
    six = six.transpose(1, 0, 2).reshape(6, width)
    small = jnp.concatenate([six, jnp.zeros((2, width), f32)], axis=0)
    full_up_bias = all_vec[:, 6 * shard_rows : 6 * shard_rows + hidden // 8].reshape(1, hidden)
    packed = hidden // 2 + 5 * width + width // 2
    output, grad_one, y0, y1, y2, y3, keep, send, sums, up_sums = pl.pallas_call(
        middle_kernel,
        name="middle",
        cost_estimate=work(15),
        out_shape=(
            struct((rows, width)),
            struct((rows, width), f32),
            struct((rows, head_width)),
            struct((rows, head_width)),
            struct((rows, head_width)),
            struct((rows, head_width)),
            struct((rows, packed)),
            struct((rows, packed)),
            struct((8, width), f32),
            struct((1, hidden), f32),
        ),
        in_specs=[smem_spec()]
        + vmem_specs(8)
        + [pl.BlockSpec(memory_space=pl.ANY)],
        out_specs=tuple(vmem_specs(10)),
        scratch_shapes=[
            pltpu.VMEM((zs, 2, shard_rows, width), bf16),
            pltpu.VMEM((4, zs, 2, shard_rows, width), bf16),
            pltpu.VMEM((zs, 2, 4, shard_rows, width), bf16),
            pltpu.VMEM((rows, hidden), f32),
            pltpu.VMEM((rows, hidden), bf16),
            pltpu.VMEM((rows, hidden), bf16),
            pltpu.VMEM((4, rows, head_width), bf16),
            pltpu.SemaphoreType.DMA((8,)),
        ],
    )(
        sc,
        c0,
        x1,
        x2,
        x3,
        token,
        cotangent[0],
        small,
        full_up_bias,
        gathered,
    )
    g1, g2, g3 = across(y1, 1), across(y2, 2), across(y3, 3)
    got = partner(send)
    quad = hidden // 8

    def call(kernel, micros, outs, *args, scratch=(), scalars=True):
        return pl.pallas_call(
            kernel,
            name=kernel.__name__.replace("_kernel", ""),
            cost_estimate=work(micros),
            out_shape=tuple(outs),
            in_specs=([smem_spec()] if scalars else []) + vmem_specs(len(args)),
            out_specs=tuple(vmem_specs(len(outs))),
            scratch_shapes=list(scratch),
        )(*(((sc,) if scalars else ()) + args))

    d_blocks = call(
        down_grad_kernel,
        4,
        [struct((zs, shard_rows, width))] * 4,
        keep,
        got,
        scratch=[pltpu.VMEM((4, shard_rows, width), bf16)],
    )
    block_rows = 2 * shard_rows + shard_rows // 2
    u_blocks = call(
        up_grad_kernel,
        4,
        [struct((zs, block_rows, quad))] * 4,
        keep,
        got,
        scratch=[pltpu.VMEM((zs, 4, shard_rows // 2, quad), bf16)],
    )
    d_got = [across(d_blocks[j], j) for j in (1, 2, 3)]
    u_got = [across(u_blocks[j], j) for j in (1, 2, 3)]
    y0, d_own, u_own = lax.optimization_barrier((y0, d_blocks[0], u_blocks[0]))

    dqkv = pl.pallas_call(
        attend_backward_kernel,
        name="attend_backward",
        cost_estimate=work(11),
        out_shape=struct((all_rows, 3 * head_width)),
        in_specs=[smem_spec()] + vmem_specs(7),
        out_specs=pl.BlockSpec(memory_space=pltpu.VMEM),
        scratch_shapes=[
            pltpu.VMEM((head_width // HEAD_DIM, all_rows, HEAD_DIM), f32),
            pltpu.VMEM((head_width // HEAD_DIM, all_rows, HEAD_DIM), f32),
        ],
    )(sc, qkv, ctx_t, lse, y0, g1, g2, g3)
    q_keep, q_send, q_sums = pl.pallas_call(
        grad_qkv_weight_kernel,
        name="grad_qkv_weight",
        cost_estimate=work(4),
        out_shape=(
            struct((zs, shard_rows, 3 * head_width)),
            struct((zs, shard_rows, 3 * head_width)),
            struct((1, 3 * head_width), f32),
        ),
        in_specs=[smem_spec()] + vmem_specs(5),
        out_specs=tuple(vmem_specs(3)),
    )(sc, token, t1, t2, t3, dqkv)
    q_got = partner(q_send)
    o0, o1, o2, o3 = pl.pallas_call(
        grad_tokens_kernel,
        name="grad_tokens",
        cost_estimate=work(4),
        out_shape=(
            struct((rows, width), f32),
            struct((rows, width)),
            struct((rows, width)),
            struct((rows, width)),
        ),
        in_specs=vmem_specs(2),
        out_specs=tuple(vmem_specs(4)),
    )(dqkv, full_qkv)
    q_blocks = call(
        level_blocks_kernel, 1, [struct((shard_rows, 3 * head_width))] * 4, q_keep, q_got
    )
    q_levels = [level_across(q_blocks[k], k) for k in (1, 2, 3)]
    r1, r2, r3 = across(o1, 1), across(o2, 2), across(o3, 3)
    d_levels = call(
        level_blocks_kernel, 1, [struct((shard_rows, width))] * 4, d_own, *d_got
    )
    d_parts = [d_levels[0]] + [level_across(d_levels[k], k) for k in (1, 2, 3)]
    u_levels = call(
        level_blocks_kernel, 1, [struct((block_rows, quad))] * 4, u_own, *u_got
    )
    u_parts = [u_levels[0]] + [level_across(u_levels[k], k) for k in (1, 2, 3)]
    (q_part,) = call(
        sum_kernel,
        1,
        [struct((shard_rows, 3 * head_width))],
        q_blocks[0],
        *q_levels,
        scalars=False,
    )
    half_rows = shard_rows + shard_rows // 2
    u_keep, u_send = call(
        split_up_kernel,
        1,
        [struct((half_rows, quad))] * 2,
        *u_parts,
        scratch=[pltpu.VMEM((block_rows, quad), bf16)],
    )
    (joined,) = call(
        join_kernel,
        1,
        [struct((shard_rows + half_rows, width))],
        *d_parts,
        u_keep,
        partner(u_send),
    )
    result_down, result_up, result_out = call(
        finish_kernel,
        2,
        [
            struct((4 * shard_rows, width), f32),
            struct((shard_rows, hidden), f32),
            struct((shard_rows, width), f32),
        ],
        joined,
        *[across(joined, j) for j in (1, 2, 3)],
    )
    (result_qkv,) = call(
        finish_qkv_kernel,
        1,
        [struct((shard_rows, 3 * width), f32)],
        q_part,
        *[across(q_part, j) for j in (1, 2, 3)],
        scratch=[pltpu.VMEM((4, shard_rows, 3 * head_width), f32)],
    )
    (grad_tokens,) = call(
        finish_tokens_kernel,
        1,
        [struct((rows, width))],
        grad_one,
        o0,
        r1,
        r2,
        r3,
        scalars=False,
    )

    q_row = lax.dynamic_update_slice(
        jnp.zeros((1, width), f32), q_sums[:, :head_width], (0, place * head_width)
    )
    v_row = lax.dynamic_update_slice(
        jnp.zeros((1, width), f32), q_sums[:, 2 * head_width :], (0, place * head_width)
    )

    def everywhere(value):
        value = value + partner(value)
        value = value + across(value, 1)
        value = value + across(value, 2)
        value = value + level_across(value, 1)
        value = value + level_across(value, 2)
        return value

    early = everywhere(
        jnp.concatenate([sums[:6], up_sums.reshape(4, width), q_row, v_row], axis=0)
    )
    shard = 2 * lax.axis_index("z") + core

    def owned(vector):
        size = vector.shape[0] // (2 * zs)
        return lax.dynamic_slice(vector, (shard * size,), (size,))

    return (
        output[None],
        grad_tokens[None],
        result_qkv,
        owned(early[10]),
        owned(early[11]),
        result_out,
        owned(early[0]),
        owned(early[1]),
        owned(early[2]),
        result_up,
        owned(early[6:10].reshape(-1)),
        result_down,
        owned(early[5]),
        owned(early[3]),
        owned(early[4]),
    )


def solution(mesh):
    seq_count, shard_count = mesh.shape["seq"], mesh.shape["shard"]
    fast = seq_count == 4 and shard_count == 8
    if fast:
        grid = mesh.devices.reshape(seq_count, shard_count // 2, 2)
        mesh = jax.sharding.Mesh(grid, AXES)
    shard = ("z", "core") if fast else "shard"
    vector, matrix, rows = P(shard), P(shard, None), P(shard, "seq", None)
    return jax.shard_map(
        fast_body if fast else body,
        mesh=mesh,
        in_specs=(
            rows,
            vector,
            matrix,
            vector,
            vector,
            matrix,
            vector,
            vector,
            vector,
            matrix,
            vector,
            matrix,
            vector,
            vector,
            vector,
            rows,
        ),
        out_specs=(
            rows,
            rows,
            matrix,
            vector,
            vector,
            matrix,
            vector,
            vector,
            vector,
            matrix,
            vector,
            matrix,
            vector,
            vector,
            vector,
        ),
        check_vma=False,
    )
```

```python
import jax
import jax.numpy as jnp
from jax import lax
from jax.experimental import pallas as pl
from jax.experimental.pallas import tpu as pltpu
from jax.sharding import PartitionSpec as P

HEAD_DIM = 64
LEN = 1024
Q_BLOCK = 512


epsilon = 1e-05
masked_score = -1000000000.0


def layer_norm(values, gain, shift):
    center = values - jnp.mean(values, axis=-1, keepdims=True)
    spread = jnp.mean(center * center, axis=-1, keepdims=True)
    return center * lax.rsqrt(spread + epsilon) * gain + shift


def gelu_exact(values):
    return jax.nn.gelu(values, approximate=False)


def contract_rows(left, right):
    return lax.dot_general(
        left, right, (((0,), (0,)), ((), ())), preferred_element_type=jnp.float32
    )


def contract_cols(left, right):
    return lax.dot_general(
        left, right, (((1,), (1,)), ((), ())), preferred_element_type=jnp.float32
    )


def block_scores(q_block, k_seq, key_valid):
    scores = jnp.einsum(
        "qhd,khd->hqk", q_block, k_seq, preferred_element_type=jnp.float32
    ) * HEAD_DIM ** (-0.5)
    return jnp.where(key_valid[None, None, :], scores, masked_score)


def attend_forward(q_seq, k_seq, v_seq, length):
    local_heads = q_seq.shape[1]
    key_valid = jnp.arange(LEN, dtype=jnp.int32) < length
    q_blocks = q_seq.reshape(LEN // Q_BLOCK, Q_BLOCK, local_heads, HEAD_DIM)

    def one_block(q_block):
        scores = block_scores(q_block, k_seq, key_valid)
        row_peak = jnp.max(scores, axis=-1, keepdims=True)
        shifted = jnp.exp(scores - row_peak)
        row_total = jnp.sum(shifted, axis=-1, keepdims=True)
        attn_probs = (shifted / row_total).astype(jnp.bfloat16)
        context = jnp.einsum("hqk,khd->qhd", attn_probs, v_seq, preferred_element_type=jnp.float32)
        return (context.astype(jnp.bfloat16), (row_peak + jnp.log(row_total))[..., 0])

    context, log_total = lax.map(one_block, q_blocks)
    return (context.reshape(LEN, local_heads, HEAD_DIM), log_total)


def attend_backward(q_seq, k_seq, v_seq, grad_seq, log_total, length):
    local_heads = q_seq.shape[1]
    score_scale = HEAD_DIM ** (-0.5)
    key_valid = jnp.arange(LEN, dtype=jnp.int32) < length
    q_blocks = q_seq.reshape(LEN // Q_BLOCK, Q_BLOCK, local_heads, HEAD_DIM)
    g_blocks = grad_seq.reshape(LEN // Q_BLOCK, Q_BLOCK, local_heads, HEAD_DIM)

    def one_block(accum, block_item):
        q_block, g_block, lse_block = block_item
        scores = block_scores(q_block, k_seq, key_valid)
        attn_probs = jnp.exp(scores - lse_block[..., None])
        grad_probs = jnp.einsum("qhd,khd->hqk", g_block, v_seq, preferred_element_type=jnp.float32)
        row_dot = jnp.sum(attn_probs * grad_probs, axis=-1, keepdims=True)
        grad_scores = (attn_probs * (grad_probs - row_dot)).astype(jnp.bfloat16)
        grad_q = (
            jnp.einsum("hqk,khd->qhd", grad_scores, k_seq, preferred_element_type=jnp.float32)
            * score_scale
        )
        grad_k = (
            accum[0]
            + jnp.einsum("hqk,qhd->khd", grad_scores, q_block, preferred_element_type=jnp.float32)
            * score_scale
        )
        grad_v = accum[1] + jnp.einsum(
            "hqk,qhd->khd",
            attn_probs.astype(jnp.bfloat16),
            g_block,
            preferred_element_type=jnp.float32,
        )
        return ((grad_k, grad_v), grad_q.astype(jnp.bfloat16))

    zero_keys = jnp.zeros((LEN, local_heads, HEAD_DIM), jnp.float32)
    (grad_k, grad_v), grad_q = lax.scan(
        one_block, (zero_keys, zero_keys), (q_blocks, g_blocks, log_total)
    )
    return (
        grad_q.reshape(LEN, local_heads, HEAD_DIM),
        grad_k.astype(jnp.bfloat16),
        grad_v.astype(jnp.bfloat16),
    )


def body(
    tokens,
    lengths,
    w_qkv,
    q_bias,
    v_bias,
    w_out,
    out_bias,
    gain_one,
    shift_one,
    w_up,
    up_bias,
    w_down,
    down_bias,
    gain_two,
    shift_two,
    cotangent,
):
    seq_count, local_len, model_width = tokens.shape
    row_count = seq_count * local_len
    head_count = model_width // HEAD_DIM
    gathered = (
        lax.all_gather(w_qkv, "shard", axis=0, tiled=True),
        lax.all_gather(q_bias, "shard", axis=0, tiled=True),
        lax.all_gather(v_bias, "shard", axis=0, tiled=True),
        lax.all_gather(w_out, "shard", axis=0, tiled=True),
        lax.all_gather(out_bias, "shard", axis=0, tiled=True),
        lax.all_gather(gain_one, "shard", axis=0, tiled=True),
        lax.all_gather(shift_one, "shard", axis=0, tiled=True),
        lax.all_gather(w_up, "shard", axis=0, tiled=True),
        lax.all_gather(up_bias, "shard", axis=0, tiled=True),
        lax.all_gather(w_down, "shard", axis=0, tiled=True),
        lax.all_gather(down_bias, "shard", axis=0, tiled=True),
        lax.all_gather(gain_two, "shard", axis=0, tiled=True),
        lax.all_gather(shift_two, "shard", axis=0, tiled=True),
    )
    (
        full_qkv,
        full_q_bias,
        full_v_bias,
        full_out,
        full_out_bias,
        full_gain_one,
        full_shift_one,
        full_up,
        full_up_bias,
        full_down,
        full_down_bias,
        full_gain_two,
        full_shift_two,
    ) = gathered
    token_rows = tokens.reshape(row_count, model_width)
    joined_bias = jnp.concatenate([full_q_bias, jnp.zeros_like(full_q_bias), full_v_bias]).astype(
        jnp.float32
    )
    qkv_rows = (
        jnp.dot(token_rows, full_qkv, preferred_element_type=jnp.float32) + joined_bias
    ).astype(jnp.bfloat16)
    qkv_tokens = qkv_rows.reshape(seq_count, local_len, 3, head_count, HEAD_DIM)
    qkv_heads = lax.all_to_all(qkv_tokens, "seq", split_axis=3, concat_axis=1, tiled=True)

    def forward_seq(seq_item):
        qkv_seq, length = seq_item
        return attend_forward(qkv_seq[:, 0], qkv_seq[:, 1], qkv_seq[:, 2], length)

    context_heads, log_total = lax.map(forward_seq, (qkv_heads, lengths))
    context_tokens = lax.all_to_all(context_heads, "seq", split_axis=1, concat_axis=2, tiled=True)
    context_rows = context_tokens.reshape(row_count, model_width)
    residual_one = (
        token_rows.astype(jnp.float32)
        + jnp.dot(context_rows, full_out, preferred_element_type=jnp.float32)
        + full_out_bias.astype(jnp.float32)
    )
    normed_one, norm_one_pull = jax.vjp(
        layer_norm,
        residual_one,
        full_gain_one.astype(jnp.float32),
        full_shift_one.astype(jnp.float32),
    )
    normed_low = normed_one.astype(jnp.bfloat16)
    up_rows = jnp.dot(
        normed_low, full_up, preferred_element_type=jnp.float32
    ) + full_up_bias.astype(jnp.float32)
    active, gelu_pull = jax.vjp(gelu_exact, up_rows)
    active_low = active.astype(jnp.bfloat16)
    residual_two = (
        normed_one
        + jnp.dot(active_low, full_down, preferred_element_type=jnp.float32)
        + full_down_bias.astype(jnp.float32)
    )
    final_rows, norm_two_pull = jax.vjp(
        layer_norm,
        residual_two,
        full_gain_two.astype(jnp.float32),
        full_shift_two.astype(jnp.float32),
    )
    output = final_rows.astype(jnp.bfloat16).reshape(tokens.shape)
    back_qkv, back_out, back_up, back_down = (full_qkv, full_out, full_up, full_down)
    grad_rows = cotangent.reshape(row_count, model_width).astype(jnp.float32)
    grad_two, grad_gain_two, grad_shift_two = norm_two_pull(grad_rows)
    grad_down_bias = jnp.sum(grad_two, axis=0)
    grad_two_low = grad_two.astype(jnp.bfloat16)
    grad_w_down = contract_rows(active_low, grad_two_low)
    grad_active = contract_cols(grad_two_low, back_down)
    (grad_up,) = gelu_pull(grad_active)
    grad_up_bias = jnp.sum(grad_up, axis=0)
    grad_up_low = grad_up.astype(jnp.bfloat16)
    grad_w_up = contract_rows(normed_low, grad_up_low)
    grad_normed = grad_two + contract_cols(grad_up_low, back_up)
    grad_one, grad_gain_one, grad_shift_one = norm_one_pull(grad_normed)
    grad_out_bias = jnp.sum(grad_one, axis=0)
    grad_one_low = grad_one.astype(jnp.bfloat16)
    grad_w_out = contract_rows(context_rows, grad_one_low)
    grad_context = contract_cols(grad_one_low, back_out).astype(jnp.bfloat16)
    grad_context = grad_context.reshape(seq_count, local_len, head_count, HEAD_DIM)
    grad_context_heads = lax.all_to_all(
        grad_context, "seq", split_axis=2, concat_axis=1, tiled=True
    )

    def backward_seq(seq_item):
        qkv_seq, grad_seq, lse_seq, length = seq_item
        grad_q, grad_k, grad_v = attend_backward(
            qkv_seq[:, 0], qkv_seq[:, 1], qkv_seq[:, 2], grad_seq, lse_seq, length
        )
        return jnp.stack([grad_q, grad_k, grad_v], axis=1)

    grad_qkv_heads = lax.map(backward_seq, (qkv_heads, grad_context_heads, log_total, lengths))
    grad_qkv_tokens = lax.all_to_all(grad_qkv_heads, "seq", split_axis=1, concat_axis=3, tiled=True)
    grad_qkv_rows = grad_qkv_tokens.reshape(row_count, 3 * model_width)
    grad_q_bias = jnp.sum(grad_qkv_rows[:, :model_width], axis=0, dtype=jnp.float32)
    grad_v_bias = jnp.sum(grad_qkv_rows[:, 2 * model_width :], axis=0, dtype=jnp.float32)
    grad_w_qkv = contract_rows(token_rows, grad_qkv_rows)
    grad_tokens = grad_one + contract_cols(grad_qkv_rows, back_qkv)
    grad_tokens = grad_tokens.astype(jnp.bfloat16).reshape(tokens.shape)
    owned = (
        lax.psum_scatter(grad_w_qkv, "shard", scatter_dimension=0, tiled=True),
        lax.psum_scatter(grad_q_bias, "shard", scatter_dimension=0, tiled=True),
        lax.psum_scatter(grad_v_bias, "shard", scatter_dimension=0, tiled=True),
        lax.psum_scatter(grad_w_out, "shard", scatter_dimension=0, tiled=True),
        lax.psum_scatter(grad_out_bias, "shard", scatter_dimension=0, tiled=True),
        lax.psum_scatter(grad_gain_one, "shard", scatter_dimension=0, tiled=True),
        lax.psum_scatter(grad_shift_one, "shard", scatter_dimension=0, tiled=True),
        lax.psum_scatter(grad_w_up, "shard", scatter_dimension=0, tiled=True),
        lax.psum_scatter(grad_up_bias, "shard", scatter_dimension=0, tiled=True),
        lax.psum_scatter(grad_w_down, "shard", scatter_dimension=0, tiled=True),
        lax.psum_scatter(grad_down_bias, "shard", scatter_dimension=0, tiled=True),
        lax.psum_scatter(grad_gain_two, "shard", scatter_dimension=0, tiled=True),
        lax.psum_scatter(grad_shift_two, "shard", scatter_dimension=0, tiled=True),
    )
    owned_columns = (
        lax.psum_scatter(
            owned[0].astype(jnp.bfloat16), "seq", scatter_dimension=1, tiled=True
        ).astype(jnp.float32),
        lax.psum_scatter(
            owned[3].astype(jnp.bfloat16), "seq", scatter_dimension=1, tiled=True
        ).astype(jnp.float32),
        lax.psum_scatter(
            owned[7].astype(jnp.bfloat16), "seq", scatter_dimension=1, tiled=True
        ).astype(jnp.float32),
        lax.psum_scatter(
            owned[9].astype(jnp.bfloat16), "seq", scatter_dimension=1, tiled=True
        ).astype(jnp.float32),
    )
    matrices = (
        lax.all_gather(owned_columns[0].astype(jnp.bfloat16), "seq", axis=1, tiled=True).astype(
            jnp.float32
        ),
        lax.all_gather(owned_columns[1].astype(jnp.bfloat16), "seq", axis=1, tiled=True).astype(
            jnp.float32
        ),
        lax.all_gather(owned_columns[2].astype(jnp.bfloat16), "seq", axis=1, tiled=True).astype(
            jnp.float32
        ),
        lax.all_gather(owned_columns[3].astype(jnp.bfloat16), "seq", axis=1, tiled=True).astype(
            jnp.float32
        ),
    )
    vectors = lax.psum(
        (
            owned[1],
            owned[2],
            owned[4],
            owned[5],
            owned[6],
            owned[8],
            owned[10],
            owned[11],
            owned[12],
        ),
        "seq",
    )
    result_qkv, result_out, result_up, result_down = (
        matrices[0],
        matrices[1],
        matrices[2],
        matrices[3],
    )
    result_q_bias, result_v_bias, result_out_bias = (vectors[0], vectors[1], vectors[2])
    result_gain_one, result_shift_one, result_up_bias = (vectors[3], vectors[4], vectors[5])
    result_down_bias, result_gain_two, result_shift_two = (vectors[6], vectors[7], vectors[8])
    return (
        output,
        grad_tokens,
        result_qkv,
        result_q_bias,
        result_v_bias,
        result_out,
        result_out_bias,
        result_gain_one,
        result_shift_one,
        result_up,
        result_up_bias,
        result_down,
        result_down_bias,
        result_gain_two,
        result_shift_two,
    )


AXES = ("seq", "z", "core")
NORMAL_SCALE = 0.3989422804014327
HALF_ROOT = 0.7071067811865476


def dot_nn(left, right):
    return lax.dot_general(
        left, right, (((1,), (0,)), ((), ())), preferred_element_type=jnp.float32
    )


def dot_nt(left, right):
    return contract_cols(left, right)


def dot_tn(left, right):
    return contract_rows(left, right)


def vmem_specs(count):
    return [pl.BlockSpec(memory_space=pltpu.VMEM)] * count


def work(micros):
    return pl.CostEstimate(
        flops=int(micros * 9e7), transcendentals=0, bytes_accessed=int(micros * 3e5)
    )


def smem_spec():
    return pl.BlockSpec(memory_space=pltpu.SMEM)


def key_bias(sc, block_rows):
    length, place = sc[0], sc[1]
    columns = []
    for j in range(4):
        position = (place ^ j) * block_rows + lax.broadcasted_iota(
            jnp.int32, (block_rows, 1), 0
        )
        columns.append(jnp.where(position < length, 0.0, masked_score))
    return jnp.concatenate(columns, axis=0)


def attend_forward_kernel(
    sc, t0, t1, t2, t3, own, other, qkv, ctx_t, c0, c1, c2, c3, lse, weight, vectors, held
):
    place, core, level = sc[1], sc[2], sc[3]
    rows = t0.shape[0]
    shard_rows = weight.shape[2]
    width = weight.shape[3]
    head_width = width // 3
    heads = head_width // HEAD_DIM
    for k in range(4):
        for block, side in ((own, core), (other, 1 - core)):
            weight[level ^ k, side] = block[k, :shard_rows, :]
            vectors[level ^ k, side] = block[k, shard_rows + 1 : shard_rows + 3, :].astype(
                jnp.float32
            )
    full = weight[...].reshape(-1, width)
    bias = (
        own[level ^ place, shard_rows : shard_rows + 1, :].astype(jnp.float32)
        + other[level ^ place, shard_rows : shard_rows + 1, :].astype(jnp.float32)
    )
    for j, block in enumerate((t0, t1, t2, t3)):
        qkv[j * rows : (j + 1) * rows, :] = (dot_nn(block[...], full) + bias).astype(jnp.bfloat16)
    mask = key_bias(sc, rows)
    def one_block(j, carry):
        span = pl.ds(pl.multiple_of(j * rows, 128), rows)
        parts = []
        q_all = qkv[span, 0:head_width] * jnp.bfloat16(HEAD_DIM**-0.5)
        for h in range(heads):
            low = h * HEAD_DIM
            q = q_all[:, low : low + HEAD_DIM]
            k = qkv[:, head_width + low : head_width + low + HEAD_DIM]
            v = qkv[:, 2 * head_width + low : 2 * head_width + low + HEAD_DIM]
            scores = dot_nt(k, q) + mask
            peak = jnp.max(scores, axis=0, keepdims=True)
            shifted = jnp.exp(scores - peak)
            total = jnp.sum(shifted, axis=0, keepdims=True)
            part = dot_tn(v, shifted.astype(jnp.bfloat16)) / total
            parts.append(part)
            lse[h : h + 1, span] = peak + jnp.log(total)
        joined = jnp.concatenate(parts, axis=0)
        ctx_t[:, span] = joined
        held[j] = joined.T.astype(jnp.bfloat16)
        return carry

    lax.fori_loop(0, 4, one_block, 0)
    for j, out in enumerate((c0, c1, c2, c3)):
        out[...] = held[j]


def attend_backward_kernel(sc, qkv, ctx_t, lse, g0, g1, g2, g3, dqkv, dk_acc, dv_acc, held):
    rows = g0.shape[0]
    head_width = g0.shape[1]
    heads = head_width // HEAD_DIM
    mask = key_bias(sc, rows)
    scale = jnp.bfloat16(HEAD_DIM**-0.5)
    for j, g_ref in enumerate((g0, g1, g2, g3)):
        held[j] = g_ref[...]
    dk_acc[...] = jnp.zeros_like(dk_acc)
    dv_acc[...] = jnp.zeros_like(dv_acc)

    def one_block(j, carry):
        span = pl.ds(pl.multiple_of(j * rows, 128), rows)
        g_all = held[j]
        product = g_all.astype(jnp.float32).T * ctx_t[:, span]
        q_all = qkv[span, 0:head_width] * scale
        parts = []
        for h in range(heads):
            low = h * HEAD_DIM
            q = q_all[:, low : low + HEAD_DIM]
            g = g_all[:, low : low + HEAD_DIM]
            k = qkv[:, head_width + low : head_width + low + HEAD_DIM]
            v = qkv[:, 2 * head_width + low : 2 * head_width + low + HEAD_DIM]
            probs = jnp.exp(dot_nt(k, q) + mask - lse[h : h + 1, span])
            row_dot = jnp.sum(product[low : low + HEAD_DIM, :], axis=0, keepdims=True)
            grad_scores = (probs * (dot_nt(v, g) - row_dot)).astype(jnp.bfloat16)
            grad_v = dot_nn(probs.astype(jnp.bfloat16), g)
            grad_k = dot_nn(grad_scores, q)
            dv_acc[h] += grad_v
            dk_acc[h] += grad_k
            parts.append(dot_tn(k, grad_scores) * (HEAD_DIM**-0.5))
        dqkv[span, 0:head_width] = jnp.concatenate(parts, axis=0).T.astype(jnp.bfloat16)
        return carry

    lax.fori_loop(0, 4, one_block, 0)
    dk = jnp.concatenate([dk_acc[h] for h in range(heads)], axis=1)
    dv = jnp.concatenate([dv_acc[h] for h in range(heads)], axis=1)
    dqkv[:, head_width:] = jnp.concatenate([dk, dv], axis=1).astype(jnp.bfloat16)


def grad_qkv_weight_kernel(sc, t0, t1, t2, t3, dqkv, keep, send, sums):
    core = sc[2]
    rows = t0.shape[0]
    total = None
    for j, block in enumerate((t0, t1, t2, t3)):
        part = dot_tn(block[...], dqkv[j * rows : (j + 1) * rows, :])
        total = part if total is None else total + part
    sums[...] = jnp.sum(dqkv[...].astype(jnp.float32), axis=0, keepdims=True)
    shard_rows = keep.shape[1]
    low = total.astype(jnp.bfloat16)
    for z in range(keep.shape[0]):
        even = low[(2 * z) * shard_rows : (2 * z + 1) * shard_rows]
        odd = low[(2 * z + 1) * shard_rows : (2 * z + 2) * shard_rows]
        keep[z] = jnp.where(core == 0, even, odd)
        send[z] = jnp.where(core == 0, odd, even)


def grad_tokens_kernel(sc, dqkv, weight, out):
    place = sc[1]
    rows = out.shape[1]
    full = weight[...].reshape(-1, weight.shape[3])
    for j in range(4):
        part = dot_nt(dqkv[j * rows : (j + 1) * rows, :], full)
        out[place ^ j] = part.astype(out.dtype)


def normalize(values):
    center = values - jnp.mean(values, axis=-1, keepdims=True)
    inverse = lax.rsqrt(jnp.mean(center * center, axis=-1, keepdims=True) + epsilon)
    return center * inverse, inverse


def normalize_back(grad, unit, inverse):
    return inverse * (
        grad
        - jnp.mean(grad, axis=-1, keepdims=True)
        - unit * jnp.mean(grad * unit, axis=-1, keepdims=True)
    )


def middle_kernel(
    sc,
    x0,
    x1,
    x2,
    x3,
    token,
    cotangent,
    small,
    up_bias,
    gathered,
    output,
    grad_one,
    y0,
    y1,
    y2,
    y3,
    keep,
    send,
    sums,
    up_sums,
    w_out,
    w_up,
    w_down,
    slope,
    active,
    grad_up,
    context,
    sems,
):
    place, core = sc[1], sc[2]
    blocks = w_up.shape[0]
    shard_rows = w_up.shape[3]
    width = w_up.shape[4]
    third = shard_rows // 3
    copies = []
    for b in range(blocks):
        copies.append(
            pltpu.make_async_copy(gathered.at[:, :, b, 0:shard_rows, :], w_up.at[b], sems.at[b])
        )
    copies.append(
        pltpu.make_async_copy(
            gathered.at[:, :, :, shard_rows : 2 * shard_rows, :], w_down, sems.at[blocks]
        )
    )
    out_copies = [
        pltpu.make_async_copy(
            gathered.at[:, :, b, 2 * shard_rows : 2 * shard_rows + third, :],
            w_out.at[:, :, b * third : (b + 1) * third, :],
            sems.at[blocks + 1 + b],
        )
        for b in range(3)
    ]
    for copy in out_copies + copies:
        copy.start()
    for copy in out_copies:
        copy.wait()
    out_rows = 2 * shard_rows

    def out_block(j):
        return w_out[place ^ j].reshape(out_rows, width)

    residual = token[...].astype(jnp.float32) + small[0:1, :]
    for j, block in enumerate((x0, x1, x2, x3)):
        residual = residual + dot_nn(block[...], out_block(j))
    unit_one, inverse_one = normalize(residual)
    gain_one = small[1:2, :]
    normed = unit_one * gain_one + small[2:3, :]
    normed_low = normed.astype(jnp.bfloat16)
    for b in range(blocks):
        copies[b].wait()
        span = slice(b * width, (b + 1) * width)
        up = dot_nn(normed_low, w_up[b].reshape(width, width)) + up_bias[:, span]
        phi = 0.5 + 0.5 * lax.erf(up * HALF_ROOT)
        slope[:, span] = phi + up * (jnp.exp(-0.5 * up * up) * NORMAL_SCALE)
        active[:, span] = (up * phi).astype(jnp.bfloat16)
    copies[blocks].wait()
    residual = normed + small[3:4, :] + dot_nn(active[...], w_down[...].reshape(-1, width))
    unit_two, inverse_two = normalize(residual)
    gain_two = small[4:5, :]
    output[...] = (unit_two * gain_two + small[5:6, :]).astype(jnp.bfloat16)
    grad = cotangent[...].astype(jnp.float32)
    sums[3:4, :] = jnp.sum(grad * unit_two, axis=0, keepdims=True)
    sums[4:5, :] = jnp.sum(grad, axis=0, keepdims=True)
    grad_two = normalize_back(grad * gain_two, unit_two, inverse_two)
    sums[5:6, :] = jnp.sum(grad_two, axis=0, keepdims=True)
    two_low = grad_two.astype(jnp.bfloat16)
    grad_normed = grad_two
    for b in range(blocks):
        span = slice(b * width, (b + 1) * width)
        rows_down = w_down[b].reshape(width, width)
        part = dot_nt(two_low, rows_down) * slope[:, span]
        up_sums[:, span] = jnp.sum(part, axis=0, keepdims=True)
        part = part.astype(jnp.bfloat16)
        grad_up[:, span] = part
        grad_normed = grad_normed + dot_nt(part, w_up[b].reshape(width, width))
    sums[1:2, :] = jnp.sum(grad_normed * unit_one, axis=0, keepdims=True)
    sums[2:3, :] = jnp.sum(grad_normed, axis=0, keepdims=True)
    first = normalize_back(grad_normed * gain_one, unit_one, inverse_one)
    sums[0:1, :] = jnp.sum(first, axis=0, keepdims=True)
    sums[6:8, :] = jnp.zeros((2, width), jnp.float32)
    grad_one[...] = first
    one_low = first.astype(jnp.bfloat16)
    for j, out in enumerate((y0, y1, y2, y3)):
        out[...] = dot_nt(one_low, out_block(j)).astype(jnp.bfloat16)
    for j, block in enumerate((x0, x1, x2, x3)):
        context[place ^ j] = block[...]
    joined = jnp.concatenate([context[j] for j in range(4)], axis=1)
    half = width // 2
    down_rows = blocks * shard_rows
    for ref, mine in ((keep, core), (send, 1 - core)):
        for z in range(4):
            even = active[:, (2 * z) * down_rows : (2 * z + 1) * down_rows]
            odd = active[:, (2 * z + 1) * down_rows : (2 * z + 2) * down_rows]
            ref[:, z * down_rows : (z + 1) * down_rows] = jnp.where(mine == 0, even, odd)
        at = 4 * down_rows
        ref[:, at : at + width] = two_low
        at += width
        ref[:, at : at + width] = normed_low
        at += width
        ref[:, at : at + 2 * width] = jnp.where(
            mine == 0, grad_up[:, : 2 * width], grad_up[:, 2 * width :]
        )
        at += 2 * width
        ref[:, at : at + width] = joined
        at += width
        ref[:, at : at + half] = jnp.where(mine == 0, one_low[:, :half], one_low[:, half:])


def down_grad_kernel(sc, keep, got, near, far, part):
    place = sc[1]
    _, zs, shard_rows, width = near.shape
    down_rows = 4 * shard_rows
    at_two = zs * down_rows
    right = slice(at_two, at_two + width)
    for z in range(zs):
        left = slice(z * down_rows, (z + 1) * down_rows)
        total = dot_tn(keep[:, left], keep[:, right]) + dot_tn(got[:, left], got[:, right])
        part[...] = total.astype(jnp.bfloat16).reshape(4, shard_rows, width)
        for out, at, j in ((near, 0, 0), (near, 1, 2), (far, 0, 1), (far, 1, 3)):
            out[at, z] = part[place ^ j]


def up_grad_kernel(sc, keep, got, near, far, part):
    place = sc[1]
    _, zs, block_rows, cols = near.shape
    quarter = part.shape[2]
    pair_rows = block_rows - quarter
    width = zs * pair_rows
    at_norm = 2 * width + width
    at_up = at_norm + width
    at_ctx = at_up + 2 * width
    at_one = at_ctx + width
    left = slice(at_ctx, at_ctx + width)
    right = slice(at_one, at_one + cols)
    total = dot_tn(keep[:, left], keep[:, right]) + dot_tn(got[:, left], got[:, right])
    part[...] = total.astype(jnp.bfloat16).reshape(part.shape)
    left = slice(at_norm, at_norm + width)
    for out, at, j in ((near, 0, 0), (near, 1, 1), (far, 0, 2), (far, 1, 3)):
        right = pl.ds(pl.multiple_of(at_up + (place ^ j) * cols, 128), cols)
        total = dot_tn(keep[:, left], keep[:, right]) + dot_tn(got[:, left], got[:, right])
        total = total.astype(jnp.bfloat16)
        for z in range(zs):
            out[at, z, :pair_rows] = total[z * pair_rows : (z + 1) * pair_rows]
            out[at, z, pair_rows:] = part[z, place ^ j]


def fold_kernel(near, got, mine, pass_on):
    for at, out in ((0, mine), (1, pass_on)):
        total = near[at].astype(jnp.float32) + got[at].astype(jnp.float32)
        out[...] = total.astype(jnp.bfloat16)


def level_fold_kernel(sc, mine, got, near, far):
    level = sc[3]
    for out, at, k in ((near, 0, 0), (near, 1, 2), (far, 0, 1), (far, 1, 3)):
        total = mine[level ^ k].astype(jnp.float32) + got[level ^ k].astype(jnp.float32)
        out[at] = total.astype(jnp.bfloat16)


def block_sum(refs):
    total = refs[0][...].astype(jnp.float32)
    for ref in refs[1:]:
        total = total + ref[...].astype(jnp.float32)
    return total


def split_up_kernel(sc, e0, e1, keep, send, held):
    core = sc[2]
    shard_rows = (keep.shape[0] * 2) // 3
    held[...] = block_sum((e0, e1)).astype(jnp.bfloat16)
    for ref, side in ((keep, core), (send, 1 - core)):
        ref[:shard_rows] = held[pl.ds(pl.multiple_of(side * shard_rows, 16), shard_rows), :]
        ref[shard_rows:] = held[2 * shard_rows :, :]


def join_kernel(sc, e0, e1, keep, got, out):
    core = sc[2]
    shard_rows = e0.shape[0]
    cols = keep.shape[1]
    out[:shard_rows] = block_sum((e0, e1)).astype(jnp.bfloat16)
    for ref, side in ((keep, core), (got, 1 - core)):
        out[shard_rows:, pl.ds(pl.multiple_of(side * cols, 128), cols)] = ref[...]


def finish_kernel(sc, b0, b1, b2, b3, down, up, out):
    place, core = sc[1], sc[2]
    shard_rows = up.shape[0]
    quarter = shard_rows // 2
    cols = b0.shape[1] // 2
    for j, ref in enumerate((b0, b1, b2, b3)):
        where = place ^ j
        rows = pl.ds(pl.multiple_of(where * shard_rows, 8), shard_rows)
        down[rows, :] = ref[:shard_rows].astype(jnp.float32)
        for side in range(2):
            at = pl.multiple_of((side * 4 + where) * cols, 128)
            up[:, pl.ds(at, cols)] = ref[
                shard_rows : 2 * shard_rows, side * cols : (side + 1) * cols
            ].astype(jnp.float32)

        @pl.when(where // 2 == core)
        def _(ref=ref, where=where):
            at = pl.multiple_of((where % 2) * quarter, 8)
            out[pl.ds(at, quarter), :] = ref[2 * shard_rows :].astype(jnp.float32)


def sum_kernel(e0, e1, out):
    out[...] = block_sum((e0, e1)).astype(out.dtype)


def finish_qkv_kernel(sc, b0, b1, b2, b3, out, held):
    place = sc[1]
    head_width = b0.shape[1] // 3
    for j, ref in enumerate((b0, b1, b2, b3)):
        held[place ^ j] = ref[...].astype(jnp.float32)
    for part in range(3):
        for s in range(4):
            at = (part * 4 + s) * head_width
            out[:, at : at + head_width] = held[s, :, part * head_width : (part + 1) * head_width]


def fast_body(
    tokens,
    lengths,
    w_qkv,
    q_bias,
    v_bias,
    w_out,
    out_bias,
    gain_one,
    shift_one,
    w_up,
    up_bias,
    w_down,
    down_bias,
    gain_two,
    shift_two,
    cotangent,
):
    bf16, f32 = jnp.bfloat16, jnp.float32
    _, rows, width = tokens.shape
    shard_rows = w_qkv.shape[0]
    hidden = w_up.shape[1]
    head_width = width // 4
    place = lax.axis_index("seq")
    core = lax.axis_index("core")
    zs = 4
    third = shard_rows // 3
    swap = [(0, 1), (1, 0)]

    def struct(shape, dtype=bf16):
        return jax.ShapeDtypeStruct(shape, dtype)

    def across(value, step):
        return lax.ppermute(value, "seq", [(i, i ^ step) for i in range(4)])

    def partner(value):
        return lax.ppermute(value, "core", swap)

    def level_across(value, step):
        return lax.ppermute(value, "z", [(i, i ^ step) for i in range(4)])

    token = tokens[0]
    quarter = jnp.concatenate(
        [
            lax.dynamic_slice_in_dim(w_up, place * width, width, axis=1),
            lax.dynamic_slice_in_dim(w_down, place * shard_rows, shard_rows, axis=0),
            lax.dynamic_slice_in_dim(w_out, jnp.minimum(place, 2) * third, third, axis=0),
        ],
        axis=0,
    )
    gathered = lax.all_gather(quarter, ("z", "core", "seq"), axis=0, tiled=True)
    gathered = gathered.reshape(zs, 2, 4, 2 * shard_rows + third, width)
    columns = lax.dynamic_index_in_dim(
        w_qkv.reshape(shard_rows, 3, 4, head_width), place, axis=2, keepdims=False
    ).reshape(shard_rows, 3 * head_width)
    pair_rows = jnp.zeros((2, 2, shard_rows), bf16)
    placed_q = lax.dynamic_update_slice(pair_rows[0], q_bias[None], (core, 0)).reshape(1, -1)
    placed_v = lax.dynamic_update_slice(pair_rows[0], v_bias[None], (core, 0)).reshape(1, -1)
    bias_row = jnp.concatenate(
        [placed_q, jnp.zeros((1, head_width), bf16), placed_v], axis=1
    )
    vectors = jnp.concatenate(
        [out_bias, gain_one, shift_one, down_bias, gain_two, shift_two, up_bias]
    )
    pad = 15 * 3 * head_width - vectors.shape[0]
    vector_rows = jnp.pad(vectors, (0, pad)).reshape(15, 3 * head_width)
    own_block = jnp.concatenate([columns, bias_row, vector_rows], axis=0)
    t1, t2, t3 = across(token, 1), across(token, 2), across(token, 3)
    own_cols = jnp.stack([own_block] + [level_across(own_block, k) for k in (1, 2, 3)])
    other_cols = partner(own_cols)
    sc = jnp.stack([lengths[0], place, core, lax.axis_index("z")]).astype(jnp.int32)
    all_rows = 4 * rows
    qkv, ctx_t, c0, c1, c2, c3, lse, full_qkv, vector_sets = pl.pallas_call(
        attend_forward_kernel,
        name="attend_forward",
        cost_estimate=work(13),
        out_shape=(
            struct((all_rows, 3 * head_width)),
            struct((head_width, all_rows), f32),
            struct((rows, head_width)),
            struct((rows, head_width)),
            struct((rows, head_width)),
            struct((rows, head_width)),
            struct((head_width // HEAD_DIM, all_rows), f32),
            struct((zs, 2, shard_rows, 3 * head_width)),
            struct((zs, 2, 2, 3 * head_width), f32),
        ),
        in_specs=[smem_spec()] + vmem_specs(6),
        out_specs=tuple(vmem_specs(9)),
        scratch_shapes=[pltpu.VMEM((4, rows, head_width), bf16)],
    )(sc, token, t1, t2, t3, own_cols, other_cols)
    x1, x2, x3 = across(c1, 1), across(c2, 2), across(c3, 3)
    all_vec = vector_sets.reshape(2 * zs, -1)
    six = all_vec[:, : 6 * shard_rows].reshape(2 * zs, 6, shard_rows)
    six = six.transpose(1, 0, 2).reshape(6, width)
    small = jnp.concatenate([six, jnp.zeros((2, width), f32)], axis=0)
    full_up_bias = all_vec[:, 6 * shard_rows : 6 * shard_rows + hidden // 8].reshape(1, hidden)
    packed = hidden // 2 + 5 * width + width // 2
    output, grad_one, y0, y1, y2, y3, keep, send, sums, up_sums = pl.pallas_call(
        middle_kernel,
        name="middle",
        cost_estimate=work(15),
        out_shape=(
            struct((rows, width)),
            struct((rows, width), f32),
            struct((rows, head_width)),
            struct((rows, head_width)),
            struct((rows, head_width)),
            struct((rows, head_width)),
            struct((rows, packed)),
            struct((rows, packed)),
            struct((8, width), f32),
            struct((1, hidden), f32),
        ),
        in_specs=[smem_spec()]
        + vmem_specs(8)
        + [pl.BlockSpec(memory_space=pl.ANY)],
        out_specs=tuple(vmem_specs(10)),
        scratch_shapes=[
            pltpu.VMEM((zs, 2, shard_rows, width), bf16),
            pltpu.VMEM((4, zs, 2, shard_rows, width), bf16),
            pltpu.VMEM((zs, 2, 4, shard_rows, width), bf16),
            pltpu.VMEM((rows, hidden), f32),
            pltpu.VMEM((rows, hidden), bf16),
            pltpu.VMEM((rows, hidden), bf16),
            pltpu.VMEM((4, rows, head_width), bf16),
            pltpu.SemaphoreType.DMA((8,)),
        ],
    )(
        sc,
        c0,
        x1,
        x2,
        x3,
        token,
        cotangent[0],
        small,
        full_up_bias,
        gathered,
    )
    g1, g2, g3 = across(y1, 1), across(y2, 2), across(y3, 3)
    got, g1, g2, g3 = lax.optimization_barrier((partner(send), g1, g2, g3))
    quad = hidden // 8

    def call(kernel, micros, outs, *args, scratch=(), scalars=True):
        return pl.pallas_call(
            kernel,
            name=kernel.__name__.replace("_kernel", ""),
            cost_estimate=work(micros),
            out_shape=tuple(outs),
            in_specs=([smem_spec()] if scalars else []) + vmem_specs(len(args)),
            out_specs=tuple(vmem_specs(len(outs))),
            scratch_shapes=list(scratch),
        )(*(((sc,) if scalars else ()) + args))

    d_near, d_far = call(
        down_grad_kernel,
        4,
        [struct((2, zs, shard_rows, width))] * 2,
        keep,
        got,
        scratch=[pltpu.VMEM((4, shard_rows, width), bf16)],
    )
    block_rows = 2 * shard_rows + shard_rows // 2
    u_near, u_far = call(
        up_grad_kernel,
        4,
        [struct((2, zs, block_rows, quad))] * 2,
        keep,
        got,
        scratch=[pltpu.VMEM((zs, 4, shard_rows // 2, quad), bf16)],
    )
    d_got = across(d_far, 1)
    u_got = across(u_far, 2)
    y0, d_near, u_near = lax.optimization_barrier((y0, d_near, u_near))

    dqkv = pl.pallas_call(
        attend_backward_kernel,
        name="attend_backward",
        cost_estimate=work(11),
        out_shape=struct((all_rows, 3 * head_width)),
        in_specs=[smem_spec()] + vmem_specs(7),
        out_specs=pl.BlockSpec(memory_space=pltpu.VMEM),
        scratch_shapes=[
            pltpu.VMEM((head_width // HEAD_DIM, all_rows, HEAD_DIM), f32),
            pltpu.VMEM((head_width // HEAD_DIM, all_rows, HEAD_DIM), f32),
            pltpu.VMEM((4, rows, head_width), bf16),
        ],
    )(sc, qkv, ctx_t, lse, y0, g1, g2, g3)
    q_keep, q_send, q_sums = pl.pallas_call(
        grad_qkv_weight_kernel,
        name="grad_qkv_weight",
        cost_estimate=work(4),
        out_shape=(
            struct((zs, shard_rows, 3 * head_width)),
            struct((zs, shard_rows, 3 * head_width)),
            struct((1, 3 * head_width), f32),
        ),
        in_specs=[smem_spec()] + vmem_specs(5),
        out_specs=tuple(vmem_specs(3)),
    )(sc, token, t1, t2, t3, dqkv)
    d_mine, d_pass = call(
        fold_kernel, 1, [struct((zs, shard_rows, width))] * 2, d_near, d_got, scalars=False
    )
    u_mine, u_pass = call(
        fold_kernel, 1, [struct((zs, block_rows, quad))] * 2, u_near, u_got, scalars=False
    )
    q_send, d_mine, u_mine = lax.optimization_barrier((q_send, d_mine, u_mine))
    q_got = partner(q_send)
    late_dqkv, q_keep = lax.optimization_barrier((dqkv, q_keep))
    (token_parts,) = call(
        grad_tokens_kernel,
        4,
        [struct((4, rows, width))],
        late_dqkv,
        full_qkv,
    )
    token_sum = lax.psum_scatter(
        token_parts.reshape(4 * rows, width), "seq", scatter_dimension=0, tiled=True
    )
    q_near, q_far = call(
        level_fold_kernel, 1, [struct((2, shard_rows, 3 * head_width))] * 2, q_keep, q_got
    )

    def level_sum(near, far, shape):
        mine, pass_on = call(
            fold_kernel, 1, [struct(shape)] * 2, near, level_across(far, 1), scalars=False
        )
        return mine, level_across(pass_on, 2)

    q_mine, q_last = level_sum(q_near, q_far, (shard_rows, 3 * head_width))
    (q_part,) = call(
        sum_kernel, 1, [struct((shard_rows, 3 * head_width))], q_mine, q_last, scalars=False
    )

    def seq_sum(mine, pass_on, shape, step):
        near, far = call(
            level_fold_kernel,
            1,
            [struct((2,) + shape[1:])] * 2,
            mine,
            across(pass_on, step),
        )
        return level_sum(near, far, shape[1:])

    d_parts = seq_sum(d_mine, d_pass, (zs, shard_rows, width), 2)
    u_parts = seq_sum(u_mine, u_pass, (zs, block_rows, quad), 1)
    half_rows = shard_rows + shard_rows // 2
    u_keep, u_send = call(
        split_up_kernel,
        1,
        [struct((half_rows, quad))] * 2,
        *u_parts,
        scratch=[pltpu.VMEM((block_rows, quad), bf16)],
    )
    (joined,) = call(
        join_kernel,
        1,
        [struct((shard_rows + half_rows, width))],
        *d_parts,
        u_keep,
        partner(u_send),
    )
    result_down, result_up, result_out = call(
        finish_kernel,
        2,
        [
            struct((4 * shard_rows, width), f32),
            struct((shard_rows, hidden), f32),
            struct((shard_rows, width), f32),
        ],
        joined,
        *[across(joined, j) for j in (1, 2, 3)],
    )
    (result_qkv,) = call(
        finish_qkv_kernel,
        1,
        [struct((shard_rows, 3 * width), f32)],
        q_part,
        *[across(q_part, j) for j in (1, 2, 3)],
        scratch=[pltpu.VMEM((4, shard_rows, 3 * head_width), f32)],
    )
    grad_tokens = (grad_one + token_sum.astype(f32)).astype(bf16)

    q_row = lax.dynamic_update_slice(
        jnp.zeros((1, width), f32), q_sums[:, :head_width], (0, place * head_width)
    )
    v_row = lax.dynamic_update_slice(
        jnp.zeros((1, width), f32), q_sums[:, 2 * head_width :], (0, place * head_width)
    )

    def everywhere(value):
        value = value + partner(value)
        value = value + across(value, 1)
        value = value + across(value, 2)
        value = value + level_across(value, 1)
        value = value + level_across(value, 2)
        return value

    vector_sums = jnp.concatenate([sums[:6], up_sums.reshape(4, width), q_row, v_row], axis=0)
    vector_sums, _ = lax.optimization_barrier((vector_sums, q_mine))
    early = everywhere(vector_sums)
    shard = 2 * lax.axis_index("z") + core

    def owned(vector):
        size = vector.shape[0] // (2 * zs)
        return lax.dynamic_slice(vector, (shard * size,), (size,))

    return (
        output[None],
        grad_tokens[None],
        result_qkv,
        owned(early[10]),
        owned(early[11]),
        result_out,
        owned(early[0]),
        owned(early[1]),
        owned(early[2]),
        result_up,
        owned(early[6:10].reshape(-1)),
        result_down,
        owned(early[5]),
        owned(early[3]),
        owned(early[4]),
    )


def solution(mesh):
    seq_count, shard_count = mesh.shape["seq"], mesh.shape["shard"]
    fast = seq_count == 4 and shard_count == 8
    if fast:
        grid = mesh.devices.reshape(seq_count, shard_count // 2, 2)
        mesh = jax.sharding.Mesh(grid, AXES)
    shard = ("z", "core") if fast else "shard"
    vector, matrix, rows = P(shard), P(shard, None), P(shard, "seq", None)
    return jax.shard_map(
        fast_body if fast else body,
        mesh=mesh,
        in_specs=(
            rows,
            vector,
            matrix,
            vector,
            vector,
            matrix,
            vector,
            vector,
            vector,
            matrix,
            vector,
            matrix,
            vector,
            vector,
            vector,
            rows,
        ),
        out_specs=(
            rows,
            rows,
            matrix,
            vector,
            vector,
            matrix,
            vector,
            vector,
            vector,
            matrix,
            vector,
            matrix,
            vector,
            vector,
            vector,
        ),
        check_vma=False,
    )
```

```python
import jax
import jax.numpy as jnp
from jax import lax
from jax.experimental import pallas as pl
from jax.experimental.pallas import tpu as pltpu
from jax.sharding import PartitionSpec as P

HEAD_DIM = 64
LEN = 1024
Q_BLOCK = 512


epsilon = 1e-05
masked_score = -1000000000.0


def layer_norm(values, gain, shift):
    center = values - jnp.mean(values, axis=-1, keepdims=True)
    spread = jnp.mean(center * center, axis=-1, keepdims=True)
    return center * lax.rsqrt(spread + epsilon) * gain + shift


def gelu_exact(values):
    return jax.nn.gelu(values, approximate=False)


def contract_rows(left, right):
    return lax.dot_general(
        left, right, (((0,), (0,)), ((), ())), preferred_element_type=jnp.float32
    )


def contract_cols(left, right):
    return lax.dot_general(
        left, right, (((1,), (1,)), ((), ())), preferred_element_type=jnp.float32
    )


def block_scores(q_block, k_seq, key_valid):
    scores = jnp.einsum(
        "qhd,khd->hqk", q_block, k_seq, preferred_element_type=jnp.float32
    ) * HEAD_DIM ** (-0.5)
    return jnp.where(key_valid[None, None, :], scores, masked_score)


def attend_forward(q_seq, k_seq, v_seq, length):
    local_heads = q_seq.shape[1]
    key_valid = jnp.arange(LEN, dtype=jnp.int32) < length
    q_blocks = q_seq.reshape(LEN // Q_BLOCK, Q_BLOCK, local_heads, HEAD_DIM)

    def one_block(q_block):
        scores = block_scores(q_block, k_seq, key_valid)
        row_peak = jnp.max(scores, axis=-1, keepdims=True)
        shifted = jnp.exp(scores - row_peak)
        row_total = jnp.sum(shifted, axis=-1, keepdims=True)
        attn_probs = (shifted / row_total).astype(jnp.bfloat16)
        context = jnp.einsum("hqk,khd->qhd", attn_probs, v_seq, preferred_element_type=jnp.float32)
        return (context.astype(jnp.bfloat16), (row_peak + jnp.log(row_total))[..., 0])

    context, log_total = lax.map(one_block, q_blocks)
    return (context.reshape(LEN, local_heads, HEAD_DIM), log_total)


def attend_backward(q_seq, k_seq, v_seq, grad_seq, log_total, length):
    local_heads = q_seq.shape[1]
    score_scale = HEAD_DIM ** (-0.5)
    key_valid = jnp.arange(LEN, dtype=jnp.int32) < length
    q_blocks = q_seq.reshape(LEN // Q_BLOCK, Q_BLOCK, local_heads, HEAD_DIM)
    g_blocks = grad_seq.reshape(LEN // Q_BLOCK, Q_BLOCK, local_heads, HEAD_DIM)

    def one_block(accum, block_item):
        q_block, g_block, lse_block = block_item
        scores = block_scores(q_block, k_seq, key_valid)
        attn_probs = jnp.exp(scores - lse_block[..., None])
        grad_probs = jnp.einsum("qhd,khd->hqk", g_block, v_seq, preferred_element_type=jnp.float32)
        row_dot = jnp.sum(attn_probs * grad_probs, axis=-1, keepdims=True)
        grad_scores = (attn_probs * (grad_probs - row_dot)).astype(jnp.bfloat16)
        grad_q = (
            jnp.einsum("hqk,khd->qhd", grad_scores, k_seq, preferred_element_type=jnp.float32)
            * score_scale
        )
        grad_k = (
            accum[0]
            + jnp.einsum("hqk,qhd->khd", grad_scores, q_block, preferred_element_type=jnp.float32)
            * score_scale
        )
        grad_v = accum[1] + jnp.einsum(
            "hqk,qhd->khd",
            attn_probs.astype(jnp.bfloat16),
            g_block,
            preferred_element_type=jnp.float32,
        )
        return ((grad_k, grad_v), grad_q.astype(jnp.bfloat16))

    zero_keys = jnp.zeros((LEN, local_heads, HEAD_DIM), jnp.float32)
    (grad_k, grad_v), grad_q = lax.scan(
        one_block, (zero_keys, zero_keys), (q_blocks, g_blocks, log_total)
    )
    return (
        grad_q.reshape(LEN, local_heads, HEAD_DIM),
        grad_k.astype(jnp.bfloat16),
        grad_v.astype(jnp.bfloat16),
    )


def body(
    tokens,
    lengths,
    w_qkv,
    q_bias,
    v_bias,
    w_out,
    out_bias,
    gain_one,
    shift_one,
    w_up,
    up_bias,
    w_down,
    down_bias,
    gain_two,
    shift_two,
    cotangent,
):
    seq_count, local_len, model_width = tokens.shape
    row_count = seq_count * local_len
    head_count = model_width // HEAD_DIM
    gathered = (
        lax.all_gather(w_qkv, "shard", axis=0, tiled=True),
        lax.all_gather(q_bias, "shard", axis=0, tiled=True),
        lax.all_gather(v_bias, "shard", axis=0, tiled=True),
        lax.all_gather(w_out, "shard", axis=0, tiled=True),
        lax.all_gather(out_bias, "shard", axis=0, tiled=True),
        lax.all_gather(gain_one, "shard", axis=0, tiled=True),
        lax.all_gather(shift_one, "shard", axis=0, tiled=True),
        lax.all_gather(w_up, "shard", axis=0, tiled=True),
        lax.all_gather(up_bias, "shard", axis=0, tiled=True),
        lax.all_gather(w_down, "shard", axis=0, tiled=True),
        lax.all_gather(down_bias, "shard", axis=0, tiled=True),
        lax.all_gather(gain_two, "shard", axis=0, tiled=True),
        lax.all_gather(shift_two, "shard", axis=0, tiled=True),
    )
    (
        full_qkv,
        full_q_bias,
        full_v_bias,
        full_out,
        full_out_bias,
        full_gain_one,
        full_shift_one,
        full_up,
        full_up_bias,
        full_down,
        full_down_bias,
        full_gain_two,
        full_shift_two,
    ) = gathered
    token_rows = tokens.reshape(row_count, model_width)
    joined_bias = jnp.concatenate([full_q_bias, jnp.zeros_like(full_q_bias), full_v_bias]).astype(
        jnp.float32
    )
    qkv_rows = (
        jnp.dot(token_rows, full_qkv, preferred_element_type=jnp.float32) + joined_bias
    ).astype(jnp.bfloat16)
    qkv_tokens = qkv_rows.reshape(seq_count, local_len, 3, head_count, HEAD_DIM)
    qkv_heads = lax.all_to_all(qkv_tokens, "seq", split_axis=3, concat_axis=1, tiled=True)

    def forward_seq(seq_item):
        qkv_seq, length = seq_item
        return attend_forward(qkv_seq[:, 0], qkv_seq[:, 1], qkv_seq[:, 2], length)

    context_heads, log_total = lax.map(forward_seq, (qkv_heads, lengths))
    context_tokens = lax.all_to_all(context_heads, "seq", split_axis=1, concat_axis=2, tiled=True)
    context_rows = context_tokens.reshape(row_count, model_width)
    residual_one = (
        token_rows.astype(jnp.float32)
        + jnp.dot(context_rows, full_out, preferred_element_type=jnp.float32)
        + full_out_bias.astype(jnp.float32)
    )
    normed_one, norm_one_pull = jax.vjp(
        layer_norm,
        residual_one,
        full_gain_one.astype(jnp.float32),
        full_shift_one.astype(jnp.float32),
    )
    normed_low = normed_one.astype(jnp.bfloat16)
    up_rows = jnp.dot(
        normed_low, full_up, preferred_element_type=jnp.float32
    ) + full_up_bias.astype(jnp.float32)
    active, gelu_pull = jax.vjp(gelu_exact, up_rows)
    active_low = active.astype(jnp.bfloat16)
    residual_two = (
        normed_one
        + jnp.dot(active_low, full_down, preferred_element_type=jnp.float32)
        + full_down_bias.astype(jnp.float32)
    )
    final_rows, norm_two_pull = jax.vjp(
        layer_norm,
        residual_two,
        full_gain_two.astype(jnp.float32),
        full_shift_two.astype(jnp.float32),
    )
    output = final_rows.astype(jnp.bfloat16).reshape(tokens.shape)
    back_qkv, back_out, back_up, back_down = (full_qkv, full_out, full_up, full_down)
    grad_rows = cotangent.reshape(row_count, model_width).astype(jnp.float32)
    grad_two, grad_gain_two, grad_shift_two = norm_two_pull(grad_rows)
    grad_down_bias = jnp.sum(grad_two, axis=0)
    grad_two_low = grad_two.astype(jnp.bfloat16)
    grad_w_down = contract_rows(active_low, grad_two_low)
    grad_active = contract_cols(grad_two_low, back_down)
    (grad_up,) = gelu_pull(grad_active)
    grad_up_bias = jnp.sum(grad_up, axis=0)
    grad_up_low = grad_up.astype(jnp.bfloat16)
    grad_w_up = contract_rows(normed_low, grad_up_low)
    grad_normed = grad_two + contract_cols(grad_up_low, back_up)
    grad_one, grad_gain_one, grad_shift_one = norm_one_pull(grad_normed)
    grad_out_bias = jnp.sum(grad_one, axis=0)
    grad_one_low = grad_one.astype(jnp.bfloat16)
    grad_w_out = contract_rows(context_rows, grad_one_low)
    grad_context = contract_cols(grad_one_low, back_out).astype(jnp.bfloat16)
    grad_context = grad_context.reshape(seq_count, local_len, head_count, HEAD_DIM)
    grad_context_heads = lax.all_to_all(
        grad_context, "seq", split_axis=2, concat_axis=1, tiled=True
    )

    def backward_seq(seq_item):
        qkv_seq, grad_seq, lse_seq, length = seq_item
        grad_q, grad_k, grad_v = attend_backward(
            qkv_seq[:, 0], qkv_seq[:, 1], qkv_seq[:, 2], grad_seq, lse_seq, length
        )
        return jnp.stack([grad_q, grad_k, grad_v], axis=1)

    grad_qkv_heads = lax.map(backward_seq, (qkv_heads, grad_context_heads, log_total, lengths))
    grad_qkv_tokens = lax.all_to_all(grad_qkv_heads, "seq", split_axis=1, concat_axis=3, tiled=True)
    grad_qkv_rows = grad_qkv_tokens.reshape(row_count, 3 * model_width)
    grad_q_bias = jnp.sum(grad_qkv_rows[:, :model_width], axis=0, dtype=jnp.float32)
    grad_v_bias = jnp.sum(grad_qkv_rows[:, 2 * model_width :], axis=0, dtype=jnp.float32)
    grad_w_qkv = contract_rows(token_rows, grad_qkv_rows)
    grad_tokens = grad_one + contract_cols(grad_qkv_rows, back_qkv)
    grad_tokens = grad_tokens.astype(jnp.bfloat16).reshape(tokens.shape)
    owned = (
        lax.psum_scatter(grad_w_qkv, "shard", scatter_dimension=0, tiled=True),
        lax.psum_scatter(grad_q_bias, "shard", scatter_dimension=0, tiled=True),
        lax.psum_scatter(grad_v_bias, "shard", scatter_dimension=0, tiled=True),
        lax.psum_scatter(grad_w_out, "shard", scatter_dimension=0, tiled=True),
        lax.psum_scatter(grad_out_bias, "shard", scatter_dimension=0, tiled=True),
        lax.psum_scatter(grad_gain_one, "shard", scatter_dimension=0, tiled=True),
        lax.psum_scatter(grad_shift_one, "shard", scatter_dimension=0, tiled=True),
        lax.psum_scatter(grad_w_up, "shard", scatter_dimension=0, tiled=True),
        lax.psum_scatter(grad_up_bias, "shard", scatter_dimension=0, tiled=True),
        lax.psum_scatter(grad_w_down, "shard", scatter_dimension=0, tiled=True),
        lax.psum_scatter(grad_down_bias, "shard", scatter_dimension=0, tiled=True),
        lax.psum_scatter(grad_gain_two, "shard", scatter_dimension=0, tiled=True),
        lax.psum_scatter(grad_shift_two, "shard", scatter_dimension=0, tiled=True),
    )
    owned_columns = (
        lax.psum_scatter(
            owned[0].astype(jnp.bfloat16), "seq", scatter_dimension=1, tiled=True
        ).astype(jnp.float32),
        lax.psum_scatter(
            owned[3].astype(jnp.bfloat16), "seq", scatter_dimension=1, tiled=True
        ).astype(jnp.float32),
        lax.psum_scatter(
            owned[7].astype(jnp.bfloat16), "seq", scatter_dimension=1, tiled=True
        ).astype(jnp.float32),
        lax.psum_scatter(
            owned[9].astype(jnp.bfloat16), "seq", scatter_dimension=1, tiled=True
        ).astype(jnp.float32),
    )
    matrices = (
        lax.all_gather(owned_columns[0].astype(jnp.bfloat16), "seq", axis=1, tiled=True).astype(
            jnp.float32
        ),
        lax.all_gather(owned_columns[1].astype(jnp.bfloat16), "seq", axis=1, tiled=True).astype(
            jnp.float32
        ),
        lax.all_gather(owned_columns[2].astype(jnp.bfloat16), "seq", axis=1, tiled=True).astype(
            jnp.float32
        ),
        lax.all_gather(owned_columns[3].astype(jnp.bfloat16), "seq", axis=1, tiled=True).astype(
            jnp.float32
        ),
    )
    vectors = lax.psum(
        (
            owned[1],
            owned[2],
            owned[4],
            owned[5],
            owned[6],
            owned[8],
            owned[10],
            owned[11],
            owned[12],
        ),
        "seq",
    )
    result_qkv, result_out, result_up, result_down = (
        matrices[0],
        matrices[1],
        matrices[2],
        matrices[3],
    )
    result_q_bias, result_v_bias, result_out_bias = (vectors[0], vectors[1], vectors[2])
    result_gain_one, result_shift_one, result_up_bias = (vectors[3], vectors[4], vectors[5])
    result_down_bias, result_gain_two, result_shift_two = (vectors[6], vectors[7], vectors[8])
    return (
        output,
        grad_tokens,
        result_qkv,
        result_q_bias,
        result_v_bias,
        result_out,
        result_out_bias,
        result_gain_one,
        result_shift_one,
        result_up,
        result_up_bias,
        result_down,
        result_down_bias,
        result_gain_two,
        result_shift_two,
    )


AXES = ("seq", "z", "core")
NORMAL_SCALE = 0.3989422804014327
HALF_ROOT = 0.7071067811865476


def dot_nn(left, right):
    return lax.dot_general(
        left, right, (((1,), (0,)), ((), ())), preferred_element_type=jnp.float32
    )


def dot_nt(left, right):
    return contract_cols(left, right)


def dot_tn(left, right):
    return contract_rows(left, right)


def vmem_specs(count):
    return [pl.BlockSpec(memory_space=pltpu.VMEM)] * count


def work(micros):
    return pl.CostEstimate(
        flops=int(micros * 9e7), transcendentals=0, bytes_accessed=int(micros * 3e5)
    )


def smem_spec():
    return pl.BlockSpec(memory_space=pltpu.SMEM)


def key_bias(sc, block_rows):
    length, place = sc[0], sc[1]
    columns = []
    for j in range(4):
        position = (place ^ j) * block_rows + lax.broadcasted_iota(
            jnp.int32, (block_rows, 1), 0
        )
        columns.append(jnp.where(position < length, 0.0, masked_score))
    return jnp.concatenate(columns, axis=0)


def attend_forward_kernel(
    sc, t0, t1, t2, t3, own, other, qkv, ctx_t, c0, c1, c2, c3, lse, weight, vectors, held
):
    place, core, level = sc[1], sc[2], sc[3]
    rows = t0.shape[0]
    shard_rows = weight.shape[2]
    width = weight.shape[3]
    head_width = width // 3
    heads = head_width // HEAD_DIM
    for k in range(4):
        for block, side in ((own, core), (other, 1 - core)):
            weight[level ^ k, side] = block[k, :shard_rows, :]
            vectors[level ^ k, side] = block[k, shard_rows + 1 : shard_rows + 3, :].astype(
                jnp.float32
            )
    full = weight[...].reshape(-1, width)
    bias = (
        own[level ^ place, shard_rows : shard_rows + 1, :].astype(jnp.float32)
        + other[level ^ place, shard_rows : shard_rows + 1, :].astype(jnp.float32)
    )
    for j, block in enumerate((t0, t1, t2, t3)):
        qkv[j * rows : (j + 1) * rows, :] = (dot_nn(block[...], full) + bias).astype(jnp.bfloat16)
    mask = key_bias(sc, rows)
    def one_block(j, carry):
        span = pl.ds(pl.multiple_of(j * rows, 128), rows)
        parts = []
        q_all = qkv[span, 0:head_width] * jnp.bfloat16(HEAD_DIM**-0.5)
        for h in range(heads):
            low = h * HEAD_DIM
            q = q_all[:, low : low + HEAD_DIM]
            k = qkv[:, head_width + low : head_width + low + HEAD_DIM]
            v = qkv[:, 2 * head_width + low : 2 * head_width + low + HEAD_DIM]
            scores = dot_nt(k, q) + mask
            peak = jnp.max(scores, axis=0, keepdims=True)
            shifted = jnp.exp(scores - peak)
            total = jnp.sum(shifted, axis=0, keepdims=True)
            part = dot_tn(v, shifted.astype(jnp.bfloat16)) / total
            parts.append(part)
            lse[h : h + 1, span] = peak + jnp.log(total)
        joined = jnp.concatenate(parts, axis=0)
        ctx_t[:, span] = joined
        held[j] = joined.T.astype(jnp.bfloat16)
        return carry

    lax.fori_loop(0, 4, one_block, 0)
    for j, out in enumerate((c0, c1, c2, c3)):
        out[...] = held[j]


def attend_backward_kernel(sc, qkv, ctx_t, lse, g0, g1, g2, g3, dqkv, dk_acc, dv_acc, held):
    rows = g0.shape[0]
    head_width = g0.shape[1]
    heads = head_width // HEAD_DIM
    mask = key_bias(sc, rows)
    scale = jnp.bfloat16(HEAD_DIM**-0.5)
    for j, g_ref in enumerate((g0, g1, g2, g3)):
        held[j] = g_ref[...]
    dk_acc[...] = jnp.zeros_like(dk_acc)
    dv_acc[...] = jnp.zeros_like(dv_acc)

    def one_block(j, carry):
        span = pl.ds(pl.multiple_of(j * rows, 128), rows)
        g_all = held[j]
        product = g_all.astype(jnp.float32).T * ctx_t[:, span]
        q_all = qkv[span, 0:head_width] * scale
        parts = []
        for h in range(heads):
            low = h * HEAD_DIM
            q = q_all[:, low : low + HEAD_DIM]
            g = g_all[:, low : low + HEAD_DIM]
            k = qkv[:, head_width + low : head_width + low + HEAD_DIM]
            v = qkv[:, 2 * head_width + low : 2 * head_width + low + HEAD_DIM]
            probs = jnp.exp(dot_nt(k, q) + mask - lse[h : h + 1, span])
            row_dot = jnp.sum(product[low : low + HEAD_DIM, :], axis=0, keepdims=True)
            grad_scores = (probs * (dot_nt(v, g) - row_dot)).astype(jnp.bfloat16)
            grad_v = dot_nn(probs.astype(jnp.bfloat16), g)
            grad_k = dot_nn(grad_scores, q)
            dv_acc[h] += grad_v
            dk_acc[h] += grad_k
            parts.append(dot_tn(k, grad_scores) * (HEAD_DIM**-0.5))
        dqkv[span, 0:head_width] = jnp.concatenate(parts, axis=0).T.astype(jnp.bfloat16)
        return carry

    lax.fori_loop(0, 4, one_block, 0)
    dk = jnp.concatenate([dk_acc[h] for h in range(heads)], axis=1)
    dv = jnp.concatenate([dv_acc[h] for h in range(heads)], axis=1)
    dqkv[:, head_width:] = jnp.concatenate([dk, dv], axis=1).astype(jnp.bfloat16)


def grad_qkv_weight_kernel(sc, t0, t1, t2, t3, dqkv, keep, send, sums):
    core = sc[2]
    rows = t0.shape[0]
    total = None
    for j, block in enumerate((t0, t1, t2, t3)):
        part = dot_tn(block[...], dqkv[j * rows : (j + 1) * rows, :])
        total = part if total is None else total + part
    sums[...] = jnp.sum(dqkv[...].astype(jnp.float32), axis=0, keepdims=True)
    shard_rows = keep.shape[1]
    low = total.astype(jnp.bfloat16)
    for z in range(keep.shape[0]):
        even = low[(2 * z) * shard_rows : (2 * z + 1) * shard_rows]
        odd = low[(2 * z + 1) * shard_rows : (2 * z + 2) * shard_rows]
        keep[z] = jnp.where(core == 0, even, odd)
        send[z] = jnp.where(core == 0, odd, even)


def grad_tokens_kernel(sc, dqkv, weight, out):
    place = sc[1]
    rows = out.shape[1]
    full = weight[...].reshape(-1, weight.shape[3])
    for j in range(4):
        part = dot_nt(dqkv[j * rows : (j + 1) * rows, :], full)
        out[place ^ j] = part.astype(out.dtype)


def normalize(values):
    center = values - jnp.mean(values, axis=-1, keepdims=True)
    inverse = lax.rsqrt(jnp.mean(center * center, axis=-1, keepdims=True) + epsilon)
    return center * inverse, inverse


def normalize_back(grad, unit, inverse):
    return inverse * (
        grad
        - jnp.mean(grad, axis=-1, keepdims=True)
        - unit * jnp.mean(grad * unit, axis=-1, keepdims=True)
    )


def middle_kernel(
    sc,
    x0,
    x1,
    x2,
    x3,
    token,
    cotangent,
    small,
    up_bias,
    gathered,
    own_down,
    other_down,
    output,
    grad_one,
    y0,
    y1,
    y2,
    y3,
    keep,
    send,
    sums,
    up_sums,
    w_out,
    w_up,
    w_down,
    slope,
    active,
    grad_up,
    context,
    sems,
):
    place, core, level = sc[1], sc[2], sc[3]
    blocks = w_up.shape[0]
    shard_rows = w_up.shape[3]
    width = w_up.shape[4]
    third = shard_rows // 3
    copies = []
    for b in range(blocks):
        copies.append(
            pltpu.make_async_copy(gathered.at[:, :, b, 0:shard_rows, :], w_up.at[b], sems.at[b])
        )
    down_copies = []
    for j in range(4):
        for k in range(4):
            for side, block in ((core, own_down), (1 - core, other_down)):
                down_copies.append(
                    pltpu.make_async_copy(
                        block.at[j, k],
                        w_down.at[level ^ k, side, place ^ j],
                        sems.at[7 + len(down_copies)],
                    )
                )
    out_copies = [
        pltpu.make_async_copy(
            gathered.at[:, :, b, shard_rows : shard_rows + third, :],
            w_out.at[:, :, b * third : (b + 1) * third, :],
            sems.at[blocks + b],
        )
        for b in range(3)
    ]
    for copy in out_copies + copies + down_copies:
        copy.start()
    for copy in out_copies:
        copy.wait()
    out_rows = 2 * shard_rows

    def out_block(j):
        return w_out[place ^ j].reshape(out_rows, width)

    residual = token[...].astype(jnp.float32) + small[0:1, :]
    for j, block in enumerate((x0, x1, x2, x3)):
        residual = residual + dot_nn(block[...], out_block(j))
    unit_one, inverse_one = normalize(residual)
    gain_one = small[1:2, :]
    normed = unit_one * gain_one + small[2:3, :]
    normed_low = normed.astype(jnp.bfloat16)
    for b in range(blocks):
        copies[b].wait()
        span = slice(b * width, (b + 1) * width)
        up = dot_nn(normed_low, w_up[b].reshape(width, width)) + up_bias[:, span]
        phi = 0.5 + 0.5 * lax.erf(up * HALF_ROOT)
        slope[:, span] = phi + up * (jnp.exp(-0.5 * up * up) * NORMAL_SCALE)
        active[:, span] = (up * phi).astype(jnp.bfloat16)
    for copy in down_copies:
        copy.wait()
    residual = normed + small[3:4, :] + dot_nn(active[...], w_down[...].reshape(-1, width))
    unit_two, inverse_two = normalize(residual)
    gain_two = small[4:5, :]
    output[...] = (unit_two * gain_two + small[5:6, :]).astype(jnp.bfloat16)
    grad = cotangent[...].astype(jnp.float32)
    sums[3:4, :] = jnp.sum(grad * unit_two, axis=0, keepdims=True)
    sums[4:5, :] = jnp.sum(grad, axis=0, keepdims=True)
    grad_two = normalize_back(grad * gain_two, unit_two, inverse_two)
    sums[5:6, :] = jnp.sum(grad_two, axis=0, keepdims=True)
    two_low = grad_two.astype(jnp.bfloat16)
    grad_normed = grad_two
    for b in range(blocks):
        span = slice(b * width, (b + 1) * width)
        rows_down = w_down[b].reshape(width, width)
        part = dot_nt(two_low, rows_down) * slope[:, span]
        up_sums[:, span] = jnp.sum(part, axis=0, keepdims=True)
        part = part.astype(jnp.bfloat16)
        grad_up[:, span] = part
        grad_normed = grad_normed + dot_nt(part, w_up[b].reshape(width, width))
    sums[1:2, :] = jnp.sum(grad_normed * unit_one, axis=0, keepdims=True)
    sums[2:3, :] = jnp.sum(grad_normed, axis=0, keepdims=True)
    first = normalize_back(grad_normed * gain_one, unit_one, inverse_one)
    sums[0:1, :] = jnp.sum(first, axis=0, keepdims=True)
    sums[6:8, :] = jnp.zeros((2, width), jnp.float32)
    grad_one[...] = first
    one_low = first.astype(jnp.bfloat16)
    for j, out in enumerate((y0, y1, y2, y3)):
        out[...] = dot_nt(one_low, out_block(j)).astype(jnp.bfloat16)
    for j, block in enumerate((x0, x1, x2, x3)):
        context[place ^ j] = block[...]
    joined = jnp.concatenate([context[j] for j in range(4)], axis=1)
    half = width // 2
    down_rows = blocks * shard_rows
    for ref, mine in ((keep, core), (send, 1 - core)):
        for z in range(4):
            even = active[:, (2 * z) * down_rows : (2 * z + 1) * down_rows]
            odd = active[:, (2 * z + 1) * down_rows : (2 * z + 2) * down_rows]
            ref[:, z * down_rows : (z + 1) * down_rows] = jnp.where(mine == 0, even, odd)
        at = 4 * down_rows
        ref[:, at : at + width] = two_low
        at += width
        ref[:, at : at + width] = normed_low
        at += width
        ref[:, at : at + 2 * width] = jnp.where(
            mine == 0, grad_up[:, : 2 * width], grad_up[:, 2 * width :]
        )
        at += 2 * width
        ref[:, at : at + width] = joined
        at += width
        ref[:, at : at + half] = jnp.where(mine == 0, one_low[:, :half], one_low[:, half:])


def down_grad_kernel(sc, keep, got, near, far, part):
    place = sc[1]
    _, zs, shard_rows, width = near.shape
    down_rows = 4 * shard_rows
    at_two = zs * down_rows
    right = slice(at_two, at_two + width)
    for z in range(zs):
        left = slice(z * down_rows, (z + 1) * down_rows)
        total = dot_tn(keep[:, left], keep[:, right]) + dot_tn(got[:, left], got[:, right])
        part[...] = total.astype(jnp.bfloat16).reshape(4, shard_rows, width)
        for out, at, j in ((near, 0, 0), (near, 1, 2), (far, 0, 1), (far, 1, 3)):
            out[at, z] = part[place ^ j]


def up_grad_kernel(sc, keep, got, near, far, part):
    place = sc[1]
    _, zs, block_rows, cols = near.shape
    quarter = part.shape[2]
    pair_rows = block_rows - quarter
    width = zs * pair_rows
    at_norm = 2 * width + width
    at_up = at_norm + width
    at_ctx = at_up + 2 * width
    at_one = at_ctx + width
    left = slice(at_ctx, at_ctx + width)
    right = slice(at_one, at_one + cols)
    total = dot_tn(keep[:, left], keep[:, right]) + dot_tn(got[:, left], got[:, right])
    part[...] = total.astype(jnp.bfloat16).reshape(part.shape)
    left = slice(at_norm, at_norm + width)
    for out, at, j in ((near, 0, 0), (near, 1, 1), (far, 0, 2), (far, 1, 3)):
        right = pl.ds(pl.multiple_of(at_up + (place ^ j) * cols, 128), cols)
        total = dot_tn(keep[:, left], keep[:, right]) + dot_tn(got[:, left], got[:, right])
        total = total.astype(jnp.bfloat16)
        for z in range(zs):
            out[at, z, :pair_rows] = total[z * pair_rows : (z + 1) * pair_rows]
            out[at, z, pair_rows:] = part[z, place ^ j]


def fold_kernel(near, got, mine, pass_on):
    for at, out in ((0, mine), (1, pass_on)):
        total = near[at].astype(jnp.float32) + got[at].astype(jnp.float32)
        out[...] = total.astype(jnp.bfloat16)


def level_fold_kernel(sc, mine, got, near, far):
    level = sc[3]
    for out, at, k in ((near, 0, 0), (near, 1, 2), (far, 0, 1), (far, 1, 3)):
        total = mine[level ^ k].astype(jnp.float32) + got[level ^ k].astype(jnp.float32)
        out[at] = total.astype(jnp.bfloat16)


def block_sum(refs):
    total = refs[0][...].astype(jnp.float32)
    for ref in refs[1:]:
        total = total + ref[...].astype(jnp.float32)
    return total


def split_up_kernel(sc, e0, e1, keep, send, held):
    core = sc[2]
    shard_rows = (keep.shape[0] * 2) // 3
    held[...] = block_sum((e0, e1)).astype(jnp.bfloat16)
    for ref, side in ((keep, core), (send, 1 - core)):
        ref[:shard_rows] = held[pl.ds(pl.multiple_of(side * shard_rows, 16), shard_rows), :]
        ref[shard_rows:] = held[2 * shard_rows :, :]


def join_kernel(sc, e0, e1, keep, got, out):
    core = sc[2]
    shard_rows = e0.shape[0]
    cols = keep.shape[1]
    out[:shard_rows] = block_sum((e0, e1)).astype(jnp.bfloat16)
    for ref, side in ((keep, core), (got, 1 - core)):
        out[shard_rows:, pl.ds(pl.multiple_of(side * cols, 128), cols)] = ref[...]


def finish_kernel(sc, b0, b1, b2, b3, down, up, out):
    place, core = sc[1], sc[2]
    shard_rows = up.shape[0]
    quarter = shard_rows // 2
    cols = b0.shape[1] // 2
    for j, ref in enumerate((b0, b1, b2, b3)):
        where = place ^ j
        rows = pl.ds(pl.multiple_of(where * shard_rows, 8), shard_rows)
        down[rows, :] = ref[:shard_rows].astype(jnp.float32)
        for side in range(2):
            at = pl.multiple_of((side * 4 + where) * cols, 128)
            up[:, pl.ds(at, cols)] = ref[
                shard_rows : 2 * shard_rows, side * cols : (side + 1) * cols
            ].astype(jnp.float32)

        @pl.when(where // 2 == core)
        def _(ref=ref, where=where):
            at = pl.multiple_of((where % 2) * quarter, 8)
            out[pl.ds(at, quarter), :] = ref[2 * shard_rows :].astype(jnp.float32)


def sum_kernel(e0, e1, out):
    out[...] = block_sum((e0, e1)).astype(out.dtype)


def finish_qkv_kernel(sc, b0, b1, b2, b3, out, held):
    place = sc[1]
    head_width = b0.shape[1] // 3
    for j, ref in enumerate((b0, b1, b2, b3)):
        held[place ^ j] = ref[...].astype(jnp.float32)
    for part in range(3):
        for s in range(4):
            at = (part * 4 + s) * head_width
            out[:, at : at + head_width] = held[s, :, part * head_width : (part + 1) * head_width]


def fast_body(
    tokens,
    lengths,
    w_qkv,
    q_bias,
    v_bias,
    w_out,
    out_bias,
    gain_one,
    shift_one,
    w_up,
    up_bias,
    w_down,
    down_bias,
    gain_two,
    shift_two,
    cotangent,
):
    bf16, f32 = jnp.bfloat16, jnp.float32
    _, rows, width = tokens.shape
    shard_rows = w_qkv.shape[0]
    hidden = w_up.shape[1]
    head_width = width // 4
    place = lax.axis_index("seq")
    core = lax.axis_index("core")
    zs = 4
    third = shard_rows // 3
    swap = [(0, 1), (1, 0)]

    def struct(shape, dtype=bf16):
        return jax.ShapeDtypeStruct(shape, dtype)

    def across(value, step):
        return lax.ppermute(value, "seq", [(i, i ^ step) for i in range(4)])

    def partner(value):
        return lax.ppermute(value, "core", swap)

    def level_across(value, step):
        return lax.ppermute(value, "z", [(i, i ^ step) for i in range(4)])

    token = tokens[0]
    quarter = jnp.concatenate(
        [
            lax.dynamic_slice_in_dim(w_up, place * width, width, axis=1),
            lax.dynamic_slice_in_dim(w_out, jnp.minimum(place, 2) * third, third, axis=0),
        ],
        axis=0,
    )
    gathered = lax.all_gather(quarter, ("z", "core", "seq"), axis=0, tiled=True)
    gathered = gathered.reshape(zs, 2, 4, shard_rows + third, width)
    columns = lax.dynamic_index_in_dim(
        w_qkv.reshape(shard_rows, 3, 4, head_width), place, axis=2, keepdims=False
    ).reshape(shard_rows, 3 * head_width)
    pair_rows = jnp.zeros((2, 2, shard_rows), bf16)
    placed_q = lax.dynamic_update_slice(pair_rows[0], q_bias[None], (core, 0)).reshape(1, -1)
    placed_v = lax.dynamic_update_slice(pair_rows[0], v_bias[None], (core, 0)).reshape(1, -1)
    bias_row = jnp.concatenate(
        [placed_q, jnp.zeros((1, head_width), bf16), placed_v], axis=1
    )
    vectors = jnp.concatenate(
        [out_bias, gain_one, shift_one, down_bias, gain_two, shift_two, up_bias]
    )
    pad = 15 * 3 * head_width - vectors.shape[0]
    vector_rows = jnp.pad(vectors, (0, pad)).reshape(15, 3 * head_width)
    own_block = jnp.concatenate([columns, bias_row, vector_rows], axis=0)
    t1, t2, t3 = across(token, 1), across(token, 2), across(token, 3)
    two_cols = jnp.stack([own_block, level_across(own_block, 1)])
    own_cols = jnp.concatenate([two_cols, level_across(two_cols, 2)])
    down_quarter = lax.dynamic_slice_in_dim(w_down, place * shard_rows, shard_rows, axis=0)
    two_down = jnp.stack([down_quarter, level_across(down_quarter, 1)])
    own_down = jnp.concatenate([two_down, level_across(two_down, 2)])
    own_down, own_cols, t1, t2, t3 = lax.optimization_barrier((own_down, own_cols, t1, t2, t3))
    other_cols = partner(own_cols)
    down_sets = [own_down] + [across(own_down, j) for j in (1, 2, 3)]
    sc = jnp.stack([lengths[0], place, core, lax.axis_index("z")]).astype(jnp.int32)
    all_rows = 4 * rows
    qkv, ctx_t, c0, c1, c2, c3, lse, full_qkv, vector_sets = pl.pallas_call(
        attend_forward_kernel,
        name="attend_forward",
        cost_estimate=work(13),
        out_shape=(
            struct((all_rows, 3 * head_width)),
            struct((head_width, all_rows), f32),
            struct((rows, head_width)),
            struct((rows, head_width)),
            struct((rows, head_width)),
            struct((rows, head_width)),
            struct((head_width // HEAD_DIM, all_rows), f32),
            struct((zs, 2, shard_rows, 3 * head_width)),
            struct((zs, 2, 2, 3 * head_width), f32),
        ),
        in_specs=[smem_spec()] + vmem_specs(6),
        out_specs=tuple(vmem_specs(9)),
        scratch_shapes=[pltpu.VMEM((4, rows, head_width), bf16)],
    )(sc, token, t1, t2, t3, own_cols, other_cols)
    x1, x2, x3 = across(c1, 1), across(c2, 2), across(c3, 3)
    down_sets[0], _ = lax.optimization_barrier((down_sets[0], c0))
    own_down = jnp.stack(down_sets)
    other_down = partner(own_down)
    all_vec = vector_sets.reshape(2 * zs, -1)
    six = all_vec[:, : 6 * shard_rows].reshape(2 * zs, 6, shard_rows)
    six = six.transpose(1, 0, 2).reshape(6, width)
    small = jnp.concatenate([six, jnp.zeros((2, width), f32)], axis=0)
    full_up_bias = all_vec[:, 6 * shard_rows : 6 * shard_rows + hidden // 8].reshape(1, hidden)
    packed = hidden // 2 + 5 * width + width // 2
    output, grad_one, y0, y1, y2, y3, keep, send, sums, up_sums = pl.pallas_call(
        middle_kernel,
        name="middle",
        cost_estimate=work(15),
        out_shape=(
            struct((rows, width)),
            struct((rows, width), f32),
            struct((rows, head_width)),
            struct((rows, head_width)),
            struct((rows, head_width)),
            struct((rows, head_width)),
            struct((rows, packed)),
            struct((rows, packed)),
            struct((8, width), f32),
            struct((1, hidden), f32),
        ),
        in_specs=[smem_spec()]
        + vmem_specs(8)
        + [pl.BlockSpec(memory_space=pl.ANY)] * 3,
        out_specs=tuple(vmem_specs(10)),
        scratch_shapes=[
            pltpu.VMEM((zs, 2, shard_rows, width), bf16),
            pltpu.VMEM((4, zs, 2, shard_rows, width), bf16),
            pltpu.VMEM((zs, 2, 4, shard_rows, width), bf16),
            pltpu.VMEM((rows, hidden), f32),
            pltpu.VMEM((rows, hidden), bf16),
            pltpu.VMEM((rows, hidden), bf16),
            pltpu.VMEM((4, rows, head_width), bf16),
            pltpu.SemaphoreType.DMA((7 + 32,)),
        ],
    )(
        sc,
        c0,
        x1,
        x2,
        x3,
        token,
        cotangent[0],
        small,
        full_up_bias,
        gathered,
        own_down,
        other_down,
    )
    g1, g2, g3 = across(y1, 1), across(y2, 2), across(y3, 3)
    got, g1, g2, g3 = lax.optimization_barrier((partner(send), g1, g2, g3))
    quad = hidden // 8

    def call(kernel, micros, outs, *args, scratch=(), scalars=True):
        return pl.pallas_call(
            kernel,
            name=kernel.__name__.replace("_kernel", ""),
            cost_estimate=work(micros),
            out_shape=tuple(outs),
            in_specs=([smem_spec()] if scalars else []) + vmem_specs(len(args)),
            out_specs=tuple(vmem_specs(len(outs))),
            scratch_shapes=list(scratch),
        )(*(((sc,) if scalars else ()) + args))

    d_near, d_far = call(
        down_grad_kernel,
        4,
        [struct((2, zs, shard_rows, width))] * 2,
        keep,
        got,
        scratch=[pltpu.VMEM((4, shard_rows, width), bf16)],
    )
    block_rows = 2 * shard_rows + shard_rows // 2
    u_near, u_far = call(
        up_grad_kernel,
        4,
        [struct((2, zs, block_rows, quad))] * 2,
        keep,
        got,
        scratch=[pltpu.VMEM((zs, 4, shard_rows // 2, quad), bf16)],
    )
    d_got = across(d_far, 1)
    u_got = across(u_far, 2)
    y0, d_near, u_near = lax.optimization_barrier((y0, d_near, u_near))

    dqkv = pl.pallas_call(
        attend_backward_kernel,
        name="attend_backward",
        cost_estimate=work(11),
        out_shape=struct((all_rows, 3 * head_width)),
        in_specs=[smem_spec()] + vmem_specs(7),
        out_specs=pl.BlockSpec(memory_space=pltpu.VMEM),
        scratch_shapes=[
            pltpu.VMEM((head_width // HEAD_DIM, all_rows, HEAD_DIM), f32),
            pltpu.VMEM((head_width // HEAD_DIM, all_rows, HEAD_DIM), f32),
            pltpu.VMEM((4, rows, head_width), bf16),
        ],
    )(sc, qkv, ctx_t, lse, y0, g1, g2, g3)
    q_keep, q_send, q_sums = pl.pallas_call(
        grad_qkv_weight_kernel,
        name="grad_qkv_weight",
        cost_estimate=work(4),
        out_shape=(
            struct((zs, shard_rows, 3 * head_width)),
            struct((zs, shard_rows, 3 * head_width)),
            struct((1, 3 * head_width), f32),
        ),
        in_specs=[smem_spec()] + vmem_specs(5),
        out_specs=tuple(vmem_specs(3)),
    )(sc, token, t1, t2, t3, dqkv)
    d_near, u_near, q_keep = lax.optimization_barrier((d_near, u_near, q_keep))
    d_mine, d_pass = call(
        fold_kernel, 1, [struct((zs, shard_rows, width))] * 2, d_near, d_got, scalars=False
    )
    u_mine, u_pass = call(
        fold_kernel, 1, [struct((zs, block_rows, quad))] * 2, u_near, u_got, scalars=False
    )
    q_got = partner(q_send)
    late_dqkv, q_keep = lax.optimization_barrier((dqkv, q_keep))
    (token_parts,) = call(
        grad_tokens_kernel,
        4,
        [struct((4, rows, width))],
        late_dqkv,
        full_qkv,
    )
    q_near, q_far = call(
        level_fold_kernel, 1, [struct((2, shard_rows, 3 * head_width))] * 2, q_keep, q_got
    )

    def level_sum(near, far, shape):
        mine, pass_on = call(
            fold_kernel, 1, [struct(shape)] * 2, near, level_across(far, 1), scalars=False
        )
        return mine, level_across(pass_on, 2)

    q_mine, q_last = level_sum(q_near, q_far, (shard_rows, 3 * head_width))
    (q_part,) = call(
        sum_kernel, 1, [struct((shard_rows, 3 * head_width))], q_mine, q_last, scalars=False
    )

    def seq_sum(mine, pass_on, shape, step):
        return call(
            level_fold_kernel,
            1,
            [struct((2,) + shape[1:])] * 2,
            mine,
            across(pass_on, step),
        )

    d_mine, u_mine, _ = lax.optimization_barrier((d_mine, u_mine, q_mine))
    d_near, d_far = seq_sum(d_mine, d_pass, (zs, shard_rows, width), 2)
    u_near, u_far = seq_sum(u_mine, u_pass, (zs, block_rows, quad), 1)
    token_parts, _, _ = lax.optimization_barrier((token_parts, u_near, d_near))
    token_sum = lax.psum_scatter(
        token_parts.reshape(4 * rows, width), "seq", scatter_dimension=0, tiled=True
    )
    d_parts = level_sum(d_near, d_far, (shard_rows, width))
    u_parts = level_sum(u_near, u_far, (block_rows, quad))
    half_rows = shard_rows + shard_rows // 2
    u_keep, u_send = call(
        split_up_kernel,
        1,
        [struct((half_rows, quad))] * 2,
        *u_parts,
        scratch=[pltpu.VMEM((block_rows, quad), bf16)],
    )
    (joined,) = call(
        join_kernel,
        1,
        [struct((shard_rows + half_rows, width))],
        *d_parts,
        u_keep,
        partner(u_send),
    )
    result_down, result_up, result_out = call(
        finish_kernel,
        2,
        [
            struct((4 * shard_rows, width), f32),
            struct((shard_rows, hidden), f32),
            struct((shard_rows, width), f32),
        ],
        joined,
        *[across(joined, j) for j in (1, 2, 3)],
    )
    (result_qkv,) = call(
        finish_qkv_kernel,
        1,
        [struct((shard_rows, 3 * width), f32)],
        q_part,
        *[across(q_part, j) for j in (1, 2, 3)],
        scratch=[pltpu.VMEM((4, shard_rows, 3 * head_width), f32)],
    )
    grad_tokens = (grad_one + token_sum.astype(f32)).astype(bf16)

    q_row = lax.dynamic_update_slice(
        jnp.zeros((1, width), f32), q_sums[:, :head_width], (0, place * head_width)
    )
    v_row = lax.dynamic_update_slice(
        jnp.zeros((1, width), f32), q_sums[:, 2 * head_width :], (0, place * head_width)
    )

    def everywhere(value):
        value = value + partner(value)
        value = value + across(value, 1)
        value = value + across(value, 2)
        value = value + level_across(value, 1)
        value = value + level_across(value, 2)
        return value

    vector_sums = jnp.concatenate([sums[:6], up_sums.reshape(4, width), q_row, v_row], axis=0)
    vector_sums, _ = lax.optimization_barrier((vector_sums, q_mine))
    early = everywhere(vector_sums)
    shard = 2 * lax.axis_index("z") + core

    def owned(vector):
        size = vector.shape[0] // (2 * zs)
        return lax.dynamic_slice(vector, (shard * size,), (size,))

    return (
        output[None],
        grad_tokens[None],
        result_qkv,
        owned(early[10]),
        owned(early[11]),
        result_out,
        owned(early[0]),
        owned(early[1]),
        owned(early[2]),
        result_up,
        owned(early[6:10].reshape(-1)),
        result_down,
        owned(early[5]),
        owned(early[3]),
        owned(early[4]),
    )


def solution(mesh):
    seq_count, shard_count = mesh.shape["seq"], mesh.shape["shard"]
    fast = seq_count == 4 and shard_count == 8
    if fast:
        grid = mesh.devices.reshape(seq_count, shard_count // 2, 2)
        mesh = jax.sharding.Mesh(grid, AXES)
    shard = ("z", "core") if fast else "shard"
    vector, matrix, rows = P(shard), P(shard, None), P(shard, "seq", None)
    return jax.shard_map(
        fast_body if fast else body,
        mesh=mesh,
        in_specs=(
            rows,
            vector,
            matrix,
            vector,
            vector,
            matrix,
            vector,
            vector,
            vector,
            matrix,
            vector,
            matrix,
            vector,
            vector,
            vector,
            rows,
        ),
        out_specs=(
            rows,
            rows,
            matrix,
            vector,
            vector,
            matrix,
            vector,
            vector,
            vector,
            matrix,
            vector,
            matrix,
            vector,
            vector,
            vector,
        ),
        check_vma=False,
    )
```

```python
import jax
import jax.numpy as jnp
from jax import lax
from jax.experimental import pallas as pl
from jax.experimental.pallas import tpu as pltpu
from jax.sharding import PartitionSpec as P

HEAD_DIM = 64
LEN = 1024
Q_BLOCK = 512


epsilon = 1e-05
masked_score = -1000000000.0


def layer_norm(values, gain, shift):
    center = values - jnp.mean(values, axis=-1, keepdims=True)
    spread = jnp.mean(center * center, axis=-1, keepdims=True)
    return center * lax.rsqrt(spread + epsilon) * gain + shift


def gelu_exact(values):
    return jax.nn.gelu(values, approximate=False)


def contract_rows(left, right):
    return lax.dot_general(
        left, right, (((0,), (0,)), ((), ())), preferred_element_type=jnp.float32
    )


def contract_cols(left, right):
    return lax.dot_general(
        left, right, (((1,), (1,)), ((), ())), preferred_element_type=jnp.float32
    )


def block_scores(q_block, k_seq, key_valid):
    scores = jnp.einsum(
        "qhd,khd->hqk", q_block, k_seq, preferred_element_type=jnp.float32
    ) * HEAD_DIM ** (-0.5)
    return jnp.where(key_valid[None, None, :], scores, masked_score)


def attend_forward(q_seq, k_seq, v_seq, length):
    local_heads = q_seq.shape[1]
    key_valid = jnp.arange(LEN, dtype=jnp.int32) < length
    q_blocks = q_seq.reshape(LEN // Q_BLOCK, Q_BLOCK, local_heads, HEAD_DIM)

    def one_block(q_block):
        scores = block_scores(q_block, k_seq, key_valid)
        row_peak = jnp.max(scores, axis=-1, keepdims=True)
        shifted = jnp.exp(scores - row_peak)
        row_total = jnp.sum(shifted, axis=-1, keepdims=True)
        attn_probs = (shifted / row_total).astype(jnp.bfloat16)
        context = jnp.einsum("hqk,khd->qhd", attn_probs, v_seq, preferred_element_type=jnp.float32)
        return (context.astype(jnp.bfloat16), (row_peak + jnp.log(row_total))[..., 0])

    context, log_total = lax.map(one_block, q_blocks)
    return (context.reshape(LEN, local_heads, HEAD_DIM), log_total)


def attend_backward(q_seq, k_seq, v_seq, grad_seq, log_total, length):
    local_heads = q_seq.shape[1]
    score_scale = HEAD_DIM ** (-0.5)
    key_valid = jnp.arange(LEN, dtype=jnp.int32) < length
    q_blocks = q_seq.reshape(LEN // Q_BLOCK, Q_BLOCK, local_heads, HEAD_DIM)
    g_blocks = grad_seq.reshape(LEN // Q_BLOCK, Q_BLOCK, local_heads, HEAD_DIM)

    def one_block(accum, block_item):
        q_block, g_block, lse_block = block_item
        scores = block_scores(q_block, k_seq, key_valid)
        attn_probs = jnp.exp(scores - lse_block[..., None])
        grad_probs = jnp.einsum("qhd,khd->hqk", g_block, v_seq, preferred_element_type=jnp.float32)
        row_dot = jnp.sum(attn_probs * grad_probs, axis=-1, keepdims=True)
        grad_scores = (attn_probs * (grad_probs - row_dot)).astype(jnp.bfloat16)
        grad_q = (
            jnp.einsum("hqk,khd->qhd", grad_scores, k_seq, preferred_element_type=jnp.float32)
            * score_scale
        )
        grad_k = (
            accum[0]
            + jnp.einsum("hqk,qhd->khd", grad_scores, q_block, preferred_element_type=jnp.float32)
            * score_scale
        )
        grad_v = accum[1] + jnp.einsum(
            "hqk,qhd->khd",
            attn_probs.astype(jnp.bfloat16),
            g_block,
            preferred_element_type=jnp.float32,
        )
        return ((grad_k, grad_v), grad_q.astype(jnp.bfloat16))

    zero_keys = jnp.zeros((LEN, local_heads, HEAD_DIM), jnp.float32)
    (grad_k, grad_v), grad_q = lax.scan(
        one_block, (zero_keys, zero_keys), (q_blocks, g_blocks, log_total)
    )
    return (
        grad_q.reshape(LEN, local_heads, HEAD_DIM),
        grad_k.astype(jnp.bfloat16),
        grad_v.astype(jnp.bfloat16),
    )


def body(
    tokens,
    lengths,
    w_qkv,
    q_bias,
    v_bias,
    w_out,
    out_bias,
    gain_one,
    shift_one,
    w_up,
    up_bias,
    w_down,
    down_bias,
    gain_two,
    shift_two,
    cotangent,
):
    seq_count, local_len, model_width = tokens.shape
    row_count = seq_count * local_len
    head_count = model_width // HEAD_DIM
    gathered = (
        lax.all_gather(w_qkv, "shard", axis=0, tiled=True),
        lax.all_gather(q_bias, "shard", axis=0, tiled=True),
        lax.all_gather(v_bias, "shard", axis=0, tiled=True),
        lax.all_gather(w_out, "shard", axis=0, tiled=True),
        lax.all_gather(out_bias, "shard", axis=0, tiled=True),
        lax.all_gather(gain_one, "shard", axis=0, tiled=True),
        lax.all_gather(shift_one, "shard", axis=0, tiled=True),
        lax.all_gather(w_up, "shard", axis=0, tiled=True),
        lax.all_gather(up_bias, "shard", axis=0, tiled=True),
        lax.all_gather(w_down, "shard", axis=0, tiled=True),
        lax.all_gather(down_bias, "shard", axis=0, tiled=True),
        lax.all_gather(gain_two, "shard", axis=0, tiled=True),
        lax.all_gather(shift_two, "shard", axis=0, tiled=True),
    )
    (
        full_qkv,
        full_q_bias,
        full_v_bias,
        full_out,
        full_out_bias,
        full_gain_one,
        full_shift_one,
        full_up,
        full_up_bias,
        full_down,
        full_down_bias,
        full_gain_two,
        full_shift_two,
    ) = gathered
    token_rows = tokens.reshape(row_count, model_width)
    joined_bias = jnp.concatenate([full_q_bias, jnp.zeros_like(full_q_bias), full_v_bias]).astype(
        jnp.float32
    )
    qkv_rows = (
        jnp.dot(token_rows, full_qkv, preferred_element_type=jnp.float32) + joined_bias
    ).astype(jnp.bfloat16)
    qkv_tokens = qkv_rows.reshape(seq_count, local_len, 3, head_count, HEAD_DIM)
    qkv_heads = lax.all_to_all(qkv_tokens, "seq", split_axis=3, concat_axis=1, tiled=True)

    def forward_seq(seq_item):
        qkv_seq, length = seq_item
        return attend_forward(qkv_seq[:, 0], qkv_seq[:, 1], qkv_seq[:, 2], length)

    context_heads, log_total = lax.map(forward_seq, (qkv_heads, lengths))
    context_tokens = lax.all_to_all(context_heads, "seq", split_axis=1, concat_axis=2, tiled=True)
    context_rows = context_tokens.reshape(row_count, model_width)
    residual_one = (
        token_rows.astype(jnp.float32)
        + jnp.dot(context_rows, full_out, preferred_element_type=jnp.float32)
        + full_out_bias.astype(jnp.float32)
    )
    normed_one, norm_one_pull = jax.vjp(
        layer_norm,
        residual_one,
        full_gain_one.astype(jnp.float32),
        full_shift_one.astype(jnp.float32),
    )
    normed_low = normed_one.astype(jnp.bfloat16)
    up_rows = jnp.dot(
        normed_low, full_up, preferred_element_type=jnp.float32
    ) + full_up_bias.astype(jnp.float32)
    active, gelu_pull = jax.vjp(gelu_exact, up_rows)
    active_low = active.astype(jnp.bfloat16)
    residual_two = (
        normed_one
        + jnp.dot(active_low, full_down, preferred_element_type=jnp.float32)
        + full_down_bias.astype(jnp.float32)
    )
    final_rows, norm_two_pull = jax.vjp(
        layer_norm,
        residual_two,
        full_gain_two.astype(jnp.float32),
        full_shift_two.astype(jnp.float32),
    )
    output = final_rows.astype(jnp.bfloat16).reshape(tokens.shape)
    back_qkv, back_out, back_up, back_down = (full_qkv, full_out, full_up, full_down)
    grad_rows = cotangent.reshape(row_count, model_width).astype(jnp.float32)
    grad_two, grad_gain_two, grad_shift_two = norm_two_pull(grad_rows)
    grad_down_bias = jnp.sum(grad_two, axis=0)
    grad_two_low = grad_two.astype(jnp.bfloat16)
    grad_w_down = contract_rows(active_low, grad_two_low)
    grad_active = contract_cols(grad_two_low, back_down)
    (grad_up,) = gelu_pull(grad_active)
    grad_up_bias = jnp.sum(grad_up, axis=0)
    grad_up_low = grad_up.astype(jnp.bfloat16)
    grad_w_up = contract_rows(normed_low, grad_up_low)
    grad_normed = grad_two + contract_cols(grad_up_low, back_up)
    grad_one, grad_gain_one, grad_shift_one = norm_one_pull(grad_normed)
    grad_out_bias = jnp.sum(grad_one, axis=0)
    grad_one_low = grad_one.astype(jnp.bfloat16)
    grad_w_out = contract_rows(context_rows, grad_one_low)
    grad_context = contract_cols(grad_one_low, back_out).astype(jnp.bfloat16)
    grad_context = grad_context.reshape(seq_count, local_len, head_count, HEAD_DIM)
    grad_context_heads = lax.all_to_all(
        grad_context, "seq", split_axis=2, concat_axis=1, tiled=True
    )

    def backward_seq(seq_item):
        qkv_seq, grad_seq, lse_seq, length = seq_item
        grad_q, grad_k, grad_v = attend_backward(
            qkv_seq[:, 0], qkv_seq[:, 1], qkv_seq[:, 2], grad_seq, lse_seq, length
        )
        return jnp.stack([grad_q, grad_k, grad_v], axis=1)

    grad_qkv_heads = lax.map(backward_seq, (qkv_heads, grad_context_heads, log_total, lengths))
    grad_qkv_tokens = lax.all_to_all(grad_qkv_heads, "seq", split_axis=1, concat_axis=3, tiled=True)
    grad_qkv_rows = grad_qkv_tokens.reshape(row_count, 3 * model_width)
    grad_q_bias = jnp.sum(grad_qkv_rows[:, :model_width], axis=0, dtype=jnp.float32)
    grad_v_bias = jnp.sum(grad_qkv_rows[:, 2 * model_width :], axis=0, dtype=jnp.float32)
    grad_w_qkv = contract_rows(token_rows, grad_qkv_rows)
    grad_tokens = grad_one + contract_cols(grad_qkv_rows, back_qkv)
    grad_tokens = grad_tokens.astype(jnp.bfloat16).reshape(tokens.shape)
    owned = (
        lax.psum_scatter(grad_w_qkv, "shard", scatter_dimension=0, tiled=True),
        lax.psum_scatter(grad_q_bias, "shard", scatter_dimension=0, tiled=True),
        lax.psum_scatter(grad_v_bias, "shard", scatter_dimension=0, tiled=True),
        lax.psum_scatter(grad_w_out, "shard", scatter_dimension=0, tiled=True),
        lax.psum_scatter(grad_out_bias, "shard", scatter_dimension=0, tiled=True),
        lax.psum_scatter(grad_gain_one, "shard", scatter_dimension=0, tiled=True),
        lax.psum_scatter(grad_shift_one, "shard", scatter_dimension=0, tiled=True),
        lax.psum_scatter(grad_w_up, "shard", scatter_dimension=0, tiled=True),
        lax.psum_scatter(grad_up_bias, "shard", scatter_dimension=0, tiled=True),
        lax.psum_scatter(grad_w_down, "shard", scatter_dimension=0, tiled=True),
        lax.psum_scatter(grad_down_bias, "shard", scatter_dimension=0, tiled=True),
        lax.psum_scatter(grad_gain_two, "shard", scatter_dimension=0, tiled=True),
        lax.psum_scatter(grad_shift_two, "shard", scatter_dimension=0, tiled=True),
    )
    owned_columns = (
        lax.psum_scatter(
            owned[0].astype(jnp.bfloat16), "seq", scatter_dimension=1, tiled=True
        ).astype(jnp.float32),
        lax.psum_scatter(
            owned[3].astype(jnp.bfloat16), "seq", scatter_dimension=1, tiled=True
        ).astype(jnp.float32),
        lax.psum_scatter(
            owned[7].astype(jnp.bfloat16), "seq", scatter_dimension=1, tiled=True
        ).astype(jnp.float32),
        lax.psum_scatter(
            owned[9].astype(jnp.bfloat16), "seq", scatter_dimension=1, tiled=True
        ).astype(jnp.float32),
    )
    matrices = (
        lax.all_gather(owned_columns[0].astype(jnp.bfloat16), "seq", axis=1, tiled=True).astype(
            jnp.float32
        ),
        lax.all_gather(owned_columns[1].astype(jnp.bfloat16), "seq", axis=1, tiled=True).astype(
            jnp.float32
        ),
        lax.all_gather(owned_columns[2].astype(jnp.bfloat16), "seq", axis=1, tiled=True).astype(
            jnp.float32
        ),
        lax.all_gather(owned_columns[3].astype(jnp.bfloat16), "seq", axis=1, tiled=True).astype(
            jnp.float32
        ),
    )
    vectors = lax.psum(
        (
            owned[1],
            owned[2],
            owned[4],
            owned[5],
            owned[6],
            owned[8],
            owned[10],
            owned[11],
            owned[12],
        ),
        "seq",
    )
    result_qkv, result_out, result_up, result_down = (
        matrices[0],
        matrices[1],
        matrices[2],
        matrices[3],
    )
    result_q_bias, result_v_bias, result_out_bias = (vectors[0], vectors[1], vectors[2])
    result_gain_one, result_shift_one, result_up_bias = (vectors[3], vectors[4], vectors[5])
    result_down_bias, result_gain_two, result_shift_two = (vectors[6], vectors[7], vectors[8])
    return (
        output,
        grad_tokens,
        result_qkv,
        result_q_bias,
        result_v_bias,
        result_out,
        result_out_bias,
        result_gain_one,
        result_shift_one,
        result_up,
        result_up_bias,
        result_down,
        result_down_bias,
        result_gain_two,
        result_shift_two,
    )


AXES = ("seq", "z", "core")
NORMAL_SCALE = 0.3989422804014327
HALF_ROOT = 0.7071067811865476


def dot_nn(left, right):
    return lax.dot_general(
        left, right, (((1,), (0,)), ((), ())), preferred_element_type=jnp.float32
    )


def dot_nt(left, right):
    return contract_cols(left, right)


def dot_tn(left, right):
    return contract_rows(left, right)


def vmem_specs(count):
    return [pl.BlockSpec(memory_space=pltpu.VMEM)] * count


def work(micros):
    return pl.CostEstimate(
        flops=int(micros * 9e7), transcendentals=0, bytes_accessed=int(micros * 3e5)
    )


def smem_spec():
    return pl.BlockSpec(memory_space=pltpu.SMEM)


def key_bias(sc, block_rows):
    length, place = sc[0], sc[1]
    columns = []
    for j in range(4):
        position = (place ^ j) * block_rows + lax.broadcasted_iota(
            jnp.int32, (block_rows, 1), 0
        )
        columns.append(jnp.where(position < length, 0.0, masked_score))
    return jnp.concatenate(columns, axis=0)


def attend_forward_kernel(
    sc, t0, t1, t2, t3, own, other, qkv, ctx_t, c0, c1, c2, c3, lse, weight, vectors, held
):
    place, core, level = sc[1], sc[2], sc[3]
    rows = t0.shape[0]
    shard_rows = weight.shape[2]
    width = weight.shape[3]
    head_width = width // 3
    heads = head_width // HEAD_DIM
    for k in range(4):
        for block, side in ((own, core), (other, 1 - core)):
            weight[level ^ k, side] = block[k, :shard_rows, :]
            vectors[level ^ k, side] = block[k, shard_rows + 1 : shard_rows + 3, :].astype(
                jnp.float32
            )
    full = weight[...].reshape(-1, width)
    bias = (
        own[level ^ place, shard_rows : shard_rows + 1, :].astype(jnp.float32)
        + other[level ^ place, shard_rows : shard_rows + 1, :].astype(jnp.float32)
    )
    for j, block in enumerate((t0, t1, t2, t3)):
        qkv[j * rows : (j + 1) * rows, :] = (dot_nn(block[...], full) + bias).astype(jnp.bfloat16)
    mask = key_bias(sc, rows)
    def one_block(j, carry):
        span = pl.ds(pl.multiple_of(j * rows, 128), rows)
        parts = []
        q_all = qkv[span, 0:head_width] * jnp.bfloat16(HEAD_DIM**-0.5)
        for h in range(heads):
            low = h * HEAD_DIM
            q = q_all[:, low : low + HEAD_DIM]
            k = qkv[:, head_width + low : head_width + low + HEAD_DIM]
            v = qkv[:, 2 * head_width + low : 2 * head_width + low + HEAD_DIM]
            scores = dot_nt(k, q) + mask
            peak = jnp.max(scores, axis=0, keepdims=True)
            shifted = jnp.exp(scores - peak)
            total = jnp.sum(shifted, axis=0, keepdims=True)
            part = dot_tn(v, shifted.astype(jnp.bfloat16)) / total
            parts.append(part)
            lse[h : h + 1, span] = peak + jnp.log(total)
        joined = jnp.concatenate(parts, axis=0)
        ctx_t[:, span] = joined
        held[j] = joined.T.astype(jnp.bfloat16)
        return carry

    lax.fori_loop(0, 4, one_block, 0)
    for j, out in enumerate((c0, c1, c2, c3)):
        out[...] = held[j]


def attend_backward_kernel(sc, qkv, ctx_t, lse, g0, g1, g2, g3, dqkv, dk_acc, dv_acc, held):
    rows = g0.shape[0]
    head_width = g0.shape[1]
    heads = head_width // HEAD_DIM
    mask = key_bias(sc, rows)
    scale = jnp.bfloat16(HEAD_DIM**-0.5)
    for j, g_ref in enumerate((g0, g1, g2, g3)):
        held[j] = g_ref[...]
    dk_acc[...] = jnp.zeros_like(dk_acc)
    dv_acc[...] = jnp.zeros_like(dv_acc)

    def one_block(j, carry):
        span = pl.ds(pl.multiple_of(j * rows, 128), rows)
        g_all = held[j]
        product = g_all.astype(jnp.float32).T * ctx_t[:, span]
        q_all = qkv[span, 0:head_width] * scale
        parts = []
        for h in range(heads):
            low = h * HEAD_DIM
            q = q_all[:, low : low + HEAD_DIM]
            g = g_all[:, low : low + HEAD_DIM]
            k = qkv[:, head_width + low : head_width + low + HEAD_DIM]
            v = qkv[:, 2 * head_width + low : 2 * head_width + low + HEAD_DIM]
            probs = jnp.exp(dot_nt(k, q) + mask - lse[h : h + 1, span])
            row_dot = jnp.sum(product[low : low + HEAD_DIM, :], axis=0, keepdims=True)
            grad_scores = (probs * (dot_nt(v, g) - row_dot)).astype(jnp.bfloat16)
            grad_v = dot_nn(probs.astype(jnp.bfloat16), g)
            grad_k = dot_nn(grad_scores, q)
            dv_acc[h] += grad_v
            dk_acc[h] += grad_k
            parts.append(dot_tn(k, grad_scores) * (HEAD_DIM**-0.5))
        dqkv[span, 0:head_width] = jnp.concatenate(parts, axis=0).T.astype(jnp.bfloat16)
        return carry

    lax.fori_loop(0, 4, one_block, 0)
    dk = jnp.concatenate([dk_acc[h] for h in range(heads)], axis=1)
    dv = jnp.concatenate([dv_acc[h] for h in range(heads)], axis=1)
    dqkv[:, head_width:] = jnp.concatenate([dk, dv], axis=1).astype(jnp.bfloat16)


def grad_qkv_weight_kernel(sc, t0, t1, t2, t3, dqkv, keep, send):
    core = sc[2]
    rows = t0.shape[0]
    total = None
    for j, block in enumerate((t0, t1, t2, t3)):
        part = dot_tn(block[...], dqkv[j * rows : (j + 1) * rows, :])
        total = part if total is None else total + part
    sums = jnp.sum(dqkv[...].astype(jnp.float32), axis=0, keepdims=True)
    sums = jnp.broadcast_to(sums, (16, sums.shape[1])).astype(jnp.bfloat16)
    shard_rows = keep.shape[1] - 16
    low = total.astype(jnp.bfloat16)
    for z in range(keep.shape[0]):
        even = low[(2 * z) * shard_rows : (2 * z + 1) * shard_rows]
        odd = low[(2 * z + 1) * shard_rows : (2 * z + 2) * shard_rows]
        keep[z, :shard_rows] = jnp.where(core == 0, even, odd)
        send[z, :shard_rows] = jnp.where(core == 0, odd, even)
        keep[z, shard_rows:] = sums
        send[z, shard_rows:] = sums


def grad_tokens_kernel(sc, dqkv, weight, out):
    place = sc[1]
    rows = out.shape[1]
    full = weight[...].reshape(-1, weight.shape[3])
    for j in range(4):
        part = dot_nt(dqkv[j * rows : (j + 1) * rows, :], full)
        out[place ^ j] = part.astype(out.dtype)


def normalize(values):
    center = values - jnp.mean(values, axis=-1, keepdims=True)
    inverse = lax.rsqrt(jnp.mean(center * center, axis=-1, keepdims=True) + epsilon)
    return center * inverse, inverse


def normalize_back(grad, unit, inverse):
    return inverse * (
        grad
        - jnp.mean(grad, axis=-1, keepdims=True)
        - unit * jnp.mean(grad * unit, axis=-1, keepdims=True)
    )


def middle_kernel(
    sc,
    x0,
    x1,
    x2,
    x3,
    token,
    cotangent,
    small,
    up_bias,
    gathered,
    own_down,
    other_down,
    output,
    grad_one,
    y0,
    y1,
    y2,
    y3,
    keep,
    send,
    sums,
    up_sums,
    w_out,
    w_up,
    w_down,
    slope,
    active,
    grad_up,
    context,
    sems,
):
    place, core, level = sc[1], sc[2], sc[3]
    blocks = w_up.shape[0]
    shard_rows = w_up.shape[3]
    width = w_up.shape[4]
    third = shard_rows // 3
    copies = []
    for b in range(blocks):
        copies.append(
            pltpu.make_async_copy(gathered.at[:, :, b, 0:shard_rows, :], w_up.at[b], sems.at[b])
        )
    down_copies = []
    for j in range(4):
        for k in range(4):
            for side, block in ((core, own_down), (1 - core, other_down)):
                down_copies.append(
                    pltpu.make_async_copy(
                        block.at[j, k],
                        w_down.at[level ^ k, side, place ^ j],
                        sems.at[7 + len(down_copies)],
                    )
                )
    out_copies = [
        pltpu.make_async_copy(
            gathered.at[:, :, b, shard_rows : shard_rows + third, :],
            w_out.at[:, :, b * third : (b + 1) * third, :],
            sems.at[blocks + b],
        )
        for b in range(3)
    ]
    for copy in out_copies + copies + down_copies:
        copy.start()
    for copy in out_copies:
        copy.wait()
    out_rows = 2 * shard_rows

    def out_block(j):
        return w_out[place ^ j].reshape(out_rows, width)

    residual = token[...].astype(jnp.float32) + small[0:1, :]
    for j, block in enumerate((x0, x1, x2, x3)):
        residual = residual + dot_nn(block[...], out_block(j))
    unit_one, inverse_one = normalize(residual)
    gain_one = small[1:2, :]
    normed = unit_one * gain_one + small[2:3, :]
    normed_low = normed.astype(jnp.bfloat16)
    for b in range(blocks):
        copies[b].wait()
        span = slice(b * width, (b + 1) * width)
        up = dot_nn(normed_low, w_up[b].reshape(width, width)) + up_bias[:, span]
        phi = 0.5 + 0.5 * lax.erf(up * HALF_ROOT)
        slope[:, span] = phi + up * (jnp.exp(-0.5 * up * up) * NORMAL_SCALE)
        active[:, span] = (up * phi).astype(jnp.bfloat16)
    for copy in down_copies:
        copy.wait()
    residual = normed + small[3:4, :] + dot_nn(active[...], w_down[...].reshape(-1, width))
    unit_two, inverse_two = normalize(residual)
    gain_two = small[4:5, :]
    output[...] = (unit_two * gain_two + small[5:6, :]).astype(jnp.bfloat16)
    grad = cotangent[...].astype(jnp.float32)
    sums[3:4, :] = jnp.sum(grad * unit_two, axis=0, keepdims=True)
    sums[4:5, :] = jnp.sum(grad, axis=0, keepdims=True)
    grad_two = normalize_back(grad * gain_two, unit_two, inverse_two)
    sums[5:6, :] = jnp.sum(grad_two, axis=0, keepdims=True)
    two_low = grad_two.astype(jnp.bfloat16)
    grad_normed = grad_two
    for b in range(blocks):
        span = slice(b * width, (b + 1) * width)
        rows_down = w_down[b].reshape(width, width)
        part = dot_nt(two_low, rows_down) * slope[:, span]
        up_sums[:, span] = jnp.sum(part, axis=0, keepdims=True)
        part = part.astype(jnp.bfloat16)
        grad_up[:, span] = part
        grad_normed = grad_normed + dot_nt(part, w_up[b].reshape(width, width))
    sums[1:2, :] = jnp.sum(grad_normed * unit_one, axis=0, keepdims=True)
    sums[2:3, :] = jnp.sum(grad_normed, axis=0, keepdims=True)
    first = normalize_back(grad_normed * gain_one, unit_one, inverse_one)
    sums[0:1, :] = jnp.sum(first, axis=0, keepdims=True)
    sums[6:8, :] = jnp.zeros((2, width), jnp.float32)
    grad_one[...] = first
    one_low = first.astype(jnp.bfloat16)
    for j, out in enumerate((y0, y1, y2, y3)):
        out[...] = dot_nt(one_low, out_block(j)).astype(jnp.bfloat16)
    for j, block in enumerate((x0, x1, x2, x3)):
        context[place ^ j] = block[...]
    joined = jnp.concatenate([context[j] for j in range(4)], axis=1)
    half = width // 2
    down_rows = blocks * shard_rows
    for ref, mine in ((keep, core), (send, 1 - core)):
        for z in range(4):
            even = active[:, (2 * z) * down_rows : (2 * z + 1) * down_rows]
            odd = active[:, (2 * z + 1) * down_rows : (2 * z + 2) * down_rows]
            ref[:, z * down_rows : (z + 1) * down_rows] = jnp.where(mine == 0, even, odd)
        at = 4 * down_rows
        ref[:, at : at + width] = two_low
        at += width
        ref[:, at : at + width] = normed_low
        at += width
        ref[:, at : at + 2 * width] = jnp.where(
            mine == 0, grad_up[:, : 2 * width], grad_up[:, 2 * width :]
        )
        at += 2 * width
        ref[:, at : at + width] = joined
        at += width
        ref[:, at : at + half] = jnp.where(mine == 0, one_low[:, :half], one_low[:, half:])


def down_grad_kernel(sc, keep, got, near, far, part):
    place = sc[1]
    _, zs, shard_rows, width = near.shape
    down_rows = 4 * shard_rows
    at_two = zs * down_rows
    right = slice(at_two, at_two + width)
    for z in range(zs):
        left = slice(z * down_rows, (z + 1) * down_rows)
        total = dot_tn(keep[:, left], keep[:, right]) + dot_tn(got[:, left], got[:, right])
        part[...] = total.astype(jnp.bfloat16).reshape(4, shard_rows, width)
        for out, at, j in ((near, 0, 0), (near, 1, 2), (far, 0, 1), (far, 1, 3)):
            out[at, z] = part[place ^ j]


def up_grad_kernel(sc, keep, got, vectors, near, far, part):
    place = sc[1]
    _, zs, block_rows, cols = near.shape
    quarter = part.shape[2]
    pair_rows = block_rows - quarter - 16
    width = zs * pair_rows
    at_norm = 2 * width + width
    at_up = at_norm + width
    at_ctx = at_up + 2 * width
    at_one = at_ctx + width
    left = slice(at_ctx, at_ctx + width)
    right = slice(at_one, at_one + cols)
    total = dot_tn(keep[:, left], keep[:, right]) + dot_tn(got[:, left], got[:, right])
    part[...] = total.astype(jnp.bfloat16).reshape(part.shape)
    left = slice(at_norm, at_norm + width)
    for out, at, j in ((near, 0, 0), (near, 1, 1), (far, 0, 2), (far, 1, 3)):
        right = pl.ds(pl.multiple_of(at_up + (place ^ j) * cols, 128), cols)
        total = dot_tn(keep[:, left], keep[:, right]) + dot_tn(got[:, left], got[:, right])
        total = total.astype(jnp.bfloat16)
        for z in range(zs):
            out[at, z, :pair_rows] = total[z * pair_rows : (z + 1) * pair_rows]
            out[at, z, pair_rows : pair_rows + quarter] = part[z, place ^ j]
            out[at, z, pair_rows + quarter :] = vectors[z]


def fold_kernel(near, got, mine, pass_on):
    for at, out in ((0, mine), (1, pass_on)):
        total = near[at].astype(jnp.float32) + got[at].astype(jnp.float32)
        out[...] = total.astype(jnp.bfloat16)


def level_fold_kernel(sc, mine, got, near, far):
    level = sc[3]
    for out, at, k in ((near, 0, 0), (near, 1, 2), (far, 0, 1), (far, 1, 3)):
        total = mine[level ^ k].astype(jnp.float32) + got[level ^ k].astype(jnp.float32)
        out[at] = total.astype(jnp.bfloat16)


def block_sum(refs):
    total = refs[0][...].astype(jnp.float32)
    for ref in refs[1:]:
        total = total + ref[...].astype(jnp.float32)
    return total


def split_up_kernel(sc, e0, e1, keep, send, held):
    core = sc[2]
    shard_rows = ((keep.shape[0] - 16) * 2) // 3
    held[...] = block_sum((e0, e1)).astype(jnp.bfloat16)
    for ref, side in ((keep, core), (send, 1 - core)):
        ref[:shard_rows] = held[pl.ds(pl.multiple_of(side * shard_rows, 16), shard_rows), :]
        ref[shard_rows:] = held[2 * shard_rows :, :]


def join_kernel(sc, e0, e1, keep, got, out, vectors):
    core = sc[2]
    shard_rows = e0.shape[0]
    cols = keep.shape[1]
    out[:shard_rows] = block_sum((e0, e1)).astype(jnp.bfloat16)
    for ref, side in ((keep, core), (got, 1 - core)):
        out[shard_rows:, pl.ds(pl.multiple_of(side * cols, 128), cols)] = ref[:-16]
    vectors[...] = keep[-16:].astype(jnp.float32) + got[-16:].astype(jnp.float32)


def finish_kernel(sc, b0, b1, b2, b3, down, up, out):
    place, core = sc[1], sc[2]
    shard_rows = up.shape[0]
    quarter = shard_rows // 2
    cols = b0.shape[1] // 2
    for j, ref in enumerate((b0, b1, b2, b3)):
        where = place ^ j
        rows = pl.ds(pl.multiple_of(where * shard_rows, 8), shard_rows)
        down[rows, :] = ref[:shard_rows].astype(jnp.float32)
        for side in range(2):
            at = pl.multiple_of((side * 4 + where) * cols, 128)
            up[:, pl.ds(at, cols)] = ref[
                shard_rows : 2 * shard_rows, side * cols : (side + 1) * cols
            ].astype(jnp.float32)

        @pl.when(where // 2 == core)
        def _(ref=ref, where=where):
            at = pl.multiple_of((where % 2) * quarter, 8)
            out[pl.ds(at, quarter), :] = ref[2 * shard_rows :].astype(jnp.float32)


def sum_kernel(e0, e1, out):
    out[...] = block_sum((e0, e1)).astype(out.dtype)


def finish_qkv_kernel(sc, b0, b1, b2, b3, out, q_out, v_out, held):
    place, core, level = sc[1], sc[2], sc[3]
    shard_rows = out.shape[0]
    head_width = b0.shape[1] // 3
    for j, ref in enumerate((b0, b1, b2, b3)):
        held[place ^ j] = ref[...].astype(jnp.float32)
    for part in range(3):
        for s in range(4):
            at = (part * 4 + s) * head_width
            out[:, at : at + head_width] = held[
                s, :shard_rows, part * head_width : (part + 1) * head_width
            ]
    row = held[level, shard_rows : shard_rows + 1, :]
    for ref, at in ((q_out, 0), (v_out, 2 * head_width)):
        ref[...] = jnp.where(
            core == 0, row[:, at : at + shard_rows], row[:, at + shard_rows : at + 2 * shard_rows]
        )


def fast_body(
    tokens,
    lengths,
    w_qkv,
    q_bias,
    v_bias,
    w_out,
    out_bias,
    gain_one,
    shift_one,
    w_up,
    up_bias,
    w_down,
    down_bias,
    gain_two,
    shift_two,
    cotangent,
):
    bf16, f32 = jnp.bfloat16, jnp.float32
    _, rows, width = tokens.shape
    shard_rows = w_qkv.shape[0]
    hidden = w_up.shape[1]
    head_width = width // 4
    place = lax.axis_index("seq")
    core = lax.axis_index("core")
    zs = 4
    third = shard_rows // 3
    swap = [(0, 1), (1, 0)]

    def struct(shape, dtype=bf16):
        return jax.ShapeDtypeStruct(shape, dtype)

    def across(value, step):
        return lax.ppermute(value, "seq", [(i, i ^ step) for i in range(4)])

    def partner(value):
        return lax.ppermute(value, "core", swap)

    def level_across(value, step):
        return lax.ppermute(value, "z", [(i, i ^ step) for i in range(4)])

    token = tokens[0]
    quarter = jnp.concatenate(
        [
            lax.dynamic_slice_in_dim(w_up, place * width, width, axis=1),
            lax.dynamic_slice_in_dim(w_out, jnp.minimum(place, 2) * third, third, axis=0),
        ],
        axis=0,
    )
    gathered = lax.all_gather(quarter, ("z", "core", "seq"), axis=0, tiled=True)
    gathered = gathered.reshape(zs, 2, 4, shard_rows + third, width)
    columns = lax.dynamic_index_in_dim(
        w_qkv.reshape(shard_rows, 3, 4, head_width), place, axis=2, keepdims=False
    ).reshape(shard_rows, 3 * head_width)
    pair_rows = jnp.zeros((2, 2, shard_rows), bf16)
    placed_q = lax.dynamic_update_slice(pair_rows[0], q_bias[None], (core, 0)).reshape(1, -1)
    placed_v = lax.dynamic_update_slice(pair_rows[0], v_bias[None], (core, 0)).reshape(1, -1)
    bias_row = jnp.concatenate(
        [placed_q, jnp.zeros((1, head_width), bf16), placed_v], axis=1
    )
    vectors = jnp.concatenate(
        [out_bias, gain_one, shift_one, down_bias, gain_two, shift_two, up_bias]
    )
    pad = 15 * 3 * head_width - vectors.shape[0]
    vector_rows = jnp.pad(vectors, (0, pad)).reshape(15, 3 * head_width)
    own_block = jnp.concatenate([columns, bias_row, vector_rows], axis=0)
    t1, t2, t3 = across(token, 1), across(token, 2), across(token, 3)
    two_cols = jnp.stack([own_block, level_across(own_block, 1)])
    own_cols = jnp.concatenate([two_cols, level_across(two_cols, 2)])
    down_quarter = lax.dynamic_slice_in_dim(w_down, place * shard_rows, shard_rows, axis=0)
    two_down = jnp.stack([down_quarter, level_across(down_quarter, 1)])
    own_down = jnp.concatenate([two_down, level_across(two_down, 2)])
    own_down, own_cols, t1, t2, t3 = lax.optimization_barrier((own_down, own_cols, t1, t2, t3))
    other_cols = partner(own_cols)
    down_sets = [own_down] + [across(own_down, j) for j in (1, 2, 3)]
    sc = jnp.stack([lengths[0], place, core, lax.axis_index("z")]).astype(jnp.int32)
    all_rows = 4 * rows
    qkv, ctx_t, c0, c1, c2, c3, lse, full_qkv, vector_sets = pl.pallas_call(
        attend_forward_kernel,
        name="attend_forward",
        cost_estimate=work(13),
        out_shape=(
            struct((all_rows, 3 * head_width)),
            struct((head_width, all_rows), f32),
            struct((rows, head_width)),
            struct((rows, head_width)),
            struct((rows, head_width)),
            struct((rows, head_width)),
            struct((head_width // HEAD_DIM, all_rows), f32),
            struct((zs, 2, shard_rows, 3 * head_width)),
            struct((zs, 2, 2, 3 * head_width), f32),
        ),
        in_specs=[smem_spec()] + vmem_specs(6),
        out_specs=tuple(vmem_specs(9)),
        scratch_shapes=[pltpu.VMEM((4, rows, head_width), bf16)],
    )(sc, token, t1, t2, t3, own_cols, other_cols)
    x1, x2, x3 = across(c1, 1), across(c2, 2), across(c3, 3)
    down_sets[0], _ = lax.optimization_barrier((down_sets[0], c0))
    own_down = jnp.stack(down_sets)
    other_down = partner(own_down)
    all_vec = vector_sets.reshape(2 * zs, -1)
    six = all_vec[:, : 6 * shard_rows].reshape(2 * zs, 6, shard_rows)
    six = six.transpose(1, 0, 2).reshape(6, width)
    small = jnp.concatenate([six, jnp.zeros((2, width), f32)], axis=0)
    full_up_bias = all_vec[:, 6 * shard_rows : 6 * shard_rows + hidden // 8].reshape(1, hidden)
    packed = hidden // 2 + 5 * width + width // 2
    output, grad_one, y0, y1, y2, y3, keep, send, sums, up_sums = pl.pallas_call(
        middle_kernel,
        name="middle",
        cost_estimate=work(15),
        out_shape=(
            struct((rows, width)),
            struct((rows, width), f32),
            struct((rows, head_width)),
            struct((rows, head_width)),
            struct((rows, head_width)),
            struct((rows, head_width)),
            struct((rows, packed)),
            struct((rows, packed)),
            struct((8, width), f32),
            struct((1, hidden), f32),
        ),
        in_specs=[smem_spec()]
        + vmem_specs(8)
        + [pl.BlockSpec(memory_space=pl.ANY)] * 3,
        out_specs=tuple(vmem_specs(10)),
        scratch_shapes=[
            pltpu.VMEM((zs, 2, shard_rows, width), bf16),
            pltpu.VMEM((4, zs, 2, shard_rows, width), bf16),
            pltpu.VMEM((zs, 2, 4, shard_rows, width), bf16),
            pltpu.VMEM((rows, hidden), f32),
            pltpu.VMEM((rows, hidden), bf16),
            pltpu.VMEM((rows, hidden), bf16),
            pltpu.VMEM((4, rows, head_width), bf16),
            pltpu.SemaphoreType.DMA((7 + 32,)),
        ],
    )(
        sc,
        c0,
        x1,
        x2,
        x3,
        token,
        cotangent[0],
        small,
        full_up_bias,
        gathered,
        own_down,
        other_down,
    )
    g1, g2, g3 = across(y1, 1), across(y2, 2), across(y3, 3)
    got, g1, g2, g3 = lax.optimization_barrier((partner(send), g1, g2, g3))
    quad = hidden // 8

    def call(kernel, micros, outs, *args, scratch=(), scalars=True):
        return pl.pallas_call(
            kernel,
            name=kernel.__name__.replace("_kernel", ""),
            cost_estimate=work(micros),
            out_shape=tuple(outs),
            in_specs=([smem_spec()] if scalars else []) + vmem_specs(len(args)),
            out_specs=tuple(vmem_specs(len(outs))),
            scratch_shapes=list(scratch),
        )(*(((sc,) if scalars else ()) + args))

    d_near, d_far = call(
        down_grad_kernel,
        4,
        [struct((2, zs, shard_rows, width))] * 2,
        keep,
        got,
        scratch=[pltpu.VMEM((4, shard_rows, width), bf16)],
    )
    block_rows = 2 * shard_rows + shard_rows // 2 + 16
    six_sets = sums[:6].reshape(6, zs, 2 * shard_rows).transpose(1, 0, 2)
    up_sets = up_sums.reshape(zs, 4, 2 * shard_rows)
    vector_rows = jnp.concatenate([six_sets, up_sets], axis=1).reshape(zs, 5, quad)
    vector_rows = jnp.pad(vector_rows.astype(bf16), ((0, 0), (0, 11), (0, 0)))
    u_near, u_far = call(
        up_grad_kernel,
        4,
        [struct((2, zs, block_rows, quad))] * 2,
        keep,
        got,
        vector_rows,
        scratch=[pltpu.VMEM((zs, 4, shard_rows // 2, quad), bf16)],
    )
    d_got = across(d_far, 1)
    u_got = across(u_far, 2)
    y0, d_near, u_near = lax.optimization_barrier((y0, d_near, u_near))

    dqkv = pl.pallas_call(
        attend_backward_kernel,
        name="attend_backward",
        cost_estimate=work(11),
        out_shape=struct((all_rows, 3 * head_width)),
        in_specs=[smem_spec()] + vmem_specs(7),
        out_specs=pl.BlockSpec(memory_space=pltpu.VMEM),
        scratch_shapes=[
            pltpu.VMEM((head_width // HEAD_DIM, all_rows, HEAD_DIM), f32),
            pltpu.VMEM((head_width // HEAD_DIM, all_rows, HEAD_DIM), f32),
            pltpu.VMEM((4, rows, head_width), bf16),
        ],
    )(sc, qkv, ctx_t, lse, y0, g1, g2, g3)
    q_rows = shard_rows + 16
    q_keep, q_send = pl.pallas_call(
        grad_qkv_weight_kernel,
        name="grad_qkv_weight",
        cost_estimate=work(4),
        out_shape=(
            struct((zs, q_rows, 3 * head_width)),
            struct((zs, q_rows, 3 * head_width)),
        ),
        in_specs=[smem_spec()] + vmem_specs(5),
        out_specs=tuple(vmem_specs(2)),
    )(sc, token, t1, t2, t3, dqkv)
    d_near, u_near, q_keep = lax.optimization_barrier((d_near, u_near, q_keep))
    d_mine, d_pass = call(
        fold_kernel, 1, [struct((zs, shard_rows, width))] * 2, d_near, d_got, scalars=False
    )
    u_mine, u_pass = call(
        fold_kernel, 1, [struct((zs, block_rows, quad))] * 2, u_near, u_got, scalars=False
    )
    q_got = partner(q_send)
    late_dqkv, q_keep = lax.optimization_barrier((dqkv, q_keep))
    (token_parts,) = call(
        grad_tokens_kernel,
        4,
        [struct((4, rows, width))],
        late_dqkv,
        full_qkv,
    )
    q_near, q_far = call(
        level_fold_kernel, 1, [struct((2, q_rows, 3 * head_width))] * 2, q_keep, q_got
    )

    def level_sum(near, far, shape):
        mine, pass_on = call(
            fold_kernel, 1, [struct(shape)] * 2, near, level_across(far, 1), scalars=False
        )
        return mine, level_across(pass_on, 2)

    q_mine, q_last = level_sum(q_near, q_far, (q_rows, 3 * head_width))
    (q_part,) = call(
        sum_kernel, 1, [struct((q_rows, 3 * head_width))], q_mine, q_last, scalars=False
    )

    def seq_sum(mine, pass_on, shape, step):
        return call(
            level_fold_kernel,
            1,
            [struct((2,) + shape[1:])] * 2,
            mine,
            across(pass_on, step),
        )

    d_mine, u_mine, _ = lax.optimization_barrier((d_mine, u_mine, q_mine))
    d_near, d_far = seq_sum(d_mine, d_pass, (zs, shard_rows, width), 2)
    u_near, u_far = seq_sum(u_mine, u_pass, (zs, block_rows, quad), 1)
    token_parts, _, _ = lax.optimization_barrier((token_parts, u_near, d_near))
    token_sum = lax.psum_scatter(
        token_parts.reshape(4 * rows, width), "seq", scatter_dimension=0, tiled=True
    )
    d_parts = level_sum(d_near, d_far, (shard_rows, width))
    u_parts = level_sum(u_near, u_far, (block_rows, quad))
    half_rows = shard_rows + shard_rows // 2 + 16
    u_keep, u_send = call(
        split_up_kernel,
        1,
        [struct((half_rows, quad))] * 2,
        *u_parts,
        scratch=[pltpu.VMEM((block_rows, quad), bf16)],
    )
    joined, vector_totals = call(
        join_kernel,
        1,
        [struct((shard_rows + half_rows - 16, width)), struct((16, quad), f32)],
        *d_parts,
        u_keep,
        partner(u_send),
    )
    q_others = [across(q_part, j) for j in (1, 2, 3)]
    joined, q_others = lax.optimization_barrier((joined, q_others))
    six = lax.dynamic_index_in_dim(
        vector_totals[:3].reshape(6, 2, shard_rows), core, axis=1, keepdims=False
    )
    result_up_bias = lax.dynamic_index_in_dim(vector_totals[3:5], core, axis=0, keepdims=False)
    result_down, result_up, result_out = call(
        finish_kernel,
        2,
        [
            struct((4 * shard_rows, width), f32),
            struct((shard_rows, hidden), f32),
            struct((shard_rows, width), f32),
        ],
        joined,
        *[across(joined, j) for j in (1, 2, 3)],
    )
    result_qkv, result_q_bias, result_v_bias = call(
        finish_qkv_kernel,
        1,
        [struct((shard_rows, 3 * width), f32)] + [struct((1, shard_rows), f32)] * 2,
        q_part,
        *q_others,
        scratch=[pltpu.VMEM((4, q_rows, 3 * head_width), f32)],
    )
    grad_tokens = (grad_one + token_sum.astype(f32)).astype(bf16)

    return (
        output[None],
        grad_tokens[None],
        result_qkv,
        result_q_bias[0],
        result_v_bias[0],
        result_out,
        six[0],
        six[1],
        six[2],
        result_up,
        result_up_bias,
        result_down,
        six[5],
        six[3],
        six[4],
    )


def solution(mesh):
    seq_count, shard_count = mesh.shape["seq"], mesh.shape["shard"]
    fast = seq_count == 4 and shard_count == 8
    if fast:
        grid = mesh.devices.reshape(seq_count, shard_count // 2, 2)
        mesh = jax.sharding.Mesh(grid, AXES)
    shard = ("z", "core") if fast else "shard"
    vector, matrix, rows = P(shard), P(shard, None), P(shard, "seq", None)
    return jax.shard_map(
        fast_body if fast else body,
        mesh=mesh,
        in_specs=(
            rows,
            vector,
            matrix,
            vector,
            vector,
            matrix,
            vector,
            vector,
            vector,
            matrix,
            vector,
            matrix,
            vector,
            vector,
            vector,
            rows,
        ),
        out_specs=(
            rows,
            rows,
            matrix,
            vector,
            vector,
            matrix,
            vector,
            vector,
            vector,
            matrix,
            vector,
            matrix,
            vector,
            vector,
            vector,
        ),
        check_vma=False,
    )
```

```python
import jax
import jax.numpy as jnp
from jax import lax
from jax.experimental import pallas as pl
from jax.experimental.pallas import tpu as pltpu
from jax.sharding import PartitionSpec as P

HEAD_DIM = 64
LEN = 1024
Q_BLOCK = 512


epsilon = 1e-05
masked_score = -1000000000.0


def layer_norm(values, gain, shift):
    center = values - jnp.mean(values, axis=-1, keepdims=True)
    spread = jnp.mean(center * center, axis=-1, keepdims=True)
    return center * lax.rsqrt(spread + epsilon) * gain + shift


def gelu_exact(values):
    return jax.nn.gelu(values, approximate=False)


def contract_rows(left, right):
    return lax.dot_general(
        left, right, (((0,), (0,)), ((), ())), preferred_element_type=jnp.float32
    )


def contract_cols(left, right):
    return lax.dot_general(
        left, right, (((1,), (1,)), ((), ())), preferred_element_type=jnp.float32
    )


def block_scores(q_block, k_seq, key_valid):
    scores = jnp.einsum(
        "qhd,khd->hqk", q_block, k_seq, preferred_element_type=jnp.float32
    ) * HEAD_DIM ** (-0.5)
    return jnp.where(key_valid[None, None, :], scores, masked_score)


def attend_forward(q_seq, k_seq, v_seq, length):
    local_heads = q_seq.shape[1]
    key_valid = jnp.arange(LEN, dtype=jnp.int32) < length
    q_blocks = q_seq.reshape(LEN // Q_BLOCK, Q_BLOCK, local_heads, HEAD_DIM)

    def one_block(q_block):
        scores = block_scores(q_block, k_seq, key_valid)
        row_peak = jnp.max(scores, axis=-1, keepdims=True)
        shifted = jnp.exp(scores - row_peak)
        row_total = jnp.sum(shifted, axis=-1, keepdims=True)
        attn_probs = (shifted / row_total).astype(jnp.bfloat16)
        context = jnp.einsum("hqk,khd->qhd", attn_probs, v_seq, preferred_element_type=jnp.float32)
        return (context.astype(jnp.bfloat16), (row_peak + jnp.log(row_total))[..., 0])

    context, log_total = lax.map(one_block, q_blocks)
    return (context.reshape(LEN, local_heads, HEAD_DIM), log_total)


def attend_backward(q_seq, k_seq, v_seq, grad_seq, log_total, length):
    local_heads = q_seq.shape[1]
    score_scale = HEAD_DIM ** (-0.5)
    key_valid = jnp.arange(LEN, dtype=jnp.int32) < length
    q_blocks = q_seq.reshape(LEN // Q_BLOCK, Q_BLOCK, local_heads, HEAD_DIM)
    g_blocks = grad_seq.reshape(LEN // Q_BLOCK, Q_BLOCK, local_heads, HEAD_DIM)

    def one_block(accum, block_item):
        q_block, g_block, lse_block = block_item
        scores = block_scores(q_block, k_seq, key_valid)
        attn_probs = jnp.exp(scores - lse_block[..., None])
        grad_probs = jnp.einsum("qhd,khd->hqk", g_block, v_seq, preferred_element_type=jnp.float32)
        row_dot = jnp.sum(attn_probs * grad_probs, axis=-1, keepdims=True)
        grad_scores = (attn_probs * (grad_probs - row_dot)).astype(jnp.bfloat16)
        grad_q = (
            jnp.einsum("hqk,khd->qhd", grad_scores, k_seq, preferred_element_type=jnp.float32)
            * score_scale
        )
        grad_k = (
            accum[0]
            + jnp.einsum("hqk,qhd->khd", grad_scores, q_block, preferred_element_type=jnp.float32)
            * score_scale
        )
        grad_v = accum[1] + jnp.einsum(
            "hqk,qhd->khd",
            attn_probs.astype(jnp.bfloat16),
            g_block,
            preferred_element_type=jnp.float32,
        )
        return ((grad_k, grad_v), grad_q.astype(jnp.bfloat16))

    zero_keys = jnp.zeros((LEN, local_heads, HEAD_DIM), jnp.float32)
    (grad_k, grad_v), grad_q = lax.scan(
        one_block, (zero_keys, zero_keys), (q_blocks, g_blocks, log_total)
    )
    return (
        grad_q.reshape(LEN, local_heads, HEAD_DIM),
        grad_k.astype(jnp.bfloat16),
        grad_v.astype(jnp.bfloat16),
    )


def body(
    tokens,
    lengths,
    w_qkv,
    q_bias,
    v_bias,
    w_out,
    out_bias,
    gain_one,
    shift_one,
    w_up,
    up_bias,
    w_down,
    down_bias,
    gain_two,
    shift_two,
    cotangent,
):
    seq_count, local_len, model_width = tokens.shape
    row_count = seq_count * local_len
    head_count = model_width // HEAD_DIM
    gathered = (
        lax.all_gather(w_qkv, "shard", axis=0, tiled=True),
        lax.all_gather(q_bias, "shard", axis=0, tiled=True),
        lax.all_gather(v_bias, "shard", axis=0, tiled=True),
        lax.all_gather(w_out, "shard", axis=0, tiled=True),
        lax.all_gather(out_bias, "shard", axis=0, tiled=True),
        lax.all_gather(gain_one, "shard", axis=0, tiled=True),
        lax.all_gather(shift_one, "shard", axis=0, tiled=True),
        lax.all_gather(w_up, "shard", axis=0, tiled=True),
        lax.all_gather(up_bias, "shard", axis=0, tiled=True),
        lax.all_gather(w_down, "shard", axis=0, tiled=True),
        lax.all_gather(down_bias, "shard", axis=0, tiled=True),
        lax.all_gather(gain_two, "shard", axis=0, tiled=True),
        lax.all_gather(shift_two, "shard", axis=0, tiled=True),
    )
    (
        full_qkv,
        full_q_bias,
        full_v_bias,
        full_out,
        full_out_bias,
        full_gain_one,
        full_shift_one,
        full_up,
        full_up_bias,
        full_down,
        full_down_bias,
        full_gain_two,
        full_shift_two,
    ) = gathered
    token_rows = tokens.reshape(row_count, model_width)
    joined_bias = jnp.concatenate([full_q_bias, jnp.zeros_like(full_q_bias), full_v_bias]).astype(
        jnp.float32
    )
    qkv_rows = (
        jnp.dot(token_rows, full_qkv, preferred_element_type=jnp.float32) + joined_bias
    ).astype(jnp.bfloat16)
    qkv_tokens = qkv_rows.reshape(seq_count, local_len, 3, head_count, HEAD_DIM)
    qkv_heads = lax.all_to_all(qkv_tokens, "seq", split_axis=3, concat_axis=1, tiled=True)

    def forward_seq(seq_item):
        qkv_seq, length = seq_item
        return attend_forward(qkv_seq[:, 0], qkv_seq[:, 1], qkv_seq[:, 2], length)

    context_heads, log_total = lax.map(forward_seq, (qkv_heads, lengths))
    context_tokens = lax.all_to_all(context_heads, "seq", split_axis=1, concat_axis=2, tiled=True)
    context_rows = context_tokens.reshape(row_count, model_width)
    residual_one = (
        token_rows.astype(jnp.float32)
        + jnp.dot(context_rows, full_out, preferred_element_type=jnp.float32)
        + full_out_bias.astype(jnp.float32)
    )
    normed_one, norm_one_pull = jax.vjp(
        layer_norm,
        residual_one,
        full_gain_one.astype(jnp.float32),
        full_shift_one.astype(jnp.float32),
    )
    normed_low = normed_one.astype(jnp.bfloat16)
    up_rows = jnp.dot(
        normed_low, full_up, preferred_element_type=jnp.float32
    ) + full_up_bias.astype(jnp.float32)
    active, gelu_pull = jax.vjp(gelu_exact, up_rows)
    active_low = active.astype(jnp.bfloat16)
    residual_two = (
        normed_one
        + jnp.dot(active_low, full_down, preferred_element_type=jnp.float32)
        + full_down_bias.astype(jnp.float32)
    )
    final_rows, norm_two_pull = jax.vjp(
        layer_norm,
        residual_two,
        full_gain_two.astype(jnp.float32),
        full_shift_two.astype(jnp.float32),
    )
    output = final_rows.astype(jnp.bfloat16).reshape(tokens.shape)
    back_qkv, back_out, back_up, back_down = (full_qkv, full_out, full_up, full_down)
    grad_rows = cotangent.reshape(row_count, model_width).astype(jnp.float32)
    grad_two, grad_gain_two, grad_shift_two = norm_two_pull(grad_rows)
    grad_down_bias = jnp.sum(grad_two, axis=0)
    grad_two_low = grad_two.astype(jnp.bfloat16)
    grad_w_down = contract_rows(active_low, grad_two_low)
    grad_active = contract_cols(grad_two_low, back_down)
    (grad_up,) = gelu_pull(grad_active)
    grad_up_bias = jnp.sum(grad_up, axis=0)
    grad_up_low = grad_up.astype(jnp.bfloat16)
    grad_w_up = contract_rows(normed_low, grad_up_low)
    grad_normed = grad_two + contract_cols(grad_up_low, back_up)
    grad_one, grad_gain_one, grad_shift_one = norm_one_pull(grad_normed)
    grad_out_bias = jnp.sum(grad_one, axis=0)
    grad_one_low = grad_one.astype(jnp.bfloat16)
    grad_w_out = contract_rows(context_rows, grad_one_low)
    grad_context = contract_cols(grad_one_low, back_out).astype(jnp.bfloat16)
    grad_context = grad_context.reshape(seq_count, local_len, head_count, HEAD_DIM)
    grad_context_heads = lax.all_to_all(
        grad_context, "seq", split_axis=2, concat_axis=1, tiled=True
    )

    def backward_seq(seq_item):
        qkv_seq, grad_seq, lse_seq, length = seq_item
        grad_q, grad_k, grad_v = attend_backward(
            qkv_seq[:, 0], qkv_seq[:, 1], qkv_seq[:, 2], grad_seq, lse_seq, length
        )
        return jnp.stack([grad_q, grad_k, grad_v], axis=1)

    grad_qkv_heads = lax.map(backward_seq, (qkv_heads, grad_context_heads, log_total, lengths))
    grad_qkv_tokens = lax.all_to_all(grad_qkv_heads, "seq", split_axis=1, concat_axis=3, tiled=True)
    grad_qkv_rows = grad_qkv_tokens.reshape(row_count, 3 * model_width)
    grad_q_bias = jnp.sum(grad_qkv_rows[:, :model_width], axis=0, dtype=jnp.float32)
    grad_v_bias = jnp.sum(grad_qkv_rows[:, 2 * model_width :], axis=0, dtype=jnp.float32)
    grad_w_qkv = contract_rows(token_rows, grad_qkv_rows)
    grad_tokens = grad_one + contract_cols(grad_qkv_rows, back_qkv)
    grad_tokens = grad_tokens.astype(jnp.bfloat16).reshape(tokens.shape)
    owned = (
        lax.psum_scatter(grad_w_qkv, "shard", scatter_dimension=0, tiled=True),
        lax.psum_scatter(grad_q_bias, "shard", scatter_dimension=0, tiled=True),
        lax.psum_scatter(grad_v_bias, "shard", scatter_dimension=0, tiled=True),
        lax.psum_scatter(grad_w_out, "shard", scatter_dimension=0, tiled=True),
        lax.psum_scatter(grad_out_bias, "shard", scatter_dimension=0, tiled=True),
        lax.psum_scatter(grad_gain_one, "shard", scatter_dimension=0, tiled=True),
        lax.psum_scatter(grad_shift_one, "shard", scatter_dimension=0, tiled=True),
        lax.psum_scatter(grad_w_up, "shard", scatter_dimension=0, tiled=True),
        lax.psum_scatter(grad_up_bias, "shard", scatter_dimension=0, tiled=True),
        lax.psum_scatter(grad_w_down, "shard", scatter_dimension=0, tiled=True),
        lax.psum_scatter(grad_down_bias, "shard", scatter_dimension=0, tiled=True),
        lax.psum_scatter(grad_gain_two, "shard", scatter_dimension=0, tiled=True),
        lax.psum_scatter(grad_shift_two, "shard", scatter_dimension=0, tiled=True),
    )
    owned_columns = (
        lax.psum_scatter(
            owned[0].astype(jnp.bfloat16), "seq", scatter_dimension=1, tiled=True
        ).astype(jnp.float32),
        lax.psum_scatter(
            owned[3].astype(jnp.bfloat16), "seq", scatter_dimension=1, tiled=True
        ).astype(jnp.float32),
        lax.psum_scatter(
            owned[7].astype(jnp.bfloat16), "seq", scatter_dimension=1, tiled=True
        ).astype(jnp.float32),
        lax.psum_scatter(
            owned[9].astype(jnp.bfloat16), "seq", scatter_dimension=1, tiled=True
        ).astype(jnp.float32),
    )
    matrices = (
        lax.all_gather(owned_columns[0].astype(jnp.bfloat16), "seq", axis=1, tiled=True).astype(
            jnp.float32
        ),
        lax.all_gather(owned_columns[1].astype(jnp.bfloat16), "seq", axis=1, tiled=True).astype(
            jnp.float32
        ),
        lax.all_gather(owned_columns[2].astype(jnp.bfloat16), "seq", axis=1, tiled=True).astype(
            jnp.float32
        ),
        lax.all_gather(owned_columns[3].astype(jnp.bfloat16), "seq", axis=1, tiled=True).astype(
            jnp.float32
        ),
    )
    vectors = lax.psum(
        (
            owned[1],
            owned[2],
            owned[4],
            owned[5],
            owned[6],
            owned[8],
            owned[10],
            owned[11],
            owned[12],
        ),
        "seq",
    )
    result_qkv, result_out, result_up, result_down = (
        matrices[0],
        matrices[1],
        matrices[2],
        matrices[3],
    )
    result_q_bias, result_v_bias, result_out_bias = (vectors[0], vectors[1], vectors[2])
    result_gain_one, result_shift_one, result_up_bias = (vectors[3], vectors[4], vectors[5])
    result_down_bias, result_gain_two, result_shift_two = (vectors[6], vectors[7], vectors[8])
    return (
        output,
        grad_tokens,
        result_qkv,
        result_q_bias,
        result_v_bias,
        result_out,
        result_out_bias,
        result_gain_one,
        result_shift_one,
        result_up,
        result_up_bias,
        result_down,
        result_down_bias,
        result_gain_two,
        result_shift_two,
    )


AXES = ("seq", "z", "core")
NORMAL_SCALE = 0.3989422804014327
HALF_ROOT = 0.7071067811865476


def dot_nn(left, right):
    return lax.dot_general(
        left, right, (((1,), (0,)), ((), ())), preferred_element_type=jnp.float32
    )


def dot_nt(left, right):
    return contract_cols(left, right)


def dot_tn(left, right):
    return contract_rows(left, right)


def vmem_specs(count):
    return [pl.BlockSpec(memory_space=pltpu.VMEM)] * count


def work(micros):
    return pl.CostEstimate(
        flops=int(micros * 9e7), transcendentals=0, bytes_accessed=int(micros * 3e5)
    )


def smem_spec():
    return pl.BlockSpec(memory_space=pltpu.SMEM)


def key_bias(sc, block_rows):
    length, place = sc[0], sc[1]
    columns = []
    for j in range(4):
        position = (place ^ j) * block_rows + lax.broadcasted_iota(
            jnp.int32, (block_rows, 1), 0
        )
        columns.append(jnp.where(position < length, 0.0, masked_score))
    return jnp.concatenate(columns, axis=0)


def attend_forward_kernel(
    sc, t0, t1, t2, t3, own, other, qkv, ctx_t, c0, c1, c2, c3, lse, weight, vectors, held
):
    place, core, level = sc[1], sc[2], sc[3]
    rows = t0.shape[0]
    shard_rows = weight.shape[2]
    width = weight.shape[3]
    head_width = width // 3
    heads = head_width // HEAD_DIM
    for k in range(4):
        for block, side in ((own, core), (other, 1 - core)):
            weight[level ^ k, side] = block[k, :shard_rows, :]
            vectors[level ^ k, side] = block[k, shard_rows + 1 : shard_rows + 3, :].astype(
                jnp.float32
            )
    full = weight[...].reshape(-1, width)
    bias = (
        own[level ^ place, shard_rows : shard_rows + 1, :].astype(jnp.float32)
        + other[level ^ place, shard_rows : shard_rows + 1, :].astype(jnp.float32)
    )
    for j, block in enumerate((t0, t1, t2, t3)):
        qkv[j * rows : (j + 1) * rows, :] = (dot_nn(block[...], full) + bias).astype(jnp.bfloat16)
    mask = key_bias(sc, rows)
    def one_block(j, carry):
        span = pl.ds(pl.multiple_of(j * rows, 128), rows)
        parts = []
        q_all = qkv[span, 0:head_width] * jnp.bfloat16(HEAD_DIM**-0.5)
        for h in range(heads):
            low = h * HEAD_DIM
            q = q_all[:, low : low + HEAD_DIM]
            k = qkv[:, head_width + low : head_width + low + HEAD_DIM]
            v = qkv[:, 2 * head_width + low : 2 * head_width + low + HEAD_DIM]
            scores = dot_nt(k, q) + mask
            peak = jnp.max(scores, axis=0, keepdims=True)
            shifted = jnp.exp(scores - peak)
            total = jnp.sum(shifted, axis=0, keepdims=True)
            part = dot_tn(v, shifted.astype(jnp.bfloat16)) / total
            parts.append(part)
            lse[h : h + 1, span] = peak + jnp.log(total)
        joined = jnp.concatenate(parts, axis=0)
        ctx_t[:, span] = joined
        held[j] = joined.T.astype(jnp.bfloat16)
        return carry

    lax.fori_loop(0, 4, one_block, 0)
    for j, out in enumerate((c0, c1, c2, c3)):
        out[...] = held[j]


def attend_backward_kernel(sc, qkv, ctx_t, lse, g0, g1, g2, g3, dqkv, dk_acc, dv_acc, held):
    rows = g0.shape[0]
    head_width = g0.shape[1]
    heads = head_width // HEAD_DIM
    mask = key_bias(sc, rows)
    scale = jnp.bfloat16(HEAD_DIM**-0.5)
    for j, g_ref in enumerate((g0, g1, g2, g3)):
        held[j] = g_ref[...]
    dk_acc[...] = jnp.zeros_like(dk_acc)
    dv_acc[...] = jnp.zeros_like(dv_acc)

    def one_block(j, carry):
        span = pl.ds(pl.multiple_of(j * rows, 128), rows)
        g_all = held[j]
        product = g_all.astype(jnp.float32).T * ctx_t[:, span]
        q_all = qkv[span, 0:head_width] * scale
        parts = []
        for h in range(heads):
            low = h * HEAD_DIM
            q = q_all[:, low : low + HEAD_DIM]
            g = g_all[:, low : low + HEAD_DIM]
            k = qkv[:, head_width + low : head_width + low + HEAD_DIM]
            v = qkv[:, 2 * head_width + low : 2 * head_width + low + HEAD_DIM]
            probs = jnp.exp(dot_nt(k, q) + mask - lse[h : h + 1, span])
            row_dot = jnp.sum(product[low : low + HEAD_DIM, :], axis=0, keepdims=True)
            grad_scores = (probs * (dot_nt(v, g) - row_dot)).astype(jnp.bfloat16)
            grad_v = dot_nn(probs.astype(jnp.bfloat16), g)
            grad_k = dot_nn(grad_scores, q)
            dv_acc[h] += grad_v
            dk_acc[h] += grad_k
            parts.append(dot_tn(k, grad_scores) * (HEAD_DIM**-0.5))
        dqkv[span, 0:head_width] = jnp.concatenate(parts, axis=0).T.astype(jnp.bfloat16)
        return carry

    lax.fori_loop(0, 4, one_block, 0)
    dk = jnp.concatenate([dk_acc[h] for h in range(heads)], axis=1)
    dv = jnp.concatenate([dv_acc[h] for h in range(heads)], axis=1)
    dqkv[:, head_width:] = jnp.concatenate([dk, dv], axis=1).astype(jnp.bfloat16)


def grad_qkv_weight_kernel(sc, t0, t1, t2, t3, dqkv, keep, send):
    core = sc[2]
    rows = t0.shape[0]
    total = None
    for j, block in enumerate((t0, t1, t2, t3)):
        part = dot_tn(block[...], dqkv[j * rows : (j + 1) * rows, :])
        total = part if total is None else total + part
    sums = jnp.sum(dqkv[...].astype(jnp.float32), axis=0, keepdims=True)
    sums = jnp.broadcast_to(sums, (16, sums.shape[1])).astype(jnp.bfloat16)
    shard_rows = keep.shape[1] - 16
    low = total.astype(jnp.bfloat16)
    for z in range(keep.shape[0]):
        even = low[(2 * z) * shard_rows : (2 * z + 1) * shard_rows]
        odd = low[(2 * z + 1) * shard_rows : (2 * z + 2) * shard_rows]
        keep[z, :shard_rows] = jnp.where(core == 0, even, odd)
        send[z, :shard_rows] = jnp.where(core == 0, odd, even)
        keep[z, shard_rows:] = sums
        send[z, shard_rows:] = sums


def grad_tokens_kernel(sc, dqkv, weight, out):
    place = sc[1]
    rows = out.shape[1]
    full = weight[...].reshape(-1, weight.shape[3])
    for j in range(4):
        part = dot_nt(dqkv[j * rows : (j + 1) * rows, :], full)
        out[place ^ j] = part.astype(out.dtype)


def normalize(values):
    center = values - jnp.mean(values, axis=-1, keepdims=True)
    inverse = lax.rsqrt(jnp.mean(center * center, axis=-1, keepdims=True) + epsilon)
    return center * inverse, inverse


def normalize_back(grad, unit, inverse):
    return inverse * (
        grad
        - jnp.mean(grad, axis=-1, keepdims=True)
        - unit * jnp.mean(grad * unit, axis=-1, keepdims=True)
    )


def middle_kernel(
    sc,
    x0,
    x1,
    x2,
    x3,
    token,
    cotangent,
    small,
    up_bias,
    gathered,
    own_down,
    other_down,
    output,
    grad_one,
    y0,
    y1,
    y2,
    y3,
    keep,
    send,
    vectors,
    w_out,
    w_up,
    w_down,
    slope,
    active,
    grad_up,
    context,
    sems,
):
    place, core, level = sc[1], sc[2], sc[3]
    blocks = w_up.shape[0]
    shard_rows = w_up.shape[3]
    width = w_up.shape[4]
    third = shard_rows // 3
    copies = []
    for b in range(blocks):
        copies.append(
            pltpu.make_async_copy(gathered.at[:, :, b, 0:shard_rows, :], w_up.at[b], sems.at[b])
        )
    down_copies = []
    for j in range(4):
        for k in range(4):
            for side, block in ((core, own_down), (1 - core, other_down)):
                down_copies.append(
                    pltpu.make_async_copy(
                        block.at[j, k],
                        w_down.at[level ^ k, side, place ^ j],
                        sems.at[7 + len(down_copies)],
                    )
                )
    out_copies = [
        pltpu.make_async_copy(
            gathered.at[:, :, b, shard_rows : shard_rows + third, :],
            w_out.at[:, :, b * third : (b + 1) * third, :],
            sems.at[blocks + b],
        )
        for b in range(3)
    ]
    for copy in out_copies + copies + down_copies:
        copy.start()
    for copy in out_copies:
        copy.wait()
    out_rows = 2 * shard_rows

    def out_block(j):
        return w_out[place ^ j].reshape(out_rows, width)

    residual = token[...].astype(jnp.float32) + small[0:1, :]
    for j, block in enumerate((x0, x1, x2, x3)):
        residual = residual + dot_nn(block[...], out_block(j))
    unit_one, inverse_one = normalize(residual)
    gain_one = small[1:2, :]
    normed = unit_one * gain_one + small[2:3, :]
    normed_low = normed.astype(jnp.bfloat16)
    for b in range(blocks):
        copies[b].wait()
        span = slice(b * width, (b + 1) * width)
        up = dot_nn(normed_low, w_up[b].reshape(width, width)) + up_bias[:, span]
        phi = 0.5 + 0.5 * lax.erf(up * HALF_ROOT)
        slope[:, span] = phi + up * (jnp.exp(-0.5 * up * up) * NORMAL_SCALE)
        active[:, span] = (up * phi).astype(jnp.bfloat16)
    for copy in down_copies:
        copy.wait()
    residual = normed + small[3:4, :] + dot_nn(active[...], w_down[...].reshape(-1, width))
    unit_two, inverse_two = normalize(residual)
    gain_two = small[4:5, :]
    output[...] = (unit_two * gain_two + small[5:6, :]).astype(jnp.bfloat16)
    grad = cotangent[...].astype(jnp.float32)
    sum_rows = {
        3: jnp.sum(grad * unit_two, axis=0, keepdims=True),
        4: jnp.sum(grad, axis=0, keepdims=True),
    }
    grad_two = normalize_back(grad * gain_two, unit_two, inverse_two)
    sum_rows[5] = jnp.sum(grad_two, axis=0, keepdims=True)
    vectors[...] = jnp.zeros_like(vectors)
    half = width // 2
    two_low = grad_two.astype(jnp.bfloat16)
    grad_normed = grad_two
    for b in range(blocks):
        span = slice(b * width, (b + 1) * width)
        rows_down = w_down[b].reshape(width, width)
        part = dot_nt(two_low, rows_down) * slope[:, span]
        up_row = jnp.sum(part, axis=0, keepdims=True).astype(jnp.bfloat16)
        vectors[b, 3:4, :] = up_row[:, :half]
        vectors[b, 4:5, :] = up_row[:, half:]
        part = part.astype(jnp.bfloat16)
        grad_up[:, span] = part
        grad_normed = grad_normed + dot_nt(part, w_up[b].reshape(width, width))
    sum_rows[1] = jnp.sum(grad_normed * unit_one, axis=0, keepdims=True)
    sum_rows[2] = jnp.sum(grad_normed, axis=0, keepdims=True)
    first = normalize_back(grad_normed * gain_one, unit_one, inverse_one)
    sum_rows[0] = jnp.sum(first, axis=0, keepdims=True)
    for z in range(4):
        at = slice(z * out_rows, (z + 1) * out_rows)
        for row in range(3):
            pair = [sum_rows[2 * row][:, at], sum_rows[2 * row + 1][:, at]]
            vectors[z, row : row + 1, :] = jnp.concatenate(pair, axis=1).astype(jnp.bfloat16)
    grad_one[...] = first
    one_low = first.astype(jnp.bfloat16)
    for j, out in enumerate((y0, y1, y2, y3)):
        out[...] = dot_nt(one_low, out_block(j)).astype(jnp.bfloat16)
    for j, block in enumerate((x0, x1, x2, x3)):
        context[place ^ j] = block[...]
    joined = jnp.concatenate([context[j] for j in range(4)], axis=1)
    down_rows = blocks * shard_rows
    for ref, mine in ((keep, core), (send, 1 - core)):
        for z in range(4):
            even = active[:, (2 * z) * down_rows : (2 * z + 1) * down_rows]
            odd = active[:, (2 * z + 1) * down_rows : (2 * z + 2) * down_rows]
            ref[:, z * down_rows : (z + 1) * down_rows] = jnp.where(mine == 0, even, odd)
        at = 4 * down_rows
        ref[:, at : at + width] = two_low
        at += width
        ref[:, at : at + width] = normed_low
        at += width
        ref[:, at : at + 2 * width] = jnp.where(
            mine == 0, grad_up[:, : 2 * width], grad_up[:, 2 * width :]
        )
        at += 2 * width
        ref[:, at : at + width] = joined
        at += width
        ref[:, at : at + half] = jnp.where(mine == 0, one_low[:, :half], one_low[:, half:])


def down_grad_kernel(sc, keep, got, near, far, part):
    place = sc[1]
    _, zs, shard_rows, width = near.shape
    down_rows = 4 * shard_rows
    at_two = zs * down_rows
    def both(where):
        return jnp.concatenate([keep[:, where], got[:, where]], axis=0)

    right = both(slice(at_two, at_two + width))
    for z in range(zs):
        total = dot_tn(both(slice(z * down_rows, (z + 1) * down_rows)), right)
        part[...] = total.astype(jnp.bfloat16).reshape(4, shard_rows, width)
        for out, at, j in ((near, 0, 0), (near, 1, 2), (far, 0, 1), (far, 1, 3)):
            out[at, z] = part[place ^ j]


def up_grad_kernel(sc, keep, got, vectors, near, far, part):
    place = sc[1]
    _, zs, block_rows, cols = near.shape
    quarter = part.shape[2]
    pair_rows = block_rows - quarter - 16
    width = zs * pair_rows
    at_norm = 2 * width + width
    at_up = at_norm + width
    at_ctx = at_up + 2 * width
    at_one = at_ctx + width
    def both(where):
        return jnp.concatenate([keep[:, where], got[:, where]], axis=0)

    total = dot_tn(both(slice(at_ctx, at_ctx + width)), both(slice(at_one, at_one + cols)))
    part[...] = total.astype(jnp.bfloat16).reshape(part.shape)
    left = both(slice(at_norm, at_norm + width)).T
    for out, at, j in ((near, 0, 0), (near, 1, 1), (far, 0, 2), (far, 1, 3)):
        right = pl.ds(pl.multiple_of(at_up + (place ^ j) * cols, 128), cols)
        total = dot_nn(left, both(right)).astype(jnp.bfloat16)
        for z in range(zs):
            out[at, z, :pair_rows] = total[z * pair_rows : (z + 1) * pair_rows]
            out[at, z, pair_rows : pair_rows + quarter] = part[z, place ^ j]
            out[at, z, pair_rows + quarter :] = vectors[z]


def fold_kernel(near, got, mine, pass_on):
    for at, out in ((0, mine), (1, pass_on)):
        total = near[at].astype(jnp.float32) + got[at].astype(jnp.float32)
        out[...] = total.astype(jnp.bfloat16)


def level_fold_kernel(sc, mine, got, near, far):
    level = sc[3]
    for out, at, k in ((near, 0, 0), (near, 1, 2), (far, 0, 1), (far, 1, 3)):
        total = mine[level ^ k].astype(jnp.float32) + got[level ^ k].astype(jnp.float32)
        out[at] = total.astype(jnp.bfloat16)


def level_merge_kernel(sc, d_mine, d_got, u_mine, u_got, near, far):
    level = sc[3]
    up_rows, cols = u_mine.shape[1:]
    rows = d_mine.shape[1]
    for out, at, k in ((near, 0, 0), (near, 1, 2), (far, 0, 1), (far, 1, 3)):
        total = u_mine[level ^ k].astype(jnp.float32) + u_got[level ^ k].astype(jnp.float32)
        out[at, :up_rows] = total.astype(jnp.bfloat16)
        total = d_mine[level ^ k].astype(jnp.float32) + d_got[level ^ k].astype(jnp.float32)
        total = total.astype(jnp.bfloat16)
        out[at, up_rows : up_rows + rows] = total[:, :cols]
        out[at, up_rows + rows :] = total[:, cols:]


def block_sum(refs):
    total = refs[0][...].astype(jnp.float32)
    for ref in refs[1:]:
        total = total + ref[...].astype(jnp.float32)
    return total


def split_up_kernel(sc, e0, e1, keep, send, down, held):
    core = sc[2]
    shard_rows, width = down.shape
    cols = width // 2
    half_rows = keep.shape[0] - shard_rows
    held[...] = block_sum((e0, e1)).astype(jnp.bfloat16)
    for ref, side in ((keep, core), (send, 1 - core)):
        ref[:shard_rows] = held[pl.ds(pl.multiple_of(side * shard_rows, 16), shard_rows), :]
        ref[shard_rows:] = held[2 * shard_rows : 2 * shard_rows + half_rows, :]
    at = 2 * shard_rows + half_rows
    down[:, :cols] = held[at : at + shard_rows, :]
    down[:, cols:] = held[at + shard_rows :, :]


def join_kernel(sc, down, keep, got, out, vectors):
    core = sc[2]
    shard_rows = down.shape[0]
    cols = keep.shape[1]
    out[:shard_rows] = down[...]
    for ref, side in ((keep, core), (got, 1 - core)):
        out[shard_rows:, pl.ds(pl.multiple_of(side * cols, 128), cols)] = ref[:-16]
    vectors[...] = keep[-16:].astype(jnp.float32) + got[-16:].astype(jnp.float32)


def finish_kernel(sc, b0, b1, b2, b3, down, up, out):
    place, core = sc[1], sc[2]
    shard_rows = up.shape[0]
    quarter = shard_rows // 2
    cols = b0.shape[1] // 2
    for j, ref in enumerate((b0, b1, b2, b3)):
        where = place ^ j
        rows = pl.ds(pl.multiple_of(where * shard_rows, 8), shard_rows)
        down[rows, :] = ref[:shard_rows].astype(jnp.float32)
        for side in range(2):
            at = pl.multiple_of((side * 4 + where) * cols, 128)
            up[:, pl.ds(at, cols)] = ref[
                shard_rows : 2 * shard_rows, side * cols : (side + 1) * cols
            ].astype(jnp.float32)

        @pl.when(where // 2 == core)
        def _(ref=ref, where=where):
            at = pl.multiple_of((where % 2) * quarter, 8)
            out[pl.ds(at, quarter), :] = ref[2 * shard_rows :].astype(jnp.float32)


def sum_kernel(e0, e1, out):
    out[...] = block_sum((e0, e1)).astype(out.dtype)


def finish_qkv_kernel(sc, b0, b1, b2, b3, out, q_out, v_out, held):
    place, core, level = sc[1], sc[2], sc[3]
    shard_rows = out.shape[0]
    head_width = b0.shape[1] // 3
    for j, ref in enumerate((b0, b1, b2, b3)):
        held[place ^ j] = ref[...].astype(jnp.float32)
    for part in range(3):
        for s in range(4):
            at = (part * 4 + s) * head_width
            out[:, at : at + head_width] = held[
                s, :shard_rows, part * head_width : (part + 1) * head_width
            ]
    row = held[level, shard_rows : shard_rows + 1, :]
    for ref, at in ((q_out, 0), (v_out, 2 * head_width)):
        ref[...] = jnp.where(
            core == 0, row[:, at : at + shard_rows], row[:, at + shard_rows : at + 2 * shard_rows]
        )


def fast_body(
    tokens,
    lengths,
    w_qkv,
    q_bias,
    v_bias,
    w_out,
    out_bias,
    gain_one,
    shift_one,
    w_up,
    up_bias,
    w_down,
    down_bias,
    gain_two,
    shift_two,
    cotangent,
):
    bf16, f32 = jnp.bfloat16, jnp.float32
    _, rows, width = tokens.shape
    shard_rows = w_qkv.shape[0]
    hidden = w_up.shape[1]
    head_width = width // 4
    place = lax.axis_index("seq")
    core = lax.axis_index("core")
    zs = 4
    third = shard_rows // 3
    swap = [(0, 1), (1, 0)]

    def struct(shape, dtype=bf16):
        return jax.ShapeDtypeStruct(shape, dtype)

    def across(value, step):
        return lax.ppermute(value, "seq", [(i, i ^ step) for i in range(4)])

    def partner(value):
        return lax.ppermute(value, "core", swap)

    def level_across(value, step):
        return lax.ppermute(value, "z", [(i, i ^ step) for i in range(4)])

    token = tokens[0]
    quarter = jnp.concatenate(
        [
            lax.dynamic_slice_in_dim(w_up, place * width, width, axis=1),
            lax.dynamic_slice_in_dim(w_out, jnp.minimum(place, 2) * third, third, axis=0),
        ],
        axis=0,
    )
    gathered = lax.all_gather(quarter, ("z", "core", "seq"), axis=0, tiled=True)
    gathered = gathered.reshape(zs, 2, 4, shard_rows + third, width)
    columns = lax.dynamic_index_in_dim(
        w_qkv.reshape(shard_rows, 3, 4, head_width), place, axis=2, keepdims=False
    ).reshape(shard_rows, 3 * head_width)
    pair_rows = jnp.zeros((2, 2, shard_rows), bf16)
    placed_q = lax.dynamic_update_slice(pair_rows[0], q_bias[None], (core, 0)).reshape(1, -1)
    placed_v = lax.dynamic_update_slice(pair_rows[0], v_bias[None], (core, 0)).reshape(1, -1)
    bias_row = jnp.concatenate(
        [placed_q, jnp.zeros((1, head_width), bf16), placed_v], axis=1
    )
    vectors = jnp.concatenate(
        [out_bias, gain_one, shift_one, down_bias, gain_two, shift_two, up_bias]
    )
    pad = 15 * 3 * head_width - vectors.shape[0]
    vector_rows = jnp.pad(vectors, (0, pad)).reshape(15, 3 * head_width)
    own_block = jnp.concatenate([columns, bias_row, vector_rows], axis=0)
    t1, t2, t3 = across(token, 1), across(token, 2), across(token, 3)
    two_cols = jnp.stack([own_block, level_across(own_block, 1)])
    own_cols = jnp.concatenate([two_cols, level_across(two_cols, 2)])
    down_quarter = lax.dynamic_slice_in_dim(w_down, place * shard_rows, shard_rows, axis=0)
    two_down = jnp.stack([down_quarter, level_across(down_quarter, 1)])
    own_down = jnp.concatenate([two_down, level_across(two_down, 2)])
    own_down, own_cols, t1, t2, t3 = lax.optimization_barrier((own_down, own_cols, t1, t2, t3))
    other_cols = partner(own_cols)
    down_sets = [own_down] + [across(own_down, j) for j in (1, 2, 3)]
    sc = jnp.stack([lengths[0], place, core, lax.axis_index("z")]).astype(jnp.int32)
    all_rows = 4 * rows
    qkv, ctx_t, c0, c1, c2, c3, lse, full_qkv, vector_sets = pl.pallas_call(
        attend_forward_kernel,
        name="attend_forward",
        cost_estimate=work(13),
        out_shape=(
            struct((all_rows, 3 * head_width)),
            struct((head_width, all_rows), f32),
            struct((rows, head_width)),
            struct((rows, head_width)),
            struct((rows, head_width)),
            struct((rows, head_width)),
            struct((head_width // HEAD_DIM, all_rows), f32),
            struct((zs, 2, shard_rows, 3 * head_width)),
            struct((zs, 2, 2, 3 * head_width), f32),
        ),
        in_specs=[smem_spec()] + vmem_specs(6),
        out_specs=tuple(vmem_specs(9)),
        scratch_shapes=[pltpu.VMEM((4, rows, head_width), bf16)],
    )(sc, token, t1, t2, t3, own_cols, other_cols)
    x1, x2, x3 = across(c1, 1), across(c2, 2), across(c3, 3)
    down_sets[0], _ = lax.optimization_barrier((down_sets[0], c0))
    own_down = jnp.stack(down_sets)
    other_down = partner(own_down)
    all_vec = vector_sets.reshape(2 * zs, -1)
    six = all_vec[:, : 6 * shard_rows].reshape(2 * zs, 6, shard_rows)
    six = six.transpose(1, 0, 2).reshape(6, width)
    small = jnp.concatenate([six, jnp.zeros((2, width), f32)], axis=0)
    full_up_bias = all_vec[:, 6 * shard_rows : 6 * shard_rows + hidden // 8].reshape(1, hidden)
    packed = hidden // 2 + 5 * width + width // 2
    output, grad_one, y0, y1, y2, y3, keep, send, vector_rows = pl.pallas_call(
        middle_kernel,
        name="middle",
        cost_estimate=work(15),
        out_shape=(
            struct((rows, width)),
            struct((rows, width), f32),
            struct((rows, head_width)),
            struct((rows, head_width)),
            struct((rows, head_width)),
            struct((rows, head_width)),
            struct((rows, packed)),
            struct((rows, packed)),
            struct((zs, 16, hidden // 8)),
        ),
        in_specs=[smem_spec()]
        + vmem_specs(8)
        + [pl.BlockSpec(memory_space=pl.ANY)] * 3,
        out_specs=tuple(vmem_specs(9)),
        scratch_shapes=[
            pltpu.VMEM((zs, 2, shard_rows, width), bf16),
            pltpu.VMEM((4, zs, 2, shard_rows, width), bf16),
            pltpu.VMEM((zs, 2, 4, shard_rows, width), bf16),
            pltpu.VMEM((rows, hidden), f32),
            pltpu.VMEM((rows, hidden), bf16),
            pltpu.VMEM((rows, hidden), bf16),
            pltpu.VMEM((4, rows, head_width), bf16),
            pltpu.SemaphoreType.DMA((7 + 32,)),
        ],
    )(
        sc,
        c0,
        x1,
        x2,
        x3,
        token,
        cotangent[0],
        small,
        full_up_bias,
        gathered,
        own_down,
        other_down,
    )
    g1, g2, g3 = across(y1, 1), across(y2, 2), across(y3, 3)
    got, g1, g2, g3 = lax.optimization_barrier((partner(send), g1, g2, g3))
    quad = hidden // 8

    def call(kernel, micros, outs, *args, scratch=(), scalars=True):
        return pl.pallas_call(
            kernel,
            name=kernel.__name__.replace("_kernel", ""),
            cost_estimate=work(micros),
            out_shape=tuple(outs),
            in_specs=([smem_spec()] if scalars else []) + vmem_specs(len(args)),
            out_specs=tuple(vmem_specs(len(outs))),
            scratch_shapes=list(scratch),
        )(*(((sc,) if scalars else ()) + args))

    d_near, d_far = call(
        down_grad_kernel,
        4,
        [struct((2, zs, shard_rows, width))] * 2,
        keep,
        got,
        scratch=[pltpu.VMEM((4, shard_rows, width), bf16)],
    )
    block_rows = 2 * shard_rows + shard_rows // 2 + 16
    u_near, u_far = call(
        up_grad_kernel,
        4,
        [struct((2, zs, block_rows, quad))] * 2,
        keep,
        got,
        vector_rows,
        scratch=[pltpu.VMEM((zs, 4, shard_rows // 2, quad), bf16)],
    )
    d_got = across(d_far, 1)
    u_got = across(u_far, 2)
    y0, d_near, u_near = lax.optimization_barrier((y0, d_near, u_near))

    dqkv = pl.pallas_call(
        attend_backward_kernel,
        name="attend_backward",
        cost_estimate=work(11),
        out_shape=struct((all_rows, 3 * head_width)),
        in_specs=[smem_spec()] + vmem_specs(7),
        out_specs=pl.BlockSpec(memory_space=pltpu.VMEM),
        scratch_shapes=[
            pltpu.VMEM((head_width // HEAD_DIM, all_rows, HEAD_DIM), f32),
            pltpu.VMEM((head_width // HEAD_DIM, all_rows, HEAD_DIM), f32),
            pltpu.VMEM((4, rows, head_width), bf16),
        ],
    )(sc, qkv, ctx_t, lse, y0, g1, g2, g3)
    q_rows = shard_rows + 16
    q_keep, q_send = pl.pallas_call(
        grad_qkv_weight_kernel,
        name="grad_qkv_weight",
        cost_estimate=work(4),
        out_shape=(
            struct((zs, q_rows, 3 * head_width)),
            struct((zs, q_rows, 3 * head_width)),
        ),
        in_specs=[smem_spec()] + vmem_specs(5),
        out_specs=tuple(vmem_specs(2)),
    )(sc, token, t1, t2, t3, dqkv)
    d_near, u_near, q_keep = lax.optimization_barrier((d_near, u_near, q_keep))
    d_mine, d_pass = call(
        fold_kernel, 1, [struct((zs, shard_rows, width))] * 2, d_near, d_got, scalars=False
    )
    u_mine, u_pass = call(
        fold_kernel, 1, [struct((zs, block_rows, quad))] * 2, u_near, u_got, scalars=False
    )
    q_got = partner(q_send)
    late_dqkv, q_keep = lax.optimization_barrier((dqkv, q_keep))
    (token_parts,) = call(
        grad_tokens_kernel,
        4,
        [struct((4, rows, width))],
        late_dqkv,
        full_qkv,
    )
    q_near, q_far = call(
        level_fold_kernel, 1, [struct((2, q_rows, 3 * head_width))] * 2, q_keep, q_got
    )

    def level_sum(near, far, shape):
        mine, pass_on = call(
            fold_kernel, 1, [struct(shape)] * 2, near, level_across(far, 1), scalars=False
        )
        return mine, level_across(pass_on, 2)

    q_mine, q_last = level_sum(q_near, q_far, (q_rows, 3 * head_width))
    (q_part,) = call(
        sum_kernel, 1, [struct((q_rows, 3 * head_width))], q_mine, q_last, scalars=False
    )

    d_mine, u_mine, _ = lax.optimization_barrier((d_mine, u_mine, q_mine))
    merged_rows = block_rows + 2 * shard_rows
    near, far = call(
        level_merge_kernel,
        2,
        [struct((2, merged_rows, quad))] * 2,
        d_mine,
        across(d_pass, 2),
        u_mine,
        across(u_pass, 1),
    )
    token_parts, _ = lax.optimization_barrier((token_parts, near))
    token_sum = lax.psum_scatter(
        token_parts.reshape(4 * rows, width), "seq", scatter_dimension=0, tiled=True
    )
    merged = level_sum(near, far, (merged_rows, quad))
    half_rows = shard_rows + shard_rows // 2 + 16
    u_keep, u_send, d_part = call(
        split_up_kernel,
        1,
        [struct((half_rows, quad))] * 2 + [struct((shard_rows, width))],
        *merged,
        scratch=[pltpu.VMEM((merged_rows, quad), bf16)],
    )
    joined, vector_totals = call(
        join_kernel,
        1,
        [struct((shard_rows + half_rows - 16, width)), struct((16, quad), f32)],
        d_part,
        u_keep,
        partner(u_send),
    )
    q_others = [across(q_part, j) for j in (1, 2, 3)]
    joined, q_others, token_sum = lax.optimization_barrier((joined, q_others, token_sum))
    six = lax.dynamic_index_in_dim(
        vector_totals[:3].reshape(6, 2, shard_rows), core, axis=1, keepdims=False
    )
    result_up_bias = lax.dynamic_index_in_dim(vector_totals[3:5], core, axis=0, keepdims=False)
    result_down, result_up, result_out = call(
        finish_kernel,
        2,
        [
            struct((4 * shard_rows, width), f32),
            struct((shard_rows, hidden), f32),
            struct((shard_rows, width), f32),
        ],
        joined,
        *[across(joined, j) for j in (1, 2, 3)],
    )
    result_qkv, result_q_bias, result_v_bias = call(
        finish_qkv_kernel,
        1,
        [struct((shard_rows, 3 * width), f32)] + [struct((1, shard_rows), f32)] * 2,
        q_part,
        *q_others,
        scratch=[pltpu.VMEM((4, q_rows, 3 * head_width), f32)],
    )
    grad_tokens = (grad_one + token_sum.astype(f32)).astype(bf16)

    return (
        output[None],
        grad_tokens[None],
        result_qkv,
        result_q_bias[0],
        result_v_bias[0],
        result_out,
        six[0],
        six[1],
        six[2],
        result_up,
        result_up_bias,
        result_down,
        six[5],
        six[3],
        six[4],
    )


def solution(mesh):
    seq_count, shard_count = mesh.shape["seq"], mesh.shape["shard"]
    fast = seq_count == 4 and shard_count == 8
    if fast:
        grid = mesh.devices.reshape(seq_count, shard_count // 2, 2)
        mesh = jax.sharding.Mesh(grid, AXES)
    shard = ("z", "core") if fast else "shard"
    vector, matrix, rows = P(shard), P(shard, None), P(shard, "seq", None)
    return jax.shard_map(
        fast_body if fast else body,
        mesh=mesh,
        in_specs=(
            rows,
            vector,
            matrix,
            vector,
            vector,
            matrix,
            vector,
            vector,
            vector,
            matrix,
            vector,
            matrix,
            vector,
            vector,
            vector,
            rows,
        ),
        out_specs=(
            rows,
            rows,
            matrix,
            vector,
            vector,
            matrix,
            vector,
            vector,
            vector,
            matrix,
            vector,
            matrix,
            vector,
            vector,
            vector,
        ),
        check_vma=False,
    )
```

```python
import jax
import jax.numpy as jnp
from jax import lax
from jax.experimental import pallas as pl
from jax.experimental.pallas import tpu as pltpu
from jax.sharding import PartitionSpec as P

HEAD_DIM = 64
LEN = 1024
Q_BLOCK = 512


epsilon = 1e-05
masked_score = -1000000000.0


def layer_norm(values, gain, shift):
    center = values - jnp.mean(values, axis=-1, keepdims=True)
    spread = jnp.mean(center * center, axis=-1, keepdims=True)
    return center * lax.rsqrt(spread + epsilon) * gain + shift


def gelu_exact(values):
    return jax.nn.gelu(values, approximate=False)


def contract_rows(left, right):
    return lax.dot_general(
        left, right, (((0,), (0,)), ((), ())), preferred_element_type=jnp.float32
    )


def contract_cols(left, right):
    return lax.dot_general(
        left, right, (((1,), (1,)), ((), ())), preferred_element_type=jnp.float32
    )


def block_scores(q_block, k_seq, key_valid):
    scores = jnp.einsum(
        "qhd,khd->hqk", q_block, k_seq, preferred_element_type=jnp.float32
    ) * HEAD_DIM ** (-0.5)
    return jnp.where(key_valid[None, None, :], scores, masked_score)


def attend_forward(q_seq, k_seq, v_seq, length):
    local_heads = q_seq.shape[1]
    key_valid = jnp.arange(LEN, dtype=jnp.int32) < length
    q_blocks = q_seq.reshape(LEN // Q_BLOCK, Q_BLOCK, local_heads, HEAD_DIM)

    def one_block(q_block):
        scores = block_scores(q_block, k_seq, key_valid)
        row_peak = jnp.max(scores, axis=-1, keepdims=True)
        shifted = jnp.exp(scores - row_peak)
        row_total = jnp.sum(shifted, axis=-1, keepdims=True)
        attn_probs = (shifted / row_total).astype(jnp.bfloat16)
        context = jnp.einsum("hqk,khd->qhd", attn_probs, v_seq, preferred_element_type=jnp.float32)
        return (context.astype(jnp.bfloat16), (row_peak + jnp.log(row_total))[..., 0])

    context, log_total = lax.map(one_block, q_blocks)
    return (context.reshape(LEN, local_heads, HEAD_DIM), log_total)


def attend_backward(q_seq, k_seq, v_seq, grad_seq, log_total, length):
    local_heads = q_seq.shape[1]
    score_scale = HEAD_DIM ** (-0.5)
    key_valid = jnp.arange(LEN, dtype=jnp.int32) < length
    q_blocks = q_seq.reshape(LEN // Q_BLOCK, Q_BLOCK, local_heads, HEAD_DIM)
    g_blocks = grad_seq.reshape(LEN // Q_BLOCK, Q_BLOCK, local_heads, HEAD_DIM)

    def one_block(accum, block_item):
        q_block, g_block, lse_block = block_item
        scores = block_scores(q_block, k_seq, key_valid)
        attn_probs = jnp.exp(scores - lse_block[..., None])
        grad_probs = jnp.einsum("qhd,khd->hqk", g_block, v_seq, preferred_element_type=jnp.float32)
        row_dot = jnp.sum(attn_probs * grad_probs, axis=-1, keepdims=True)
        grad_scores = (attn_probs * (grad_probs - row_dot)).astype(jnp.bfloat16)
        grad_q = (
            jnp.einsum("hqk,khd->qhd", grad_scores, k_seq, preferred_element_type=jnp.float32)
            * score_scale
        )
        grad_k = (
            accum[0]
            + jnp.einsum("hqk,qhd->khd", grad_scores, q_block, preferred_element_type=jnp.float32)
            * score_scale
        )
        grad_v = accum[1] + jnp.einsum(
            "hqk,qhd->khd",
            attn_probs.astype(jnp.bfloat16),
            g_block,
            preferred_element_type=jnp.float32,
        )
        return ((grad_k, grad_v), grad_q.astype(jnp.bfloat16))

    zero_keys = jnp.zeros((LEN, local_heads, HEAD_DIM), jnp.float32)
    (grad_k, grad_v), grad_q = lax.scan(
        one_block, (zero_keys, zero_keys), (q_blocks, g_blocks, log_total)
    )
    return (
        grad_q.reshape(LEN, local_heads, HEAD_DIM),
        grad_k.astype(jnp.bfloat16),
        grad_v.astype(jnp.bfloat16),
    )


def body(
    tokens,
    lengths,
    w_qkv,
    q_bias,
    v_bias,
    w_out,
    out_bias,
    gain_one,
    shift_one,
    w_up,
    up_bias,
    w_down,
    down_bias,
    gain_two,
    shift_two,
    cotangent,
):
    seq_count, local_len, model_width = tokens.shape
    row_count = seq_count * local_len
    head_count = model_width // HEAD_DIM
    gathered = (
        lax.all_gather(w_qkv, "shard", axis=0, tiled=True),
        lax.all_gather(q_bias, "shard", axis=0, tiled=True),
        lax.all_gather(v_bias, "shard", axis=0, tiled=True),
        lax.all_gather(w_out, "shard", axis=0, tiled=True),
        lax.all_gather(out_bias, "shard", axis=0, tiled=True),
        lax.all_gather(gain_one, "shard", axis=0, tiled=True),
        lax.all_gather(shift_one, "shard", axis=0, tiled=True),
        lax.all_gather(w_up, "shard", axis=0, tiled=True),
        lax.all_gather(up_bias, "shard", axis=0, tiled=True),
        lax.all_gather(w_down, "shard", axis=0, tiled=True),
        lax.all_gather(down_bias, "shard", axis=0, tiled=True),
        lax.all_gather(gain_two, "shard", axis=0, tiled=True),
        lax.all_gather(shift_two, "shard", axis=0, tiled=True),
    )
    (
        full_qkv,
        full_q_bias,
        full_v_bias,
        full_out,
        full_out_bias,
        full_gain_one,
        full_shift_one,
        full_up,
        full_up_bias,
        full_down,
        full_down_bias,
        full_gain_two,
        full_shift_two,
    ) = gathered
    token_rows = tokens.reshape(row_count, model_width)
    joined_bias = jnp.concatenate([full_q_bias, jnp.zeros_like(full_q_bias), full_v_bias]).astype(
        jnp.float32
    )
    qkv_rows = (
        jnp.dot(token_rows, full_qkv, preferred_element_type=jnp.float32) + joined_bias
    ).astype(jnp.bfloat16)
    qkv_tokens = qkv_rows.reshape(seq_count, local_len, 3, head_count, HEAD_DIM)
    qkv_heads = lax.all_to_all(qkv_tokens, "seq", split_axis=3, concat_axis=1, tiled=True)

    def forward_seq(seq_item):
        qkv_seq, length = seq_item
        return attend_forward(qkv_seq[:, 0], qkv_seq[:, 1], qkv_seq[:, 2], length)

    context_heads, log_total = lax.map(forward_seq, (qkv_heads, lengths))
    context_tokens = lax.all_to_all(context_heads, "seq", split_axis=1, concat_axis=2, tiled=True)
    context_rows = context_tokens.reshape(row_count, model_width)
    residual_one = (
        token_rows.astype(jnp.float32)
        + jnp.dot(context_rows, full_out, preferred_element_type=jnp.float32)
        + full_out_bias.astype(jnp.float32)
    )
    normed_one, norm_one_pull = jax.vjp(
        layer_norm,
        residual_one,
        full_gain_one.astype(jnp.float32),
        full_shift_one.astype(jnp.float32),
    )
    normed_low = normed_one.astype(jnp.bfloat16)
    up_rows = jnp.dot(
        normed_low, full_up, preferred_element_type=jnp.float32
    ) + full_up_bias.astype(jnp.float32)
    active, gelu_pull = jax.vjp(gelu_exact, up_rows)
    active_low = active.astype(jnp.bfloat16)
    residual_two = (
        normed_one
        + jnp.dot(active_low, full_down, preferred_element_type=jnp.float32)
        + full_down_bias.astype(jnp.float32)
    )
    final_rows, norm_two_pull = jax.vjp(
        layer_norm,
        residual_two,
        full_gain_two.astype(jnp.float32),
        full_shift_two.astype(jnp.float32),
    )
    output = final_rows.astype(jnp.bfloat16).reshape(tokens.shape)
    back_qkv, back_out, back_up, back_down = (full_qkv, full_out, full_up, full_down)
    grad_rows = cotangent.reshape(row_count, model_width).astype(jnp.float32)
    grad_two, grad_gain_two, grad_shift_two = norm_two_pull(grad_rows)
    grad_down_bias = jnp.sum(grad_two, axis=0)
    grad_two_low = grad_two.astype(jnp.bfloat16)
    grad_w_down = contract_rows(active_low, grad_two_low)
    grad_active = contract_cols(grad_two_low, back_down)
    (grad_up,) = gelu_pull(grad_active)
    grad_up_bias = jnp.sum(grad_up, axis=0)
    grad_up_low = grad_up.astype(jnp.bfloat16)
    grad_w_up = contract_rows(normed_low, grad_up_low)
    grad_normed = grad_two + contract_cols(grad_up_low, back_up)
    grad_one, grad_gain_one, grad_shift_one = norm_one_pull(grad_normed)
    grad_out_bias = jnp.sum(grad_one, axis=0)
    grad_one_low = grad_one.astype(jnp.bfloat16)
    grad_w_out = contract_rows(context_rows, grad_one_low)
    grad_context = contract_cols(grad_one_low, back_out).astype(jnp.bfloat16)
    grad_context = grad_context.reshape(seq_count, local_len, head_count, HEAD_DIM)
    grad_context_heads = lax.all_to_all(
        grad_context, "seq", split_axis=2, concat_axis=1, tiled=True
    )

    def backward_seq(seq_item):
        qkv_seq, grad_seq, lse_seq, length = seq_item
        grad_q, grad_k, grad_v = attend_backward(
            qkv_seq[:, 0], qkv_seq[:, 1], qkv_seq[:, 2], grad_seq, lse_seq, length
        )
        return jnp.stack([grad_q, grad_k, grad_v], axis=1)

    grad_qkv_heads = lax.map(backward_seq, (qkv_heads, grad_context_heads, log_total, lengths))
    grad_qkv_tokens = lax.all_to_all(grad_qkv_heads, "seq", split_axis=1, concat_axis=3, tiled=True)
    grad_qkv_rows = grad_qkv_tokens.reshape(row_count, 3 * model_width)
    grad_q_bias = jnp.sum(grad_qkv_rows[:, :model_width], axis=0, dtype=jnp.float32)
    grad_v_bias = jnp.sum(grad_qkv_rows[:, 2 * model_width :], axis=0, dtype=jnp.float32)
    grad_w_qkv = contract_rows(token_rows, grad_qkv_rows)
    grad_tokens = grad_one + contract_cols(grad_qkv_rows, back_qkv)
    grad_tokens = grad_tokens.astype(jnp.bfloat16).reshape(tokens.shape)
    owned = (
        lax.psum_scatter(grad_w_qkv, "shard", scatter_dimension=0, tiled=True),
        lax.psum_scatter(grad_q_bias, "shard", scatter_dimension=0, tiled=True),
        lax.psum_scatter(grad_v_bias, "shard", scatter_dimension=0, tiled=True),
        lax.psum_scatter(grad_w_out, "shard", scatter_dimension=0, tiled=True),
        lax.psum_scatter(grad_out_bias, "shard", scatter_dimension=0, tiled=True),
        lax.psum_scatter(grad_gain_one, "shard", scatter_dimension=0, tiled=True),
        lax.psum_scatter(grad_shift_one, "shard", scatter_dimension=0, tiled=True),
        lax.psum_scatter(grad_w_up, "shard", scatter_dimension=0, tiled=True),
        lax.psum_scatter(grad_up_bias, "shard", scatter_dimension=0, tiled=True),
        lax.psum_scatter(grad_w_down, "shard", scatter_dimension=0, tiled=True),
        lax.psum_scatter(grad_down_bias, "shard", scatter_dimension=0, tiled=True),
        lax.psum_scatter(grad_gain_two, "shard", scatter_dimension=0, tiled=True),
        lax.psum_scatter(grad_shift_two, "shard", scatter_dimension=0, tiled=True),
    )
    owned_columns = (
        lax.psum_scatter(
            owned[0].astype(jnp.bfloat16), "seq", scatter_dimension=1, tiled=True
        ).astype(jnp.float32),
        lax.psum_scatter(
            owned[3].astype(jnp.bfloat16), "seq", scatter_dimension=1, tiled=True
        ).astype(jnp.float32),
        lax.psum_scatter(
            owned[7].astype(jnp.bfloat16), "seq", scatter_dimension=1, tiled=True
        ).astype(jnp.float32),
        lax.psum_scatter(
            owned[9].astype(jnp.bfloat16), "seq", scatter_dimension=1, tiled=True
        ).astype(jnp.float32),
    )
    matrices = (
        lax.all_gather(owned_columns[0].astype(jnp.bfloat16), "seq", axis=1, tiled=True).astype(
            jnp.float32
        ),
        lax.all_gather(owned_columns[1].astype(jnp.bfloat16), "seq", axis=1, tiled=True).astype(
            jnp.float32
        ),
        lax.all_gather(owned_columns[2].astype(jnp.bfloat16), "seq", axis=1, tiled=True).astype(
            jnp.float32
        ),
        lax.all_gather(owned_columns[3].astype(jnp.bfloat16), "seq", axis=1, tiled=True).astype(
            jnp.float32
        ),
    )
    vectors = lax.psum(
        (
            owned[1],
            owned[2],
            owned[4],
            owned[5],
            owned[6],
            owned[8],
            owned[10],
            owned[11],
            owned[12],
        ),
        "seq",
    )
    result_qkv, result_out, result_up, result_down = (
        matrices[0],
        matrices[1],
        matrices[2],
        matrices[3],
    )
    result_q_bias, result_v_bias, result_out_bias = (vectors[0], vectors[1], vectors[2])
    result_gain_one, result_shift_one, result_up_bias = (vectors[3], vectors[4], vectors[5])
    result_down_bias, result_gain_two, result_shift_two = (vectors[6], vectors[7], vectors[8])
    return (
        output,
        grad_tokens,
        result_qkv,
        result_q_bias,
        result_v_bias,
        result_out,
        result_out_bias,
        result_gain_one,
        result_shift_one,
        result_up,
        result_up_bias,
        result_down,
        result_down_bias,
        result_gain_two,
        result_shift_two,
    )


AXES = ("seq", "z", "core")
NORMAL_SCALE = 0.3989422804014327
HALF_ROOT = 0.7071067811865476


def dot_nn(left, right):
    return lax.dot_general(
        left, right, (((1,), (0,)), ((), ())), preferred_element_type=jnp.float32
    )


def dot_nt(left, right):
    return contract_cols(left, right)


def dot_tn(left, right):
    return contract_rows(left, right)


def vmem_specs(count):
    return [pl.BlockSpec(memory_space=pltpu.VMEM)] * count


def work(micros):
    return pl.CostEstimate(
        flops=int(micros * 9e7), transcendentals=0, bytes_accessed=int(micros * 3e5)
    )


def smem_spec():
    return pl.BlockSpec(memory_space=pltpu.SMEM)


def key_bias(sc, block_rows):
    length, place = sc[0], sc[1]
    columns = []
    for j in range(4):
        position = (place ^ j) * block_rows + lax.broadcasted_iota(
            jnp.int32, (block_rows, 1), 0
        )
        columns.append(jnp.where(position < length, 0.0, masked_score))
    return jnp.concatenate(columns, axis=0)


def attend_forward_kernel(
    sc, t0, t1, t2, t3, own, other, qkv, ctx_t, c0, c1, c2, c3, lse, weight, vectors, held
):
    place, core, level = sc[1], sc[2], sc[3]
    rows = t0.shape[0]
    shard_rows = weight.shape[2]
    width = weight.shape[3]
    head_width = width // 3
    heads = head_width // HEAD_DIM
    for k in range(4):
        for block, side in ((own, core), (other, 1 - core)):
            weight[level ^ k, side] = block[k, :shard_rows, :]
            vectors[level ^ k, side] = block[k, shard_rows + 1 : shard_rows + 3, :].astype(
                jnp.float32
            )
    full = weight[...].reshape(-1, width)
    bias = (
        own[level ^ place, shard_rows : shard_rows + 1, :].astype(jnp.float32)
        + other[level ^ place, shard_rows : shard_rows + 1, :].astype(jnp.float32)
    )
    for j, block in enumerate((t0, t1, t2, t3)):
        qkv[j * rows : (j + 1) * rows, :] = (dot_nn(block[...], full) + bias).astype(jnp.bfloat16)
    mask = key_bias(sc, rows)
    def one_block(j, carry):
        span = pl.ds(pl.multiple_of(j * rows, 128), rows)
        parts = []
        q_all = qkv[span, 0:head_width] * jnp.bfloat16(HEAD_DIM**-0.5)
        for h in range(heads):
            low = h * HEAD_DIM
            q = q_all[:, low : low + HEAD_DIM]
            k = qkv[:, head_width + low : head_width + low + HEAD_DIM]
            v = qkv[:, 2 * head_width + low : 2 * head_width + low + HEAD_DIM]
            scores = dot_nt(k, q) + mask
            peak = jnp.max(scores, axis=0, keepdims=True)
            shifted = jnp.exp(scores - peak)
            total = jnp.sum(shifted, axis=0, keepdims=True)
            part = dot_tn(v, shifted.astype(jnp.bfloat16)) / total
            parts.append(part)
            lse[h : h + 1, span] = peak + jnp.log(total)
        joined = jnp.concatenate(parts, axis=0)
        ctx_t[:, span] = joined
        held[j] = joined.T.astype(jnp.bfloat16)
        return carry

    lax.fori_loop(0, 4, one_block, 0)
    for j, out in enumerate((c0, c1, c2, c3)):
        out[...] = held[j]


def attend_backward_kernel(sc, qkv, ctx_t, lse, g0, g1, g2, g3, dqkv, dk_acc, dv_acc, held):
    rows = g0.shape[0]
    head_width = g0.shape[1]
    heads = head_width // HEAD_DIM
    mask = key_bias(sc, rows)
    scale = jnp.bfloat16(HEAD_DIM**-0.5)
    for j, g_ref in enumerate((g0, g1, g2, g3)):
        held[j] = g_ref[...]
    dk_acc[...] = jnp.zeros_like(dk_acc)
    dv_acc[...] = jnp.zeros_like(dv_acc)

    def one_block(j, carry):
        span = pl.ds(pl.multiple_of(j * rows, 128), rows)
        g_all = held[j]
        product = g_all.astype(jnp.float32).T * ctx_t[:, span]
        q_all = qkv[span, 0:head_width] * scale
        parts = []
        for h in range(heads):
            low = h * HEAD_DIM
            q = q_all[:, low : low + HEAD_DIM]
            g = g_all[:, low : low + HEAD_DIM]
            k = qkv[:, head_width + low : head_width + low + HEAD_DIM]
            v = qkv[:, 2 * head_width + low : 2 * head_width + low + HEAD_DIM]
            probs = jnp.exp(dot_nt(k, q) + mask - lse[h : h + 1, span])
            row_dot = jnp.sum(product[low : low + HEAD_DIM, :], axis=0, keepdims=True)
            grad_scores = (probs * (dot_nt(v, g) - row_dot)).astype(jnp.bfloat16)
            grad_v = dot_nn(probs.astype(jnp.bfloat16), g)
            grad_k = dot_nn(grad_scores, q)
            dv_acc[h] += grad_v
            dk_acc[h] += grad_k
            parts.append(dot_tn(k, grad_scores) * (HEAD_DIM**-0.5))
        dqkv[span, 0:head_width] = jnp.concatenate(parts, axis=0).T.astype(jnp.bfloat16)
        return carry

    lax.fori_loop(0, 4, one_block, 0)
    dk = jnp.concatenate([dk_acc[h] for h in range(heads)], axis=1)
    dv = jnp.concatenate([dv_acc[h] for h in range(heads)], axis=1)
    dqkv[:, head_width:] = jnp.concatenate([dk, dv], axis=1).astype(jnp.bfloat16)


def grad_qkv_weight_kernel(sc, t0, t1, t2, t3, dqkv, keep, send):
    core = sc[2]
    rows = t0.shape[0]
    total = None
    for j, block in enumerate((t0, t1, t2, t3)):
        part = dot_tn(block[...], dqkv[j * rows : (j + 1) * rows, :])
        total = part if total is None else total + part
    sums = jnp.sum(dqkv[...].astype(jnp.float32), axis=0, keepdims=True)
    sums = jnp.broadcast_to(sums, (16, sums.shape[1])).astype(jnp.bfloat16)
    shard_rows = keep.shape[1] - 16
    low = total.astype(jnp.bfloat16)
    for z in range(keep.shape[0]):
        even = low[(2 * z) * shard_rows : (2 * z + 1) * shard_rows]
        odd = low[(2 * z + 1) * shard_rows : (2 * z + 2) * shard_rows]
        keep[z, :shard_rows] = jnp.where(core == 0, even, odd)
        send[z, :shard_rows] = jnp.where(core == 0, odd, even)
        keep[z, shard_rows:] = sums
        send[z, shard_rows:] = sums


def grad_tokens_kernel(sc, dqkv, weight, out):
    place = sc[1]
    rows = out.shape[1]
    full = weight[...].reshape(-1, weight.shape[3])
    for j in range(4):
        part = dot_nt(dqkv[j * rows : (j + 1) * rows, :], full)
        out[place ^ j] = part.astype(out.dtype)


def normalize(values):
    center = values - jnp.mean(values, axis=-1, keepdims=True)
    inverse = lax.rsqrt(jnp.mean(center * center, axis=-1, keepdims=True) + epsilon)
    return center * inverse, inverse


def normalize_back(grad, unit, inverse):
    return inverse * (
        grad
        - jnp.mean(grad, axis=-1, keepdims=True)
        - unit * jnp.mean(grad * unit, axis=-1, keepdims=True)
    )


def middle_kernel(
    sc,
    x0,
    x1,
    x2,
    x3,
    token,
    cotangent,
    small,
    up_bias,
    gathered,
    own_down,
    other_down,
    own_out,
    other_out,
    output,
    grad_one,
    y0,
    y1,
    y2,
    y3,
    keep,
    send,
    vectors,
    w_out,
    w_up,
    w_down,
    slope,
    active,
    grad_up,
    context,
    sems,
):
    place, core, level = sc[1], sc[2], sc[3]
    blocks = w_up.shape[0]
    shard_rows = w_up.shape[3]
    width = w_up.shape[4]
    copies = []
    for b in range(blocks):
        copies.append(
            pltpu.make_async_copy(gathered.at[:, :, b, 0:shard_rows, :], w_up.at[b], sems.at[b])
        )
    down_copies = []
    for j in range(4):
        for k in range(4):
            for side, block in ((core, own_down), (1 - core, other_down)):
                down_copies.append(
                    pltpu.make_async_copy(
                        block.at[j, k],
                        w_down.at[level ^ k, side, place ^ j],
                        sems.at[7 + len(down_copies)],
                    )
                )
    out_copies = []
    for k in range(4):
        for side, block in ((core, own_out), (1 - core, other_out)):
            out_copies.append(
                pltpu.make_async_copy(
                    block.at[k], w_out.at[level ^ k, side], sems.at[40 + len(out_copies)]
                )
            )
    for copy in out_copies + copies + down_copies:
        copy.start()
    for copy in out_copies:
        copy.wait()
    out_rows = 2 * shard_rows

    def out_block(j):
        return w_out[place ^ j].reshape(out_rows, width)

    residual = token[...].astype(jnp.float32) + small[0:1, :]
    for j, block in enumerate((x0, x1, x2, x3)):
        residual = residual + dot_nn(block[...], out_block(j))
    unit_one, inverse_one = normalize(residual)
    gain_one = small[1:2, :]
    normed = unit_one * gain_one + small[2:3, :]
    normed_low = normed.astype(jnp.bfloat16)
    for b in range(blocks):
        copies[b].wait()
        span = slice(b * width, (b + 1) * width)
        up = dot_nn(normed_low, w_up[b].reshape(width, width)) + up_bias[:, span]
        phi = 0.5 + 0.5 * lax.erf(up * HALF_ROOT)
        slope[:, span] = phi + up * (jnp.exp(-0.5 * up * up) * NORMAL_SCALE)
        active[:, span] = (up * phi).astype(jnp.bfloat16)
    for copy in down_copies:
        copy.wait()
    residual = normed + small[3:4, :] + dot_nn(active[...], w_down[...].reshape(-1, width))
    unit_two, inverse_two = normalize(residual)
    gain_two = small[4:5, :]
    output[...] = (unit_two * gain_two + small[5:6, :]).astype(jnp.bfloat16)
    grad = cotangent[...].astype(jnp.float32)
    sum_rows = {
        3: jnp.sum(grad * unit_two, axis=0, keepdims=True),
        4: jnp.sum(grad, axis=0, keepdims=True),
    }
    grad_two = normalize_back(grad * gain_two, unit_two, inverse_two)
    sum_rows[5] = jnp.sum(grad_two, axis=0, keepdims=True)
    vectors[...] = jnp.zeros_like(vectors)
    half = width // 2
    two_low = grad_two.astype(jnp.bfloat16)
    grad_normed = grad_two
    for b in range(blocks):
        span = slice(b * width, (b + 1) * width)
        rows_down = w_down[b].reshape(width, width)
        part = dot_nt(two_low, rows_down) * slope[:, span]
        up_row = jnp.sum(part, axis=0, keepdims=True).astype(jnp.bfloat16)
        vectors[b, 3:4, :] = up_row[:, :half]
        vectors[b, 4:5, :] = up_row[:, half:]
        part = part.astype(jnp.bfloat16)
        grad_up[:, span] = part
        grad_normed = grad_normed + dot_nt(part, w_up[b].reshape(width, width))
    sum_rows[1] = jnp.sum(grad_normed * unit_one, axis=0, keepdims=True)
    sum_rows[2] = jnp.sum(grad_normed, axis=0, keepdims=True)
    first = normalize_back(grad_normed * gain_one, unit_one, inverse_one)
    sum_rows[0] = jnp.sum(first, axis=0, keepdims=True)
    for z in range(4):
        at = slice(z * out_rows, (z + 1) * out_rows)
        for row in range(3):
            pair = [sum_rows[2 * row][:, at], sum_rows[2 * row + 1][:, at]]
            vectors[z, row : row + 1, :] = jnp.concatenate(pair, axis=1).astype(jnp.bfloat16)
    grad_one[...] = first
    one_low = first.astype(jnp.bfloat16)
    for j, out in enumerate((y0, y1, y2, y3)):
        out[...] = dot_nt(one_low, out_block(j)).astype(jnp.bfloat16)
    for j, block in enumerate((x0, x1, x2, x3)):
        context[place ^ j] = block[...]
    joined = jnp.concatenate([context[j] for j in range(4)], axis=1)
    down_rows = blocks * shard_rows
    for ref, mine in ((keep, core), (send, 1 - core)):
        for z in range(4):
            even = active[:, (2 * z) * down_rows : (2 * z + 1) * down_rows]
            odd = active[:, (2 * z + 1) * down_rows : (2 * z + 2) * down_rows]
            ref[:, z * down_rows : (z + 1) * down_rows] = jnp.where(mine == 0, even, odd)
        at = 4 * down_rows
        ref[:, at : at + width] = two_low
        at += width
        ref[:, at : at + width] = normed_low
        at += width
        ref[:, at : at + 2 * width] = jnp.where(
            mine == 0, grad_up[:, : 2 * width], grad_up[:, 2 * width :]
        )
        at += 2 * width
        ref[:, at : at + width] = joined
        at += width
        ref[:, at : at + half] = jnp.where(mine == 0, one_low[:, :half], one_low[:, half:])


def down_grad_kernel(sc, keep, got, near, far, part):
    place = sc[1]
    _, zs, shard_rows, width = near.shape
    down_rows = 4 * shard_rows
    at_two = zs * down_rows
    def both(where):
        return jnp.concatenate([keep[:, where], got[:, where]], axis=0)

    right = both(slice(at_two, at_two + width))
    for z in range(zs):
        total = dot_tn(both(slice(z * down_rows, (z + 1) * down_rows)), right)
        part[...] = total.astype(jnp.bfloat16).reshape(4, shard_rows, width)
        for out, at, j in ((near, 0, 0), (near, 1, 2), (far, 0, 1), (far, 1, 3)):
            out[at, z] = part[place ^ j]


def up_grad_kernel(sc, keep, got, vectors, near, far, part):
    place = sc[1]
    _, zs, block_rows, cols = near.shape
    quarter = part.shape[2]
    pair_rows = block_rows - quarter - 16
    width = zs * pair_rows
    at_norm = 2 * width + width
    at_up = at_norm + width
    at_ctx = at_up + 2 * width
    at_one = at_ctx + width
    def both(where):
        return jnp.concatenate([keep[:, where], got[:, where]], axis=0)

    total = dot_tn(both(slice(at_ctx, at_ctx + width)), both(slice(at_one, at_one + cols)))
    part[...] = total.astype(jnp.bfloat16).reshape(part.shape)
    left = both(slice(at_norm, at_norm + width)).T
    for out, at, j in ((near, 0, 0), (near, 1, 1), (far, 0, 2), (far, 1, 3)):
        right = pl.ds(pl.multiple_of(at_up + (place ^ j) * cols, 128), cols)
        total = dot_nn(left, both(right)).astype(jnp.bfloat16)
        for z in range(zs):
            out[at, z, :pair_rows] = total[z * pair_rows : (z + 1) * pair_rows]
            out[at, z, pair_rows : pair_rows + quarter] = part[z, place ^ j]
            out[at, z, pair_rows + quarter :] = vectors[z]


def fold_kernel(near, got, mine, pass_on):
    for at, out in ((0, mine), (1, pass_on)):
        total = near[at].astype(jnp.float32) + got[at].astype(jnp.float32)
        out[...] = total.astype(jnp.bfloat16)


def level_fold_kernel(sc, mine, got, near, far):
    level = sc[3]
    for out, at, k in ((near, 0, 0), (near, 1, 2), (far, 0, 1), (far, 1, 3)):
        total = mine[level ^ k].astype(jnp.float32) + got[level ^ k].astype(jnp.float32)
        out[at] = total.astype(jnp.bfloat16)


def level_merge_kernel(sc, d_mine, d_got, u_mine, u_got, near, far):
    level = sc[3]
    up_rows, cols = u_mine.shape[1:]
    rows = d_mine.shape[1]
    for out, at, k in ((near, 0, 0), (near, 1, 2), (far, 0, 1), (far, 1, 3)):
        total = u_mine[level ^ k].astype(jnp.float32) + u_got[level ^ k].astype(jnp.float32)
        out[at, :up_rows] = total.astype(jnp.bfloat16)
        total = d_mine[level ^ k].astype(jnp.float32) + d_got[level ^ k].astype(jnp.float32)
        total = total.astype(jnp.bfloat16)
        out[at, up_rows : up_rows + rows] = total[:, :cols]
        out[at, up_rows + rows :] = total[:, cols:]


def block_sum(refs):
    total = refs[0][...].astype(jnp.float32)
    for ref in refs[1:]:
        total = total + ref[...].astype(jnp.float32)
    return total


def split_up_kernel(sc, e0, e1, keep, send, down, held):
    core = sc[2]
    shard_rows, width = down.shape
    cols = width // 2
    half_rows = keep.shape[0] - shard_rows
    held[...] = block_sum((e0, e1)).astype(jnp.bfloat16)
    for ref, side in ((keep, core), (send, 1 - core)):
        ref[:shard_rows] = held[pl.ds(pl.multiple_of(side * shard_rows, 16), shard_rows), :]
        ref[shard_rows:] = held[2 * shard_rows : 2 * shard_rows + half_rows, :]
    at = 2 * shard_rows + half_rows
    down[:, :cols] = held[at : at + shard_rows, :]
    down[:, cols:] = held[at + shard_rows :, :]


def join_kernel(sc, down, keep, got, out, six, up_row):
    core = sc[2]
    shard_rows = down.shape[0]
    cols = keep.shape[1]
    out[:shard_rows] = down[...]
    for ref, side in ((keep, core), (got, 1 - core)):
        out[shard_rows:, pl.ds(pl.multiple_of(side * cols, 128), cols)] = ref[:-16]
    vectors = keep[-16:].astype(jnp.float32) + got[-16:].astype(jnp.float32)
    for row in range(3):
        for side in range(2):
            pair = vectors[row : row + 1, side * 2 * shard_rows : (side + 1) * 2 * shard_rows]
            six[2 * row + side : 2 * row + side + 1, :] = jnp.where(
                core == 0, pair[:, :shard_rows], pair[:, shard_rows:]
            )
    up_row[...] = jnp.where(core == 0, vectors[3:4], vectors[4:5])


def finish_kernel(sc, b0, b1, b2, b3, down, up, out):
    place, core = sc[1], sc[2]
    shard_rows = up.shape[0]
    quarter = shard_rows // 2
    cols = b0.shape[1] // 2
    for j, ref in enumerate((b0, b1, b2, b3)):
        where = place ^ j
        rows = pl.ds(pl.multiple_of(where * shard_rows, 8), shard_rows)
        down[rows, :] = ref[:shard_rows].astype(jnp.float32)
        for side in range(2):
            at = pl.multiple_of((side * 4 + where) * cols, 128)
            up[:, pl.ds(at, cols)] = ref[
                shard_rows : 2 * shard_rows, side * cols : (side + 1) * cols
            ].astype(jnp.float32)

        @pl.when(where // 2 == core)
        def _(ref=ref, where=where):
            at = pl.multiple_of((where % 2) * quarter, 8)
            out[pl.ds(at, quarter), :] = ref[2 * shard_rows :].astype(jnp.float32)


def sum_kernel(e0, e1, out):
    out[...] = block_sum((e0, e1)).astype(out.dtype)


def finish_qkv_kernel(sc, b0, b1, b2, b3, out, q_out, v_out, held):
    place, core, level = sc[1], sc[2], sc[3]
    shard_rows = out.shape[0]
    head_width = b0.shape[1] // 3
    for j, ref in enumerate((b0, b1, b2, b3)):
        held[place ^ j] = ref[...].astype(jnp.float32)
    for part in range(3):
        for s in range(4):
            at = (part * 4 + s) * head_width
            out[:, at : at + head_width] = held[
                s, :shard_rows, part * head_width : (part + 1) * head_width
            ]
    row = held[level, shard_rows : shard_rows + 1, :]
    for ref, at in ((q_out, 0), (v_out, 2 * head_width)):
        ref[...] = jnp.where(
            core == 0, row[:, at : at + shard_rows], row[:, at + shard_rows : at + 2 * shard_rows]
        )


def fast_body(
    tokens,
    lengths,
    w_qkv,
    q_bias,
    v_bias,
    w_out,
    out_bias,
    gain_one,
    shift_one,
    w_up,
    up_bias,
    w_down,
    down_bias,
    gain_two,
    shift_two,
    cotangent,
):
    bf16, f32 = jnp.bfloat16, jnp.float32
    _, rows, width = tokens.shape
    shard_rows = w_qkv.shape[0]
    hidden = w_up.shape[1]
    head_width = width // 4
    place = lax.axis_index("seq")
    core = lax.axis_index("core")
    zs = 4
    swap = [(0, 1), (1, 0)]

    def struct(shape, dtype=bf16):
        return jax.ShapeDtypeStruct(shape, dtype)

    def across(value, step):
        return lax.ppermute(value, "seq", [(i, i ^ step) for i in range(4)])

    def partner(value):
        return lax.ppermute(value, "core", swap)

    def level_across(value, step):
        return lax.ppermute(value, "z", [(i, i ^ step) for i in range(4)])

    token = tokens[0]
    quarter = jnp.concatenate(
        [
            lax.dynamic_slice_in_dim(w_up, place * width, width, axis=1),
        ],
        axis=0,
    )
    gathered = lax.all_gather(quarter, ("z", "core", "seq"), axis=0, tiled=True)
    gathered = gathered.reshape(zs, 2, 4, shard_rows, width)
    columns = lax.dynamic_index_in_dim(
        w_qkv.reshape(shard_rows, 3, 4, head_width), place, axis=2, keepdims=False
    ).reshape(shard_rows, 3 * head_width)
    pair_rows = jnp.zeros((2, 2, shard_rows), bf16)
    placed_q = lax.dynamic_update_slice(pair_rows[0], q_bias[None], (core, 0)).reshape(1, -1)
    placed_v = lax.dynamic_update_slice(pair_rows[0], v_bias[None], (core, 0)).reshape(1, -1)
    bias_row = jnp.concatenate(
        [placed_q, jnp.zeros((1, head_width), bf16), placed_v], axis=1
    )
    vectors = jnp.concatenate(
        [out_bias, gain_one, shift_one, down_bias, gain_two, shift_two, up_bias]
    )
    pad = 15 * 3 * head_width - vectors.shape[0]
    vector_rows = jnp.pad(vectors, (0, pad)).reshape(15, 3 * head_width)
    own_block = jnp.concatenate([columns, bias_row, vector_rows], axis=0)
    t1, t2, t3 = across(token, 1), across(token, 2), across(token, 3)
    two_cols = jnp.stack([own_block, level_across(own_block, 1)])
    own_cols = jnp.concatenate([two_cols, level_across(two_cols, 2)])
    down_quarter = lax.dynamic_slice_in_dim(w_down, place * shard_rows, shard_rows, axis=0)
    two_down = jnp.stack([down_quarter, level_across(down_quarter, 1)])
    own_down = jnp.concatenate([two_down, level_across(two_down, 2)])
    own_down, own_cols, t1, t2, t3 = lax.optimization_barrier((own_down, own_cols, t1, t2, t3))
    other_cols = partner(own_cols)
    late_out, _ = lax.optimization_barrier((w_out, own_cols))
    two_out = jnp.stack([late_out, level_across(late_out, 1)])
    own_out = jnp.concatenate([two_out, level_across(two_out, 2)])
    other_out = partner(own_out)
    t1, own_out = lax.optimization_barrier((t1, own_out))
    down_sets = [own_down] + [across(own_down, j) for j in (1, 2, 3)]
    sc = jnp.stack([lengths[0], place, core, lax.axis_index("z")]).astype(jnp.int32)
    all_rows = 4 * rows
    qkv, ctx_t, c0, c1, c2, c3, lse, full_qkv, vector_sets = pl.pallas_call(
        attend_forward_kernel,
        name="attend_forward",
        cost_estimate=work(13),
        out_shape=(
            struct((all_rows, 3 * head_width)),
            struct((head_width, all_rows), f32),
            struct((rows, head_width)),
            struct((rows, head_width)),
            struct((rows, head_width)),
            struct((rows, head_width)),
            struct((head_width // HEAD_DIM, all_rows), f32),
            struct((zs, 2, shard_rows, 3 * head_width)),
            struct((zs, 2, 2, 3 * head_width), f32),
        ),
        in_specs=[smem_spec()] + vmem_specs(6),
        out_specs=tuple(vmem_specs(9)),
        scratch_shapes=[pltpu.VMEM((4, rows, head_width), bf16)],
    )(sc, token, t1, t2, t3, own_cols, other_cols)
    x1, x2, x3 = across(c1, 1), across(c2, 2), across(c3, 3)
    down_sets[0], _ = lax.optimization_barrier((down_sets[0], c0))
    own_down = jnp.stack(down_sets)
    other_down = partner(own_down)
    all_vec = vector_sets.reshape(2 * zs, -1)
    six = all_vec[:, : 6 * shard_rows].reshape(2 * zs, 6, shard_rows)
    six = six.transpose(1, 0, 2).reshape(6, width)
    small = jnp.concatenate([six, jnp.zeros((2, width), f32)], axis=0)
    full_up_bias = all_vec[:, 6 * shard_rows : 6 * shard_rows + hidden // 8].reshape(1, hidden)
    packed = hidden // 2 + 5 * width + width // 2
    output, grad_one, y0, y1, y2, y3, keep, send, vector_rows = pl.pallas_call(
        middle_kernel,
        name="middle",
        cost_estimate=work(15),
        out_shape=(
            struct((rows, width)),
            struct((rows, width), f32),
            struct((rows, head_width)),
            struct((rows, head_width)),
            struct((rows, head_width)),
            struct((rows, head_width)),
            struct((rows, packed)),
            struct((rows, packed)),
            struct((zs, 16, hidden // 8)),
        ),
        in_specs=[smem_spec()]
        + vmem_specs(8)
        + [pl.BlockSpec(memory_space=pl.ANY)] * 5,
        out_specs=tuple(vmem_specs(9)),
        scratch_shapes=[
            pltpu.VMEM((zs, 2, shard_rows, width), bf16),
            pltpu.VMEM((4, zs, 2, shard_rows, width), bf16),
            pltpu.VMEM((zs, 2, 4, shard_rows, width), bf16),
            pltpu.VMEM((rows, hidden), f32),
            pltpu.VMEM((rows, hidden), bf16),
            pltpu.VMEM((rows, hidden), bf16),
            pltpu.VMEM((4, rows, head_width), bf16),
            pltpu.SemaphoreType.DMA((48,)),
        ],
    )(
        sc,
        c0,
        x1,
        x2,
        x3,
        token,
        cotangent[0],
        small,
        full_up_bias,
        gathered,
        own_down,
        other_down,
        own_out,
        other_out,
    )
    g1, g2, g3 = across(y1, 1), across(y2, 2), across(y3, 3)
    got, g1, g2, g3 = lax.optimization_barrier((partner(send), g1, g2, g3))
    quad = hidden // 8

    def call(kernel, micros, outs, *args, scratch=(), scalars=True):
        return pl.pallas_call(
            kernel,
            name=kernel.__name__.replace("_kernel", ""),
            cost_estimate=work(micros),
            out_shape=tuple(outs),
            in_specs=([smem_spec()] if scalars else []) + vmem_specs(len(args)),
            out_specs=tuple(vmem_specs(len(outs))),
            scratch_shapes=list(scratch),
        )(*(((sc,) if scalars else ()) + args))

    d_near, d_far = call(
        down_grad_kernel,
        4,
        [struct((2, zs, shard_rows, width))] * 2,
        keep,
        got,
        scratch=[pltpu.VMEM((4, shard_rows, width), bf16)],
    )
    block_rows = 2 * shard_rows + shard_rows // 2 + 16
    u_near, u_far = call(
        up_grad_kernel,
        4,
        [struct((2, zs, block_rows, quad))] * 2,
        keep,
        got,
        vector_rows,
        scratch=[pltpu.VMEM((zs, 4, shard_rows // 2, quad), bf16)],
    )
    d_got = across(d_far, 1)
    u_got = across(u_far, 2)
    y0, d_near, u_near = lax.optimization_barrier((y0, d_near, u_near))

    dqkv = pl.pallas_call(
        attend_backward_kernel,
        name="attend_backward",
        cost_estimate=work(11),
        out_shape=struct((all_rows, 3 * head_width)),
        in_specs=[smem_spec()] + vmem_specs(7),
        out_specs=pl.BlockSpec(memory_space=pltpu.VMEM),
        scratch_shapes=[
            pltpu.VMEM((head_width // HEAD_DIM, all_rows, HEAD_DIM), f32),
            pltpu.VMEM((head_width // HEAD_DIM, all_rows, HEAD_DIM), f32),
            pltpu.VMEM((4, rows, head_width), bf16),
        ],
    )(sc, qkv, ctx_t, lse, y0, g1, g2, g3)
    q_rows = shard_rows + 16
    q_keep, q_send = pl.pallas_call(
        grad_qkv_weight_kernel,
        name="grad_qkv_weight",
        cost_estimate=work(4),
        out_shape=(
            struct((zs, q_rows, 3 * head_width)),
            struct((zs, q_rows, 3 * head_width)),
        ),
        in_specs=[smem_spec()] + vmem_specs(5),
        out_specs=tuple(vmem_specs(2)),
    )(sc, token, t1, t2, t3, dqkv)
    d_near, u_near, q_keep = lax.optimization_barrier((d_near, u_near, q_keep))
    d_mine, d_pass = call(
        fold_kernel, 1, [struct((zs, shard_rows, width))] * 2, d_near, d_got, scalars=False
    )
    u_mine, u_pass = call(
        fold_kernel, 1, [struct((zs, block_rows, quad))] * 2, u_near, u_got, scalars=False
    )
    q_got = partner(q_send)
    late_dqkv, q_keep = lax.optimization_barrier((dqkv, q_keep))
    (token_parts,) = call(
        grad_tokens_kernel,
        4,
        [struct((4, rows, width))],
        late_dqkv,
        full_qkv,
    )
    q_near, q_far = call(
        level_fold_kernel, 1, [struct((2, q_rows, 3 * head_width))] * 2, q_keep, q_got
    )

    def level_sum(near, far, shape):
        mine, pass_on = call(
            fold_kernel, 1, [struct(shape)] * 2, near, level_across(far, 1), scalars=False
        )
        return mine, level_across(pass_on, 2)

    q_mine, q_last = level_sum(q_near, q_far, (q_rows, 3 * head_width))
    (q_part,) = call(
        sum_kernel, 1, [struct((q_rows, 3 * head_width))], q_mine, q_last, scalars=False
    )

    d_mine, u_mine, _ = lax.optimization_barrier((d_mine, u_mine, q_mine))
    merged_rows = block_rows + 2 * shard_rows
    near, far = call(
        level_merge_kernel,
        2,
        [struct((2, merged_rows, quad))] * 2,
        d_mine,
        across(d_pass, 2),
        u_mine,
        across(u_pass, 1),
    )
    token_parts, _ = lax.optimization_barrier((token_parts, near))
    token_sum = lax.psum_scatter(
        token_parts.reshape(4 * rows, width), "seq", scatter_dimension=0, tiled=True
    )
    near, q_part = lax.optimization_barrier((near, q_part))
    q_others = [across(q_part, j) for j in (1, 2, 3)]
    merged = level_sum(near, far, (merged_rows, quad))
    merged, q_others = lax.optimization_barrier((merged, q_others))
    half_rows = shard_rows + shard_rows // 2 + 16
    u_keep, u_send, d_part = call(
        split_up_kernel,
        1,
        [struct((half_rows, quad))] * 2 + [struct((shard_rows, width))],
        *merged,
        scratch=[pltpu.VMEM((merged_rows, quad), bf16)],
    )
    joined, six, up_row = call(
        join_kernel,
        1,
        [struct((shard_rows + half_rows - 16, width)), struct((8, shard_rows), f32), struct((1, quad), f32)],
        d_part,
        u_keep,
        partner(u_send),
    )
    joined, token_sum, q_others = lax.optimization_barrier((joined, token_sum, q_others))
    result_down, result_up, result_out = call(
        finish_kernel,
        2,
        [
            struct((4 * shard_rows, width), f32),
            struct((shard_rows, hidden), f32),
            struct((shard_rows, width), f32),
        ],
        joined,
        *[across(joined, j) for j in (1, 2, 3)],
    )
    result_qkv, result_q_bias, result_v_bias = call(
        finish_qkv_kernel,
        1,
        [struct((shard_rows, 3 * width), f32)] + [struct((1, shard_rows), f32)] * 2,
        q_part,
        *q_others,
        scratch=[pltpu.VMEM((4, q_rows, 3 * head_width), f32)],
    )
    grad_tokens = (grad_one + token_sum.astype(f32)).astype(bf16)

    return (
        output[None],
        grad_tokens[None],
        result_qkv,
        result_q_bias[0],
        result_v_bias[0],
        result_out,
        six[0],
        six[1],
        six[2],
        result_up,
        up_row[0],
        result_down,
        six[5],
        six[3],
        six[4],
    )


def solution(mesh):
    seq_count, shard_count = mesh.shape["seq"], mesh.shape["shard"]
    fast = seq_count == 4 and shard_count == 8
    if fast:
        grid = mesh.devices.reshape(seq_count, shard_count // 2, 2)
        mesh = jax.sharding.Mesh(grid, AXES)
    shard = ("z", "core") if fast else "shard"
    vector, matrix, rows = P(shard), P(shard, None), P(shard, "seq", None)
    return jax.shard_map(
        fast_body if fast else body,
        mesh=mesh,
        in_specs=(
            rows,
            vector,
            matrix,
            vector,
            vector,
            matrix,
            vector,
            vector,
            vector,
            matrix,
            vector,
            matrix,
            vector,
            vector,
            vector,
            rows,
        ),
        out_specs=(
            rows,
            rows,
            matrix,
            vector,
            vector,
            matrix,
            vector,
            vector,
            vector,
            matrix,
            vector,
            matrix,
            vector,
            vector,
            vector,
        ),
        check_vma=False,
    )
```

```python
import jax
import jax.numpy as jnp
from jax import lax
from jax.experimental import pallas as pl
from jax.experimental.pallas import tpu as pltpu
from jax.sharding import PartitionSpec as P

HEAD_DIM = 64
LEN = 1024
Q_BLOCK = 512


epsilon = 1e-05
masked_score = -1000000000.0


def layer_norm(values, gain, shift):
    center = values - jnp.mean(values, axis=-1, keepdims=True)
    spread = jnp.mean(center * center, axis=-1, keepdims=True)
    return center * lax.rsqrt(spread + epsilon) * gain + shift


def gelu_exact(values):
    return jax.nn.gelu(values, approximate=False)


def contract_rows(left, right):
    return lax.dot_general(
        left, right, (((0,), (0,)), ((), ())), preferred_element_type=jnp.float32
    )


def contract_cols(left, right):
    return lax.dot_general(
        left, right, (((1,), (1,)), ((), ())), preferred_element_type=jnp.float32
    )


def block_scores(q_block, k_seq, key_valid):
    scores = jnp.einsum(
        "qhd,khd->hqk", q_block, k_seq, preferred_element_type=jnp.float32
    ) * HEAD_DIM ** (-0.5)
    return jnp.where(key_valid[None, None, :], scores, masked_score)


def attend_forward(q_seq, k_seq, v_seq, length):
    local_heads = q_seq.shape[1]
    key_valid = jnp.arange(LEN, dtype=jnp.int32) < length
    q_blocks = q_seq.reshape(LEN // Q_BLOCK, Q_BLOCK, local_heads, HEAD_DIM)

    def one_block(q_block):
        scores = block_scores(q_block, k_seq, key_valid)
        row_peak = jnp.max(scores, axis=-1, keepdims=True)
        shifted = jnp.exp(scores - row_peak)
        row_total = jnp.sum(shifted, axis=-1, keepdims=True)
        attn_probs = (shifted / row_total).astype(jnp.bfloat16)
        context = jnp.einsum("hqk,khd->qhd", attn_probs, v_seq, preferred_element_type=jnp.float32)
        return (context.astype(jnp.bfloat16), (row_peak + jnp.log(row_total))[..., 0])

    context, log_total = lax.map(one_block, q_blocks)
    return (context.reshape(LEN, local_heads, HEAD_DIM), log_total)


def attend_backward(q_seq, k_seq, v_seq, grad_seq, log_total, length):
    local_heads = q_seq.shape[1]
    score_scale = HEAD_DIM ** (-0.5)
    key_valid = jnp.arange(LEN, dtype=jnp.int32) < length
    q_blocks = q_seq.reshape(LEN // Q_BLOCK, Q_BLOCK, local_heads, HEAD_DIM)
    g_blocks = grad_seq.reshape(LEN // Q_BLOCK, Q_BLOCK, local_heads, HEAD_DIM)

    def one_block(accum, block_item):
        q_block, g_block, lse_block = block_item
        scores = block_scores(q_block, k_seq, key_valid)
        attn_probs = jnp.exp(scores - lse_block[..., None])
        grad_probs = jnp.einsum("qhd,khd->hqk", g_block, v_seq, preferred_element_type=jnp.float32)
        row_dot = jnp.sum(attn_probs * grad_probs, axis=-1, keepdims=True)
        grad_scores = (attn_probs * (grad_probs - row_dot)).astype(jnp.bfloat16)
        grad_q = (
            jnp.einsum("hqk,khd->qhd", grad_scores, k_seq, preferred_element_type=jnp.float32)
            * score_scale
        )
        grad_k = (
            accum[0]
            + jnp.einsum("hqk,qhd->khd", grad_scores, q_block, preferred_element_type=jnp.float32)
            * score_scale
        )
        grad_v = accum[1] + jnp.einsum(
            "hqk,qhd->khd",
            attn_probs.astype(jnp.bfloat16),
            g_block,
            preferred_element_type=jnp.float32,
        )
        return ((grad_k, grad_v), grad_q.astype(jnp.bfloat16))

    zero_keys = jnp.zeros((LEN, local_heads, HEAD_DIM), jnp.float32)
    (grad_k, grad_v), grad_q = lax.scan(
        one_block, (zero_keys, zero_keys), (q_blocks, g_blocks, log_total)
    )
    return (
        grad_q.reshape(LEN, local_heads, HEAD_DIM),
        grad_k.astype(jnp.bfloat16),
        grad_v.astype(jnp.bfloat16),
    )


def body(
    tokens,
    lengths,
    w_qkv,
    q_bias,
    v_bias,
    w_out,
    out_bias,
    gain_one,
    shift_one,
    w_up,
    up_bias,
    w_down,
    down_bias,
    gain_two,
    shift_two,
    cotangent,
):
    seq_count, local_len, model_width = tokens.shape
    row_count = seq_count * local_len
    head_count = model_width // HEAD_DIM
    gathered = (
        lax.all_gather(w_qkv, "shard", axis=0, tiled=True),
        lax.all_gather(q_bias, "shard", axis=0, tiled=True),
        lax.all_gather(v_bias, "shard", axis=0, tiled=True),
        lax.all_gather(w_out, "shard", axis=0, tiled=True),
        lax.all_gather(out_bias, "shard", axis=0, tiled=True),
        lax.all_gather(gain_one, "shard", axis=0, tiled=True),
        lax.all_gather(shift_one, "shard", axis=0, tiled=True),
        lax.all_gather(w_up, "shard", axis=0, tiled=True),
        lax.all_gather(up_bias, "shard", axis=0, tiled=True),
        lax.all_gather(w_down, "shard", axis=0, tiled=True),
        lax.all_gather(down_bias, "shard", axis=0, tiled=True),
        lax.all_gather(gain_two, "shard", axis=0, tiled=True),
        lax.all_gather(shift_two, "shard", axis=0, tiled=True),
    )
    (
        full_qkv,
        full_q_bias,
        full_v_bias,
        full_out,
        full_out_bias,
        full_gain_one,
        full_shift_one,
        full_up,
        full_up_bias,
        full_down,
        full_down_bias,
        full_gain_two,
        full_shift_two,
    ) = gathered
    token_rows = tokens.reshape(row_count, model_width)
    joined_bias = jnp.concatenate([full_q_bias, jnp.zeros_like(full_q_bias), full_v_bias]).astype(
        jnp.float32
    )
    qkv_rows = (
        jnp.dot(token_rows, full_qkv, preferred_element_type=jnp.float32) + joined_bias
    ).astype(jnp.bfloat16)
    qkv_tokens = qkv_rows.reshape(seq_count, local_len, 3, head_count, HEAD_DIM)
    qkv_heads = lax.all_to_all(qkv_tokens, "seq", split_axis=3, concat_axis=1, tiled=True)

    def forward_seq(seq_item):
        qkv_seq, length = seq_item
        return attend_forward(qkv_seq[:, 0], qkv_seq[:, 1], qkv_seq[:, 2], length)

    context_heads, log_total = lax.map(forward_seq, (qkv_heads, lengths))
    context_tokens = lax.all_to_all(context_heads, "seq", split_axis=1, concat_axis=2, tiled=True)
    context_rows = context_tokens.reshape(row_count, model_width)
    residual_one = (
        token_rows.astype(jnp.float32)
        + jnp.dot(context_rows, full_out, preferred_element_type=jnp.float32)
        + full_out_bias.astype(jnp.float32)
    )
    normed_one, norm_one_pull = jax.vjp(
        layer_norm,
        residual_one,
        full_gain_one.astype(jnp.float32),
        full_shift_one.astype(jnp.float32),
    )
    normed_low = normed_one.astype(jnp.bfloat16)
    up_rows = jnp.dot(
        normed_low, full_up, preferred_element_type=jnp.float32
    ) + full_up_bias.astype(jnp.float32)
    active, gelu_pull = jax.vjp(gelu_exact, up_rows)
    active_low = active.astype(jnp.bfloat16)
    residual_two = (
        normed_one
        + jnp.dot(active_low, full_down, preferred_element_type=jnp.float32)
        + full_down_bias.astype(jnp.float32)
    )
    final_rows, norm_two_pull = jax.vjp(
        layer_norm,
        residual_two,
        full_gain_two.astype(jnp.float32),
        full_shift_two.astype(jnp.float32),
    )
    output = final_rows.astype(jnp.bfloat16).reshape(tokens.shape)
    back_qkv, back_out, back_up, back_down = (full_qkv, full_out, full_up, full_down)
    grad_rows = cotangent.reshape(row_count, model_width).astype(jnp.float32)
    grad_two, grad_gain_two, grad_shift_two = norm_two_pull(grad_rows)
    grad_down_bias = jnp.sum(grad_two, axis=0)
    grad_two_low = grad_two.astype(jnp.bfloat16)
    grad_w_down = contract_rows(active_low, grad_two_low)
    grad_active = contract_cols(grad_two_low, back_down)
    (grad_up,) = gelu_pull(grad_active)
    grad_up_bias = jnp.sum(grad_up, axis=0)
    grad_up_low = grad_up.astype(jnp.bfloat16)
    grad_w_up = contract_rows(normed_low, grad_up_low)
    grad_normed = grad_two + contract_cols(grad_up_low, back_up)
    grad_one, grad_gain_one, grad_shift_one = norm_one_pull(grad_normed)
    grad_out_bias = jnp.sum(grad_one, axis=0)
    grad_one_low = grad_one.astype(jnp.bfloat16)
    grad_w_out = contract_rows(context_rows, grad_one_low)
    grad_context = contract_cols(grad_one_low, back_out).astype(jnp.bfloat16)
    grad_context = grad_context.reshape(seq_count, local_len, head_count, HEAD_DIM)
    grad_context_heads = lax.all_to_all(
        grad_context, "seq", split_axis=2, concat_axis=1, tiled=True
    )

    def backward_seq(seq_item):
        qkv_seq, grad_seq, lse_seq, length = seq_item
        grad_q, grad_k, grad_v = attend_backward(
            qkv_seq[:, 0], qkv_seq[:, 1], qkv_seq[:, 2], grad_seq, lse_seq, length
        )
        return jnp.stack([grad_q, grad_k, grad_v], axis=1)

    grad_qkv_heads = lax.map(backward_seq, (qkv_heads, grad_context_heads, log_total, lengths))
    grad_qkv_tokens = lax.all_to_all(grad_qkv_heads, "seq", split_axis=1, concat_axis=3, tiled=True)
    grad_qkv_rows = grad_qkv_tokens.reshape(row_count, 3 * model_width)
    grad_q_bias = jnp.sum(grad_qkv_rows[:, :model_width], axis=0, dtype=jnp.float32)
    grad_v_bias = jnp.sum(grad_qkv_rows[:, 2 * model_width :], axis=0, dtype=jnp.float32)
    grad_w_qkv = contract_rows(token_rows, grad_qkv_rows)
    grad_tokens = grad_one + contract_cols(grad_qkv_rows, back_qkv)
    grad_tokens = grad_tokens.astype(jnp.bfloat16).reshape(tokens.shape)
    owned = (
        lax.psum_scatter(grad_w_qkv, "shard", scatter_dimension=0, tiled=True),
        lax.psum_scatter(grad_q_bias, "shard", scatter_dimension=0, tiled=True),
        lax.psum_scatter(grad_v_bias, "shard", scatter_dimension=0, tiled=True),
        lax.psum_scatter(grad_w_out, "shard", scatter_dimension=0, tiled=True),
        lax.psum_scatter(grad_out_bias, "shard", scatter_dimension=0, tiled=True),
        lax.psum_scatter(grad_gain_one, "shard", scatter_dimension=0, tiled=True),
        lax.psum_scatter(grad_shift_one, "shard", scatter_dimension=0, tiled=True),
        lax.psum_scatter(grad_w_up, "shard", scatter_dimension=0, tiled=True),
        lax.psum_scatter(grad_up_bias, "shard", scatter_dimension=0, tiled=True),
        lax.psum_scatter(grad_w_down, "shard", scatter_dimension=0, tiled=True),
        lax.psum_scatter(grad_down_bias, "shard", scatter_dimension=0, tiled=True),
        lax.psum_scatter(grad_gain_two, "shard", scatter_dimension=0, tiled=True),
        lax.psum_scatter(grad_shift_two, "shard", scatter_dimension=0, tiled=True),
    )
    owned_columns = (
        lax.psum_scatter(
            owned[0].astype(jnp.bfloat16), "seq", scatter_dimension=1, tiled=True
        ).astype(jnp.float32),
        lax.psum_scatter(
            owned[3].astype(jnp.bfloat16), "seq", scatter_dimension=1, tiled=True
        ).astype(jnp.float32),
        lax.psum_scatter(
            owned[7].astype(jnp.bfloat16), "seq", scatter_dimension=1, tiled=True
        ).astype(jnp.float32),
        lax.psum_scatter(
            owned[9].astype(jnp.bfloat16), "seq", scatter_dimension=1, tiled=True
        ).astype(jnp.float32),
    )
    matrices = (
        lax.all_gather(owned_columns[0].astype(jnp.bfloat16), "seq", axis=1, tiled=True).astype(
            jnp.float32
        ),
        lax.all_gather(owned_columns[1].astype(jnp.bfloat16), "seq", axis=1, tiled=True).astype(
            jnp.float32
        ),
        lax.all_gather(owned_columns[2].astype(jnp.bfloat16), "seq", axis=1, tiled=True).astype(
            jnp.float32
        ),
        lax.all_gather(owned_columns[3].astype(jnp.bfloat16), "seq", axis=1, tiled=True).astype(
            jnp.float32
        ),
    )
    vectors = lax.psum(
        (
            owned[1],
            owned[2],
            owned[4],
            owned[5],
            owned[6],
            owned[8],
            owned[10],
            owned[11],
            owned[12],
        ),
        "seq",
    )
    result_qkv, result_out, result_up, result_down = (
        matrices[0],
        matrices[1],
        matrices[2],
        matrices[3],
    )
    result_q_bias, result_v_bias, result_out_bias = (vectors[0], vectors[1], vectors[2])
    result_gain_one, result_shift_one, result_up_bias = (vectors[3], vectors[4], vectors[5])
    result_down_bias, result_gain_two, result_shift_two = (vectors[6], vectors[7], vectors[8])
    return (
        output,
        grad_tokens,
        result_qkv,
        result_q_bias,
        result_v_bias,
        result_out,
        result_out_bias,
        result_gain_one,
        result_shift_one,
        result_up,
        result_up_bias,
        result_down,
        result_down_bias,
        result_gain_two,
        result_shift_two,
    )


AXES = ("seq", "z", "core")
NORMAL_SCALE = 0.3989422804014327
HALF_ROOT = 0.7071067811865476


def dot_nn(left, right):
    return lax.dot_general(
        left, right, (((1,), (0,)), ((), ())), preferred_element_type=jnp.float32
    )


def dot_nt(left, right):
    return contract_cols(left, right)


def dot_tn(left, right):
    return contract_rows(left, right)


def vmem_specs(count):
    return [pl.BlockSpec(memory_space=pltpu.VMEM)] * count


def work(micros):
    return pl.CostEstimate(
        flops=int(micros * 9e7), transcendentals=0, bytes_accessed=int(micros * 3e5)
    )


def smem_spec():
    return pl.BlockSpec(memory_space=pltpu.SMEM)


def key_bias(sc, block_rows):
    length, place = sc[0], sc[1]
    columns = []
    for j in range(4):
        position = (place ^ j) * block_rows + lax.broadcasted_iota(
            jnp.int32, (block_rows, 1), 0
        )
        columns.append(jnp.where(position < length, 0.0, masked_score))
    return jnp.concatenate(columns, axis=0)


def pack_kernel(place_ref, weight, *refs):
    vectors, out = refs[:-1], refs[-1]
    place = place_ref[0]
    rows = weight.shape[0]
    head_width = out.shape[1] // 3
    for part in range(3):
        chosen = weight[:, part * 4 * head_width : (part * 4 + 1) * head_width]
        for s in range(1, 4):
            at = (part * 4 + s) * head_width
            chosen = jnp.where(place == s, weight[:, at : at + head_width], chosen)
        out[:rows, part * head_width : (part + 1) * head_width] = chosen
    out[rows:, :] = jnp.zeros((out.shape[0] - rows, out.shape[1]), out.dtype)
    for row, vector in enumerate(vectors):
        out[rows + row : rows + row + 1, : vector.shape[1]] = vector[...]


def attend_forward_kernel(
    sc, t0, t1, t2, t3, own, other, qkv, ctx_t, c0, c1, c2, c3, lse, weight, small, up_bias, held, vectors
):
    place, core, level = sc[1], sc[2], sc[3]
    rows = t0.shape[0]
    shard_rows = weight.shape[2]
    width = weight.shape[3]
    head_width = width // 3
    heads = head_width // HEAD_DIM
    for k in range(4):
        for block, side in ((own, core), (other, 1 - core)):
            weight[level ^ k, side] = block[k, :shard_rows, :]
            vectors[level ^ k, side] = block[k, shard_rows:, :].astype(jnp.float32)
    full = weight[...].reshape(-1, width)
    pairs = [
        vectors[place, side, row : row + 1, :shard_rows] for row in (0, 1) for side in (0, 1)
    ]
    gap = jnp.zeros((1, head_width), jnp.float32)
    bias = jnp.concatenate(pairs[:2] + [gap] + pairs[2:], axis=1)
    up_cols = up_bias.shape[1] // 8
    small[...] = jnp.zeros_like(small)
    for r in range(8):
        z, side = r // 2, r % 2
        at = slice(r * shard_rows, (r + 1) * shard_rows)
        for row in range(6):
            small[row : row + 1, at] = vectors[z, side, 2 + row : 3 + row, :shard_rows]
        up_bias[:, r * up_cols : (r + 1) * up_cols] = vectors[z, side, 8:9, :up_cols]
    for j, block in enumerate((t0, t1, t2, t3)):
        qkv[j * rows : (j + 1) * rows, :] = (dot_nn(block[...], full) + bias).astype(jnp.bfloat16)
    mask = key_bias(sc, rows)
    def one_block(j, carry):
        span = pl.ds(pl.multiple_of(j * rows, 128), rows)
        parts = []
        q_all = qkv[span, 0:head_width] * jnp.bfloat16(HEAD_DIM**-0.5)
        for h in range(heads):
            low = h * HEAD_DIM
            q = q_all[:, low : low + HEAD_DIM]
            k = qkv[:, head_width + low : head_width + low + HEAD_DIM]
            v = qkv[:, 2 * head_width + low : 2 * head_width + low + HEAD_DIM]
            scores = dot_nt(k, q) + mask
            peak = jnp.max(scores, axis=0, keepdims=True)
            shifted = jnp.exp(scores - peak)
            total = jnp.sum(shifted, axis=0, keepdims=True)
            part = dot_tn(v, shifted.astype(jnp.bfloat16)) / total
            parts.append(part)
            lse[h : h + 1, span] = peak + jnp.log(total)
        joined = jnp.concatenate(parts, axis=0)
        ctx_t[:, span] = joined
        held[j] = joined.T.astype(jnp.bfloat16)
        return carry

    lax.fori_loop(0, 4, one_block, 0)
    for j, out in enumerate((c0, c1, c2, c3)):
        out[...] = held[j]


def attend_backward_kernel(sc, qkv, ctx_t, lse, g0, g1, g2, g3, dqkv, dk_acc, dv_acc, held):
    rows = g0.shape[0]
    head_width = g0.shape[1]
    heads = head_width // HEAD_DIM
    mask = key_bias(sc, rows)
    scale = jnp.bfloat16(HEAD_DIM**-0.5)
    for j, g_ref in enumerate((g0, g1, g2, g3)):
        held[j] = g_ref[...]
    dk_acc[...] = jnp.zeros_like(dk_acc)
    dv_acc[...] = jnp.zeros_like(dv_acc)

    def one_block(j, carry):
        span = pl.ds(pl.multiple_of(j * rows, 128), rows)
        g_all = held[j]
        product = g_all.astype(jnp.float32).T * ctx_t[:, span]
        q_all = qkv[span, 0:head_width] * scale
        parts = []
        for h in range(heads):
            low = h * HEAD_DIM
            q = q_all[:, low : low + HEAD_DIM]
            g = g_all[:, low : low + HEAD_DIM]
            k = qkv[:, head_width + low : head_width + low + HEAD_DIM]
            v = qkv[:, 2 * head_width + low : 2 * head_width + low + HEAD_DIM]
            probs = jnp.exp(dot_nt(k, q) + mask - lse[h : h + 1, span])
            row_dot = jnp.sum(product[low : low + HEAD_DIM, :], axis=0, keepdims=True)
            grad_scores = (probs * (dot_nt(v, g) - row_dot)).astype(jnp.bfloat16)
            grad_v = dot_nn(probs.astype(jnp.bfloat16), g)
            grad_k = dot_nn(grad_scores, q)
            dv_acc[h] += grad_v
            dk_acc[h] += grad_k
            parts.append(dot_tn(k, grad_scores) * (HEAD_DIM**-0.5))
        dqkv[span, 0:head_width] = jnp.concatenate(parts, axis=0).T.astype(jnp.bfloat16)
        return carry

    lax.fori_loop(0, 4, one_block, 0)
    dk = jnp.concatenate([dk_acc[h] for h in range(heads)], axis=1)
    dv = jnp.concatenate([dv_acc[h] for h in range(heads)], axis=1)
    dqkv[:, head_width:] = jnp.concatenate([dk, dv], axis=1).astype(jnp.bfloat16)


def grad_qkv_weight_kernel(sc, t0, t1, t2, t3, dqkv, keep, send):
    core = sc[2]
    rows = t0.shape[0]
    total = None
    for j, block in enumerate((t0, t1, t2, t3)):
        part = dot_tn(block[...], dqkv[j * rows : (j + 1) * rows, :])
        total = part if total is None else total + part
    sums = jnp.sum(dqkv[...].astype(jnp.float32), axis=0, keepdims=True)
    sums = jnp.broadcast_to(sums, (16, sums.shape[1])).astype(jnp.bfloat16)
    shard_rows = keep.shape[1] - 16
    low = total.astype(jnp.bfloat16)
    for z in range(keep.shape[0]):
        even = low[(2 * z) * shard_rows : (2 * z + 1) * shard_rows]
        odd = low[(2 * z + 1) * shard_rows : (2 * z + 2) * shard_rows]
        keep[z, :shard_rows] = jnp.where(core == 0, even, odd)
        send[z, :shard_rows] = jnp.where(core == 0, odd, even)
        keep[z, shard_rows:] = sums
        send[z, shard_rows:] = sums


def grad_tokens_kernel(sc, dqkv, weight, out):
    place = sc[1]
    rows = out.shape[1]
    full = weight[...].reshape(-1, weight.shape[3])
    for j in range(4):
        part = dot_nt(dqkv[j * rows : (j + 1) * rows, :], full)
        out[place ^ j] = part.astype(out.dtype)


def normalize(values):
    center = values - jnp.mean(values, axis=-1, keepdims=True)
    inverse = lax.rsqrt(jnp.mean(center * center, axis=-1, keepdims=True) + epsilon)
    return center * inverse, inverse


def normalize_back(grad, unit, inverse):
    return inverse * (
        grad
        - jnp.mean(grad, axis=-1, keepdims=True)
        - unit * jnp.mean(grad * unit, axis=-1, keepdims=True)
    )


def middle_kernel(
    sc,
    x0,
    x1,
    x2,
    x3,
    token,
    cotangent,
    small,
    up_bias,
    gathered,
    own_down,
    other_down,
    own_out,
    other_out,
    output,
    grad_one,
    y0,
    y1,
    y2,
    y3,
    keep,
    send,
    vectors,
    w_out,
    w_up,
    w_down,
    slope,
    active,
    grad_up,
    context,
    sems,
):
    place, core, level = sc[1], sc[2], sc[3]
    blocks = w_up.shape[0]
    shard_rows = w_up.shape[3]
    width = w_up.shape[4]
    copies = []
    for b in range(blocks):
        copies.append(
            pltpu.make_async_copy(gathered.at[:, :, b, 0:shard_rows, :], w_up.at[b], sems.at[b])
        )
    down_copies = []
    for j in range(4):
        for k in range(4):
            for side, block in ((core, own_down), (1 - core, other_down)):
                down_copies.append(
                    pltpu.make_async_copy(
                        block.at[j, k],
                        w_down.at[level ^ k, side, place ^ j],
                        sems.at[7 + len(down_copies)],
                    )
                )
    out_copies = []
    for k in range(4):
        for side, block in ((core, own_out), (1 - core, other_out)):
            out_copies.append(
                pltpu.make_async_copy(
                    block.at[k], w_out.at[level ^ k, side], sems.at[40 + len(out_copies)]
                )
            )
    for copy in out_copies + copies + down_copies:
        copy.start()
    for copy in out_copies:
        copy.wait()
    out_rows = 2 * shard_rows

    def out_block(j):
        return w_out[place ^ j].reshape(out_rows, width)

    residual = token[...].astype(jnp.float32) + small[0:1, :]
    for j, block in enumerate((x0, x1, x2, x3)):
        residual = residual + dot_nn(block[...], out_block(j))
    unit_one, inverse_one = normalize(residual)
    gain_one = small[1:2, :]
    normed = unit_one * gain_one + small[2:3, :]
    normed_low = normed.astype(jnp.bfloat16)
    for b in range(blocks):
        copies[b].wait()
        span = slice(b * width, (b + 1) * width)
        up = dot_nn(normed_low, w_up[b].reshape(width, width)) + up_bias[:, span]
        phi = 0.5 + 0.5 * lax.erf(up * HALF_ROOT)
        slope[:, span] = phi + up * (jnp.exp(-0.5 * up * up) * NORMAL_SCALE)
        active[:, span] = (up * phi).astype(jnp.bfloat16)
    for copy in down_copies:
        copy.wait()
    residual = normed + small[3:4, :] + dot_nn(active[...], w_down[...].reshape(-1, width))
    unit_two, inverse_two = normalize(residual)
    gain_two = small[4:5, :]
    output[...] = (unit_two * gain_two + small[5:6, :]).astype(jnp.bfloat16)
    grad = cotangent[...].astype(jnp.float32)
    sum_rows = {
        3: jnp.sum(grad * unit_two, axis=0, keepdims=True),
        4: jnp.sum(grad, axis=0, keepdims=True),
    }
    grad_two = normalize_back(grad * gain_two, unit_two, inverse_two)
    sum_rows[5] = jnp.sum(grad_two, axis=0, keepdims=True)
    vectors[...] = jnp.zeros_like(vectors)
    half = width // 2
    two_low = grad_two.astype(jnp.bfloat16)
    grad_normed = grad_two
    for b in range(blocks):
        span = slice(b * width, (b + 1) * width)
        rows_down = w_down[b].reshape(width, width)
        part = dot_nt(two_low, rows_down) * slope[:, span]
        up_row = jnp.sum(part, axis=0, keepdims=True).astype(jnp.bfloat16)
        vectors[b, 3:4, :] = up_row[:, :half]
        vectors[b, 4:5, :] = up_row[:, half:]
        part = part.astype(jnp.bfloat16)
        grad_up[:, span] = part
        grad_normed = grad_normed + dot_nt(part, w_up[b].reshape(width, width))
    sum_rows[1] = jnp.sum(grad_normed * unit_one, axis=0, keepdims=True)
    sum_rows[2] = jnp.sum(grad_normed, axis=0, keepdims=True)
    first = normalize_back(grad_normed * gain_one, unit_one, inverse_one)
    sum_rows[0] = jnp.sum(first, axis=0, keepdims=True)
    for z in range(4):
        at = slice(z * out_rows, (z + 1) * out_rows)
        for row in range(3):
            pair = [sum_rows[2 * row][:, at], sum_rows[2 * row + 1][:, at]]
            vectors[z, row : row + 1, :] = jnp.concatenate(pair, axis=1).astype(jnp.bfloat16)
    grad_one[...] = first
    one_low = first.astype(jnp.bfloat16)
    for j, out in enumerate((y0, y1, y2, y3)):
        out[...] = dot_nt(one_low, out_block(j)).astype(jnp.bfloat16)
    for j, block in enumerate((x0, x1, x2, x3)):
        context[place ^ j] = block[...]
    joined = jnp.concatenate([context[j] for j in range(4)], axis=1)
    down_rows = blocks * shard_rows
    for ref, mine in ((keep, core), (send, 1 - core)):
        for z in range(4):
            even = active[:, (2 * z) * down_rows : (2 * z + 1) * down_rows]
            odd = active[:, (2 * z + 1) * down_rows : (2 * z + 2) * down_rows]
            ref[:, z * down_rows : (z + 1) * down_rows] = jnp.where(mine == 0, even, odd)
        at = 4 * down_rows
        ref[:, at : at + width] = two_low
        at += width
        ref[:, at : at + width] = normed_low
        at += width
        ref[:, at : at + 2 * width] = jnp.where(
            mine == 0, grad_up[:, : 2 * width], grad_up[:, 2 * width :]
        )
        at += 2 * width
        ref[:, at : at + width] = joined
        at += width
        ref[:, at : at + half] = jnp.where(mine == 0, one_low[:, :half], one_low[:, half:])


def down_grad_kernel(sc, keep, got, near, far, part):
    place = sc[1]
    _, zs, shard_rows, width = near.shape
    down_rows = 4 * shard_rows
    at_two = zs * down_rows
    def both(where):
        return jnp.concatenate([keep[:, where], got[:, where]], axis=0)

    right = both(slice(at_two, at_two + width))
    for z in range(zs):
        total = dot_tn(both(slice(z * down_rows, (z + 1) * down_rows)), right)
        part[...] = total.astype(jnp.bfloat16).reshape(4, shard_rows, width)
        for out, at, j in ((near, 0, 0), (near, 1, 2), (far, 0, 1), (far, 1, 3)):
            out[at, z] = part[place ^ j]


def up_grad_kernel(sc, keep, got, vectors, near, far, part):
    place = sc[1]
    _, zs, block_rows, cols = near.shape
    quarter = part.shape[2]
    pair_rows = block_rows - quarter - 16
    width = zs * pair_rows
    at_norm = 2 * width + width
    at_up = at_norm + width
    at_ctx = at_up + 2 * width
    at_one = at_ctx + width
    def both(where):
        return jnp.concatenate([keep[:, where], got[:, where]], axis=0)

    total = dot_tn(both(slice(at_ctx, at_ctx + width)), both(slice(at_one, at_one + cols)))
    part[...] = total.astype(jnp.bfloat16).reshape(part.shape)
    left = both(slice(at_norm, at_norm + width)).T
    for out, at, j in ((near, 0, 0), (near, 1, 1), (far, 0, 2), (far, 1, 3)):
        right = pl.ds(pl.multiple_of(at_up + (place ^ j) * cols, 128), cols)
        total = dot_nn(left, both(right)).astype(jnp.bfloat16)
        for z in range(zs):
            out[at, z, :pair_rows] = total[z * pair_rows : (z + 1) * pair_rows]
            out[at, z, pair_rows : pair_rows + quarter] = part[z, place ^ j]
            out[at, z, pair_rows + quarter :] = vectors[z]


def fold_kernel(near, got, mine, pass_on):
    for at, out in ((0, mine), (1, pass_on)):
        total = near[at].astype(jnp.float32) + got[at].astype(jnp.float32)
        out[...] = total.astype(jnp.bfloat16)


def level_fold_kernel(sc, mine, got, near, far):
    level = sc[3]
    for out, at, k in ((near, 0, 0), (near, 1, 2), (far, 0, 1), (far, 1, 3)):
        total = mine[level ^ k].astype(jnp.float32) + got[level ^ k].astype(jnp.float32)
        out[at] = total.astype(jnp.bfloat16)


def level_merge_kernel(sc, d_mine, d_got, u_mine, u_got, near, far):
    level = sc[3]
    up_rows, cols = u_mine.shape[1:]
    rows = d_mine.shape[1]
    for out, at, k in ((near, 0, 0), (near, 1, 2), (far, 0, 1), (far, 1, 3)):
        total = u_mine[level ^ k].astype(jnp.float32) + u_got[level ^ k].astype(jnp.float32)
        out[at, :up_rows] = total.astype(jnp.bfloat16)
        total = d_mine[level ^ k].astype(jnp.float32) + d_got[level ^ k].astype(jnp.float32)
        total = total.astype(jnp.bfloat16)
        out[at, up_rows : up_rows + rows] = total[:, :cols]
        out[at, up_rows + rows :] = total[:, cols:]


def block_sum(refs):
    total = refs[0][...].astype(jnp.float32)
    for ref in refs[1:]:
        total = total + ref[...].astype(jnp.float32)
    return total


def split_up_kernel(sc, e0, e1, keep, send, down, held):
    core = sc[2]
    shard_rows, width = down.shape
    cols = width // 2
    half_rows = keep.shape[0] - shard_rows
    held[...] = block_sum((e0, e1)).astype(jnp.bfloat16)
    for ref, side in ((keep, core), (send, 1 - core)):
        ref[:shard_rows] = held[pl.ds(pl.multiple_of(side * shard_rows, 16), shard_rows), :]
        ref[shard_rows:] = held[2 * shard_rows : 2 * shard_rows + half_rows, :]
    at = 2 * shard_rows + half_rows
    down[:, :cols] = held[at : at + shard_rows, :]
    down[:, cols:] = held[at + shard_rows :, :]


def join_kernel(sc, down, keep, got, out, six, up_row):
    core = sc[2]
    shard_rows = down.shape[0]
    cols = keep.shape[1]
    out[:shard_rows] = down[...]
    for ref, side in ((keep, core), (got, 1 - core)):
        out[shard_rows:, pl.ds(pl.multiple_of(side * cols, 128), cols)] = ref[:-16]
    vectors = keep[-16:].astype(jnp.float32) + got[-16:].astype(jnp.float32)
    for row in range(3):
        for side in range(2):
            pair = vectors[row : row + 1, side * 2 * shard_rows : (side + 1) * 2 * shard_rows]
            six[2 * row + side : 2 * row + side + 1, :] = jnp.where(
                core == 0, pair[:, :shard_rows], pair[:, shard_rows:]
            )
    up_row[...] = jnp.where(core == 0, vectors[3:4], vectors[4:5])


def finish_kernel(sc, b0, b1, b2, b3, down, up, out):
    place, core = sc[1], sc[2]
    shard_rows = up.shape[0]
    quarter = shard_rows // 2
    cols = b0.shape[1] // 2
    for j, ref in enumerate((b0, b1, b2, b3)):
        where = place ^ j
        rows = pl.ds(pl.multiple_of(where * shard_rows, 8), shard_rows)
        down[rows, :] = ref[:shard_rows].astype(jnp.float32)
        for side in range(2):
            at = pl.multiple_of((side * 4 + where) * cols, 128)
            up[:, pl.ds(at, cols)] = ref[
                shard_rows : 2 * shard_rows, side * cols : (side + 1) * cols
            ].astype(jnp.float32)

        @pl.when(where // 2 == core)
        def _(ref=ref, where=where):
            at = pl.multiple_of((where % 2) * quarter, 8)
            out[pl.ds(at, quarter), :] = ref[2 * shard_rows :].astype(jnp.float32)


def sum_kernel(e0, e1, out):
    out[...] = block_sum((e0, e1)).astype(out.dtype)


def finish_qkv_kernel(sc, b0, b1, b2, b3, out, q_out, v_out, held):
    place, core, level = sc[1], sc[2], sc[3]
    shard_rows = out.shape[0]
    head_width = b0.shape[1] // 3
    for j, ref in enumerate((b0, b1, b2, b3)):
        held[place ^ j] = ref[...].astype(jnp.float32)
    for part in range(3):
        for s in range(4):
            at = (part * 4 + s) * head_width
            out[:, at : at + head_width] = held[
                s, :shard_rows, part * head_width : (part + 1) * head_width
            ]
    row = held[level, shard_rows : shard_rows + 1, :]
    for ref, at in ((q_out, 0), (v_out, 2 * head_width)):
        ref[...] = jnp.where(
            core == 0, row[:, at : at + shard_rows], row[:, at + shard_rows : at + 2 * shard_rows]
        )


def fast_body(
    tokens,
    lengths,
    w_qkv,
    q_bias,
    v_bias,
    w_out,
    out_bias,
    gain_one,
    shift_one,
    w_up,
    up_bias,
    w_down,
    down_bias,
    gain_two,
    shift_two,
    cotangent,
):
    bf16, f32 = jnp.bfloat16, jnp.float32
    _, rows, width = tokens.shape
    shard_rows = w_qkv.shape[0]
    hidden = w_up.shape[1]
    head_width = width // 4
    place = lax.axis_index("seq")
    core = lax.axis_index("core")
    zs = 4
    swap = [(0, 1), (1, 0)]

    def struct(shape, dtype=bf16):
        return jax.ShapeDtypeStruct(shape, dtype)

    def across(value, step):
        return lax.ppermute(value, "seq", [(i, i ^ step) for i in range(4)])

    def partner(value):
        return lax.ppermute(value, "core", swap)

    def level_across(value, step):
        return lax.ppermute(value, "z", [(i, i ^ step) for i in range(4)])

    token = tokens[0]
    quarter = jnp.concatenate(
        [
            lax.dynamic_slice_in_dim(w_up, place * width, width, axis=1),
        ],
        axis=0,
    )
    gathered = lax.all_gather(quarter, ("z", "core", "seq"), axis=0, tiled=True)
    gathered = gathered.reshape(zs, 2, 4, shard_rows, width)
    vectors = (q_bias, v_bias, out_bias, gain_one, shift_one)
    vectors += (down_bias, gain_two, shift_two, up_bias)
    own_block = pl.pallas_call(
        pack_kernel,
        name="pack",
        cost_estimate=work(2),
        out_shape=struct((shard_rows + 16, 3 * head_width)),
        in_specs=[smem_spec()] + vmem_specs(1 + len(vectors)),
        out_specs=pl.BlockSpec(memory_space=pltpu.VMEM),
    )(place[None].astype(jnp.int32), w_qkv, *[vector[None] for vector in vectors])
    t1, t2, t3 = across(token, 1), across(token, 2), across(token, 3)
    two_cols = jnp.stack([own_block, level_across(own_block, 1)])
    own_cols = jnp.concatenate([two_cols, level_across(two_cols, 2)])
    down_quarter = lax.dynamic_slice_in_dim(w_down, place * shard_rows, shard_rows, axis=0)
    two_down = jnp.stack([down_quarter, level_across(down_quarter, 1)])
    own_down = jnp.concatenate([two_down, level_across(two_down, 2)])
    own_down, own_cols, t1, t2, t3 = lax.optimization_barrier((own_down, own_cols, t1, t2, t3))
    other_cols = partner(own_cols)
    late_out, _ = lax.optimization_barrier((w_out, own_cols))
    two_out = jnp.stack([late_out, level_across(late_out, 1)])
    own_out = jnp.concatenate([two_out, level_across(two_out, 2)])
    other_out = partner(own_out)
    t1, own_out = lax.optimization_barrier((t1, own_out))
    down_sets = [own_down] + [across(own_down, j) for j in (1, 2, 3)]
    sc = jnp.stack([lengths[0], place, core, lax.axis_index("z")]).astype(jnp.int32)
    all_rows = 4 * rows
    qkv, ctx_t, c0, c1, c2, c3, lse, full_qkv, small, full_up_bias = pl.pallas_call(
        attend_forward_kernel,
        name="attend_forward",
        cost_estimate=work(13),
        out_shape=(
            struct((all_rows, 3 * head_width)),
            struct((head_width, all_rows), f32),
            struct((rows, head_width)),
            struct((rows, head_width)),
            struct((rows, head_width)),
            struct((rows, head_width)),
            struct((head_width // HEAD_DIM, all_rows), f32),
            struct((zs, 2, shard_rows, 3 * head_width)),
            struct((8, width), f32),
            struct((1, hidden), f32),
        ),
        in_specs=[smem_spec()] + vmem_specs(6),
        out_specs=tuple(vmem_specs(10)),
        scratch_shapes=[
            pltpu.VMEM((4, rows, head_width), bf16),
            pltpu.VMEM((zs, 2, 16, 3 * head_width), f32),
        ],
    )(sc, token, t1, t2, t3, own_cols, other_cols)
    x1, x2, x3 = across(c1, 1), across(c2, 2), across(c3, 3)
    down_sets[0], _ = lax.optimization_barrier((down_sets[0], c0))
    own_down = jnp.stack(down_sets)
    other_down = partner(own_down)
    packed = hidden // 2 + 5 * width + width // 2
    output, grad_one, y0, y1, y2, y3, keep, send, vector_rows = pl.pallas_call(
        middle_kernel,
        name="middle",
        cost_estimate=work(15),
        out_shape=(
            struct((rows, width)),
            struct((rows, width), f32),
            struct((rows, head_width)),
            struct((rows, head_width)),
            struct((rows, head_width)),
            struct((rows, head_width)),
            struct((rows, packed)),
            struct((rows, packed)),
            struct((zs, 16, hidden // 8)),
        ),
        in_specs=[smem_spec()]
        + vmem_specs(8)
        + [pl.BlockSpec(memory_space=pl.ANY)] * 5,
        out_specs=tuple(vmem_specs(9)),
        scratch_shapes=[
            pltpu.VMEM((zs, 2, shard_rows, width), bf16),
            pltpu.VMEM((4, zs, 2, shard_rows, width), bf16),
            pltpu.VMEM((zs, 2, 4, shard_rows, width), bf16),
            pltpu.VMEM((rows, hidden), f32),
            pltpu.VMEM((rows, hidden), bf16),
            pltpu.VMEM((rows, hidden), bf16),
            pltpu.VMEM((4, rows, head_width), bf16),
            pltpu.SemaphoreType.DMA((48,)),
        ],
    )(
        sc,
        c0,
        x1,
        x2,
        x3,
        token,
        cotangent[0],
        small,
        full_up_bias,
        gathered,
        own_down,
        other_down,
        own_out,
        other_out,
    )
    g1, g2, g3 = across(y1, 1), across(y2, 2), across(y3, 3)
    got, g1, g2, g3 = lax.optimization_barrier((partner(send), g1, g2, g3))
    quad = hidden // 8

    def call(kernel, micros, outs, *args, scratch=(), scalars=True):
        return pl.pallas_call(
            kernel,
            name=kernel.__name__.replace("_kernel", ""),
            cost_estimate=work(micros),
            out_shape=tuple(outs),
            in_specs=([smem_spec()] if scalars else []) + vmem_specs(len(args)),
            out_specs=tuple(vmem_specs(len(outs))),
            scratch_shapes=list(scratch),
        )(*(((sc,) if scalars else ()) + args))

    d_near, d_far = call(
        down_grad_kernel,
        4,
        [struct((2, zs, shard_rows, width))] * 2,
        keep,
        got,
        scratch=[pltpu.VMEM((4, shard_rows, width), bf16)],
    )
    block_rows = 2 * shard_rows + shard_rows // 2 + 16
    u_near, u_far = call(
        up_grad_kernel,
        4,
        [struct((2, zs, block_rows, quad))] * 2,
        keep,
        got,
        vector_rows,
        scratch=[pltpu.VMEM((zs, 4, shard_rows // 2, quad), bf16)],
    )
    d_got = across(d_far, 1)
    u_got = across(u_far, 2)
    y0, d_near, u_near = lax.optimization_barrier((y0, d_near, u_near))

    dqkv = pl.pallas_call(
        attend_backward_kernel,
        name="attend_backward",
        cost_estimate=work(11),
        out_shape=struct((all_rows, 3 * head_width)),
        in_specs=[smem_spec()] + vmem_specs(7),
        out_specs=pl.BlockSpec(memory_space=pltpu.VMEM),
        scratch_shapes=[
            pltpu.VMEM((head_width // HEAD_DIM, all_rows, HEAD_DIM), f32),
            pltpu.VMEM((head_width // HEAD_DIM, all_rows, HEAD_DIM), f32),
            pltpu.VMEM((4, rows, head_width), bf16),
        ],
    )(sc, qkv, ctx_t, lse, y0, g1, g2, g3)
    q_rows = shard_rows + 16
    q_keep, q_send = pl.pallas_call(
        grad_qkv_weight_kernel,
        name="grad_qkv_weight",
        cost_estimate=work(4),
        out_shape=(
            struct((zs, q_rows, 3 * head_width)),
            struct((zs, q_rows, 3 * head_width)),
        ),
        in_specs=[smem_spec()] + vmem_specs(5),
        out_specs=tuple(vmem_specs(2)),
    )(sc, token, t1, t2, t3, dqkv)
    d_near, u_near, q_keep = lax.optimization_barrier((d_near, u_near, q_keep))
    d_mine, d_pass = call(
        fold_kernel, 1, [struct((zs, shard_rows, width))] * 2, d_near, d_got, scalars=False
    )
    u_mine, u_pass = call(
        fold_kernel, 1, [struct((zs, block_rows, quad))] * 2, u_near, u_got, scalars=False
    )
    q_got = partner(q_send)
    late_dqkv, q_keep = lax.optimization_barrier((dqkv, q_keep))
    (token_parts,) = call(
        grad_tokens_kernel,
        4,
        [struct((4, rows, width))],
        late_dqkv,
        full_qkv,
    )
    q_near, q_far = call(
        level_fold_kernel, 1, [struct((2, q_rows, 3 * head_width))] * 2, q_keep, q_got
    )

    def level_sum(near, far, shape):
        mine, pass_on = call(
            fold_kernel, 1, [struct(shape)] * 2, near, level_across(far, 1), scalars=False
        )
        return mine, level_across(pass_on, 2)

    q_mine, q_last = level_sum(q_near, q_far, (q_rows, 3 * head_width))
    (q_part,) = call(
        sum_kernel, 1, [struct((q_rows, 3 * head_width))], q_mine, q_last, scalars=False
    )

    d_mine, u_mine, _ = lax.optimization_barrier((d_mine, u_mine, q_mine))
    merged_rows = block_rows + 2 * shard_rows
    near, far = call(
        level_merge_kernel,
        2,
        [struct((2, merged_rows, quad))] * 2,
        d_mine,
        across(d_pass, 2),
        u_mine,
        across(u_pass, 1),
    )
    token_parts, _ = lax.optimization_barrier((token_parts, near))
    token_sum = lax.psum_scatter(
        token_parts.reshape(4 * rows, width), "seq", scatter_dimension=0, tiled=True
    )
    q_others = [across(q_part, j) for j in (1, 2, 3)]
    near, _ = lax.optimization_barrier((near, q_last))
    merged = level_sum(near, far, (merged_rows, quad))
    merged, q_others = lax.optimization_barrier((merged, q_others))
    half_rows = shard_rows + shard_rows // 2 + 16
    u_keep, u_send, d_part = call(
        split_up_kernel,
        1,
        [struct((half_rows, quad))] * 2 + [struct((shard_rows, width))],
        *merged,
        scratch=[pltpu.VMEM((merged_rows, quad), bf16)],
    )
    joined, six, up_row = call(
        join_kernel,
        1,
        [struct((shard_rows + half_rows - 16, width)), struct((8, shard_rows), f32), struct((1, quad), f32)],
        d_part,
        u_keep,
        partner(u_send),
    )
    joined, token_sum, q_others = lax.optimization_barrier((joined, token_sum, q_others))
    result_down, result_up, result_out = call(
        finish_kernel,
        2,
        [
            struct((4 * shard_rows, width), f32),
            struct((shard_rows, hidden), f32),
            struct((shard_rows, width), f32),
        ],
        joined,
        *[across(joined, j) for j in (1, 2, 3)],
    )
    result_qkv, result_q_bias, result_v_bias = call(
        finish_qkv_kernel,
        1,
        [struct((shard_rows, 3 * width), f32)] + [struct((1, shard_rows), f32)] * 2,
        q_part,
        *q_others,
        scratch=[pltpu.VMEM((4, q_rows, 3 * head_width), f32)],
    )
    grad_tokens = (grad_one + token_sum.astype(f32)).astype(bf16)

    return (
        output[None],
        grad_tokens[None],
        result_qkv,
        result_q_bias[0],
        result_v_bias[0],
        result_out,
        six[0],
        six[1],
        six[2],
        result_up,
        up_row[0],
        result_down,
        six[5],
        six[3],
        six[4],
    )


def solution(mesh):
    seq_count, shard_count = mesh.shape["seq"], mesh.shape["shard"]
    fast = seq_count == 4 and shard_count == 8
    if fast:
        grid = mesh.devices.reshape(seq_count, shard_count // 2, 2)
        mesh = jax.sharding.Mesh(grid, AXES)
    shard = ("z", "core") if fast else "shard"
    vector, matrix, rows = P(shard), P(shard, None), P(shard, "seq", None)
    return jax.shard_map(
        fast_body if fast else body,
        mesh=mesh,
        in_specs=(
            rows,
            vector,
            matrix,
            vector,
            vector,
            matrix,
            vector,
            vector,
            vector,
            matrix,
            vector,
            matrix,
            vector,
            vector,
            vector,
            rows,
        ),
        out_specs=(
            rows,
            rows,
            matrix,
            vector,
            vector,
            matrix,
            vector,
            vector,
            vector,
            matrix,
            vector,
            matrix,
            vector,
            vector,
            vector,
        ),
        check_vma=False,
    )
```

```python
import jax
import jax.numpy as jnp
from jax import lax
from jax.experimental import pallas as pl
from jax.experimental.pallas import tpu as pltpu
from jax.sharding import PartitionSpec as P

HEAD_DIM = 64
LEN = 1024
Q_BLOCK = 512


epsilon = 1e-05
masked_score = -1000000000.0


def layer_norm(values, gain, shift):
    center = values - jnp.mean(values, axis=-1, keepdims=True)
    spread = jnp.mean(center * center, axis=-1, keepdims=True)
    return center * lax.rsqrt(spread + epsilon) * gain + shift


def gelu_exact(values):
    return jax.nn.gelu(values, approximate=False)


def contract_rows(left, right):
    return lax.dot_general(
        left, right, (((0,), (0,)), ((), ())), preferred_element_type=jnp.float32
    )


def contract_cols(left, right):
    return lax.dot_general(
        left, right, (((1,), (1,)), ((), ())), preferred_element_type=jnp.float32
    )


def block_scores(q_block, k_seq, key_valid):
    scores = jnp.einsum(
        "qhd,khd->hqk", q_block, k_seq, preferred_element_type=jnp.float32
    ) * HEAD_DIM ** (-0.5)
    return jnp.where(key_valid[None, None, :], scores, masked_score)


def attend_forward(q_seq, k_seq, v_seq, length):
    local_heads = q_seq.shape[1]
    key_valid = jnp.arange(LEN, dtype=jnp.int32) < length
    q_blocks = q_seq.reshape(LEN // Q_BLOCK, Q_BLOCK, local_heads, HEAD_DIM)

    def one_block(q_block):
        scores = block_scores(q_block, k_seq, key_valid)
        row_peak = jnp.max(scores, axis=-1, keepdims=True)
        shifted = jnp.exp(scores - row_peak)
        row_total = jnp.sum(shifted, axis=-1, keepdims=True)
        attn_probs = (shifted / row_total).astype(jnp.bfloat16)
        context = jnp.einsum("hqk,khd->qhd", attn_probs, v_seq, preferred_element_type=jnp.float32)
        return (context.astype(jnp.bfloat16), (row_peak + jnp.log(row_total))[..., 0])

    context, log_total = lax.map(one_block, q_blocks)
    return (context.reshape(LEN, local_heads, HEAD_DIM), log_total)


def attend_backward(q_seq, k_seq, v_seq, grad_seq, log_total, length):
    local_heads = q_seq.shape[1]
    score_scale = HEAD_DIM ** (-0.5)
    key_valid = jnp.arange(LEN, dtype=jnp.int32) < length
    q_blocks = q_seq.reshape(LEN // Q_BLOCK, Q_BLOCK, local_heads, HEAD_DIM)
    g_blocks = grad_seq.reshape(LEN // Q_BLOCK, Q_BLOCK, local_heads, HEAD_DIM)

    def one_block(accum, block_item):
        q_block, g_block, lse_block = block_item
        scores = block_scores(q_block, k_seq, key_valid)
        attn_probs = jnp.exp(scores - lse_block[..., None])
        grad_probs = jnp.einsum("qhd,khd->hqk", g_block, v_seq, preferred_element_type=jnp.float32)
        row_dot = jnp.sum(attn_probs * grad_probs, axis=-1, keepdims=True)
        grad_scores = (attn_probs * (grad_probs - row_dot)).astype(jnp.bfloat16)
        grad_q = (
            jnp.einsum("hqk,khd->qhd", grad_scores, k_seq, preferred_element_type=jnp.float32)
            * score_scale
        )
        grad_k = (
            accum[0]
            + jnp.einsum("hqk,qhd->khd", grad_scores, q_block, preferred_element_type=jnp.float32)
            * score_scale
        )
        grad_v = accum[1] + jnp.einsum(
            "hqk,qhd->khd",
            attn_probs.astype(jnp.bfloat16),
            g_block,
            preferred_element_type=jnp.float32,
        )
        return ((grad_k, grad_v), grad_q.astype(jnp.bfloat16))

    zero_keys = jnp.zeros((LEN, local_heads, HEAD_DIM), jnp.float32)
    (grad_k, grad_v), grad_q = lax.scan(
        one_block, (zero_keys, zero_keys), (q_blocks, g_blocks, log_total)
    )
    return (
        grad_q.reshape(LEN, local_heads, HEAD_DIM),
        grad_k.astype(jnp.bfloat16),
        grad_v.astype(jnp.bfloat16),
    )


def body(
    tokens,
    lengths,
    w_qkv,
    q_bias,
    v_bias,
    w_out,
    out_bias,
    gain_one,
    shift_one,
    w_up,
    up_bias,
    w_down,
    down_bias,
    gain_two,
    shift_two,
    cotangent,
):
    seq_count, local_len, model_width = tokens.shape
    row_count = seq_count * local_len
    head_count = model_width // HEAD_DIM
    gathered = (
        lax.all_gather(w_qkv, "shard", axis=0, tiled=True),
        lax.all_gather(q_bias, "shard", axis=0, tiled=True),
        lax.all_gather(v_bias, "shard", axis=0, tiled=True),
        lax.all_gather(w_out, "shard", axis=0, tiled=True),
        lax.all_gather(out_bias, "shard", axis=0, tiled=True),
        lax.all_gather(gain_one, "shard", axis=0, tiled=True),
        lax.all_gather(shift_one, "shard", axis=0, tiled=True),
        lax.all_gather(w_up, "shard", axis=0, tiled=True),
        lax.all_gather(up_bias, "shard", axis=0, tiled=True),
        lax.all_gather(w_down, "shard", axis=0, tiled=True),
        lax.all_gather(down_bias, "shard", axis=0, tiled=True),
        lax.all_gather(gain_two, "shard", axis=0, tiled=True),
        lax.all_gather(shift_two, "shard", axis=0, tiled=True),
    )
    (
        full_qkv,
        full_q_bias,
        full_v_bias,
        full_out,
        full_out_bias,
        full_gain_one,
        full_shift_one,
        full_up,
        full_up_bias,
        full_down,
        full_down_bias,
        full_gain_two,
        full_shift_two,
    ) = gathered
    token_rows = tokens.reshape(row_count, model_width)
    joined_bias = jnp.concatenate([full_q_bias, jnp.zeros_like(full_q_bias), full_v_bias]).astype(
        jnp.float32
    )
    qkv_rows = (
        jnp.dot(token_rows, full_qkv, preferred_element_type=jnp.float32) + joined_bias
    ).astype(jnp.bfloat16)
    qkv_tokens = qkv_rows.reshape(seq_count, local_len, 3, head_count, HEAD_DIM)
    qkv_heads = lax.all_to_all(qkv_tokens, "seq", split_axis=3, concat_axis=1, tiled=True)

    def forward_seq(seq_item):
        qkv_seq, length = seq_item
        return attend_forward(qkv_seq[:, 0], qkv_seq[:, 1], qkv_seq[:, 2], length)

    context_heads, log_total = lax.map(forward_seq, (qkv_heads, lengths))
    context_tokens = lax.all_to_all(context_heads, "seq", split_axis=1, concat_axis=2, tiled=True)
    context_rows = context_tokens.reshape(row_count, model_width)
    residual_one = (
        token_rows.astype(jnp.float32)
        + jnp.dot(context_rows, full_out, preferred_element_type=jnp.float32)
        + full_out_bias.astype(jnp.float32)
    )
    normed_one, norm_one_pull = jax.vjp(
        layer_norm,
        residual_one,
        full_gain_one.astype(jnp.float32),
        full_shift_one.astype(jnp.float32),
    )
    normed_low = normed_one.astype(jnp.bfloat16)
    up_rows = jnp.dot(
        normed_low, full_up, preferred_element_type=jnp.float32
    ) + full_up_bias.astype(jnp.float32)
    active, gelu_pull = jax.vjp(gelu_exact, up_rows)
    active_low = active.astype(jnp.bfloat16)
    residual_two = (
        normed_one
        + jnp.dot(active_low, full_down, preferred_element_type=jnp.float32)
        + full_down_bias.astype(jnp.float32)
    )
    final_rows, norm_two_pull = jax.vjp(
        layer_norm,
        residual_two,
        full_gain_two.astype(jnp.float32),
        full_shift_two.astype(jnp.float32),
    )
    output = final_rows.astype(jnp.bfloat16).reshape(tokens.shape)
    back_qkv, back_out, back_up, back_down = (full_qkv, full_out, full_up, full_down)
    grad_rows = cotangent.reshape(row_count, model_width).astype(jnp.float32)
    grad_two, grad_gain_two, grad_shift_two = norm_two_pull(grad_rows)
    grad_down_bias = jnp.sum(grad_two, axis=0)
    grad_two_low = grad_two.astype(jnp.bfloat16)
    grad_w_down = contract_rows(active_low, grad_two_low)
    grad_active = contract_cols(grad_two_low, back_down)
    (grad_up,) = gelu_pull(grad_active)
    grad_up_bias = jnp.sum(grad_up, axis=0)
    grad_up_low = grad_up.astype(jnp.bfloat16)
    grad_w_up = contract_rows(normed_low, grad_up_low)
    grad_normed = grad_two + contract_cols(grad_up_low, back_up)
    grad_one, grad_gain_one, grad_shift_one = norm_one_pull(grad_normed)
    grad_out_bias = jnp.sum(grad_one, axis=0)
    grad_one_low = grad_one.astype(jnp.bfloat16)
    grad_w_out = contract_rows(context_rows, grad_one_low)
    grad_context = contract_cols(grad_one_low, back_out).astype(jnp.bfloat16)
    grad_context = grad_context.reshape(seq_count, local_len, head_count, HEAD_DIM)
    grad_context_heads = lax.all_to_all(
        grad_context, "seq", split_axis=2, concat_axis=1, tiled=True
    )

    def backward_seq(seq_item):
        qkv_seq, grad_seq, lse_seq, length = seq_item
        grad_q, grad_k, grad_v = attend_backward(
            qkv_seq[:, 0], qkv_seq[:, 1], qkv_seq[:, 2], grad_seq, lse_seq, length
        )
        return jnp.stack([grad_q, grad_k, grad_v], axis=1)

    grad_qkv_heads = lax.map(backward_seq, (qkv_heads, grad_context_heads, log_total, lengths))
    grad_qkv_tokens = lax.all_to_all(grad_qkv_heads, "seq", split_axis=1, concat_axis=3, tiled=True)
    grad_qkv_rows = grad_qkv_tokens.reshape(row_count, 3 * model_width)
    grad_q_bias = jnp.sum(grad_qkv_rows[:, :model_width], axis=0, dtype=jnp.float32)
    grad_v_bias = jnp.sum(grad_qkv_rows[:, 2 * model_width :], axis=0, dtype=jnp.float32)
    grad_w_qkv = contract_rows(token_rows, grad_qkv_rows)
    grad_tokens = grad_one + contract_cols(grad_qkv_rows, back_qkv)
    grad_tokens = grad_tokens.astype(jnp.bfloat16).reshape(tokens.shape)
    owned = (
        lax.psum_scatter(grad_w_qkv, "shard", scatter_dimension=0, tiled=True),
        lax.psum_scatter(grad_q_bias, "shard", scatter_dimension=0, tiled=True),
        lax.psum_scatter(grad_v_bias, "shard", scatter_dimension=0, tiled=True),
        lax.psum_scatter(grad_w_out, "shard", scatter_dimension=0, tiled=True),
        lax.psum_scatter(grad_out_bias, "shard", scatter_dimension=0, tiled=True),
        lax.psum_scatter(grad_gain_one, "shard", scatter_dimension=0, tiled=True),
        lax.psum_scatter(grad_shift_one, "shard", scatter_dimension=0, tiled=True),
        lax.psum_scatter(grad_w_up, "shard", scatter_dimension=0, tiled=True),
        lax.psum_scatter(grad_up_bias, "shard", scatter_dimension=0, tiled=True),
        lax.psum_scatter(grad_w_down, "shard", scatter_dimension=0, tiled=True),
        lax.psum_scatter(grad_down_bias, "shard", scatter_dimension=0, tiled=True),
        lax.psum_scatter(grad_gain_two, "shard", scatter_dimension=0, tiled=True),
        lax.psum_scatter(grad_shift_two, "shard", scatter_dimension=0, tiled=True),
    )
    owned_columns = (
        lax.psum_scatter(
            owned[0].astype(jnp.bfloat16), "seq", scatter_dimension=1, tiled=True
        ).astype(jnp.float32),
        lax.psum_scatter(
            owned[3].astype(jnp.bfloat16), "seq", scatter_dimension=1, tiled=True
        ).astype(jnp.float32),
        lax.psum_scatter(
            owned[7].astype(jnp.bfloat16), "seq", scatter_dimension=1, tiled=True
        ).astype(jnp.float32),
        lax.psum_scatter(
            owned[9].astype(jnp.bfloat16), "seq", scatter_dimension=1, tiled=True
        ).astype(jnp.float32),
    )
    matrices = (
        lax.all_gather(owned_columns[0].astype(jnp.bfloat16), "seq", axis=1, tiled=True).astype(
            jnp.float32
        ),
        lax.all_gather(owned_columns[1].astype(jnp.bfloat16), "seq", axis=1, tiled=True).astype(
            jnp.float32
        ),
        lax.all_gather(owned_columns[2].astype(jnp.bfloat16), "seq", axis=1, tiled=True).astype(
            jnp.float32
        ),
        lax.all_gather(owned_columns[3].astype(jnp.bfloat16), "seq", axis=1, tiled=True).astype(
            jnp.float32
        ),
    )
    vectors = lax.psum(
        (
            owned[1],
            owned[2],
            owned[4],
            owned[5],
            owned[6],
            owned[8],
            owned[10],
            owned[11],
            owned[12],
        ),
        "seq",
    )
    result_qkv, result_out, result_up, result_down = (
        matrices[0],
        matrices[1],
        matrices[2],
        matrices[3],
    )
    result_q_bias, result_v_bias, result_out_bias = (vectors[0], vectors[1], vectors[2])
    result_gain_one, result_shift_one, result_up_bias = (vectors[3], vectors[4], vectors[5])
    result_down_bias, result_gain_two, result_shift_two = (vectors[6], vectors[7], vectors[8])
    return (
        output,
        grad_tokens,
        result_qkv,
        result_q_bias,
        result_v_bias,
        result_out,
        result_out_bias,
        result_gain_one,
        result_shift_one,
        result_up,
        result_up_bias,
        result_down,
        result_down_bias,
        result_gain_two,
        result_shift_two,
    )


AXES = ("seq", "z", "core")
NORMAL_SCALE = 0.3989422804014327
HALF_ROOT = 0.7071067811865476


def dot_nn(left, right):
    return lax.dot_general(
        left, right, (((1,), (0,)), ((), ())), preferred_element_type=jnp.float32
    )


def dot_nt(left, right):
    return contract_cols(left, right)


def dot_tn(left, right):
    return contract_rows(left, right)


def vmem_specs(count):
    return [pl.BlockSpec(memory_space=pltpu.VMEM)] * count


def work(micros):
    return pl.CostEstimate(
        flops=int(micros * 9e7), transcendentals=0, bytes_accessed=int(micros * 3e5)
    )


def smem_spec():
    return pl.BlockSpec(memory_space=pltpu.SMEM)


def key_bias(sc, block_rows):
    length, place = sc[0], sc[1]
    columns = []
    for j in range(4):
        position = (place ^ j) * block_rows + lax.broadcasted_iota(
            jnp.int32, (block_rows, 1), 0
        )
        columns.append(jnp.where(position < length, 0.0, masked_score))
    return jnp.concatenate(columns, axis=0)


def pack_kernel(place_ref, weight, *refs):
    vectors, out = refs[:-1], refs[-1]
    place = place_ref[0]
    rows = weight.shape[0]
    head_width = out.shape[1] // 3
    for part in range(3):
        chosen = weight[:, part * 4 * head_width : (part * 4 + 1) * head_width]
        for s in range(1, 4):
            at = (part * 4 + s) * head_width
            chosen = jnp.where(place == s, weight[:, at : at + head_width], chosen)
        out[:rows, part * head_width : (part + 1) * head_width] = chosen
    out[rows:, :] = jnp.zeros((out.shape[0] - rows, out.shape[1]), out.dtype)
    for row, vector in enumerate(vectors):
        out[rows + row : rows + row + 1, : vector.shape[1]] = vector[...]


def attend_forward_kernel(
    sc, t0, t1, t2, t3, own, other, qkv, ctx_t, c0, c1, c2, c3, lse, weight, small, up_bias, held, vectors
):
    place, core, level = sc[1], sc[2], sc[3]
    rows = t0.shape[0]
    shard_rows = weight.shape[2]
    width = weight.shape[3]
    head_width = width // 3
    heads = head_width // HEAD_DIM
    for k in range(4):
        for block, side in ((own, core), (other, 1 - core)):
            weight[level ^ k, side] = block[k, :shard_rows, :]
            vectors[level ^ k, side] = block[k, shard_rows:, :].astype(jnp.float32)
    full = weight[...].reshape(-1, width)
    pairs = [
        vectors[place, side, row : row + 1, :shard_rows] for row in (0, 1) for side in (0, 1)
    ]
    gap = jnp.zeros((1, head_width), jnp.float32)
    bias = jnp.concatenate(pairs[:2] + [gap] + pairs[2:], axis=1)
    up_cols = up_bias.shape[1] // 8
    small[...] = jnp.zeros_like(small)
    for r in range(8):
        z, side = r // 2, r % 2
        at = slice(r * shard_rows, (r + 1) * shard_rows)
        for row in range(6):
            small[row : row + 1, at] = vectors[z, side, 2 + row : 3 + row, :shard_rows]
        up_bias[:, r * up_cols : (r + 1) * up_cols] = vectors[z, side, 8:9, :up_cols]
    for j, block in enumerate((t0, t1, t2, t3)):
        qkv[j * rows : (j + 1) * rows, :] = (dot_nn(block[...], full) + bias).astype(jnp.bfloat16)
    mask = key_bias(sc, rows)
    def one_block(j, carry):
        span = pl.ds(pl.multiple_of(j * rows, 128), rows)
        parts = []
        q_all = qkv[span, 0:head_width] * jnp.bfloat16(HEAD_DIM**-0.5)
        for h in range(heads):
            low = h * HEAD_DIM
            q = q_all[:, low : low + HEAD_DIM]
            k = qkv[:, head_width + low : head_width + low + HEAD_DIM]
            v = qkv[:, 2 * head_width + low : 2 * head_width + low + HEAD_DIM]
            scores = dot_nt(k, q) + mask
            peak = jnp.max(scores, axis=0, keepdims=True)
            shifted = jnp.exp(scores - peak)
            total = jnp.sum(shifted, axis=0, keepdims=True)
            part = dot_tn(v, shifted.astype(jnp.bfloat16)) / total
            parts.append(part)
            lse[h : h + 1, span] = peak + jnp.log(total)
        joined = jnp.concatenate(parts, axis=0)
        ctx_t[:, span] = joined
        held[j] = joined.T.astype(jnp.bfloat16)
        return carry

    lax.fori_loop(0, 4, one_block, 0)
    for j, out in enumerate((c0, c1, c2, c3)):
        out[...] = held[j]


def attend_backward_kernel(sc, qkv, ctx_t, lse, g0, g1, g2, g3, dqkv, dk_acc, dv_acc, held):
    rows = g0.shape[0]
    head_width = g0.shape[1]
    heads = head_width // HEAD_DIM
    mask = key_bias(sc, rows)
    scale = jnp.bfloat16(HEAD_DIM**-0.5)
    for j, g_ref in enumerate((g0, g1, g2, g3)):
        held[j] = g_ref[...]
    dk_acc[...] = jnp.zeros_like(dk_acc)
    dv_acc[...] = jnp.zeros_like(dv_acc)

    def one_block(j, carry):
        span = pl.ds(pl.multiple_of(j * rows, 128), rows)
        g_all = held[j]
        product = g_all.astype(jnp.float32).T * ctx_t[:, span]
        q_all = qkv[span, 0:head_width] * scale
        parts = []
        for h in range(heads):
            low = h * HEAD_DIM
            q = q_all[:, low : low + HEAD_DIM]
            g = g_all[:, low : low + HEAD_DIM]
            k = qkv[:, head_width + low : head_width + low + HEAD_DIM]
            v = qkv[:, 2 * head_width + low : 2 * head_width + low + HEAD_DIM]
            probs = jnp.exp(dot_nt(k, q) + mask - lse[h : h + 1, span])
            row_dot = jnp.sum(product[low : low + HEAD_DIM, :], axis=0, keepdims=True)
            grad_scores = (probs * (dot_nt(v, g) - row_dot)).astype(jnp.bfloat16)
            grad_v = dot_nn(probs.astype(jnp.bfloat16), g)
            grad_k = dot_nn(grad_scores, q)
            dv_acc[h] += grad_v
            dk_acc[h] += grad_k
            parts.append(dot_tn(k, grad_scores) * (HEAD_DIM**-0.5))
        dqkv[span, 0:head_width] = jnp.concatenate(parts, axis=0).T.astype(jnp.bfloat16)
        return carry

    lax.fori_loop(0, 4, one_block, 0)
    dk = jnp.concatenate([dk_acc[h] for h in range(heads)], axis=1)
    dv = jnp.concatenate([dv_acc[h] for h in range(heads)], axis=1)
    dqkv[:, head_width:] = jnp.concatenate([dk, dv], axis=1).astype(jnp.bfloat16)


def grad_qkv_weight_kernel(sc, t0, t1, t2, t3, dqkv, keep, send):
    core = sc[2]
    rows = t0.shape[0]
    total = None
    for j, block in enumerate((t0, t1, t2, t3)):
        part = dot_tn(block[...], dqkv[j * rows : (j + 1) * rows, :])
        total = part if total is None else total + part
    sums = jnp.sum(dqkv[...].astype(jnp.float32), axis=0, keepdims=True)
    sums = jnp.broadcast_to(sums, (16, sums.shape[1])).astype(jnp.bfloat16)
    shard_rows = keep.shape[1] - 16
    low = total.astype(jnp.bfloat16)
    for z in range(keep.shape[0]):
        even = low[(2 * z) * shard_rows : (2 * z + 1) * shard_rows]
        odd = low[(2 * z + 1) * shard_rows : (2 * z + 2) * shard_rows]
        keep[z, :shard_rows] = jnp.where(core == 0, even, odd)
        send[z, :shard_rows] = jnp.where(core == 0, odd, even)
        keep[z, shard_rows:] = sums
        send[z, shard_rows:] = sums


def grad_tokens_kernel(sc, dqkv, weight, out):
    place = sc[1]
    rows = out.shape[1]
    full = weight[...].reshape(-1, weight.shape[3])
    for j in range(4):
        part = dot_nt(dqkv[j * rows : (j + 1) * rows, :], full)
        out[place ^ j] = part.astype(out.dtype)


def normalize(values):
    center = values - jnp.mean(values, axis=-1, keepdims=True)
    inverse = lax.rsqrt(jnp.mean(center * center, axis=-1, keepdims=True) + epsilon)
    return center * inverse, inverse


def normalize_back(grad, unit, inverse):
    return inverse * (
        grad
        - jnp.mean(grad, axis=-1, keepdims=True)
        - unit * jnp.mean(grad * unit, axis=-1, keepdims=True)
    )


def middle_kernel(
    sc,
    x0,
    x1,
    x2,
    x3,
    token,
    cotangent,
    small,
    up_bias,
    gathered,
    own_down,
    other_down,
    own_out,
    other_out,
    output,
    grad_one,
    y0,
    y1,
    y2,
    y3,
    keep,
    send,
    vectors,
    w_out,
    w_up,
    w_down,
    slope,
    active,
    grad_up,
    context,
    sems,
):
    place, core, level = sc[1], sc[2], sc[3]
    blocks = w_up.shape[0]
    shard_rows = w_up.shape[3]
    width = w_up.shape[4]
    copies = []
    for b in range(blocks):
        copies.append(
            pltpu.make_async_copy(gathered.at[:, :, b, 0:shard_rows, :], w_up.at[b], sems.at[b])
        )
    down_copies = []
    for j in range(4):
        for k in range(4):
            for side, block in ((core, own_down), (1 - core, other_down)):
                down_copies.append(
                    pltpu.make_async_copy(
                        block.at[j, k],
                        w_down.at[level ^ k, side, place ^ j],
                        sems.at[7 + len(down_copies)],
                    )
                )
    out_copies = []
    for k in range(4):
        for side, block in ((core, own_out), (1 - core, other_out)):
            out_copies.append(
                pltpu.make_async_copy(
                    block.at[k], w_out.at[level ^ k, side], sems.at[40 + len(out_copies)]
                )
            )
    for copy in out_copies + copies + down_copies:
        copy.start()
    for copy in out_copies:
        copy.wait()
    out_rows = 2 * shard_rows

    def out_block(j):
        return w_out[place ^ j].reshape(out_rows, width)

    residual = token[...].astype(jnp.float32) + small[0:1, :]
    for j, block in enumerate((x0, x1, x2, x3)):
        residual = residual + dot_nn(block[...], out_block(j))
    unit_one, inverse_one = normalize(residual)
    gain_one = small[1:2, :]
    normed = unit_one * gain_one + small[2:3, :]
    normed_low = normed.astype(jnp.bfloat16)
    for b in range(blocks):
        copies[b].wait()
        span = slice(b * width, (b + 1) * width)
        up = dot_nn(normed_low, w_up[b].reshape(width, width)) + up_bias[:, span]
        phi = 0.5 + 0.5 * lax.erf(up * HALF_ROOT)
        slope[:, span] = phi + up * (jnp.exp(-0.5 * up * up) * NORMAL_SCALE)
        active[:, span] = (up * phi).astype(jnp.bfloat16)
    for copy in down_copies:
        copy.wait()
    residual = normed + small[3:4, :] + dot_nn(active[...], w_down[...].reshape(-1, width))
    unit_two, inverse_two = normalize(residual)
    gain_two = small[4:5, :]
    output[...] = (unit_two * gain_two + small[5:6, :]).astype(jnp.bfloat16)
    grad = cotangent[...].astype(jnp.float32)
    sum_rows = {
        3: jnp.sum(grad * unit_two, axis=0, keepdims=True),
        4: jnp.sum(grad, axis=0, keepdims=True),
    }
    grad_two = normalize_back(grad * gain_two, unit_two, inverse_two)
    sum_rows[5] = jnp.sum(grad_two, axis=0, keepdims=True)
    vectors[...] = jnp.zeros_like(vectors)
    half = width // 2
    two_low = grad_two.astype(jnp.bfloat16)
    grad_normed = grad_two
    for b in range(blocks):
        span = slice(b * width, (b + 1) * width)
        rows_down = w_down[b].reshape(width, width)
        part = dot_nt(two_low, rows_down) * slope[:, span]
        up_row = jnp.sum(part, axis=0, keepdims=True).astype(jnp.bfloat16)
        vectors[b, 3:4, :] = up_row[:, :half]
        vectors[b, 4:5, :] = up_row[:, half:]
        part = part.astype(jnp.bfloat16)
        grad_up[:, span] = part
        grad_normed = grad_normed + dot_nt(part, w_up[b].reshape(width, width))
    sum_rows[1] = jnp.sum(grad_normed * unit_one, axis=0, keepdims=True)
    sum_rows[2] = jnp.sum(grad_normed, axis=0, keepdims=True)
    first = normalize_back(grad_normed * gain_one, unit_one, inverse_one)
    sum_rows[0] = jnp.sum(first, axis=0, keepdims=True)
    for z in range(4):
        at = slice(z * out_rows, (z + 1) * out_rows)
        for row in range(3):
            pair = [sum_rows[2 * row][:, at], sum_rows[2 * row + 1][:, at]]
            vectors[z, row : row + 1, :] = jnp.concatenate(pair, axis=1).astype(jnp.bfloat16)
    grad_one[...] = first
    one_low = first.astype(jnp.bfloat16)
    for j, out in enumerate((y0, y1, y2, y3)):
        out[...] = dot_nt(one_low, out_block(j)).astype(jnp.bfloat16)
    for j, block in enumerate((x0, x1, x2, x3)):
        context[place ^ j] = block[...]
    joined = jnp.concatenate([context[j] for j in range(4)], axis=1)
    down_rows = blocks * shard_rows
    for ref, mine in ((keep, core), (send, 1 - core)):
        for z in range(4):
            even = active[:, (2 * z) * down_rows : (2 * z + 1) * down_rows]
            odd = active[:, (2 * z + 1) * down_rows : (2 * z + 2) * down_rows]
            ref[:, z * down_rows : (z + 1) * down_rows] = jnp.where(mine == 0, even, odd)
        at = 4 * down_rows
        ref[:, at : at + width] = two_low
        at += width
        ref[:, at : at + width] = normed_low
        at += width
        ref[:, at : at + 2 * width] = jnp.where(
            mine == 0, grad_up[:, : 2 * width], grad_up[:, 2 * width :]
        )
        at += 2 * width
        ref[:, at : at + width] = joined
        at += width
        ref[:, at : at + half] = jnp.where(mine == 0, one_low[:, :half], one_low[:, half:])


def down_grad_kernel(sc, keep, got, near, far, part):
    place = sc[1]
    _, zs, shard_rows, width = near.shape
    down_rows = 4 * shard_rows
    at_two = zs * down_rows
    def both(where):
        return jnp.concatenate([keep[:, where], got[:, where]], axis=0)

    right = both(slice(at_two, at_two + width))
    for z in range(zs):
        total = dot_tn(both(slice(z * down_rows, (z + 1) * down_rows)), right)
        part[...] = total.astype(jnp.bfloat16).reshape(4, shard_rows, width)
        for out, at, j in ((near, 0, 0), (near, 1, 2), (far, 0, 1), (far, 1, 3)):
            out[at, z] = part[place ^ j]


def up_grad_kernel(sc, keep, got, vectors, near, far, part):
    place = sc[1]
    _, zs, block_rows, cols = near.shape
    quarter = part.shape[2]
    pair_rows = block_rows - quarter - 16
    width = zs * pair_rows
    at_norm = 2 * width + width
    at_up = at_norm + width
    at_ctx = at_up + 2 * width
    at_one = at_ctx + width
    def both(where):
        return jnp.concatenate([keep[:, where], got[:, where]], axis=0)

    total = dot_tn(both(slice(at_ctx, at_ctx + width)), both(slice(at_one, at_one + cols)))
    part[...] = total.astype(jnp.bfloat16).reshape(part.shape)
    left = both(slice(at_norm, at_norm + width)).T
    for out, at, j in ((near, 0, 0), (near, 1, 1), (far, 0, 2), (far, 1, 3)):
        right = pl.ds(pl.multiple_of(at_up + (place ^ j) * cols, 128), cols)
        total = dot_nn(left, both(right)).astype(jnp.bfloat16)
        for z in range(zs):
            out[at, z, :pair_rows] = total[z * pair_rows : (z + 1) * pair_rows]
            out[at, z, pair_rows : pair_rows + quarter] = part[z, place ^ j]
            out[at, z, pair_rows + quarter :] = vectors[z]


def fold_kernel(near, got, mine, pass_on):
    for at, out in ((0, mine), (1, pass_on)):
        total = near[at].astype(jnp.float32) + got[at].astype(jnp.float32)
        out[...] = total.astype(jnp.bfloat16)


def level_fold_kernel(sc, mine, got, near, far):
    level = sc[3]
    for out, at, k in ((near, 0, 0), (near, 1, 2), (far, 0, 1), (far, 1, 3)):
        total = mine[level ^ k].astype(jnp.float32) + got[level ^ k].astype(jnp.float32)
        out[at] = total.astype(jnp.bfloat16)


def level_merge_kernel(sc, d_mine, d_got, u_mine, u_got, *outs):
    level = sc[3]
    up_rows, cols = u_mine.shape[1:]
    rows = d_mine.shape[1]
    for k, out in enumerate(outs):
        total = u_mine[level ^ k].astype(jnp.float32) + u_got[level ^ k].astype(jnp.float32)
        out[:up_rows] = total.astype(jnp.bfloat16)
        total = d_mine[level ^ k].astype(jnp.float32) + d_got[level ^ k].astype(jnp.float32)
        total = total.astype(jnp.bfloat16)
        out[up_rows : up_rows + rows] = total[:, :cols]
        out[up_rows + rows :] = total[:, cols:]


def block_sum(refs):
    total = refs[0][...].astype(jnp.float32)
    for ref in refs[1:]:
        total = total + ref[...].astype(jnp.float32)
    return total


def split_up_kernel(sc, e0, e1, e2, e3, keep, send, down, held):
    core = sc[2]
    shard_rows, width = down.shape
    cols = width // 2
    half_rows = keep.shape[0] - shard_rows
    held[...] = block_sum((e0, e1, e2, e3)).astype(jnp.bfloat16)
    for ref, side in ((keep, core), (send, 1 - core)):
        ref[:shard_rows] = held[pl.ds(pl.multiple_of(side * shard_rows, 16), shard_rows), :]
        ref[shard_rows:] = held[2 * shard_rows : 2 * shard_rows + half_rows, :]
    at = 2 * shard_rows + half_rows
    down[:, :cols] = held[at : at + shard_rows, :]
    down[:, cols:] = held[at + shard_rows :, :]


def join_kernel(sc, down, keep, got, out, six, up_row):
    core = sc[2]
    shard_rows = down.shape[0]
    cols = keep.shape[1]
    out[:shard_rows] = down[...]
    for ref, side in ((keep, core), (got, 1 - core)):
        out[shard_rows:, pl.ds(pl.multiple_of(side * cols, 128), cols)] = ref[:-16]
    vectors = keep[-16:].astype(jnp.float32) + got[-16:].astype(jnp.float32)
    for row in range(3):
        for side in range(2):
            pair = vectors[row : row + 1, side * 2 * shard_rows : (side + 1) * 2 * shard_rows]
            six[2 * row + side : 2 * row + side + 1, :] = jnp.where(
                core == 0, pair[:, :shard_rows], pair[:, shard_rows:]
            )
    up_row[...] = jnp.where(core == 0, vectors[3:4], vectors[4:5])


def finish_kernel(sc, b0, b1, b2, b3, down, up, out):
    place, core = sc[1], sc[2]
    shard_rows = up.shape[0]
    quarter = shard_rows // 2
    cols = b0.shape[1] // 2
    for j, ref in enumerate((b0, b1, b2, b3)):
        where = place ^ j
        rows = pl.ds(pl.multiple_of(where * shard_rows, 8), shard_rows)
        down[rows, :] = ref[:shard_rows].astype(jnp.float32)
        for side in range(2):
            at = pl.multiple_of((side * 4 + where) * cols, 128)
            up[:, pl.ds(at, cols)] = ref[
                shard_rows : 2 * shard_rows, side * cols : (side + 1) * cols
            ].astype(jnp.float32)

        @pl.when(where // 2 == core)
        def _(ref=ref, where=where):
            at = pl.multiple_of((where % 2) * quarter, 8)
            out[pl.ds(at, quarter), :] = ref[2 * shard_rows :].astype(jnp.float32)


def sum_kernel(e0, e1, out):
    out[...] = block_sum((e0, e1)).astype(out.dtype)


def finish_qkv_kernel(sc, b0, b1, b2, b3, out, q_out, v_out, held):
    place, core, level = sc[1], sc[2], sc[3]
    shard_rows = out.shape[0]
    head_width = b0.shape[1] // 3
    for j, ref in enumerate((b0, b1, b2, b3)):
        held[place ^ j] = ref[...].astype(jnp.float32)
    for part in range(3):
        for s in range(4):
            at = (part * 4 + s) * head_width
            out[:, at : at + head_width] = held[
                s, :shard_rows, part * head_width : (part + 1) * head_width
            ]
    row = held[level, shard_rows : shard_rows + 1, :]
    for ref, at in ((q_out, 0), (v_out, 2 * head_width)):
        ref[...] = jnp.where(
            core == 0, row[:, at : at + shard_rows], row[:, at + shard_rows : at + 2 * shard_rows]
        )


def fast_body(
    tokens,
    lengths,
    w_qkv,
    q_bias,
    v_bias,
    w_out,
    out_bias,
    gain_one,
    shift_one,
    w_up,
    up_bias,
    w_down,
    down_bias,
    gain_two,
    shift_two,
    cotangent,
):
    bf16, f32 = jnp.bfloat16, jnp.float32
    _, rows, width = tokens.shape
    shard_rows = w_qkv.shape[0]
    hidden = w_up.shape[1]
    head_width = width // 4
    place = lax.axis_index("seq")
    core = lax.axis_index("core")
    zs = 4
    swap = [(0, 1), (1, 0)]

    def struct(shape, dtype=bf16):
        return jax.ShapeDtypeStruct(shape, dtype)

    def across(value, step):
        return lax.ppermute(value, "seq", [(i, i ^ step) for i in range(4)])

    def partner(value):
        return lax.ppermute(value, "core", swap)

    def level_across(value, step):
        return lax.ppermute(value, "z", [(i, i ^ step) for i in range(4)])

    token = tokens[0]
    quarter = jnp.concatenate(
        [
            lax.dynamic_slice_in_dim(w_up, place * width, width, axis=1),
        ],
        axis=0,
    )
    gathered = lax.all_gather(quarter, ("z", "core", "seq"), axis=0, tiled=True)
    gathered = gathered.reshape(zs, 2, 4, shard_rows, width)
    vectors = (q_bias, v_bias, out_bias, gain_one, shift_one)
    vectors += (down_bias, gain_two, shift_two, up_bias)
    own_block = pl.pallas_call(
        pack_kernel,
        name="pack",
        cost_estimate=work(2),
        out_shape=struct((shard_rows + 16, 3 * head_width)),
        in_specs=[smem_spec()] + vmem_specs(1 + len(vectors)),
        out_specs=pl.BlockSpec(memory_space=pltpu.VMEM),
    )(place[None].astype(jnp.int32), w_qkv, *[vector[None] for vector in vectors])
    t1, t2, t3 = across(token, 1), across(token, 2), across(token, 3)
    two_cols = jnp.stack([own_block, level_across(own_block, 1)])
    own_cols = jnp.concatenate([two_cols, level_across(two_cols, 2)])
    down_quarter = lax.dynamic_slice_in_dim(w_down, place * shard_rows, shard_rows, axis=0)
    two_down = jnp.stack([down_quarter, level_across(down_quarter, 1)])
    own_down = jnp.concatenate([two_down, level_across(two_down, 2)])
    own_down, own_cols, t1, t2, t3 = lax.optimization_barrier((own_down, own_cols, t1, t2, t3))
    other_cols = partner(own_cols)
    late_out, _ = lax.optimization_barrier((w_out, own_cols))
    two_out = jnp.stack([late_out, level_across(late_out, 1)])
    own_out = jnp.concatenate([two_out, level_across(two_out, 2)])
    other_out = partner(own_out)
    t1, own_out = lax.optimization_barrier((t1, own_out))
    down_sets = [own_down] + [across(own_down, j) for j in (1, 2, 3)]
    sc = jnp.stack([lengths[0], place, core, lax.axis_index("z")]).astype(jnp.int32)
    all_rows = 4 * rows
    qkv, ctx_t, c0, c1, c2, c3, lse, full_qkv, small, full_up_bias = pl.pallas_call(
        attend_forward_kernel,
        name="attend_forward",
        cost_estimate=work(13),
        out_shape=(
            struct((all_rows, 3 * head_width)),
            struct((head_width, all_rows), f32),
            struct((rows, head_width)),
            struct((rows, head_width)),
            struct((rows, head_width)),
            struct((rows, head_width)),
            struct((head_width // HEAD_DIM, all_rows), f32),
            struct((zs, 2, shard_rows, 3 * head_width)),
            struct((8, width), f32),
            struct((1, hidden), f32),
        ),
        in_specs=[smem_spec()] + vmem_specs(6),
        out_specs=tuple(vmem_specs(10)),
        scratch_shapes=[
            pltpu.VMEM((4, rows, head_width), bf16),
            pltpu.VMEM((zs, 2, 16, 3 * head_width), f32),
        ],
    )(sc, token, t1, t2, t3, own_cols, other_cols)
    x1, x2, x3 = across(c1, 1), across(c2, 2), across(c3, 3)
    down_sets[0], _ = lax.optimization_barrier((down_sets[0], c0))
    own_down = jnp.stack(down_sets)
    other_down = partner(own_down)
    packed = hidden // 2 + 5 * width + width // 2
    output, grad_one, y0, y1, y2, y3, keep, send, vector_rows = pl.pallas_call(
        middle_kernel,
        name="middle",
        cost_estimate=work(15),
        out_shape=(
            struct((rows, width)),
            struct((rows, width), f32),
            struct((rows, head_width)),
            struct((rows, head_width)),
            struct((rows, head_width)),
            struct((rows, head_width)),
            struct((rows, packed)),
            struct((rows, packed)),
            struct((zs, 16, hidden // 8)),
        ),
        in_specs=[smem_spec()]
        + vmem_specs(8)
        + [pl.BlockSpec(memory_space=pl.ANY)] * 5,
        out_specs=tuple(vmem_specs(9)),
        scratch_shapes=[
            pltpu.VMEM((zs, 2, shard_rows, width), bf16),
            pltpu.VMEM((4, zs, 2, shard_rows, width), bf16),
            pltpu.VMEM((zs, 2, 4, shard_rows, width), bf16),
            pltpu.VMEM((rows, hidden), f32),
            pltpu.VMEM((rows, hidden), bf16),
            pltpu.VMEM((rows, hidden), bf16),
            pltpu.VMEM((4, rows, head_width), bf16),
            pltpu.SemaphoreType.DMA((48,)),
        ],
    )(
        sc,
        c0,
        x1,
        x2,
        x3,
        token,
        cotangent[0],
        small,
        full_up_bias,
        gathered,
        own_down,
        other_down,
        own_out,
        other_out,
    )
    g1, g2, g3 = across(y1, 1), across(y2, 2), across(y3, 3)
    got, g1, g2, g3 = lax.optimization_barrier((partner(send), g1, g2, g3))
    quad = hidden // 8

    def call(kernel, micros, outs, *args, scratch=(), scalars=True):
        return pl.pallas_call(
            kernel,
            name=kernel.__name__.replace("_kernel", ""),
            cost_estimate=work(micros),
            out_shape=tuple(outs),
            in_specs=([smem_spec()] if scalars else []) + vmem_specs(len(args)),
            out_specs=tuple(vmem_specs(len(outs))),
            scratch_shapes=list(scratch),
        )(*(((sc,) if scalars else ()) + args))

    d_near, d_far = call(
        down_grad_kernel,
        4,
        [struct((2, zs, shard_rows, width))] * 2,
        keep,
        got,
        scratch=[pltpu.VMEM((4, shard_rows, width), bf16)],
    )
    block_rows = 2 * shard_rows + shard_rows // 2 + 16
    u_near, u_far = call(
        up_grad_kernel,
        4,
        [struct((2, zs, block_rows, quad))] * 2,
        keep,
        got,
        vector_rows,
        scratch=[pltpu.VMEM((zs, 4, shard_rows // 2, quad), bf16)],
    )
    d_got = across(d_far, 1)
    u_got = across(u_far, 2)
    y0, d_near, u_near = lax.optimization_barrier((y0, d_near, u_near))

    dqkv = pl.pallas_call(
        attend_backward_kernel,
        name="attend_backward",
        cost_estimate=work(11),
        out_shape=struct((all_rows, 3 * head_width)),
        in_specs=[smem_spec()] + vmem_specs(7),
        out_specs=pl.BlockSpec(memory_space=pltpu.VMEM),
        scratch_shapes=[
            pltpu.VMEM((head_width // HEAD_DIM, all_rows, HEAD_DIM), f32),
            pltpu.VMEM((head_width // HEAD_DIM, all_rows, HEAD_DIM), f32),
            pltpu.VMEM((4, rows, head_width), bf16),
        ],
    )(sc, qkv, ctx_t, lse, y0, g1, g2, g3)
    q_rows = shard_rows + 16
    q_keep, q_send = pl.pallas_call(
        grad_qkv_weight_kernel,
        name="grad_qkv_weight",
        cost_estimate=work(4),
        out_shape=(
            struct((zs, q_rows, 3 * head_width)),
            struct((zs, q_rows, 3 * head_width)),
        ),
        in_specs=[smem_spec()] + vmem_specs(5),
        out_specs=tuple(vmem_specs(2)),
    )(sc, token, t1, t2, t3, dqkv)
    d_near, u_near, q_keep = lax.optimization_barrier((d_near, u_near, q_keep))
    d_mine, d_pass = call(
        fold_kernel, 1, [struct((zs, shard_rows, width))] * 2, d_near, d_got, scalars=False
    )
    u_mine, u_pass = call(
        fold_kernel, 1, [struct((zs, block_rows, quad))] * 2, u_near, u_got, scalars=False
    )
    q_got = partner(q_send)
    late_dqkv, q_keep = lax.optimization_barrier((dqkv, q_keep))
    (token_parts,) = call(
        grad_tokens_kernel,
        4,
        [struct((4, rows, width))],
        late_dqkv,
        full_qkv,
    )
    q_near, q_far = call(
        level_fold_kernel, 1, [struct((2, q_rows, 3 * head_width))] * 2, q_keep, q_got
    )

    def level_sum(near, far, shape):
        mine, pass_on = call(
            fold_kernel, 1, [struct(shape)] * 2, near, level_across(far, 1), scalars=False
        )
        return mine, level_across(pass_on, 2)

    q_mine, q_last = level_sum(q_near, q_far, (q_rows, 3 * head_width))
    (q_part,) = call(
        sum_kernel, 1, [struct((q_rows, 3 * head_width))], q_mine, q_last, scalars=False
    )

    d_mine, u_mine, _ = lax.optimization_barrier((d_mine, u_mine, q_mine))
    merged_rows = block_rows + 2 * shard_rows
    blocks = call(
        level_merge_kernel,
        2,
        [struct((merged_rows, quad))] * 4,
        d_mine,
        across(d_pass, 2),
        u_mine,
        across(u_pass, 1),
    )
    token_parts, _ = lax.optimization_barrier((token_parts, blocks[0]))
    token_sum = lax.psum_scatter(
        token_parts.reshape(4 * rows, width), "seq", scatter_dimension=0, tiled=True
    )
    q_others = [across(q_part, j) for j in (1, 2, 3)]
    merged = [blocks[0]] + [level_across(blocks[k], k) for k in (1, 2, 3)]
    merged, q_others = lax.optimization_barrier((merged, q_others))
    half_rows = shard_rows + shard_rows // 2 + 16
    u_keep, u_send, d_part = call(
        split_up_kernel,
        1,
        [struct((half_rows, quad))] * 2 + [struct((shard_rows, width))],
        *merged,
        scratch=[pltpu.VMEM((merged_rows, quad), bf16)],
    )
    joined, six, up_row = call(
        join_kernel,
        1,
        [struct((shard_rows + half_rows - 16, width)), struct((8, shard_rows), f32), struct((1, quad), f32)],
        d_part,
        u_keep,
        partner(u_send),
    )
    joined, token_sum, q_others = lax.optimization_barrier((joined, token_sum, q_others))
    result_down, result_up, result_out = call(
        finish_kernel,
        2,
        [
            struct((4 * shard_rows, width), f32),
            struct((shard_rows, hidden), f32),
            struct((shard_rows, width), f32),
        ],
        joined,
        *[across(joined, j) for j in (1, 2, 3)],
    )
    result_qkv, result_q_bias, result_v_bias = call(
        finish_qkv_kernel,
        1,
        [struct((shard_rows, 3 * width), f32)] + [struct((1, shard_rows), f32)] * 2,
        q_part,
        *q_others,
        scratch=[pltpu.VMEM((4, q_rows, 3 * head_width), f32)],
    )
    grad_tokens = (grad_one + token_sum.astype(f32)).astype(bf16)

    return (
        output[None],
        grad_tokens[None],
        result_qkv,
        result_q_bias[0],
        result_v_bias[0],
        result_out,
        six[0],
        six[1],
        six[2],
        result_up,
        up_row[0],
        result_down,
        six[5],
        six[3],
        six[4],
    )


def solution(mesh):
    seq_count, shard_count = mesh.shape["seq"], mesh.shape["shard"]
    fast = seq_count == 4 and shard_count == 8
    if fast:
        grid = mesh.devices.reshape(seq_count, shard_count // 2, 2)
        mesh = jax.sharding.Mesh(grid, AXES)
    shard = ("z", "core") if fast else "shard"
    vector, matrix, rows = P(shard), P(shard, None), P(shard, "seq", None)
    return jax.shard_map(
        fast_body if fast else body,
        mesh=mesh,
        in_specs=(
            rows,
            vector,
            matrix,
            vector,
            vector,
            matrix,
            vector,
            vector,
            vector,
            matrix,
            vector,
            matrix,
            vector,
            vector,
            vector,
            rows,
        ),
        out_specs=(
            rows,
            rows,
            matrix,
            vector,
            vector,
            matrix,
            vector,
            vector,
            vector,
            matrix,
            vector,
            matrix,
            vector,
            vector,
            vector,
        ),
        check_vma=False,
    )
```
